32 devices in a mesh: dp: 8 (over z, core), tensor: 4 (over y, x).
Axes of the slice: x: 2, y: 2, z: 4, core: 2. Of those that a mesh axis runs over, the one named last changes fastest.
Arguments:
- hidden: bfloat16 [8192, 2048], P('dp'), may hold values from -6 to 6
- lengths: int32 [8], P('dp'), may hold values from 256 to 1024, as said below
- routes: int32 [8192, 6], P('dp'), may hold values from 0 to 15, all different within a row; in each aligned block of 1024 rows (0 to 1023, 1024 to 2047, ...) at most 512 rows name the same one
- attn_gain: bfloat16 [2048], P('dp'), may hold values from 0.5 to 1.5
- w_query: bfloat16 [2048, 3072], P('dp', 'tensor'), may hold values from -0.125 to 0.125
- w_kv_down: bfloat16 [2048, 576], P('dp'), may hold values from -0.125 to 0.125
- kv_gain: bfloat16 [512], P('dp'), may hold values from 0.5 to 1.5
- w_kv_up: bfloat16 [512, 4096], P('dp', 'tensor'), may hold values from -0.25 to 0.25
- w_out: bfloat16 [2048, 2048], P('tensor', 'dp'), may hold values from -2 to 2
- ffn_gain: bfloat16 [2048], P('dp'), may hold values from 0.5 to 1.5
- w_router: bfloat16 [2048, 16], P('dp'), may hold values from -0.0625 to 0.0625
- w_expert_in: bfloat16 [16, 2, 2048, 1408], P(None, None, 'dp', 'tensor'), may hold values from -0.125 to 0.125
- w_expert_out: bfloat16 [16, 1408, 2048], P(None, 'tensor', 'dp'), may hold values from -1.75 to 1.75
- w_shared_in: bfloat16 [2, 2048, 2816], P(None, 'dp', 'tensor'), may hold values from -0.125 to 0.125
- w_shared_out: bfloat16 [2816, 2048], P('tensor', 'dp'), may hold values from -0.1875 to 0.1875
- cotangent: bfloat16 [8192, 2048], P('dp'), may hold values from -6 to 6
Outputs:
- output: bfloat16 [8192, 2048], P('dp')
- grad_hidden: bfloat16 [8192, 2048], P('dp')
- grad_attn_gain: float32 [2048], P('dp')
- grad_w_query: float32 [2048, 3072], P('dp', 'tensor')
- grad_w_kv_down: float32 [2048, 576], P('dp')
- grad_kv_gain: float32 [512], P('dp')
- grad_w_kv_up: float32 [512, 4096], P('dp', 'tensor')
- grad_w_out: float32 [2048, 2048], P('tensor', 'dp')
- grad_ffn_gain: float32 [2048], P('dp')
- grad_w_router: float32 [2048, 16], P('dp')
- grad_w_expert_in: float32 [16, 2, 2048, 1408], P(None, None, 'dp', 'tensor')
- grad_w_expert_out: float32 [16, 1408, 2048], P(None, 'tensor', 'dp')
- grad_w_shared_in: float32 [2, 2048, 2816], P(None, 'dp', 'tensor')
- grad_w_shared_out: float32 [2816, 2048], P('tensor', 'dp')
The draws below stay inside these ranges and needn't reach their ends.
Inputs may be any that keep to these rules, and one draw needn't show every extreme that they name: `lengths`: valid tokens of a slot; at least one slot is full. `routes`: each row names 6 different experts; among the 1024 rows of one slot no expert is named more than 512 times, a bound that some block reaches.
All inputs are finite; a program needn't handle non-finite values.
Results may differ from the reference program's by a relative error of at most 0.028.
Values may be sent and summed in bfloat16 or wider, within the bound.
No kernel may reach another device: no remote copies, remote signals or barrier semaphores. Data moves between devices by JAX's collectives and lax.ppermute only.
A program may use at most 448 MiB of HBM per device.

```python
import math
import jax
import jax.numpy as jnp
import numpy as np
from jax import lax

D = 2048
H = 16
NOPE = 128
ROPE = 64
VDIM = 128
LATENT = 512
FFE = 1408
TOP = 6
EXPERTS = 16
SEQ = 1024
FFS = 2816
CAP = 512
SLOTS = 8
TOKENS = 8192


def draw_lengths(key, part):
    first, second = jax.random.split(key)
    values = jax.random.randint(first, (SLOTS,), SEQ // 4, SEQ + 1, dtype=jnp.int32)
    full_slot = jax.random.randint(second, (), 0, SLOTS, dtype=jnp.int32)
    return jnp.where(jnp.arange(SLOTS, dtype=jnp.int32) == full_slot, SEQ, values).astype(jnp.int32)


def block_levels(stream_key, dims, shards, low, top_value):
    factor_of = 1.0
    for dim, parts in shards:
        draws = jax.random.uniform(jax.random.fold_in(jax.random.fold_in(stream_key, 6), dim), (parts,), jnp.float32, low / len(shards), top_value / len(shards))
        factor_of = factor_of * jnp.repeat(jnp.exp(draws), dims[dim] // parts).reshape((-1,) + (1,) * (len(dims) - 1 - dim))
    return factor_of


def assign_block(stream_key, own, number, rows, number_of, top, most, skew):
    ranking = jax.random.permutation(stream_key, number_of)
    packed, common = load_shares(number_of, rows * top, most, skew, True), load_shares(number_of, rows * top, most, skew, False)
    places = jnp.arange(number_of)

    def named(tallies, rotation):
        used = int((tallies > 0).sum())
        fixed = max(1, used // 4)
        moved = fixed + (places - fixed + rotation * (used - fixed)) % max(1, number_of - fixed)
        return jnp.zeros((number_of,), jnp.int32).at[ranking[jnp.where(places < fixed, places, moved)]].set(jnp.asarray(tallies, jnp.int32))

    tallies = jnp.where(number % 4 == 0, named(packed, number // 4), named(common, number - number // 4 - 1))
    mixed = jax.random.permutation(jax.random.fold_in(own, 3), number_of)
    giver, sink = mixed[0:number_of // 2 * 2:2], mixed[1:number_of // 2 * 2:2]
    room = jnp.minimum(tallies[giver] - 1, most - tallies[sink]) // 2
    room = jnp.where((giver == ranking[0]) | (sink == ranking[0]) | (tallies[sink] == 0), 0, jnp.maximum(room, 0))
    moved = jax.random.randint(jax.random.fold_in(own, 4), (number_of // 2,), 0, 1 << 20) % (room + 1)
    tallies = tallies.at[giver].add(-moved).at[sink].add(moved)
    members = jnp.searchsorted(jnp.cumsum(tallies), jnp.arange(rows * top), side="right").astype(jnp.int32)
    grid = members.reshape(top, rows).T
    grid = grid[jax.random.permutation(jax.random.fold_in(own, 1), rows)]
    rotation = jax.random.randint(jax.random.fold_in(own, 2), (rows, 1), 0, top)
    return jnp.take_along_axis(grid, (jnp.arange(top)[None, :] + rotation) % top, axis=1)


def load_shares(count, total, reach, slope, full):
    loads = [(1 << 20) // math.isqrt(grade ** slope) + 1 for grade in range(1, count + 1)]
    largest = reach if full else min(reach, max(-(-total // count), total * loads[0] // sum(loads)))
    least = 1 if total - largest >= count - 1 else 0
    given, spare = [largest] + [least] * (count - 1), total - largest - least * (count - 1)
    while spare > 0:
        candidates = [i for i in range(1, count) if given[i] < largest] or [i for i in range(1, count) if given[i] < reach]
        pool, remaining = sum([loads[i] for i in candidates]), spare
        for i in candidates:
            more = min(reach - given[i], max(1, remaining * loads[i] // pool), spare)
            given[i] = given[i] + more
            spare = spare - more
    return np.array(given)


def scatter_about(own_key, dims, scale, limit, cuts=(), kind=jnp.bfloat16):
    gain = block_levels(own_key, dims, cuts, -0.22, 0.18) if cuts else 1.0
    values = jax.random.normal(own_key, dims, jnp.float32) * scale * gain
    return jnp.minimum(jnp.maximum(values, -limit), limit).astype(kind)


def setup_inputs(seed: int = 0) -> dict:
    arg_keys = jax.random.split(jax.random.key(seed), 17)
    hidden = scatter_about(arg_keys[0], (TOKENS, D), 1.0, 6.0, ((0, 8),))
    lengths = draw_lengths(jax.random.fold_in(arg_keys[16], 71), 0)
    routes_keys = jax.random.split(jax.random.fold_in(arg_keys[2], 1), TOKENS // SEQ)
    routes_turns = jax.random.permutation(jax.random.fold_in(arg_keys[2], 3), TOKENS // SEQ)
    routes = jax.vmap(lambda own, number: assign_block(jax.random.fold_in(arg_keys[2], 2), own, number, SEQ, EXPERTS, TOP, CAP, 1))(routes_keys, routes_turns).reshape((TOKENS, TOP))
    attn_gain = jnp.clip(1.0 + 0.1 * jax.random.normal(arg_keys[3], (D,), jnp.float32), 0.5, 1.5).astype(jnp.bfloat16)
    w_query = scatter_about(arg_keys[4], (D, H * (NOPE + ROPE)), D ** -0.5, 0.125, ((0, 8), (1, 4)))
    w_kv_down = scatter_about(arg_keys[5], (D, LATENT + ROPE), D ** -0.5, 0.125, ((0, 8),))
    kv_gain = jnp.clip(1.0 + 0.1 * jax.random.normal(arg_keys[6], (LATENT,), jnp.float32), 0.5, 1.5).astype(jnp.bfloat16)
    w_kv_up = scatter_about(arg_keys[7], (LATENT, H * (NOPE + VDIM)), LATENT ** -0.5, 0.25, ((0, 8), (1, 4)))
    w_out = scatter_about(arg_keys[8], (H * VDIM, D), (max(H * VDIM // 256, 1)) ** -0.5, 2.0, ((0, 4), (1, 8)))
    ffn_gain = jnp.clip(1.0 + 0.1 * jax.random.normal(arg_keys[9], (D,), jnp.float32), 0.5, 1.5).astype(jnp.bfloat16)
    w_router = scatter_about(arg_keys[10], (D, EXPERTS), (4 * D) ** -0.5, 0.0625, ((0, 8),))
    w_expert_in = scatter_about(arg_keys[11], (EXPERTS, 2, D, FFE), D ** -0.5, 0.125, ((2, 8), (3, 4)))
    w_expert_out = scatter_about(arg_keys[12], (EXPERTS, FFE, D), (max(FFE // 128, 1)) ** -0.5, 1.75, ((1, 4), (2, 8)))
    w_shared_in = scatter_about(arg_keys[13], (2, D, FFS), D ** -0.5, 0.125, ((1, 8), (2, 4)))
    w_shared_out = scatter_about(arg_keys[14], (FFS, D), (FFS // 3) ** -0.5, 0.1875, ((0, 4), (1, 8)))
    cotangent = scatter_about(arg_keys[15], (TOKENS, D), 1.0, 6.0, ((0, 8),))
    return {"hidden": hidden, "lengths": lengths, "routes": routes, "attn_gain": attn_gain, "w_query": w_query, "w_kv_down": w_kv_down, "kv_gain": kv_gain, "w_kv_up": w_kv_up, "w_out": w_out, "ffn_gain": ffn_gain, "w_router": w_router, "w_expert_in": w_expert_in, "w_expert_out": w_expert_out, "w_shared_in": w_shared_in, "w_shared_out": w_shared_out, "cotangent": cotangent}


EPSILON = 1e-06
NEGATIVE = -1e+30
HIGH = lax.Precision.HIGHEST

@jax.custom_vjp
def low(v):
    return lax.optimization_barrier(v.astype(jnp.bfloat16)).astype(jnp.float32)

@jax.custom_vjp
def low_back(v):
    return v

def low_keep(v):
    return (low(v), None)

def low_pass(kept, grad):
    return (grad,)

def back_keep(v):
    return (v, None)

def back_low(kept, grad):
    return (low(grad),)
low.defvjp(low_keep, low_pass)
low_back.defvjp(back_keep, back_low)

def rotate(values, cosine, sine):
    half = values.shape[-1] // 2
    first = values[..., :half]
    second = values[..., half:]
    return jnp.concatenate([first * cosine - second * sine, second * cosine + first * sine], -1)

def angle_tables(rows_count):
    positions = jnp.arange(rows_count, dtype=jnp.float32)
    freqs = jnp.exp(jnp.arange(ROPE // 2, dtype=jnp.float32) * (-2.0 * math.log(10000.0) / ROPE))
    angles = positions[:, None] * freqs[None, :]
    return (jnp.cos(angles), jnp.sin(angles))

def slot_table(route_ids, rows_count):
    flat = route_ids.reshape(-1)
    onehot = (flat[:, None] == jnp.arange(EXPERTS, dtype=jnp.int32)[None, :]).astype(jnp.int32)
    before = jnp.cumsum(onehot, axis=0) - onehot
    position = lax.optimization_barrier(jnp.sum(before * onehot, axis=1))
    slot_index = (flat * CAP + position).astype(jnp.int32)
    owners = jnp.arange(rows_count * TOP, dtype=jnp.int32) // TOP
    source = jnp.full((EXPERTS * CAP,), rows_count, jnp.int32).at[slot_index].set(owners)
    return (slot_index, source)

def normalize(values):
    return values * lax.rsqrt(lax.optimization_barrier(jnp.mean(values * values, axis=-1, keepdims=True)) + EPSILON)

def expert_apply(items):
    rows_in, weight_in, weight_out = items
    gate_up = low_back(jnp.einsum('rd,gdf->grf', rows_in, weight_in, precision=HIGH))
    active = low(jax.nn.silu(gate_up[0]) * gate_up[1])
    return low_back(jnp.dot(active, weight_out, precision=HIGH))

def layer(inputs, params, valid_length, route, slot_index, source):
    gain_attn, query_w, down_w, gain_kv, up_w, out_w, gain_ffn, router_w, expert_in, expert_out, shared_in, shared_out = params
    cosine, sine = angle_tables(SEQ)
    normed_low = low(normalize(inputs) * gain_attn)
    query = low_back(jnp.dot(normed_low, query_w, precision=HIGH)).reshape(SEQ, H, NOPE + ROPE)
    query_cat = low(jnp.concatenate([query[..., :NOPE], rotate(query[..., NOPE:], cosine[:, None, :], sine[:, None, :])], -1))
    latent_all = low_back(jnp.dot(normed_low, down_w, precision=HIGH))
    latent_low = low(normalize(latent_all[:, :LATENT]) * gain_kv)
    key_rope = low(rotate(latent_all[:, LATENT:], cosine, sine))
    keys_values = low(low_back(jnp.dot(latent_low, up_w, precision=HIGH))).reshape(SEQ, H, NOPE + VDIM)
    raw = jnp.einsum('ihd,jhd->hij', query_cat[..., :NOPE], keys_values[..., :NOPE], precision=HIGH)
    raw = raw + jnp.einsum('ihd,jd->hij', query_cat[..., NOPE:], key_rope, precision=HIGH)
    raw = raw * (NOPE + ROPE) ** (-0.5)
    positions = jnp.arange(SEQ, dtype=jnp.int32)
    allowed = (positions[None, :] <= positions[:, None]) & (positions[None, :] < valid_length)
    scores = jnp.where(allowed[None], low_back(raw), NEGATIVE)
    probs_low = low(jax.nn.softmax(scores, axis=-1))
    attended = jnp.einsum('hij,jhd->ihd', probs_low, keys_values[..., NOPE:], precision=HIGH).reshape(SEQ, H * VDIM)
    attended_low = low(low_back(attended))
    residual = inputs + low_back(jnp.dot(attended_low, out_w, precision=HIGH))
    ffn_low = low(normalize(residual) * gain_ffn)
    router_probs = jax.nn.softmax(jnp.dot(ffn_low, router_w, precision=HIGH), axis=-1)
    gate_values = jnp.take_along_axis(router_probs, route, axis=1)
    ffn_pad = jnp.concatenate([ffn_low, jnp.zeros((1, D), jnp.float32)], 0)
    expert_rows = ffn_pad[source].reshape(EXPERTS, CAP, D)
    expert_outs = lax.map(jax.checkpoint(expert_apply), (expert_rows, expert_in, expert_out))
    pair_outs = expert_outs.reshape(EXPERTS * CAP, D)[slot_index].reshape(SEQ, TOP, D)
    routed = lax.optimization_barrier(jnp.sum(gate_values[:, :, None] * pair_outs, axis=1))
    shared_pre = low_back(jnp.einsum('sd,gdf->gsf', ffn_low, shared_in, precision=HIGH))
    shared_act = low(jax.nn.silu(shared_pre[0]) * shared_pre[1])
    shared_part = low_back(jnp.dot(shared_act, shared_out, precision=HIGH))
    return residual + routed + shared_part

def reference(hidden, lengths, routes, attn_gain, w_query, w_kv_down, kv_gain, w_kv_up, w_out, ffn_gain, w_router, w_expert_in, w_expert_out, w_shared_in, w_shared_out, cotangent):
    weights = (attn_gain.astype(jnp.float32), w_query.astype(jnp.float32), w_kv_down.astype(jnp.float32), kv_gain.astype(jnp.float32), w_kv_up.astype(jnp.float32), w_out.astype(jnp.float32), ffn_gain.astype(jnp.float32), w_router.astype(jnp.float32), w_expert_in.astype(jnp.float32), w_expert_out.astype(jnp.float32), w_shared_in.astype(jnp.float32), w_shared_out.astype(jnp.float32))
    hidden_slots = hidden.astype(jnp.float32).reshape(SLOTS, SEQ, D)
    cot_slots = cotangent.astype(jnp.float32).reshape(SLOTS, SEQ, D)
    route_slots = routes.reshape(SLOTS, SEQ, TOP)

    def slot_step(totals, items):
        inputs, valid_length, route, cot = items
        slot_index, source = slot_table(route, SEQ)

        def forward(values, params):
            return layer(values, params, valid_length, route, slot_index, source)
        result, pull = jax.vjp(forward, inputs, weights)
        valid = (jnp.arange(SEQ, dtype=jnp.int32) < valid_length).astype(result.dtype)
        input_grad, weight_grads = pull(cot * valid[:, None])
        totals = jax.tree.map(lambda a, b: a + b, totals, weight_grads)
        return (totals, (result.astype(jnp.bfloat16), input_grad.astype(jnp.bfloat16)))
    initial = jax.tree.map(jnp.zeros_like, weights)
    totals, (results, input_grads) = lax.scan(slot_step, initial, (hidden_slots, lengths, route_slots, cot_slots))
    return (results.reshape(TOKENS, D), input_grads.reshape(TOKENS, D), totals[0], totals[1], totals[2], totals[3], totals[4], totals[5], totals[6], totals[7], totals[8], totals[9], totals[10], totals[11])
```

```python
import functools
import math

import jax
import jax.numpy as jnp
from jax import lax
from jax.experimental import pallas as pl
from jax.experimental.pallas import tpu as pltpu
from jax.sharding import PartitionSpec as P

NOPE = 128
ROPE = 64
VDIM = 128
LATENT = 512
TOP = 6
EXPERTS = 16
CAP = 512

EPSILON = 1e-06
NEGATIVE = -1e30
F32 = jnp.float32
BF16 = jnp.bfloat16


def dot(a, b):
    return jnp.dot(a, b, preferred_element_type=F32)


def dot_nt(a, b):
    return lax.dot_general(a, b, (((1,), (1,)), ((), ())), preferred_element_type=F32)


def dot_tn(a, b):
    return lax.dot_general(a, b, (((0,), (0,)), ((), ())), preferred_element_type=F32)


def rotate(first, second, cosine, sine):
    return first * cosine - second * sine, second * cosine + first * sine


def rotate_back(first, second, cosine, sine):
    return first * cosine + second * sine, second * cosine - first * sine


def angle_tables(rows_count):
    positions = jnp.arange(rows_count, dtype=F32)
    freqs = jnp.exp(jnp.arange(ROPE // 2, dtype=F32) * (-2.0 * math.log(10000.0) / ROPE))
    angles = positions[:, None] * freqs[None, :]
    return (jnp.cos(angles), jnp.sin(angles))


def inverse_rms(values):
    return lax.rsqrt(jnp.mean(values * values, axis=-1, keepdims=True) + EPSILON)


class Layout:
    def __init__(self, n_dp, n_tensor):
        self.dp, self.t = n_dp, n_tensor
        self.q = n_dp * n_tensor // EXPERTS
        self.z = n_dp // self.q
        if self.z * self.t != EXPERTS or self.z * self.q != n_dp:
            raise ValueError("mesh")
        self.z_groups = [[c + self.q * z for z in range(self.z)] for c in range(self.q)]

    def over_t(self, values, k):
        if k == 0:
            return values
        return lax.ppermute(values, "tensor", [(i, i ^ k) for i in range(self.t)])

    def over_z(self, values, k):
        if k == 0:
            return values
        return lax.ppermute(values, "dp", [(d, d ^ (k * self.q)) for d in range(self.dp)])

    def over_c(self, values, k):
        if k == 0:
            return values
        return lax.ppermute(values, "dp", [(d, d ^ k) for d in range(self.dp)])


def piece_columns(lay, part, d_loc):
    ratio = lay.q * d_loc // part

    def block(ids, kz):
        return ids[0] ^ kz ^ (ids[2] // ratio)

    def first(ids, kc):
        offset = (ids[1] ^ kc) * d_loc
        return pl.multiple_of(((offset // part) ^ (ids[2] % ratio)) * part + offset % part, 128)

    return block, first


def lay_out_weights(lay, ids, stacks, f_loc, d_loc, width):
    ffe = f_loc * lay.t
    block, first = piece_columns(lay, width // lay.t, d_loc)

    def kernel(ids_ref, *refs):
        sources, (in_ref, out_ref) = refs[: lay.q], refs[lay.q :]
        for kc in range(lay.q):
            columns = pl.ds(first(ids_ref, kc), d_loc)
            for g in range(2):
                in_ref[g, :, columns] = sources[kc][0, g]
            out_ref[:, columns] = sources[kc][0, 2]

    own_in, own_out = pl.pallas_call(
        kernel,
        out_shape=(
            jax.ShapeDtypeStruct((2, ffe, width), BF16),
            jax.ShapeDtypeStruct((ffe, width), BF16),
        ),
        grid_spec=pltpu.PrefetchScalarGridSpec(
            num_scalar_prefetch=1,
            grid=(lay.t, lay.z),
            in_specs=[
                pl.BlockSpec((1, 3, f_loc, d_loc), lambda kt, kz, ids: (kt * lay.z + kz, 0, 0, 0))
            ]
            * lay.q,
            out_specs=(
                pl.BlockSpec(
                    (2, f_loc, lay.q * d_loc), lambda kt, kz, ids: (0, kt, block(ids, kz))
                ),
                pl.BlockSpec((f_loc, lay.q * d_loc), lambda kt, kz, ids: (kt, block(ids, kz))),
            ),
        ),
        cost_estimate=pl.CostEstimate(
            flops=0, bytes_accessed=12 * ffe * width, transcendentals=0
        ),
        compiler_params=pltpu.CompilerParams(vmem_limit_bytes=32 << 20),
        name="lay_out_weights",
    )(ids, *stacks)
    return own_in.reshape(2 * ffe, width), own_out


def take_apart(lay, ids, grad_in, grad_out, f_loc, d_loc, width):
    ffe = f_loc * lay.t
    block, first = piece_columns(lay, width // lay.t, d_loc)

    def kernel(ids_ref, in_ref, out_ref, *targets):
        for kc in range(lay.q):
            columns = pl.ds(first(ids_ref, kc), d_loc)
            for g in range(2):
                targets[kc][0, g] = in_ref[g, :, columns]
            targets[kc][0, 2] = out_ref[:, columns]

    shape = jax.ShapeDtypeStruct((lay.t * lay.z, 3, f_loc, d_loc), BF16)
    spec = pl.BlockSpec((1, 3, f_loc, d_loc), lambda kt, kz, ids: (kt * lay.z + kz, 0, 0, 0))
    return pl.pallas_call(
        kernel,
        out_shape=(shape,) * lay.q,
        grid_spec=pltpu.PrefetchScalarGridSpec(
            num_scalar_prefetch=1,
            grid=(lay.t, lay.z),
            in_specs=[
                pl.BlockSpec(
                    (2, f_loc, lay.q * d_loc), lambda kt, kz, ids: (0, kt, block(ids, kz))
                ),
                pl.BlockSpec((f_loc, lay.q * d_loc), lambda kt, kz, ids: (kt, block(ids, kz))),
            ],
            out_specs=(spec,) * lay.q,
        ),
        cost_estimate=pl.CostEstimate(
            flops=0, bytes_accessed=12 * ffe * width, transcendentals=0
        ),
        compiler_params=pltpu.CompilerParams(vmem_limit_bytes=32 << 20),
        name="take_apart",
    )(ids, grad_in.reshape(2, ffe, width), grad_out)


def home_gradients(lay, ids, pieces, f_loc, d_loc):
    def kernel(ids_ref, piece_ref, in_ref, out_ref):
        in_ref[0] = piece_ref[0, :2].astype(F32)
        out_ref[0] = piece_ref[0, 2].astype(F32)

    def pick(e, ids):
        return ((ids[2] ^ (e % lay.t)) * lay.z + (ids[0] ^ (e // lay.t)), 0, 0, 0)

    grad_in, grad_out = pl.pallas_call(
        kernel,
        out_shape=(
            jax.ShapeDtypeStruct((EXPERTS, 2, f_loc, d_loc), F32),
            jax.ShapeDtypeStruct((EXPERTS, f_loc, d_loc), F32),
        ),
        grid_spec=pltpu.PrefetchScalarGridSpec(
            num_scalar_prefetch=1,
            grid=(EXPERTS,),
            in_specs=[pl.BlockSpec((1, 3, f_loc, d_loc), pick)],
            out_specs=(
                pl.BlockSpec((1, 2, f_loc, d_loc), lambda e, ids: (e, 0, 0, 0)),
                pl.BlockSpec((1, f_loc, d_loc), lambda e, ids: (e, 0, 0)),
            ),
        ),
        cost_estimate=pl.CostEstimate(
            flops=0, bytes_accessed=18 * EXPERTS * f_loc * d_loc, transcendentals=0
        ),
        name="home_gradients",
    )(ids, pieces)
    return jnp.swapaxes(grad_in, 2, 3), grad_out


def score_block(q_ref, r_ref, k_ref, kr_ref, head, step, keys, block, length, scale):
    half = r_ref.shape[1] // 2
    lanes = lax.broadcasted_iota(jnp.int32, r_ref.shape, 1) % half // (ROPE // 2)
    turned = jnp.where(lanes == head, r_ref[...], jnp.zeros_like(r_ref))
    raw = lax.dot_general(
        q_ref[...], k_ref[:keys], (((1,), (1,)), ((), ())), preferred_element_type=F32
    ) + lax.dot_general(
        turned, kr_ref[:keys], (((1,), (1,)), ((), ())), preferred_element_type=F32
    )
    rows = lax.broadcasted_iota(jnp.int32, raw.shape, 0) + step * block
    cols = lax.broadcasted_iota(jnp.int32, raw.shape, 1)
    allowed = (cols <= rows) & (cols < length)
    return jnp.where(allowed, raw * scale, NEGATIVE), turned


def attend(length, query, query_rope, kv, key_rope, heads, scale):
    rows = query.shape[0]
    block = min(256, rows)
    steps = rows // block

    def kernel(len_ref, q_ref, r_ref, k_ref, v_ref, kr_ref, o_ref, total_ref):
        head, step = pl.program_id(0), pl.program_id(1)
        for n in range(steps):

            @pl.when(step == n)
            def _(n=n):
                keys = (n + 1) * block
                scores, _ = score_block(
                    q_ref, r_ref, k_ref, kr_ref, head, n, keys, block, len_ref[0], scale
                )
                highest = jnp.max(scores, axis=-1, keepdims=True)
                expo = jnp.exp(scores - highest)
                totals = jnp.sum(expo, axis=-1, keepdims=True)
                weights = (expo * (1.0 / totals)).astype(BF16)
                o_ref[...] = dot(weights, v_ref[:keys]).astype(BF16)
                total_ref[0] = jnp.broadcast_to(highest + jnp.log(totals), (block, 128))

    return pl.pallas_call(
        kernel,
        out_shape=(
            jax.ShapeDtypeStruct((rows, heads * VDIM), BF16),
            jax.ShapeDtypeStruct((heads, rows, 128), F32),
        ),
        grid_spec=pltpu.PrefetchScalarGridSpec(
            num_scalar_prefetch=1,
            grid=(heads, steps),
            in_specs=[
                pl.BlockSpec((block, NOPE), lambda h, i, n: (i, h)),
                pl.BlockSpec((block, query_rope.shape[1]), lambda h, i, n: (i, 0)),
                pl.BlockSpec((rows, NOPE), lambda h, i, n: (0, 2 * h)),
                pl.BlockSpec((rows, VDIM), lambda h, i, n: (0, 2 * h + 1)),
                pl.BlockSpec((rows, key_rope.shape[1]), lambda h, i, n: (0, 0)),
            ],
            out_specs=(
                pl.BlockSpec((block, VDIM), lambda h, i, n: (i, h)),
                pl.BlockSpec((1, block, 128), lambda h, i, n: (h, i, 0)),
            ),
        ),
        cost_estimate=pl.CostEstimate(
            flops=heads * rows * rows * 512,
            bytes_accessed=8 * rows * heads * 512,
            transcendentals=heads * rows * rows,
        ),
        compiler_params=pltpu.CompilerParams(vmem_limit_bytes=32 << 20),
        name="attend",
    )(length, query, query_rope, kv, kv, key_rope)


def attend_back(length, query, query_rope, kv, key_rope, out_grad, log_totals, heads, scale):
    rows = query.shape[0]
    block = min(256, rows)
    steps = rows // block
    turned_cols = query_rope.shape[1]

    def kernel(
        len_ref, q_ref, r_ref, k_ref, v_ref, kr_ref, do_ref, total_ref,
        dq_ref, dr_ref, dkv_ref, dkr_ref, dk_acc, dv_acc,
    ):
        head, step = pl.program_id(0), pl.program_id(1)

        @pl.when(step == 0)
        def _():
            dk_acc[...] = jnp.zeros_like(dk_acc)
            dv_acc[...] = jnp.zeros_like(dv_acc)

        @pl.when((step == 0) & (head == 0))
        def _():
            dr_ref[...] = jnp.zeros_like(dr_ref)
            dkr_ref[...] = jnp.zeros_like(dkr_ref)

        for n in range(steps):

            @pl.when(step == n)
            def _(n=n):
                keys = (n + 1) * block
                scores, turned = score_block(
                    q_ref, r_ref, k_ref, kr_ref, head, n, keys, block, len_ref[0], scale
                )
                probs = jnp.exp(scores - total_ref[0][:, :1])
                prob_grad = lax.dot_general(
                    do_ref[...], v_ref[:keys], (((1,), (1,)), ((), ())), preferred_element_type=F32
                )
                centre = jnp.sum(probs * prob_grad, axis=-1, keepdims=True)
                score_grad = (probs * (prob_grad - centre)).astype(BF16)
                probs_low = probs.astype(BF16)
                dq_ref[...] = (dot(score_grad, k_ref[:keys]) * scale).astype(BF16)
                half = turned_cols // 2
                lanes = lax.broadcasted_iota(jnp.int32, (block, turned_cols), 1)
                lanes = lanes % half // (ROPE // 2)
                turned_grad = dot(score_grad, kr_ref[:keys]) * scale
                dr_ref[n * block : keys] += jnp.where(lanes == head, turned_grad, 0.0)
                dk_acc[:keys] += dot_tn(score_grad, q_ref[...]) * scale
                dkr_ref[:keys] += dot_tn(score_grad, turned) * scale
                dv_acc[:keys] += dot_tn(probs_low, do_ref[...])

        @pl.when(step == steps - 1)
        def _():
            dkv_ref[:, :NOPE] = dk_acc[...].astype(BF16)
            dkv_ref[:, NOPE:] = dv_acc[...].astype(BF16)

    return pl.pallas_call(
        kernel,
        out_shape=(
            jax.ShapeDtypeStruct((rows, heads * NOPE), BF16),
            jax.ShapeDtypeStruct((rows, turned_cols), F32),
            jax.ShapeDtypeStruct((rows, heads * (NOPE + VDIM)), BF16),
            jax.ShapeDtypeStruct((rows, turned_cols), F32),
        ),
        grid_spec=pltpu.PrefetchScalarGridSpec(
            num_scalar_prefetch=1,
            grid=(heads, steps),
            in_specs=[
                pl.BlockSpec((block, NOPE), lambda h, i, n: (i, h)),
                pl.BlockSpec((block, turned_cols), lambda h, i, n: (i, 0)),
                pl.BlockSpec((rows, NOPE), lambda h, i, n: (0, 2 * h)),
                pl.BlockSpec((rows, VDIM), lambda h, i, n: (0, 2 * h + 1)),
                pl.BlockSpec((rows, turned_cols), lambda h, i, n: (0, 0)),
                pl.BlockSpec((block, VDIM), lambda h, i, n: (i, h)),
                pl.BlockSpec((1, block, 128), lambda h, i, n: (h, i, 0)),
            ],
            out_specs=(
                pl.BlockSpec((block, NOPE), lambda h, i, n: (i, h)),
                pl.BlockSpec((rows, turned_cols), lambda h, i, n: (0, 0)),
                pl.BlockSpec((rows, NOPE + VDIM), lambda h, i, n: (0, h)),
                pl.BlockSpec((rows, turned_cols), lambda h, i, n: (0, 0)),
            ),
            scratch_shapes=[pltpu.VMEM((rows, NOPE), F32), pltpu.VMEM((rows, VDIM), F32)],
        ),
        cost_estimate=pl.CostEstimate(
            flops=heads * rows * rows * 1600,
            bytes_accessed=16 * rows * heads * 512,
            transcendentals=heads * rows * rows,
        ),
        compiler_params=pltpu.CompilerParams(vmem_limit_bytes=40 << 20),
        name="attend_back",
    )(length, query, query_rope, kv, kv, key_rope, out_grad, log_totals)


def in_order(values, me, count):
    zero = jnp.zeros_like(values[0])
    ordered = []
    for j in range(count):
        total = zero
        for k in range(count):
            total = jnp.where((me ^ k) == j, values[k], total)
        ordered.append(total)
    return jnp.stack(ordered)


def body(
    lay,
    hidden,
    lengths,
    routes,
    attn_gain,
    w_query,
    w_kv_down,
    kv_gain,
    w_kv_up,
    w_out,
    ffn_gain,
    w_router,
    w_expert_in,
    w_expert_out,
    w_shared_in,
    w_shared_out,
    cotangent,
):
    rows, width = hidden.shape
    nz, nt, nq, ndp = lay.z, lay.t, lay.q, lay.dp
    me_dp = lax.axis_index("dp")
    me_t = lax.axis_index("tensor")
    me_z = me_dp // nq
    me_c = me_dp % nq
    part = width // nt
    d_loc = w_query.shape[0]
    f_loc = w_expert_out.shape[1]
    ffe = f_loc * nt
    heads = w_query.shape[1] // (NOPE + ROPE)
    score_scale = (NOPE + ROPE) ** (-0.5)

    def own_part(values):
        return lax.dynamic_slice_in_dim(values, me_t * part, part, 1)

    def gather_z(values):
        return lax.all_gather(values, "dp", axis=0, tiled=False, axis_index_groups=lay.z_groups)

    def scatter_z(values):
        return lax.psum_scatter(
            values, "dp", scatter_dimension=0, tiled=False, axis_index_groups=lay.z_groups
        )

    def gather_t(values):
        return lax.all_gather(values, "tensor", axis=1, tiled=True)

    def scatter_t(values):
        return lax.psum_scatter(values, "tensor", scatter_dimension=1, tiled=True)

    ids = jnp.stack([me_z, me_c, me_t]).astype(jnp.int32)

    packed = jnp.concatenate(
        [jnp.swapaxes(w_expert_in, 2, 3), w_expert_out[:, None]], 1
    ).reshape(nz, nt, 3, f_loc, d_loc)
    plane = [
        lay.over_t(lax.dynamic_index_in_dim(packed, me_t ^ k, 1, keepdims=False), k)
        for k in range(nt)
    ]
    pieces = jnp.stack(
        [
            lay.over_z(lax.dynamic_index_in_dim(plane[kt], me_z ^ kz, 0, keepdims=False), kz)
            for kt in range(nt)
            for kz in range(nz)
        ]
    )
    own_in, own_out = lay_out_weights(
        lay, ids, [lay.over_c(pieces, k) for k in range(nq)], f_loc, d_loc, width
    )

    lat_loc = kv_gain.shape[0]
    q_rows, down_rows, out_rows = w_query.shape[1], w_kv_down.shape[1], w_out.shape[0]
    half = ROPE // 2

    def by_kind(turned):
        split = turned.reshape(heads, NOPE + ROPE, -1)
        return jnp.concatenate(
            [
                split[:, :NOPE].reshape(heads * NOPE, -1),
                split[:, NOPE : NOPE + half].reshape(heads * half, -1),
                split[:, NOPE + half :].reshape(heads * half, -1),
            ],
            0,
        )

    def by_head(rows_in):
        nope = rows_in[: heads * NOPE].reshape(heads, NOPE, -1)
        first = rows_in[heads * NOPE : heads * (NOPE + half)].reshape(heads, half, -1)
        second = rows_in[heads * (NOPE + half) :].reshape(heads, half, -1)
        return jnp.concatenate([nope, first, second], 1).reshape(heads * (NOPE + ROPE), -1)

    gains = jnp.stack([attn_gain, ffn_gain, jnp.pad(kv_gain, (0, d_loc - lat_loc))])
    front_pack = jnp.concatenate(
        [
            by_kind(jnp.transpose(w_query)),
            jnp.transpose(w_kv_down),
            jnp.transpose(w_router),
            jnp.pad(gains, ((0, 13), (0, 0))),
            w_out,
            w_kv_up.reshape(-1, d_loc),
        ],
        0,
    )
    front = lax.all_gather(front_pack, "dp", axis=0, tiled=False)

    def rows_of(first, count):
        return jnp.swapaxes(front[:, first : first + count], 0, 1).reshape(count, width)

    query_t = rows_of(0, q_rows)
    down_t = rows_of(q_rows, down_rows)
    at = q_rows + down_rows
    router_t = rows_of(at, EXPERTS)
    gain_attn = front[:, at + EXPERTS].reshape(-1)
    gain_ffn = front[:, at + EXPERTS + 1].reshape(-1)
    gain_kv = front[:, at + EXPERTS + 2, :lat_loc].reshape(-1)
    at = at + 2 * EXPERTS
    out_w = rows_of(at, out_rows)
    up_w = front[:, at + out_rows :].reshape(LATENT, heads * (NOPE + VDIM))

    route_own = jnp.pad(jnp.transpose(routes), ((0, -TOP % 8), (0, 0)), constant_values=-1)
    route_all = in_order([lay.over_z(route_own, k) for k in range(nz)], me_z, nz)
    plane_ids = me_z * nt + (me_t ^ jnp.arange(nt, dtype=jnp.int32))
    member = jnp.any(route_all[:, :, :, None] == plane_ids[None, None, None, :], axis=1)
    row_ids = lax.broadcasted_iota(jnp.int32, (rows, rows), 0)
    col_ids = lax.broadcasted_iota(jnp.int32, (rows, rows), 1)
    before = (col_ids < row_ids).astype(BF16)
    position = jnp.einsum("ij,sje->sie", before, member.astype(BF16), preferred_element_type=F32)
    key = jnp.where(member, position.astype(jnp.int32), -1)
    key = jnp.transpose(key, (0, 2, 1))
    slots_iota = lax.broadcasted_iota(jnp.int32, (1, 1, CAP, 1), 2)
    place = (key[:, :, None, :] == slots_iota).astype(BF16)
    own_place = key[:, 0, None, :] == slots_iota[0]

    def dispatch(values):
        picked = jnp.einsum("sepk,skd->espd", place, values, preferred_element_type=F32)
        picked = picked.astype(BF16).reshape(nt, nz * CAP, part)
        return jnp.concatenate([lay.over_t(picked[k], k) for k in range(nt)], 1)

    def send_back(values):
        return [lay.over_t(values[:, k * part : (k + 1) * part], k) for k in range(nt)]

    def combine(parts):
        parts = jnp.stack(parts).reshape(nt, nz, CAP, part)
        summed = jnp.einsum("sepk,espd->skd", place, parts, preferred_element_type=F32)
        return scatter_z(summed.astype(BF16)).astype(F32)

    valid_length = lengths[0]
    valid_rows = lax.broadcasted_iota(jnp.int32, (rows, 1), 0) < valid_length
    cot_low = jnp.where(valid_rows, cotangent, jnp.zeros_like(cotangent))
    cot_part = own_part(cot_low)
    cot_rows = dispatch(gather_z(cot_part))

    cosine, sine = angle_tables(rows)
    wide_cos, wide_sin = jnp.tile(cosine, (1, heads)), jnp.tile(sine, (1, heads))
    inputs = hidden.astype(F32)
    attn_inverse = inverse_rms(inputs)
    attn_scale = gain_attn.astype(F32)
    normed_low = (inputs * attn_inverse * attn_scale).astype(BF16)
    query = dot_nt(normed_low, query_t)
    nope_cols = heads * NOPE
    query_nope = query[:, :nope_cols].astype(BF16)
    query_rope = jnp.concatenate(
        rotate(
            query[:, nope_cols : nope_cols + heads * half],
            query[:, nope_cols + heads * half :],
            wide_cos,
            wide_sin,
        ),
        1,
    ).astype(BF16)
    latent_all = dot_nt(normed_low, down_t)
    latent = latent_all[:, :LATENT]
    kv_inverse = inverse_rms(latent)
    latent_hat = latent * kv_inverse
    kv_scale = gain_kv.astype(F32)
    latent_low = (latent_hat * kv_scale).astype(BF16)
    key_first, key_second = rotate(
        latent_all[:, LATENT : LATENT + half], latent_all[:, LATENT + half :], cosine, sine
    )
    key_rope = jnp.concatenate(
        [jnp.tile(key_first, (1, heads)), jnp.tile(key_second, (1, heads))], 1
    ).astype(BF16)
    keys_values = dot(latent_low, up_w).astype(BF16)
    attended_low, log_totals = attend(
        lengths, query_nope, query_rope, keys_values, key_rope, heads, score_scale
    )
    attn_sum = scatter_t(dot(attended_low, out_w).astype(BF16)).astype(F32)
    residual = own_part(hidden).astype(F32) + attn_sum

    def row_mean(values):
        partial = jnp.sum(values, axis=-1).reshape(-1, 128)
        return lax.psum(partial, "tensor").reshape(-1, 1) * (1.0 / width)

    ffn_inverse = lax.rsqrt(row_mean(residual * residual) + EPSILON)
    ffn_hat = residual * ffn_inverse
    ffn_scale = lax.dynamic_slice_in_dim(gain_ffn, me_t * part, part, 0).astype(F32)
    ffn_part = (ffn_hat * ffn_scale).astype(BF16)

    expert_rows = dispatch(gather_z(ffn_part))
    ffn_low = gather_t(ffn_part)
    router_probs = jax.nn.softmax(dot_nt(ffn_low, router_t), axis=-1)
    probs_turned = jnp.transpose(router_probs).reshape(EXPERTS, -1, 128)
    own_probs = in_order(
        [
            lay.over_z(
                lax.dynamic_index_in_dim(
                    probs_turned, (me_z ^ k) * nt + me_t, 0, keepdims=False
                ),
                k,
            )
            for k in range(nz)
        ],
        me_z,
        nz,
    ).reshape(nz, rows)
    gate_rows = jnp.sum(jnp.where(own_place, own_probs[:, None, :], 0.0), axis=-1).reshape(
        nz * CAP, 1
    )
    gate_up = dot_nt(expert_rows, own_in)
    gate_pre, up_pre = gate_up[:, :ffe], gate_up[:, ffe:]
    gate_sig = jax.nn.sigmoid(gate_pre)
    gate_silu = gate_pre * gate_sig
    active = (gate_silu * up_pre).astype(BF16)
    rows_out = (dot(active, own_out) * gate_rows).astype(BF16)
    out_parts = send_back(rows_out)
    active_grad_raw = dot_nt(cot_rows, own_out)
    gate_grad = jnp.sum(active.astype(F32) * active_grad_raw, axis=-1).reshape(nz, CAP)
    active_grad = active_grad_raw * gate_rows
    pre_low = jnp.concatenate(
        [
            active_grad * up_pre * gate_sig * (1.0 + gate_pre * (1.0 - gate_sig)),
            active_grad * gate_silu,
        ],
        1,
    ).astype(BF16)
    gated_active = (active.astype(F32) * gate_rows).astype(BF16)
    rows_grad = dot(pre_low, own_in).astype(BF16)
    grad_parts = send_back(rows_grad)
    routed = combine(out_parts)
    grad_in_own = dot_tn(pre_low, expert_rows).astype(BF16)
    grad_out_own = dot_tn(gated_active, cot_rows).astype(BF16)
    grad_pieces = take_apart(lay, ids, grad_in_own, grad_out_own, f_loc, d_loc, width)
    grad_parts, grad_pieces = lax.optimization_barrier((grad_parts, grad_pieces))
    routed_grad = combine(grad_parts)

    token_grad = jnp.sum(jnp.where(own_place, gate_grad[:, :, None], 0.0), axis=1)
    token_grad = token_grad.reshape(nz, -1, 128)
    token_plane = jnp.stack(
        [
            lay.over_z(lax.dynamic_index_in_dim(token_grad, me_z ^ k, 0, keepdims=False), k)
            for k in range(nz)
        ]
    )
    token_home = jnp.stack([lay.over_t(token_plane, k) for k in range(nt)])
    experts = jnp.arange(EXPERTS, dtype=jnp.int32)
    came_from = (me_t ^ (experts % nt)) * nz + (me_z ^ (experts // nt))
    probs_grad = lax.dot_general(
        token_home.reshape(EXPERTS, rows),
        (experts[:, None] == came_from[None, :]).astype(F32),
        (((0,), (0,)), ((), ())),
        precision=lax.Precision.HIGHEST,
        preferred_element_type=F32,
    )

    ffs = w_shared_out.shape[0]
    shared_all = lax.all_gather(
        jnp.concatenate([jnp.swapaxes(w_shared_in, 1, 2).reshape(2 * ffs, d_loc), w_shared_out], 0),
        "dp",
        axis=0,
        tiled=False,
    )
    shared_in = jnp.swapaxes(shared_all[:, : 2 * ffs], 0, 1).reshape(2 * ffs, width)
    shared_out = jnp.swapaxes(shared_all[:, 2 * ffs :], 0, 1).reshape(ffs, width)
    shared_pre = dot_nt(ffn_low, shared_in)
    shared_gate, shared_up = shared_pre[:, :ffs], shared_pre[:, ffs:]
    shared_sig = jax.nn.sigmoid(shared_gate)
    shared_silu = shared_gate * shared_sig
    shared_act = (shared_silu * shared_up).astype(BF16)
    shared_part = scatter_t(dot(shared_act, shared_out).astype(BF16)).astype(F32)
    shared_act_grad = dot_nt(cot_low, shared_out)
    shared_pre_grad = jnp.concatenate(
        [
            shared_act_grad * shared_up * shared_sig * (1.0 + shared_gate * (1.0 - shared_sig)),
            shared_act_grad * shared_silu,
        ],
        1,
    ).astype(BF16)
    grad_shared_in = dot_tn(shared_pre_grad, ffn_low)
    grad_shared_out = dot_tn(shared_act, cot_low)
    shared_grad = scatter_t(dot(shared_pre_grad, shared_in).astype(BF16)).astype(F32)

    logits_grad = router_probs * (
        probs_grad - jnp.sum(router_probs * probs_grad, axis=-1, keepdims=True)
    )
    router_part = lax.dot_general(
        logits_grad,
        ffn_low.astype(F32),
        (((0,), (0,)), ((), ())),
        precision=lax.Precision.HIGHEST,
        preferred_element_type=F32,
    )
    router_slice = lax.dynamic_slice_in_dim(router_t, me_t * part, part, 1)
    ffn_grad = (
        shared_grad
        + routed_grad
        + lax.dot_general(
            logits_grad,
            router_slice.astype(F32),
            (((1,), (0,)), ((), ())),
            precision=lax.Precision.HIGHEST,
            preferred_element_type=F32,
        )
    )
    scaled = ffn_scale * ffn_grad
    ffn_gain_part = jnp.sum(ffn_grad * ffn_hat, axis=0)
    residual_grad = cot_part.astype(F32) + ffn_inverse * (
        scaled - ffn_hat * row_mean(ffn_hat * scaled)
    )
    residual_low = gather_t(residual_grad.astype(BF16))

    output = gather_t((residual + routed + shared_part).astype(BF16))

    grad_class = sum(lay.over_c(grad_pieces[k], k).astype(F32) for k in range(nq)).astype(BF16)
    grad_class = grad_class.reshape(nt, nz, 3, f_loc, d_loc)
    grad_plane = [lay.over_z(grad_class[:, k], k) for k in range(nz)]
    grad_home = jnp.stack(
        [lay.over_t(grad_plane[kz][kt], kt) for kt in range(nt) for kz in range(nz)]
    )
    grad_expert_in, grad_expert_out = home_gradients(lay, ids, grad_home, f_loc, d_loc)

    grad_out_w = dot_tn(attended_low, residual_low)
    attended_grad = dot_nt(residual_low, out_w).astype(BF16)
    query_nope_grad, query_turned_grad, kv_grad, rope_grad = attend_back(
        lengths,
        query_nope,
        query_rope,
        keys_values,
        key_rope,
        attended_grad,
        log_totals,
        heads,
        score_scale,
    )
    turned_first, turned_second = rotate_back(
        query_turned_grad[:, : heads * half], query_turned_grad[:, heads * half :], wide_cos, wide_sin
    )
    query_grad = jnp.concatenate(
        [query_nope_grad, turned_first.astype(BF16), turned_second.astype(BF16)], 1
    )
    rope_sum = rope_grad.reshape(rows, 2, heads, half).sum(2)
    key_rope_part = jnp.concatenate(
        rotate_back(rope_sum[:, 0], rope_sum[:, 1], cosine, sine), 1
    )
    latent_part = dot_nt(kv_grad, up_w)
    latent_sum = lax.psum(
        jnp.concatenate([latent_part, key_rope_part], -1).astype(BF16), "tensor"
    ).astype(F32)
    normed_grad_q = scatter_t(dot(query_grad, query_t).astype(BF16)).astype(F32)
    latent_grad, key_rope_grad = latent_sum[:, :LATENT], latent_sum[:, LATENT:]
    grad_kv_gain = jnp.sum(latent_grad * latent_hat, axis=0)
    scaled_kv = kv_scale * latent_grad
    latent_back = kv_inverse * (
        scaled_kv - latent_hat * jnp.mean(latent_hat * scaled_kv, axis=-1, keepdims=True)
    )
    down_grad = jnp.concatenate([latent_back, key_rope_grad], -1).astype(BF16)
    down_slice = lax.dynamic_slice_in_dim(down_t, me_t * part, part, 1)
    normed_grad = normed_grad_q + dot(down_grad, down_slice)
    attn_hat = own_part(hidden).astype(F32) * attn_inverse
    scaled_in = lax.dynamic_slice_in_dim(attn_scale, me_t * part, part, 0) * normed_grad
    attn_gain_part = jnp.sum(normed_grad * attn_hat, axis=0)
    input_grad = residual_grad + attn_inverse * (
        scaled_in - attn_hat * row_mean(attn_hat * scaled_in)
    )
    grad_hidden = gather_t(input_grad.astype(BF16))

    def sum_dp(values):
        return lax.psum_scatter(values, "dp", scatter_dimension=0, tiled=False).astype(F32)

    def by_owner(values):
        return jnp.swapaxes(values.astype(BF16).reshape(-1, ndp, d_loc), 0, 1)

    gain_parts = lax.all_gather(
        jnp.concatenate([attn_gain_part[None], ffn_gain_part[None]], 0), "tensor", axis=1, tiled=True
    )
    kv_gain_row = jnp.pad(
        grad_kv_gain.reshape(ndp, lat_loc), ((0, 0), (0, d_loc - lat_loc))
    ).reshape(1, width)
    front_sum = sum_dp(
        jnp.concatenate(
            [
                by_owner(dot_tn(query_grad, normed_low)),
                by_owner(dot_tn(down_grad, normed_low)),
                by_owner(router_part),
                by_owner(jnp.pad(jnp.concatenate([gain_parts, kv_gain_row], 0), ((0, 13), (0, 0)))),
                by_owner(grad_out_w),
                dot_tn(latent_low, kv_grad).astype(BF16).reshape(ndp, -1, d_loc),
            ],
            1,
        )
    )
    shared_sum = sum_dp(
        jnp.concatenate([by_owner(grad_shared_in), by_owner(grad_shared_out)], 1)
    )
    at = q_rows + down_rows
    gain_rows = front_sum[at + EXPERTS : at + EXPERTS + 3]
    return (
        output,
        grad_hidden,
        gain_rows[0],
        jnp.transpose(by_head(front_sum[:q_rows])),
        jnp.transpose(front_sum[q_rows:at]),
        gain_rows[2, :lat_loc],
        front_sum[at + 2 * EXPERTS + out_rows :].reshape(w_kv_up.shape),
        front_sum[at + 2 * EXPERTS : at + 2 * EXPERTS + out_rows],
        gain_rows[1],
        jnp.transpose(front_sum[at : at + EXPERTS]),
        grad_expert_in,
        grad_expert_out,
        jnp.swapaxes(shared_sum[: 2 * ffs].reshape(2, ffs, d_loc), 1, 2),
        shared_sum[2 * ffs :],
    )


def solution(mesh):
    return jax.shard_map(
        functools.partial(body, Layout(mesh.shape["dp"], mesh.shape["tensor"])),
        mesh=mesh,
        in_specs=(
            P("dp", None),
            P("dp"),
            P("dp", None),
            P("dp"),
            P("dp", "tensor"),
            P("dp", None),
            P("dp"),
            P("dp", "tensor"),
            P("tensor", "dp"),
            P("dp"),
            P("dp", None),
            P(None, None, "dp", "tensor"),
            P(None, "tensor", "dp"),
            P(None, "dp", "tensor"),
            P("tensor", "dp"),
            P("dp", None),
        ),
        out_specs=(
            P("dp", None),
            P("dp", None),
            P("dp"),
            P("dp", "tensor"),
            P("dp", None),
            P("dp"),
            P("dp", "tensor"),
            P("tensor", "dp"),
            P("dp"),
            P("dp", None),
            P(None, None, "dp", "tensor"),
            P(None, "tensor", "dp"),
            P(None, "dp", "tensor"),
            P("tensor", "dp"),
        ),
        check_vma=False,
    )
```

```python
import functools
import math

import jax
import jax.numpy as jnp
from jax import lax
from jax.experimental import pallas as pl
from jax.experimental.pallas import tpu as pltpu
from jax.sharding import PartitionSpec as P

NOPE = 128
ROPE = 64
VDIM = 128
LATENT = 512
TOP = 6
EXPERTS = 16
CAP = 512

EPSILON = 1e-06
NEGATIVE = -1e30
F32 = jnp.float32
BF16 = jnp.bfloat16


def dot(a, b):
    return jnp.dot(a, b, preferred_element_type=F32)


def dot_nt(a, b):
    return lax.dot_general(a, b, (((1,), (1,)), ((), ())), preferred_element_type=F32)


def dot_tn(a, b):
    return lax.dot_general(a, b, (((0,), (0,)), ((), ())), preferred_element_type=F32)


def rotate(first, second, cosine, sine):
    return first * cosine - second * sine, second * cosine + first * sine


def rotate_back(first, second, cosine, sine):
    return first * cosine + second * sine, second * cosine - first * sine


def angle_tables(rows_count):
    positions = jnp.arange(rows_count, dtype=F32)
    freqs = jnp.exp(jnp.arange(ROPE // 2, dtype=F32) * (-2.0 * math.log(10000.0) / ROPE))
    angles = positions[:, None] * freqs[None, :]
    return (jnp.cos(angles), jnp.sin(angles))


def inverse_rms(values):
    return lax.rsqrt(jnp.mean(values * values, axis=-1, keepdims=True) + EPSILON)


class Layout:
    def __init__(self, n_dp, n_tensor):
        self.dp, self.t = n_dp, n_tensor
        self.q = n_dp * n_tensor // EXPERTS
        self.z = n_dp // self.q
        if self.z * self.t != EXPERTS or self.z * self.q != n_dp:
            raise ValueError("mesh")
        self.z_groups = [[c + self.q * z for z in range(self.z)] for c in range(self.q)]

    def over_t(self, values, k):
        if k == 0:
            return values
        return lax.ppermute(values, "tensor", [(i, i ^ k) for i in range(self.t)])

    def over_z(self, values, k):
        if k == 0:
            return values
        return lax.ppermute(values, "dp", [(d, d ^ (k * self.q)) for d in range(self.dp)])

    def over_c(self, values, k):
        if k == 0:
            return values
        return lax.ppermute(values, "dp", [(d, d ^ k) for d in range(self.dp)])


def lay_out_weights(lay, ids, stacks, f_loc, d_loc, width):
    ffe = f_loc * lay.t

    def kernel(ids_ref, *refs):
        sources, (in_ref, out_ref) = refs[: lay.q], refs[lay.q :]
        for kc in range(lay.q):
            columns = pl.ds(pl.multiple_of((ids_ref[1] ^ kc) * d_loc, 128), d_loc)
            for g in range(2):
                in_ref[g, :, columns] = sources[kc][0, g]
            out_ref[:, columns] = sources[kc][0, 2]

    own_in, own_out = pl.pallas_call(
        kernel,
        out_shape=(
            jax.ShapeDtypeStruct((2, ffe, width), BF16),
            jax.ShapeDtypeStruct((ffe, width), BF16),
        ),
        grid_spec=pltpu.PrefetchScalarGridSpec(
            num_scalar_prefetch=1,
            grid=(lay.t, lay.z),
            in_specs=[
                pl.BlockSpec((1, 3, f_loc, d_loc), lambda kt, kz, ids: (kz * lay.t + kt, 0, 0, 0))
            ]
            * lay.q,
            out_specs=(
                pl.BlockSpec(
                    (2, f_loc, lay.q * d_loc), lambda kt, kz, ids: (0, kt, kz)
                ),
                pl.BlockSpec((f_loc, lay.q * d_loc), lambda kt, kz, ids: (kt, kz)),
            ),
        ),
        cost_estimate=pl.CostEstimate(
            flops=0, bytes_accessed=12 * ffe * width, transcendentals=0
        ),
        compiler_params=pltpu.CompilerParams(vmem_limit_bytes=32 << 20),
        name="lay_out_weights",
    )(ids, *stacks)
    return own_in.reshape(2 * ffe, width), own_out


def take_apart(lay, ids, grad_in, grad_out, f_loc, d_loc, width):
    ffe = f_loc * lay.t

    def kernel(ids_ref, in_ref, out_ref, *targets):
        for kc in range(lay.q):
            columns = pl.ds(pl.multiple_of((ids_ref[1] ^ kc) * d_loc, 128), d_loc)
            for g in range(2):
                targets[kc][0, g] = in_ref[g, :, columns]
            targets[kc][0, 2] = out_ref[:, columns]

    shape = jax.ShapeDtypeStruct((lay.t * lay.z, 3, f_loc, d_loc), BF16)
    spec = pl.BlockSpec((1, 3, f_loc, d_loc), lambda kt, kz, ids: (kz * lay.t + kt, 0, 0, 0))
    return pl.pallas_call(
        kernel,
        out_shape=(shape,) * lay.q,
        grid_spec=pltpu.PrefetchScalarGridSpec(
            num_scalar_prefetch=1,
            grid=(lay.t, lay.z),
            in_specs=[
                pl.BlockSpec(
                    (2, f_loc, lay.q * d_loc), lambda kt, kz, ids: (0, kt, kz)
                ),
                pl.BlockSpec((f_loc, lay.q * d_loc), lambda kt, kz, ids: (kt, kz)),
            ],
            out_specs=(spec,) * lay.q,
        ),
        cost_estimate=pl.CostEstimate(
            flops=0, bytes_accessed=12 * ffe * width, transcendentals=0
        ),
        compiler_params=pltpu.CompilerParams(vmem_limit_bytes=32 << 20),
        name="take_apart",
    )(ids, grad_in.reshape(2, ffe, width), grad_out)


def home_gradients(lay, ids, pieces, f_loc, d_loc):
    def kernel(ids_ref, piece_ref, in_ref, out_ref):
        in_ref[0] = piece_ref[0, :2].astype(F32)
        out_ref[0] = piece_ref[0, 2].astype(F32)

    def pick(e, ids):
        return (e % lay.t * lay.z + e // lay.t, 0, 0, 0)

    grad_in, grad_out = pl.pallas_call(
        kernel,
        out_shape=(
            jax.ShapeDtypeStruct((EXPERTS, 2, f_loc, d_loc), F32),
            jax.ShapeDtypeStruct((EXPERTS, f_loc, d_loc), F32),
        ),
        grid_spec=pltpu.PrefetchScalarGridSpec(
            num_scalar_prefetch=1,
            grid=(EXPERTS,),
            in_specs=[pl.BlockSpec((1, 3, f_loc, d_loc), pick)],
            out_specs=(
                pl.BlockSpec((1, 2, f_loc, d_loc), lambda e, ids: (e, 0, 0, 0)),
                pl.BlockSpec((1, f_loc, d_loc), lambda e, ids: (e, 0, 0)),
            ),
        ),
        cost_estimate=pl.CostEstimate(
            flops=0, bytes_accessed=18 * EXPERTS * f_loc * d_loc, transcendentals=0
        ),
        name="home_gradients",
    )(ids, pieces)
    return jnp.swapaxes(grad_in, 2, 3), grad_out


def join_columns(parts, me, count):
    rows, part = parts[0].shape
    block = min(256, rows)

    def kernel(me_ref, *refs):
        for k in range(count):

            @pl.when(pl.program_id(1) == k)
            def _(k=k):
                refs[count][...] = refs[k][...]

    return pl.pallas_call(
        kernel,
        out_shape=jax.ShapeDtypeStruct((rows, count * part), parts[0].dtype),
        grid_spec=pltpu.PrefetchScalarGridSpec(
            num_scalar_prefetch=1,
            grid=(rows // block, count),
            in_specs=[pl.BlockSpec((block, part), lambda i, k, me: (i, 0))] * count,
            out_specs=pl.BlockSpec((block, part), lambda i, k, me: (i, me[0] ^ k)),
        ),
        cost_estimate=pl.CostEstimate(
            flops=0, bytes_accessed=4 * rows * part * count, transcendentals=0
        ),
        name="join_columns",
    )(me.reshape(1).astype(jnp.int32), *parts)


def score_block(q_ref, r_ref, k_ref, kr_ref, head, step, keys, block, length, scale):
    half = r_ref.shape[1] // 2
    lanes = lax.broadcasted_iota(jnp.int32, r_ref.shape, 1) % half // (ROPE // 2)
    turned = jnp.where(lanes == head, r_ref[...], jnp.zeros_like(r_ref))
    raw = lax.dot_general(
        q_ref[...], k_ref[:keys], (((1,), (1,)), ((), ())), preferred_element_type=F32
    ) + lax.dot_general(
        turned, kr_ref[:keys], (((1,), (1,)), ((), ())), preferred_element_type=F32
    )
    rows = lax.broadcasted_iota(jnp.int32, raw.shape, 0) + step * block
    cols = lax.broadcasted_iota(jnp.int32, raw.shape, 1)
    allowed = (cols <= rows) & (cols < length)
    return jnp.where(allowed, raw * scale, NEGATIVE), turned


def attend(length, query, query_rope, kv, key_rope, heads, scale):
    rows = query.shape[0]
    block = min(256, rows)
    steps = rows // block

    def kernel(len_ref, q_ref, r_ref, k_ref, v_ref, kr_ref, o_ref, total_ref):
        head, step = pl.program_id(0), pl.program_id(1)
        for n in range(steps):

            @pl.when(step == n)
            def _(n=n):
                keys = (n + 1) * block
                scores, _ = score_block(
                    q_ref, r_ref, k_ref, kr_ref, head, n, keys, block, len_ref[0], scale
                )
                highest = jnp.max(scores, axis=-1, keepdims=True)
                expo = jnp.exp(scores - highest)
                totals = jnp.sum(expo, axis=-1, keepdims=True)
                weights = (expo * (1.0 / totals)).astype(BF16)
                o_ref[...] = dot(weights, v_ref[:keys]).astype(BF16)
                total_ref[0] = jnp.broadcast_to(highest + jnp.log(totals), (block, 128))

    return pl.pallas_call(
        kernel,
        out_shape=(
            jax.ShapeDtypeStruct((rows, heads * VDIM), BF16),
            jax.ShapeDtypeStruct((heads, rows, 128), F32),
        ),
        grid_spec=pltpu.PrefetchScalarGridSpec(
            num_scalar_prefetch=1,
            grid=(heads, steps),
            in_specs=[
                pl.BlockSpec((block, NOPE), lambda h, i, n: (i, h)),
                pl.BlockSpec((block, query_rope.shape[1]), lambda h, i, n: (i, 0)),
                pl.BlockSpec((rows, NOPE), lambda h, i, n: (0, 2 * h)),
                pl.BlockSpec((rows, VDIM), lambda h, i, n: (0, 2 * h + 1)),
                pl.BlockSpec((rows, key_rope.shape[1]), lambda h, i, n: (0, 0)),
            ],
            out_specs=(
                pl.BlockSpec((block, VDIM), lambda h, i, n: (i, h)),
                pl.BlockSpec((1, block, 128), lambda h, i, n: (h, i, 0)),
            ),
        ),
        cost_estimate=pl.CostEstimate(
            flops=heads * rows * rows * 512,
            bytes_accessed=8 * rows * heads * 512,
            transcendentals=heads * rows * rows,
        ),
        compiler_params=pltpu.CompilerParams(vmem_limit_bytes=32 << 20),
        name="attend",
    )(length, query, query_rope, kv, kv, key_rope)


def attend_back(length, query, query_rope, kv, key_rope, out_grad, log_totals, heads, scale):
    rows = query.shape[0]
    block = min(256, rows)
    steps = rows // block
    turned_cols = query_rope.shape[1]

    def kernel(
        len_ref, q_ref, r_ref, k_ref, v_ref, kr_ref, do_ref, total_ref,
        dq_ref, dr_ref, dkv_ref, dkr_ref, dk_acc, dv_acc,
    ):
        head, step = pl.program_id(0), pl.program_id(1)

        @pl.when(step == 0)
        def _():
            dk_acc[...] = jnp.zeros_like(dk_acc)
            dv_acc[...] = jnp.zeros_like(dv_acc)

        @pl.when((step == 0) & (head == 0))
        def _():
            dr_ref[...] = jnp.zeros_like(dr_ref)
            dkr_ref[...] = jnp.zeros_like(dkr_ref)

        for n in range(steps):

            @pl.when(step == n)
            def _(n=n):
                keys = (n + 1) * block
                scores, turned = score_block(
                    q_ref, r_ref, k_ref, kr_ref, head, n, keys, block, len_ref[0], scale
                )
                probs = jnp.exp(scores - total_ref[0][:, :1])
                prob_grad = lax.dot_general(
                    do_ref[...], v_ref[:keys], (((1,), (1,)), ((), ())), preferred_element_type=F32
                )
                centre = jnp.sum(probs * prob_grad, axis=-1, keepdims=True)
                score_grad = (probs * (prob_grad - centre)).astype(BF16)
                probs_low = probs.astype(BF16)
                dq_ref[...] = (dot(score_grad, k_ref[:keys]) * scale).astype(BF16)
                half = turned_cols // 2
                lanes = lax.broadcasted_iota(jnp.int32, (block, turned_cols), 1)
                lanes = lanes % half // (ROPE // 2)
                turned_grad = dot(score_grad, kr_ref[:keys]) * scale
                dr_ref[n * block : keys] += jnp.where(lanes == head, turned_grad, 0.0)
                dk_acc[:keys] += dot_tn(score_grad, q_ref[...]) * scale
                dkr_ref[:keys] += dot_tn(score_grad, turned) * scale
                dv_acc[:keys] += dot_tn(probs_low, do_ref[...])

        @pl.when(step == steps - 1)
        def _():
            dkv_ref[:, :NOPE] = dk_acc[...].astype(BF16)
            dkv_ref[:, NOPE:] = dv_acc[...].astype(BF16)

    return pl.pallas_call(
        kernel,
        out_shape=(
            jax.ShapeDtypeStruct((rows, heads * NOPE), BF16),
            jax.ShapeDtypeStruct((rows, turned_cols), F32),
            jax.ShapeDtypeStruct((rows, heads * (NOPE + VDIM)), BF16),
            jax.ShapeDtypeStruct((rows, turned_cols), F32),
        ),
        grid_spec=pltpu.PrefetchScalarGridSpec(
            num_scalar_prefetch=1,
            grid=(heads, steps),
            in_specs=[
                pl.BlockSpec((block, NOPE), lambda h, i, n: (i, h)),
                pl.BlockSpec((block, turned_cols), lambda h, i, n: (i, 0)),
                pl.BlockSpec((rows, NOPE), lambda h, i, n: (0, 2 * h)),
                pl.BlockSpec((rows, VDIM), lambda h, i, n: (0, 2 * h + 1)),
                pl.BlockSpec((rows, turned_cols), lambda h, i, n: (0, 0)),
                pl.BlockSpec((block, VDIM), lambda h, i, n: (i, h)),
                pl.BlockSpec((1, block, 128), lambda h, i, n: (h, i, 0)),
            ],
            out_specs=(
                pl.BlockSpec((block, NOPE), lambda h, i, n: (i, h)),
                pl.BlockSpec((rows, turned_cols), lambda h, i, n: (0, 0)),
                pl.BlockSpec((rows, NOPE + VDIM), lambda h, i, n: (0, h)),
                pl.BlockSpec((rows, turned_cols), lambda h, i, n: (0, 0)),
            ),
            scratch_shapes=[pltpu.VMEM((rows, NOPE), F32), pltpu.VMEM((rows, VDIM), F32)],
        ),
        cost_estimate=pl.CostEstimate(
            flops=heads * rows * rows * 1600,
            bytes_accessed=16 * rows * heads * 512,
            transcendentals=heads * rows * rows,
        ),
        compiler_params=pltpu.CompilerParams(vmem_limit_bytes=40 << 20),
        name="attend_back",
    )(length, query, query_rope, kv, kv, key_rope, out_grad, log_totals)


def in_order(values, me, count):
    zero = jnp.zeros_like(values[0])
    ordered = []
    for j in range(count):
        total = zero
        for k in range(count):
            total = jnp.where((me ^ k) == j, values[k], total)
        ordered.append(total)
    return jnp.stack(ordered)


def body(
    lay,
    hidden,
    lengths,
    routes,
    attn_gain,
    w_query,
    w_kv_down,
    kv_gain,
    w_kv_up,
    w_out,
    ffn_gain,
    w_router,
    w_expert_in,
    w_expert_out,
    w_shared_in,
    w_shared_out,
    cotangent,
):
    rows, width = hidden.shape
    nz, nt, nq, ndp = lay.z, lay.t, lay.q, lay.dp
    me_dp = lax.axis_index("dp")
    me_t = lax.axis_index("tensor")
    me_z = me_dp // nq
    me_c = me_dp % nq
    part = width // nt
    d_loc = w_query.shape[0]
    f_loc = w_expert_out.shape[1]
    ffe = f_loc * nt
    heads = w_query.shape[1] // (NOPE + ROPE)
    score_scale = (NOPE + ROPE) ** (-0.5)

    def own_part(values):
        return lax.dynamic_slice_in_dim(values, me_t * part, part, 1)

    def gather_z(values):
        return lax.all_gather(values, "dp", axis=0, tiled=False, axis_index_groups=lay.z_groups)

    def scatter_z(values):
        return lax.psum_scatter(
            values, "dp", scatter_dimension=0, tiled=False, axis_index_groups=lay.z_groups
        )

    def gather_t(values):
        return lax.all_gather(values, "tensor", axis=1, tiled=True)

    def scatter_t(values):
        return lax.psum_scatter(
            values.astype(BF16), "tensor", scatter_dimension=1, tiled=True
        ).astype(F32)

    def swap_t(values):
        return lax.all_to_all(values, "tensor", split_axis=0, concat_axis=0, tiled=True)

    def swap_z(values):
        return lax.all_to_all(
            values,
            "dp",
            split_axis=0,
            concat_axis=0,
            axis_index_groups=lay.z_groups,
            tiled=True,
        )

    def gather_t_direct(values):
        return join_columns([lay.over_t(values, k) for k in range(nt)], me_t, nt)

    def part_for(values, k):
        return lax.dynamic_slice_in_dim(values, (me_t ^ k) * part, part, 1)

    def scatter_t_direct(values):
        total = part_for(values, 0)
        for k in range(1, nt):
            total = total + lay.over_t(part_for(values, k).astype(BF16), k).astype(F32)
        return total

    ids = jnp.stack([me_z, me_c, me_t]).astype(jnp.int32)

    packed = jnp.concatenate(
        [jnp.swapaxes(w_expert_in, 2, 3), w_expert_out[:, None]], 1
    ).reshape(nz, nt, 3, f_loc, d_loc)
    by_column = swap_t(jnp.swapaxes(packed, 0, 1))

    lat_loc = kv_gain.shape[0]
    q_rows, down_rows, out_rows = w_query.shape[1], w_kv_down.shape[1], w_out.shape[0]
    half = ROPE // 2

    def by_kind(turned):
        split = turned.reshape(heads, NOPE + ROPE, -1)
        return jnp.concatenate(
            [
                split[:, :NOPE].reshape(heads * NOPE, -1),
                split[:, NOPE : NOPE + half].reshape(heads * half, -1),
                split[:, NOPE + half :].reshape(heads * half, -1),
            ],
            0,
        )

    def by_head(rows_in):
        nope = rows_in[: heads * NOPE].reshape(heads, NOPE, -1)
        first = rows_in[heads * NOPE : heads * (NOPE + half)].reshape(heads, half, -1)
        second = rows_in[heads * (NOPE + half) :].reshape(heads, half, -1)
        return jnp.concatenate([nope, first, second], 1).reshape(heads * (NOPE + ROPE), -1)

    gains = jnp.stack([attn_gain, ffn_gain, jnp.pad(kv_gain, (0, d_loc - lat_loc))])
    front_pack = jnp.concatenate(
        [
            by_kind(jnp.transpose(w_query)),
            jnp.transpose(w_kv_down),
            jnp.transpose(w_router),
            jnp.pad(gains, ((0, 13), (0, 0))),
            w_out,
            w_kv_up.reshape(-1, d_loc),
        ],
        0,
    )
    front = lax.all_gather(front_pack, "dp", axis=0, tiled=False)

    valid_length = lengths[0]
    valid_rows = lax.broadcasted_iota(jnp.int32, (rows, 1), 0) < valid_length
    cot_low = jnp.where(valid_rows, cotangent, jnp.zeros_like(cotangent))
    cot_part = own_part(cot_low)
    route_rows = jnp.transpose(routes).astype(BF16).reshape(-1)
    route_rows = jnp.pad(route_rows, (0, -route_rows.shape[0] % (16 * part))).reshape(-1, part)
    front, by_column, cot_ready = lax.optimization_barrier(
        (front, by_column, jnp.concatenate([cot_part, route_rows], 0))
    )
    by_plane = swap_z(jnp.swapaxes(by_column, 0, 1))
    cot_all = gather_z(cot_ready)

    route_all = cot_all[:, rows:].reshape(nz, -1)[:, : TOP * rows].reshape(nz, TOP, rows)
    plane_ids = (me_z * nt + jnp.arange(nt, dtype=jnp.int32)).astype(F32)
    member = jnp.any(route_all.astype(F32)[:, :, :, None] == plane_ids[None, None, None, :], axis=1)
    row_ids = lax.broadcasted_iota(jnp.int32, (rows, rows), 0)
    col_ids = lax.broadcasted_iota(jnp.int32, (rows, rows), 1)
    before = (col_ids < row_ids).astype(BF16)
    position = jnp.einsum("ij,sje->sei", before, member.astype(BF16), preferred_element_type=F32)
    key = jnp.where(jnp.swapaxes(member, 1, 2), position.astype(jnp.int32), -1)
    slots_iota = lax.broadcasted_iota(jnp.int32, (1, 1, CAP, 1), 2)

    def place_of(keys):
        return (keys[:, :, None, :] == slots_iota).astype(BF16)

    place = place_of(key)
    keys_near = [lax.dynamic_index_in_dim(key, me_t ^ k, 1, keepdims=False) for k in range(nt)]
    place_near = place_of(jnp.stack(keys_near, 1))
    own_place = keys_near[0][:, None, :] == slots_iota[0]

    def pick_rows(values):
        picked = jnp.einsum("sepk,skd->espd", place, values, preferred_element_type=F32)
        return picked.astype(BF16).reshape(nt, nz * CAP, part)

    def send_out(picked):
        return jnp.swapaxes(swap_t(picked), 0, 1).reshape(nz * CAP, width)

    def send_back(values):
        return [lay.over_t(part_for(values, k), k) for k in range(nt)]

    def combine(parts):
        parts = jnp.stack(parts).reshape(nt, nz, CAP, part)
        summed = jnp.einsum("sepk,espd->skd", place_near, parts, preferred_element_type=F32)
        return summed.astype(BF16)


    def rows_of(first, count):
        return jnp.swapaxes(front[:, first : first + count], 0, 1).reshape(count, width)

    query_t = rows_of(0, q_rows)
    down_t = rows_of(q_rows, down_rows)
    at = q_rows + down_rows
    router_t = rows_of(at, EXPERTS)
    gain_attn = front[:, at + EXPERTS].reshape(-1)
    gain_ffn = front[:, at + EXPERTS + 1].reshape(-1)
    gain_kv = front[:, at + EXPERTS + 2, :lat_loc].reshape(-1)
    at = at + 2 * EXPERTS
    out_w = rows_of(at, out_rows)
    up_w = front[:, at + out_rows :].reshape(LATENT, heads * (NOPE + VDIM))

    cosine, sine = angle_tables(rows)
    wide_cos, wide_sin = jnp.tile(cosine, (1, heads)), jnp.tile(sine, (1, heads))
    inputs = hidden.astype(F32)
    attn_inverse = inverse_rms(inputs)
    attn_scale = gain_attn.astype(F32)
    normed_low = (inputs * attn_inverse * attn_scale).astype(BF16)
    query = dot_nt(normed_low, query_t)
    nope_cols = heads * NOPE
    query_nope = query[:, :nope_cols].astype(BF16)
    query_rope = jnp.concatenate(
        rotate(
            query[:, nope_cols : nope_cols + heads * half],
            query[:, nope_cols + heads * half :],
            wide_cos,
            wide_sin,
        ),
        1,
    ).astype(BF16)
    latent_all = dot_nt(normed_low, down_t)
    latent = latent_all[:, :LATENT]
    kv_inverse = inverse_rms(latent)
    latent_hat = latent * kv_inverse
    kv_scale = gain_kv.astype(F32)
    latent_low = (latent_hat * kv_scale).astype(BF16)
    key_first, key_second = rotate(
        latent_all[:, LATENT : LATENT + half], latent_all[:, LATENT + half :], cosine, sine
    )
    key_rope = jnp.concatenate(
        [jnp.tile(key_first, (1, heads)), jnp.tile(key_second, (1, heads))], 1
    ).astype(BF16)
    keys_values = dot(latent_low, up_w).astype(BF16)
    attended_low, log_totals = attend(
        lengths, query_nope, query_rope, keys_values, key_rope, heads, score_scale
    )
    attn_part, cot_all = lax.optimization_barrier((dot(attended_low, out_w), cot_all))
    attn_sum = scatter_t(attn_part)
    residual = own_part(hidden).astype(F32) + attn_sum

    def row_mean(values):
        partial = jnp.sum(values, axis=-1).reshape(-1, 128)
        return lax.psum(partial, "tensor").reshape(-1, 1) * (1.0 / width)

    ffn_inverse = lax.rsqrt(row_mean(residual * residual) + EPSILON)
    ffn_hat = residual * ffn_inverse
    ffn_scale = lax.dynamic_slice_in_dim(gain_ffn, me_t * part, part, 0).astype(F32)
    ffn_part = (ffn_hat * ffn_scale).astype(BF16)

    ffn_part, cot_picked = lax.optimization_barrier((ffn_part, pick_rows(cot_all[:, :rows])))
    ffn_all = gather_z(ffn_part)
    cot_rows = send_out(cot_picked)
    picked = pick_rows(ffn_all)
    ffn_low = gather_t(ffn_part)
    shared_pack = jnp.concatenate(
        [jnp.swapaxes(w_shared_in, 1, 2).reshape(-1, d_loc), w_shared_out], 0
    )
    picked, shared_pack = lax.optimization_barrier((picked, shared_pack))
    expert_rows = send_out(picked)
    shared_all = lax.all_gather(shared_pack, "dp", axis=0, tiled=False)
    pieces = by_plane.reshape(nz * nt, 3, f_loc, d_loc)
    own_in, own_out = lay_out_weights(
        lay, ids, [lay.over_c(pieces, k) for k in range(nq)], f_loc, d_loc, width
    )
    router_probs = jax.nn.softmax(dot_nt(ffn_low, router_t), axis=-1)
    probs_turned = jnp.transpose(router_probs).reshape(EXPERTS, -1, 128)
    own_probs = in_order(
        [
            lay.over_z(
                lax.dynamic_index_in_dim(
                    probs_turned, (me_z ^ k) * nt + me_t, 0, keepdims=False
                ),
                k,
            )
            for k in range(nz)
        ],
        me_z,
        nz,
    ).reshape(nz, rows)
    gate_rows = jnp.sum(jnp.where(own_place, own_probs[:, None, :], 0.0), axis=-1).reshape(
        nz * CAP, 1
    )
    gate_up = dot_nt(expert_rows, own_in)
    gate_pre, up_pre = gate_up[:, :ffe], gate_up[:, ffe:]
    gate_sig = jax.nn.sigmoid(gate_pre)
    gate_silu = gate_pre * gate_sig
    active = (gate_silu * up_pre).astype(BF16)
    rows_out = (dot(active, own_out) * gate_rows).astype(BF16)
    out_parts = send_back(rows_out)
    active_grad_raw = dot_nt(cot_rows, own_out)
    gate_grad = jnp.sum(active.astype(F32) * active_grad_raw, axis=-1).reshape(nz, CAP)
    active_grad = active_grad_raw * gate_rows
    pre_low = jnp.concatenate(
        [
            active_grad * up_pre * gate_sig * (1.0 + gate_pre * (1.0 - gate_sig)),
            active_grad * gate_silu,
        ],
        1,
    ).astype(BF16)
    gated_active = (active.astype(F32) * gate_rows).astype(BF16)
    rows_grad = dot(pre_low, own_in).astype(BF16)
    grad_parts = send_back(rows_grad)
    routed = combine(out_parts)
    grad_in_own = dot_tn(pre_low, expert_rows).astype(BF16)
    grad_out_own = dot_tn(gated_active, cot_rows).astype(BF16)
    grad_pieces = take_apart(lay, ids, grad_in_own, grad_out_own, f_loc, d_loc, width)
    grad_parts, grad_pieces, routed = lax.optimization_barrier((grad_parts, grad_pieces, routed))
    routed = scatter_z(routed).astype(F32)
    routed_grad = scatter_z(combine(grad_parts)).astype(F32)
    grad_class = sum(lay.over_c(grad_pieces[k], k).astype(F32) for k in range(nq)).astype(BF16)
    routed_grad, grad_class = lax.optimization_barrier((routed_grad, grad_class))
    grad_plane = swap_z(grad_class.reshape(nz, nt, 3, f_loc, d_loc))

    token_grad = jnp.sum(jnp.where(own_place, gate_grad[:, :, None], 0.0), axis=1)
    token_grad = token_grad.reshape(nz, -1, 128)
    token_plane = jnp.stack(
        [
            lay.over_z(lax.dynamic_index_in_dim(token_grad, me_z ^ k, 0, keepdims=False), k)
            for k in range(nz)
        ]
    )
    token_home = jnp.stack([lay.over_t(token_plane, k) for k in range(nt)])
    experts = jnp.arange(EXPERTS, dtype=jnp.int32)
    came_from = (me_t ^ (experts % nt)) * nz + (me_z ^ (experts // nt))
    probs_grad = lax.dot_general(
        token_home.reshape(EXPERTS, rows),
        (experts[:, None] == came_from[None, :]).astype(F32),
        (((0,), (0,)), ((), ())),
        precision=lax.Precision.HIGHEST,
        preferred_element_type=F32,
    )

    ffs = w_shared_out.shape[0]
    shared_in = jnp.swapaxes(shared_all[:, : 2 * ffs], 0, 1).reshape(2 * ffs, width)
    shared_out = jnp.swapaxes(shared_all[:, 2 * ffs :], 0, 1).reshape(ffs, width)
    shared_pre = dot_nt(ffn_low, shared_in)
    shared_gate, shared_up = shared_pre[:, :ffs], shared_pre[:, ffs:]
    shared_sig = jax.nn.sigmoid(shared_gate)
    shared_silu = shared_gate * shared_sig
    shared_act = (shared_silu * shared_up).astype(BF16)
    shared_part = scatter_t_direct(dot(shared_act, shared_out))
    shared_act_grad = dot_nt(cot_low, shared_out)
    shared_pre_grad = jnp.concatenate(
        [
            shared_act_grad * shared_up * shared_sig * (1.0 + shared_gate * (1.0 - shared_sig)),
            shared_act_grad * shared_silu,
        ],
        1,
    ).astype(BF16)
    grad_shared_in = dot_tn(shared_pre_grad, ffn_low)
    grad_shared_out = dot_tn(shared_act, cot_low)
    shared_grad = scatter_t_direct(dot(shared_pre_grad, shared_in))

    logits_grad = router_probs * (
        probs_grad - jnp.sum(router_probs * probs_grad, axis=-1, keepdims=True)
    )
    router_part = lax.dot_general(
        logits_grad,
        ffn_low.astype(F32),
        (((0,), (0,)), ((), ())),
        precision=lax.Precision.HIGHEST,
        preferred_element_type=F32,
    )
    router_slice = lax.dynamic_slice_in_dim(router_t, me_t * part, part, 1)
    ffn_grad = (
        shared_grad
        + routed_grad
        + lax.dot_general(
            logits_grad,
            router_slice.astype(F32),
            (((1,), (0,)), ((), ())),
            precision=lax.Precision.HIGHEST,
            preferred_element_type=F32,
        )
    )
    scaled = ffn_scale * ffn_grad
    ffn_gain_part = jnp.sum(ffn_grad * ffn_hat, axis=0)
    residual_grad = cot_part.astype(F32) + ffn_inverse * (
        scaled - ffn_hat * row_mean(ffn_hat * scaled)
    )
    residual_low = gather_t(residual_grad.astype(BF16))

    output = gather_t_direct((residual + routed + shared_part).astype(BF16))

    grad_out_w = dot_tn(attended_low, residual_low)
    attended_grad = dot_nt(residual_low, out_w).astype(BF16)
    query_nope_grad, query_turned_grad, kv_grad, rope_grad = attend_back(
        lengths,
        query_nope,
        query_rope,
        keys_values,
        key_rope,
        attended_grad,
        log_totals,
        heads,
        score_scale,
    )
    turned_first, turned_second = rotate_back(
        query_turned_grad[:, : heads * half], query_turned_grad[:, heads * half :], wide_cos, wide_sin
    )
    query_grad = jnp.concatenate(
        [query_nope_grad, turned_first.astype(BF16), turned_second.astype(BF16)], 1
    )
    rope_sum = rope_grad.reshape(rows, 2, heads, half).sum(2)
    key_rope_part = jnp.concatenate(
        rotate_back(rope_sum[:, 0], rope_sum[:, 1], cosine, sine), 1
    )
    latent_part = dot_nt(kv_grad, up_w)
    grad_kv_gain = jnp.sum(latent_part * latent_hat, axis=0)
    scaled_kv = kv_scale * latent_part
    latent_back = kv_inverse * (
        scaled_kv - latent_hat * jnp.mean(latent_hat * scaled_kv, axis=-1, keepdims=True)
    )
    down_grad = jnp.concatenate([latent_back, key_rope_part], -1).astype(BF16)
    normed_grad = scatter_t(dot(query_grad, query_t) + dot(down_grad, down_t))
    normed_grad, grad_plane = lax.optimization_barrier((normed_grad, grad_plane))
    attn_hat = own_part(hidden).astype(F32) * attn_inverse
    scaled_in = lax.dynamic_slice_in_dim(attn_scale, me_t * part, part, 0) * normed_grad
    attn_gain_part = jnp.sum(normed_grad * attn_hat, axis=0)
    input_grad = residual_grad + attn_inverse * (
        scaled_in - attn_hat * row_mean(attn_hat * scaled_in)
    )
    grad_home = swap_t(jnp.swapaxes(grad_plane, 0, 1)).reshape(EXPERTS, 3, f_loc, d_loc)
    grad_expert_in, grad_expert_out = home_gradients(lay, ids, grad_home, f_loc, d_loc)
    grad_hidden = gather_t(input_grad.astype(BF16))

    def sum_dp(values):
        return lax.psum_scatter(values, "dp", scatter_dimension=0, tiled=False).astype(F32)

    def by_owner(values):
        return jnp.swapaxes(values.astype(BF16).reshape(-1, ndp, d_loc), 0, 1)

    def spread(values):
        return lax.dynamic_update_slice(
            jnp.zeros((1, width), F32), values[None], (jnp.int32(0), me_t * part)
        )

    kv_gain_row = jnp.pad(
        grad_kv_gain.reshape(ndp, lat_loc), ((0, 0), (0, d_loc - lat_loc))
    ).reshape(1, width)
    gain_grads = jnp.concatenate([spread(attn_gain_part), spread(ffn_gain_part), kv_gain_row], 0)
    front_sum = sum_dp(
        jnp.concatenate(
            [
                by_owner(dot_tn(down_grad, normed_low)),
                by_owner(jnp.pad(gain_grads, ((0, 13), (0, 0)))),
                by_owner(router_part),
                by_owner(dot_tn(query_grad, normed_low)),
                by_owner(grad_out_w),
                dot_tn(latent_low, kv_grad).astype(BF16).reshape(ndp, -1, d_loc),
            ],
            1,
        )
    )
    shared_grads = jnp.concatenate([by_owner(grad_shared_in), by_owner(grad_shared_out)], 1)
    front_sum, shared_grads = lax.optimization_barrier((front_sum, shared_grads))
    shared_sum = sum_dp(shared_grads)
    own_sum = lax.psum(front_sum[: down_rows + EXPERTS], "tensor")
    at = down_rows + 2 * EXPERTS
    return (
        output,
        grad_hidden,
        own_sum[down_rows],
        jnp.transpose(by_head(front_sum[at : at + q_rows])),
        jnp.transpose(own_sum[:down_rows]),
        own_sum[down_rows + 2, :lat_loc],
        front_sum[at + q_rows + out_rows :].reshape(w_kv_up.shape),
        front_sum[at + q_rows : at + q_rows + out_rows],
        own_sum[down_rows + 1],
        jnp.transpose(front_sum[down_rows + EXPERTS : at]),
        grad_expert_in,
        grad_expert_out,
        jnp.swapaxes(shared_sum[: 2 * ffs].reshape(2, ffs, d_loc), 1, 2),
        shared_sum[2 * ffs :],
    )


def solution(mesh):
    return jax.shard_map(
        functools.partial(body, Layout(mesh.shape["dp"], mesh.shape["tensor"])),
        mesh=mesh,
        in_specs=(
            P("dp", None),
            P("dp"),
            P("dp", None),
            P("dp"),
            P("dp", "tensor"),
            P("dp", None),
            P("dp"),
            P("dp", "tensor"),
            P("tensor", "dp"),
            P("dp"),
            P("dp", None),
            P(None, None, "dp", "tensor"),
            P(None, "tensor", "dp"),
            P(None, "dp", "tensor"),
            P("tensor", "dp"),
            P("dp", None),
        ),
        out_specs=(
            P("dp", None),
            P("dp", None),
            P("dp"),
            P("dp", "tensor"),
            P("dp", None),
            P("dp"),
            P("dp", "tensor"),
            P("tensor", "dp"),
            P("dp"),
            P("dp", None),
            P(None, None, "dp", "tensor"),
            P(None, "tensor", "dp"),
            P(None, "dp", "tensor"),
            P("tensor", "dp"),
        ),
        check_vma=False,
    )
```

```python
import functools
import math

import jax
import jax.numpy as jnp
from jax import lax
from jax.experimental import pallas as pl
from jax.experimental.pallas import tpu as pltpu
from jax.sharding import PartitionSpec as P

NOPE = 128
ROPE = 64
VDIM = 128
LATENT = 512
TOP = 6
EXPERTS = 16
CAP = 512

EPSILON = 1e-06
NEGATIVE = -1e30
F32 = jnp.float32
BF16 = jnp.bfloat16


def dot(a, b):
    return jnp.dot(a, b, preferred_element_type=F32)


def dot_nt(a, b):
    return lax.dot_general(a, b, (((1,), (1,)), ((), ())), preferred_element_type=F32)


def dot_tn(a, b):
    return lax.dot_general(a, b, (((0,), (0,)), ((), ())), preferred_element_type=F32)


def rotate(first, second, cosine, sine):
    return first * cosine - second * sine, second * cosine + first * sine


def rotate_back(first, second, cosine, sine):
    return first * cosine + second * sine, second * cosine - first * sine


def angle_tables(rows_count):
    positions = jnp.arange(rows_count, dtype=F32)
    freqs = jnp.exp(jnp.arange(ROPE // 2, dtype=F32) * (-2.0 * math.log(10000.0) / ROPE))
    angles = positions[:, None] * freqs[None, :]
    return (jnp.cos(angles), jnp.sin(angles))


def inverse_rms(values):
    return lax.rsqrt(jnp.mean(values * values, axis=-1, keepdims=True) + EPSILON)


class Layout:
    def __init__(self, n_dp, n_tensor):
        self.dp, self.t = n_dp, n_tensor
        self.q = n_dp * n_tensor // EXPERTS
        self.z = n_dp // self.q
        if self.z * self.t != EXPERTS or self.z * self.q != n_dp:
            raise ValueError("mesh")
        self.z_groups = [[c + self.q * z for z in range(self.z)] for c in range(self.q)]

    def over_t(self, values, k):
        if k == 0:
            return values
        return lax.ppermute(values, "tensor", [(i, i ^ k) for i in range(self.t)])

    def over_z(self, values, k):
        if k == 0:
            return values
        return lax.ppermute(values, "dp", [(d, d ^ (k * self.q)) for d in range(self.dp)])

    def over_c(self, values, k):
        if k == 0:
            return values
        return lax.ppermute(values, "dp", [(d, d ^ k) for d in range(self.dp)])


def lay_out_weights(lay, ids, stacks, f_loc, d_loc, width):
    ffe = f_loc * lay.t

    def kernel(ids_ref, *refs):
        sources, (in_ref, out_ref) = refs[: lay.q], refs[lay.q :]
        for kc in range(lay.q):
            columns = pl.ds(pl.multiple_of((ids_ref[1] ^ kc) * d_loc, 128), d_loc)
            for g in range(2):
                in_ref[g, :, columns] = sources[kc][0, g]
            out_ref[:, columns] = sources[kc][0, 2]

    own_in, own_out = pl.pallas_call(
        kernel,
        out_shape=(
            jax.ShapeDtypeStruct((2, ffe, width), BF16),
            jax.ShapeDtypeStruct((ffe, width), BF16),
        ),
        grid_spec=pltpu.PrefetchScalarGridSpec(
            num_scalar_prefetch=1,
            grid=(lay.t, lay.z),
            in_specs=[
                pl.BlockSpec((1, 3, f_loc, d_loc), lambda kt, kz, ids: (kz * lay.t + kt, 0, 0, 0))
            ]
            * lay.q,
            out_specs=(
                pl.BlockSpec(
                    (2, f_loc, lay.q * d_loc), lambda kt, kz, ids: (0, kt, kz)
                ),
                pl.BlockSpec((f_loc, lay.q * d_loc), lambda kt, kz, ids: (kt, kz)),
            ),
        ),
        cost_estimate=pl.CostEstimate(
            flops=0, bytes_accessed=12 * ffe * width, transcendentals=0
        ),
        compiler_params=pltpu.CompilerParams(vmem_limit_bytes=32 << 20),
        name="lay_out_weights",
    )(ids, *stacks)
    return own_in.reshape(2 * ffe, width), own_out


def take_apart(lay, ids, grad_in, grad_out, f_loc, d_loc, width):
    ffe = f_loc * lay.t

    def kernel(ids_ref, in_ref, out_ref, *targets):
        for kc in range(lay.q):
            columns = pl.ds(pl.multiple_of((ids_ref[1] ^ kc) * d_loc, 128), d_loc)
            for g in range(2):
                targets[kc][0, g] = in_ref[g, :, columns]
            targets[kc][0, 2] = out_ref[:, columns]

    shape = jax.ShapeDtypeStruct((lay.t * lay.z, 3, f_loc, d_loc), BF16)
    spec = pl.BlockSpec((1, 3, f_loc, d_loc), lambda kt, kz, ids: (kz * lay.t + kt, 0, 0, 0))
    return pl.pallas_call(
        kernel,
        out_shape=(shape,) * lay.q,
        grid_spec=pltpu.PrefetchScalarGridSpec(
            num_scalar_prefetch=1,
            grid=(lay.t, lay.z),
            in_specs=[
                pl.BlockSpec(
                    (2, f_loc, lay.q * d_loc), lambda kt, kz, ids: (0, kt, kz)
                ),
                pl.BlockSpec((f_loc, lay.q * d_loc), lambda kt, kz, ids: (kt, kz)),
            ],
            out_specs=(spec,) * lay.q,
        ),
        cost_estimate=pl.CostEstimate(
            flops=0, bytes_accessed=12 * ffe * width, transcendentals=0
        ),
        compiler_params=pltpu.CompilerParams(vmem_limit_bytes=32 << 20),
        name="take_apart",
    )(ids, grad_in.reshape(2, ffe, width), grad_out)


def home_gradients(lay, ids, pieces, f_loc, d_loc):
    def kernel(ids_ref, piece_ref, in_ref, out_ref):
        in_ref[0] = piece_ref[0, :2].astype(F32)
        out_ref[0] = piece_ref[0, 2].astype(F32)

    def pick(e, ids):
        return (e % lay.t * lay.z + e // lay.t, 0, 0, 0)

    grad_in, grad_out = pl.pallas_call(
        kernel,
        out_shape=(
            jax.ShapeDtypeStruct((EXPERTS, 2, f_loc, d_loc), F32),
            jax.ShapeDtypeStruct((EXPERTS, f_loc, d_loc), F32),
        ),
        grid_spec=pltpu.PrefetchScalarGridSpec(
            num_scalar_prefetch=1,
            grid=(EXPERTS,),
            in_specs=[pl.BlockSpec((1, 3, f_loc, d_loc), pick)],
            out_specs=(
                pl.BlockSpec((1, 2, f_loc, d_loc), lambda e, ids: (e, 0, 0, 0)),
                pl.BlockSpec((1, f_loc, d_loc), lambda e, ids: (e, 0, 0)),
            ),
        ),
        cost_estimate=pl.CostEstimate(
            flops=0, bytes_accessed=18 * EXPERTS * f_loc * d_loc, transcendentals=0
        ),
        name="home_gradients",
    )(ids, pieces)
    return jnp.swapaxes(grad_in, 2, 3), grad_out


def join_columns(parts, me, count):
    rows, part = parts[0].shape
    block = min(256, rows)

    def kernel(me_ref, *refs):
        for k in range(count):

            @pl.when(pl.program_id(1) == k)
            def _(k=k):
                refs[count][...] = refs[k][...]

    return pl.pallas_call(
        kernel,
        out_shape=jax.ShapeDtypeStruct((rows, count * part), parts[0].dtype),
        grid_spec=pltpu.PrefetchScalarGridSpec(
            num_scalar_prefetch=1,
            grid=(rows // block, count),
            in_specs=[pl.BlockSpec((block, part), lambda i, k, me: (i, 0))] * count,
            out_specs=pl.BlockSpec((block, part), lambda i, k, me: (i, me[0] ^ k)),
        ),
        cost_estimate=pl.CostEstimate(
            flops=0, bytes_accessed=4 * rows * part * count, transcendentals=0
        ),
        name="join_columns",
    )(me.reshape(1).astype(jnp.int32), *parts)


def score_block(q_ref, r_ref, k_ref, kr_ref, head, step, keys, block, length, scale):
    half = r_ref.shape[1] // 2
    lanes = lax.broadcasted_iota(jnp.int32, r_ref.shape, 1) % half // (ROPE // 2)
    turned = jnp.where(lanes == head, r_ref[...], jnp.zeros_like(r_ref))
    raw = lax.dot_general(
        q_ref[...], k_ref[:keys], (((1,), (1,)), ((), ())), preferred_element_type=F32
    ) + lax.dot_general(
        turned, kr_ref[:keys], (((1,), (1,)), ((), ())), preferred_element_type=F32
    )
    rows = lax.broadcasted_iota(jnp.int32, raw.shape, 0) + step * block
    cols = lax.broadcasted_iota(jnp.int32, raw.shape, 1)
    allowed = (cols <= rows) & (cols < length)
    return jnp.where(allowed, raw * scale, NEGATIVE), turned


def attend(length, query, query_rope, kv, key_rope, heads, scale):
    rows = query.shape[0]
    block = min(256, rows)
    steps = rows // block

    def kernel(len_ref, q_ref, r_ref, k_ref, v_ref, kr_ref, o_ref, total_ref):
        head, step = pl.program_id(0), pl.program_id(1)
        for n in range(steps):

            @pl.when(step == n)
            def _(n=n):
                keys = (n + 1) * block
                scores, _ = score_block(
                    q_ref, r_ref, k_ref, kr_ref, head, n, keys, block, len_ref[0], scale
                )
                highest = jnp.max(scores, axis=-1, keepdims=True)
                expo = jnp.exp(scores - highest)
                totals = jnp.sum(expo, axis=-1, keepdims=True)
                weights = (expo * (1.0 / totals)).astype(BF16)
                o_ref[...] = dot(weights, v_ref[:keys]).astype(BF16)
                total_ref[0] = jnp.broadcast_to(highest + jnp.log(totals), (block, 128))

    return pl.pallas_call(
        kernel,
        out_shape=(
            jax.ShapeDtypeStruct((rows, heads * VDIM), BF16),
            jax.ShapeDtypeStruct((heads, rows, 128), F32),
        ),
        grid_spec=pltpu.PrefetchScalarGridSpec(
            num_scalar_prefetch=1,
            grid=(heads, steps),
            in_specs=[
                pl.BlockSpec((block, NOPE), lambda h, i, n: (i, h)),
                pl.BlockSpec((block, query_rope.shape[1]), lambda h, i, n: (i, 0)),
                pl.BlockSpec((rows, NOPE), lambda h, i, n: (0, 2 * h)),
                pl.BlockSpec((rows, VDIM), lambda h, i, n: (0, 2 * h + 1)),
                pl.BlockSpec((rows, key_rope.shape[1]), lambda h, i, n: (0, 0)),
            ],
            out_specs=(
                pl.BlockSpec((block, VDIM), lambda h, i, n: (i, h)),
                pl.BlockSpec((1, block, 128), lambda h, i, n: (h, i, 0)),
            ),
        ),
        cost_estimate=pl.CostEstimate(
            flops=heads * rows * rows * 512,
            bytes_accessed=8 * rows * heads * 512,
            transcendentals=heads * rows * rows,
        ),
        compiler_params=pltpu.CompilerParams(vmem_limit_bytes=32 << 20),
        name="attend",
    )(length, query, query_rope, kv, kv, key_rope)


def attend_back(length, query, query_rope, kv, key_rope, out_grad, log_totals, heads, scale):
    rows = query.shape[0]
    block = min(256, rows)
    steps = rows // block
    turned_cols = query_rope.shape[1]

    def kernel(
        len_ref, q_ref, r_ref, k_ref, v_ref, kr_ref, do_ref, total_ref,
        dq_ref, dr_ref, dkv_ref, dkr_ref, dk_acc, dv_acc,
    ):
        head, step = pl.program_id(0), pl.program_id(1)

        @pl.when(step == 0)
        def _():
            dk_acc[...] = jnp.zeros_like(dk_acc)
            dv_acc[...] = jnp.zeros_like(dv_acc)

        @pl.when((step == 0) & (head == 0))
        def _():
            dr_ref[...] = jnp.zeros_like(dr_ref)
            dkr_ref[...] = jnp.zeros_like(dkr_ref)

        for n in range(steps):

            @pl.when(step == n)
            def _(n=n):
                keys = (n + 1) * block
                scores, turned = score_block(
                    q_ref, r_ref, k_ref, kr_ref, head, n, keys, block, len_ref[0], scale
                )
                probs = jnp.exp(scores - total_ref[0][:, :1])
                prob_grad = lax.dot_general(
                    do_ref[...], v_ref[:keys], (((1,), (1,)), ((), ())), preferred_element_type=F32
                )
                centre = jnp.sum(probs * prob_grad, axis=-1, keepdims=True)
                score_grad = (probs * (prob_grad - centre)).astype(BF16)
                probs_low = probs.astype(BF16)
                dq_ref[...] = (dot(score_grad, k_ref[:keys]) * scale).astype(BF16)
                half = turned_cols // 2
                lanes = lax.broadcasted_iota(jnp.int32, (block, turned_cols), 1)
                lanes = lanes % half // (ROPE // 2)
                turned_grad = dot(score_grad, kr_ref[:keys]) * scale
                dr_ref[n * block : keys] += jnp.where(lanes == head, turned_grad, 0.0)
                dk_acc[:keys] += dot_tn(score_grad, q_ref[...]) * scale
                dkr_ref[:keys] += dot_tn(score_grad, turned) * scale
                dv_acc[:keys] += dot_tn(probs_low, do_ref[...])

        @pl.when(step == steps - 1)
        def _():
            dkv_ref[:, :NOPE] = dk_acc[...].astype(BF16)
            dkv_ref[:, NOPE:] = dv_acc[...].astype(BF16)

    return pl.pallas_call(
        kernel,
        out_shape=(
            jax.ShapeDtypeStruct((rows, heads * NOPE), BF16),
            jax.ShapeDtypeStruct((rows, turned_cols), F32),
            jax.ShapeDtypeStruct((rows, heads * (NOPE + VDIM)), BF16),
            jax.ShapeDtypeStruct((rows, turned_cols), F32),
        ),
        grid_spec=pltpu.PrefetchScalarGridSpec(
            num_scalar_prefetch=1,
            grid=(heads, steps),
            in_specs=[
                pl.BlockSpec((block, NOPE), lambda h, i, n: (i, h)),
                pl.BlockSpec((block, turned_cols), lambda h, i, n: (i, 0)),
                pl.BlockSpec((rows, NOPE), lambda h, i, n: (0, 2 * h)),
                pl.BlockSpec((rows, VDIM), lambda h, i, n: (0, 2 * h + 1)),
                pl.BlockSpec((rows, turned_cols), lambda h, i, n: (0, 0)),
                pl.BlockSpec((block, VDIM), lambda h, i, n: (i, h)),
                pl.BlockSpec((1, block, 128), lambda h, i, n: (h, i, 0)),
            ],
            out_specs=(
                pl.BlockSpec((block, NOPE), lambda h, i, n: (i, h)),
                pl.BlockSpec((rows, turned_cols), lambda h, i, n: (0, 0)),
                pl.BlockSpec((rows, NOPE + VDIM), lambda h, i, n: (0, h)),
                pl.BlockSpec((rows, turned_cols), lambda h, i, n: (0, 0)),
            ),
            scratch_shapes=[pltpu.VMEM((rows, NOPE), F32), pltpu.VMEM((rows, VDIM), F32)],
        ),
        cost_estimate=pl.CostEstimate(
            flops=heads * rows * rows * 1600,
            bytes_accessed=16 * rows * heads * 512,
            transcendentals=heads * rows * rows,
        ),
        compiler_params=pltpu.CompilerParams(vmem_limit_bytes=40 << 20),
        name="attend_back",
    )(length, query, query_rope, kv, kv, key_rope, out_grad, log_totals)


def in_order(values, me, count):
    zero = jnp.zeros_like(values[0])
    ordered = []
    for j in range(count):
        total = zero
        for k in range(count):
            total = jnp.where((me ^ k) == j, values[k], total)
        ordered.append(total)
    return jnp.stack(ordered)


def body(
    lay,
    hidden,
    lengths,
    routes,
    attn_gain,
    w_query,
    w_kv_down,
    kv_gain,
    w_kv_up,
    w_out,
    ffn_gain,
    w_router,
    w_expert_in,
    w_expert_out,
    w_shared_in,
    w_shared_out,
    cotangent,
):
    rows, width = hidden.shape
    nz, nt, nq, ndp = lay.z, lay.t, lay.q, lay.dp
    me_dp = lax.axis_index("dp")
    me_t = lax.axis_index("tensor")
    me_z = me_dp // nq
    me_c = me_dp % nq
    part = width // nt
    d_loc = w_query.shape[0]
    f_loc = w_expert_out.shape[1]
    ffe = f_loc * nt
    heads = w_query.shape[1] // (NOPE + ROPE)
    score_scale = (NOPE + ROPE) ** (-0.5)

    def own_part(values):
        return lax.dynamic_slice_in_dim(values, me_t * part, part, 1)

    def gather_z(values):
        return lax.all_gather(values, "dp", axis=0, tiled=False, axis_index_groups=lay.z_groups)

    def scatter_z(values):
        return lax.psum_scatter(
            values, "dp", scatter_dimension=0, tiled=False, axis_index_groups=lay.z_groups
        )

    def gather_t(values):
        return lax.all_gather(values, "tensor", axis=1, tiled=True)

    def scatter_t(values):
        return lax.psum_scatter(
            values.astype(BF16), "tensor", scatter_dimension=1, tiled=True
        ).astype(F32)

    def swap_t(values):
        return lax.all_to_all(values, "tensor", split_axis=0, concat_axis=0, tiled=True)

    def swap_z(values):
        return lax.all_to_all(
            values,
            "dp",
            split_axis=0,
            concat_axis=0,
            axis_index_groups=lay.z_groups,
            tiled=True,
        )

    def gather_t_direct(values):
        return join_columns([lay.over_t(values, k) for k in range(nt)], me_t, nt)

    def part_for(values, k):
        return lax.dynamic_slice_in_dim(values, (me_t ^ k) * part, part, 1)

    def scatter_t_direct(values):
        total = part_for(values, 0)
        for k in range(1, nt):
            total = total + lay.over_t(part_for(values, k).astype(BF16), k).astype(F32)
        return total

    ids = jnp.stack([me_z, me_c, me_t]).astype(jnp.int32)

    packed = jnp.concatenate(
        [jnp.swapaxes(w_expert_in, 2, 3), w_expert_out[:, None]], 1
    ).reshape(nz, nt, 3, f_loc, d_loc)
    by_column = swap_t(jnp.swapaxes(packed, 0, 1))

    lat_loc = kv_gain.shape[0]
    q_rows, down_rows, out_rows = w_query.shape[1], w_kv_down.shape[1], w_out.shape[0]
    half = ROPE // 2

    def by_kind(turned):
        split = turned.reshape(heads, NOPE + ROPE, -1)
        return jnp.concatenate(
            [
                split[:, :NOPE].reshape(heads * NOPE, -1),
                split[:, NOPE : NOPE + half].reshape(heads * half, -1),
                split[:, NOPE + half :].reshape(heads * half, -1),
            ],
            0,
        )

    def by_head(rows_in):
        nope = rows_in[: heads * NOPE].reshape(heads, NOPE, -1)
        first = rows_in[heads * NOPE : heads * (NOPE + half)].reshape(heads, half, -1)
        second = rows_in[heads * (NOPE + half) :].reshape(heads, half, -1)
        return jnp.concatenate([nope, first, second], 1).reshape(heads * (NOPE + ROPE), -1)

    gains = jnp.stack([attn_gain, ffn_gain, jnp.pad(kv_gain, (0, d_loc - lat_loc))])
    front_pack = jnp.concatenate(
        [
            by_kind(jnp.transpose(w_query)),
            jnp.transpose(w_kv_down),
            jnp.transpose(w_router),
            jnp.pad(gains, ((0, 13), (0, 0))),
            w_out,
            w_kv_up.reshape(-1, d_loc),
        ],
        0,
    )
    front = lax.all_gather(front_pack, "dp", axis=0, tiled=False)

    valid_length = lengths[0]
    valid_rows = lax.broadcasted_iota(jnp.int32, (rows, 1), 0) < valid_length
    cot_low = jnp.where(valid_rows, cotangent, jnp.zeros_like(cotangent))
    cot_part = own_part(cot_low)
    route_rows = jnp.transpose(routes).astype(BF16).reshape(-1)
    route_rows = jnp.pad(route_rows, (0, -route_rows.shape[0] % (16 * part))).reshape(-1, part)
    inputs = hidden.astype(F32)
    attn_inverse = inverse_rms(inputs)
    cosine, sine = angle_tables(rows)
    wide_cos, wide_sin = jnp.tile(cosine, (1, heads)), jnp.tile(sine, (1, heads))
    front, cot_ready, attn_inverse, wide_cos, wide_sin = lax.optimization_barrier(
        (
            front,
            jnp.concatenate([cot_part, route_rows], 0),
            attn_inverse,
            wide_cos,
            wide_sin,
        )
    )
    cot_all = gather_z(cot_ready)

    route_all = cot_all[:, rows:].reshape(nz, -1)[:, : TOP * rows].reshape(nz, TOP, rows)
    plane_ids = (me_z * nt + jnp.arange(nt, dtype=jnp.int32)).astype(F32)
    member = jnp.any(route_all.astype(F32)[:, :, :, None] == plane_ids[None, None, None, :], axis=1)
    row_ids = lax.broadcasted_iota(jnp.int32, (rows, rows), 0)
    col_ids = lax.broadcasted_iota(jnp.int32, (rows, rows), 1)
    before = (col_ids < row_ids).astype(BF16)
    position = jnp.einsum("ij,sje->sei", before, member.astype(BF16), preferred_element_type=F32)
    key = jnp.where(jnp.swapaxes(member, 1, 2), position.astype(jnp.int32), -1)
    slots_iota = lax.broadcasted_iota(jnp.int32, (1, 1, CAP, 1), 2)

    def place_of(keys):
        return (keys[:, :, None, :] == slots_iota).astype(BF16)

    place = place_of(key)
    keys_near = [lax.dynamic_index_in_dim(key, me_t ^ k, 1, keepdims=False) for k in range(nt)]
    place_near = place_of(jnp.stack(keys_near, 1))
    own_place = keys_near[0][:, None, :] == slots_iota[0]

    def pick_rows(places, values):
        picked = jnp.einsum("sepk,skd->espd", places, values, preferred_element_type=F32)
        return picked.astype(BF16).reshape(nt, nz * CAP, part)

    def send_out(picked):
        return jnp.swapaxes(swap_t(picked), 0, 1).reshape(nz * CAP, width)

    def send_back(values):
        return swap_t(jnp.swapaxes(values.reshape(nz * CAP, nt, part), 0, 1))

    def combine(parts):
        parts = parts.reshape(nt, nz, CAP, part)
        summed = jnp.einsum("sepk,espd->skd", place, parts, preferred_element_type=F32)
        return summed.astype(BF16)


    def rows_of(first, count):
        return jnp.swapaxes(front[:, first : first + count], 0, 1).reshape(count, width)

    query_t = rows_of(0, q_rows)
    down_t = rows_of(q_rows, down_rows)
    at = q_rows + down_rows
    router_t = rows_of(at, EXPERTS)
    gain_attn = front[:, at + EXPERTS].reshape(-1)
    gain_ffn = front[:, at + EXPERTS + 1].reshape(-1)
    gain_kv = front[:, at + EXPERTS + 2, :lat_loc].reshape(-1)
    at = at + 2 * EXPERTS
    out_w = rows_of(at, out_rows)
    up_w = front[:, at + out_rows :].reshape(LATENT, heads * (NOPE + VDIM))

    attn_scale = gain_attn.astype(F32)
    normed_low = (inputs * attn_inverse * attn_scale).astype(BF16)
    query = dot_nt(normed_low, query_t)
    nope_cols = heads * NOPE
    query_nope = query[:, :nope_cols].astype(BF16)
    query_rope = jnp.concatenate(
        rotate(
            query[:, nope_cols : nope_cols + heads * half],
            query[:, nope_cols + heads * half :],
            wide_cos,
            wide_sin,
        ),
        1,
    ).astype(BF16)
    turned_t = jnp.concatenate(
        [down_t[:LATENT]]
        + [down_t[LATENT : LATENT + half]] * heads
        + [down_t[LATENT + half :]] * heads,
        0,
    )
    latent_all = dot_nt(normed_low, turned_t)
    latent_all, by_column = lax.optimization_barrier((latent_all, by_column))
    by_plane = swap_z(jnp.swapaxes(by_column, 0, 1))
    latent = latent_all[:, :LATENT]
    kv_inverse = inverse_rms(latent)
    latent_hat = latent * kv_inverse
    kv_scale = gain_kv.astype(F32)
    latent_low = (latent_hat * kv_scale).astype(BF16)
    key_rope = jnp.concatenate(
        rotate(
            latent_all[:, LATENT : LATENT + heads * half],
            latent_all[:, LATENT + heads * half :],
            wide_cos,
            wide_sin,
        ),
        1,
    ).astype(BF16)
    keys_values = dot(latent_low, up_w).astype(BF16)
    attended_low, log_totals = attend(
        lengths, query_nope, query_rope, keys_values, key_rope, heads, score_scale
    )
    attn_part, cot_all = lax.optimization_barrier((dot(attended_low, out_w), cot_all))
    attn_sum = scatter_t(attn_part)
    residual = own_part(hidden).astype(F32) + attn_sum

    def row_mean(values):
        partial = jnp.sum(values, axis=-1).reshape(-1, 128)
        return lax.psum(partial, "tensor").reshape(-1, 1) * (1.0 / width)

    ffn_inverse = lax.rsqrt(row_mean(residual * residual) + EPSILON)
    ffn_hat = residual * ffn_inverse
    ffn_scale = lax.dynamic_slice_in_dim(gain_ffn, me_t * part, part, 0).astype(F32)
    ffn_part = (ffn_hat * ffn_scale).astype(BF16)

    ffn_part, cot_picked = lax.optimization_barrier((ffn_part, pick_rows(place_near, cot_all[:, :rows])))
    ffn_all = gather_z(ffn_part)
    cot_rows = join_columns([lay.over_t(cot_picked[k], k) for k in range(nt)], me_t, nt)
    ffn_low = gather_t_direct(ffn_part)
    ffn_all, cot_rows, ffn_low = lax.optimization_barrier((ffn_all, cot_rows, ffn_low))
    picked = pick_rows(place, ffn_all)
    shared_pack = jnp.concatenate(
        [jnp.swapaxes(w_shared_in, 1, 2).reshape(-1, d_loc), w_shared_out], 0
    )
    picked, shared_pack = lax.optimization_barrier((picked, shared_pack))
    expert_rows = send_out(picked)
    shared_all = lax.all_gather(shared_pack, "dp", axis=0, tiled=False)
    pieces = by_plane.reshape(nz * nt, 3, f_loc, d_loc)
    own_in, own_out = lay_out_weights(
        lay, ids, [lay.over_c(pieces, k) for k in range(nq)], f_loc, d_loc, width
    )
    router_probs = jax.nn.softmax(dot_nt(ffn_low, router_t), axis=-1)
    probs_turned = jnp.transpose(router_probs).reshape(EXPERTS, -1, 128)
    own_probs = in_order(
        [
            lay.over_z(
                lax.dynamic_index_in_dim(
                    probs_turned, (me_z ^ k) * nt + me_t, 0, keepdims=False
                ),
                k,
            )
            for k in range(nz)
        ],
        me_z,
        nz,
    ).reshape(nz, rows)
    gate_rows = jnp.sum(jnp.where(own_place, own_probs[:, None, :], 0.0), axis=-1).reshape(
        nz * CAP, 1
    )
    gate_up = dot_nt(expert_rows, own_in)
    gate_pre, up_pre = gate_up[:, :ffe], gate_up[:, ffe:]
    gate_sig = jax.nn.sigmoid(gate_pre)
    gate_silu = gate_pre * gate_sig
    active = (gate_silu * up_pre).astype(BF16)
    rows_out = (dot(active, own_out) * gate_rows).astype(BF16)
    rows_out, cot_rows = lax.optimization_barrier((rows_out, cot_rows))
    out_parts = send_back(rows_out)
    active_grad_raw = dot_nt(cot_rows, own_out)
    gate_grad = jnp.sum(active.astype(F32) * active_grad_raw, axis=-1).reshape(nz, CAP)
    active_grad = active_grad_raw * gate_rows
    pre_low = jnp.concatenate(
        [
            active_grad * up_pre * gate_sig * (1.0 + gate_pre * (1.0 - gate_sig)),
            active_grad * gate_silu,
        ],
        1,
    ).astype(BF16)
    gated_active = (active.astype(F32) * gate_rows).astype(BF16)
    rows_grad = dot(pre_low, own_in).astype(BF16)
    rows_grad, out_parts = lax.optimization_barrier((rows_grad, out_parts))
    grad_parts = send_back(rows_grad)
    routed, pre_low = lax.optimization_barrier((combine(out_parts), pre_low))
    routed = scatter_z(routed).astype(F32)
    grad_in_own = dot_tn(pre_low, expert_rows).astype(BF16)
    grad_out_own = dot_tn(gated_active, cot_rows).astype(BF16)
    grad_parts, grad_in_own, grad_out_own = lax.optimization_barrier(
        (grad_parts, grad_in_own, grad_out_own)
    )
    grad_pieces = take_apart(lay, ids, grad_in_own, grad_out_own, f_loc, d_loc, width)
    grad_class = sum(lay.over_c(grad_pieces[k], k).astype(F32) for k in range(nq)).astype(BF16)
    routed_grad = scatter_z(combine(grad_parts)).astype(F32)
    grad_plane = swap_z(grad_class.reshape(nz, nt, 3, f_loc, d_loc))

    token_grad = jnp.sum(jnp.where(own_place, gate_grad[:, :, None], 0.0), axis=1)
    token_grad = token_grad.reshape(nz, -1, 128)
    token_plane = jnp.stack(
        [
            lay.over_z(lax.dynamic_index_in_dim(token_grad, me_z ^ k, 0, keepdims=False), k)
            for k in range(nz)
        ]
    )
    token_home = jnp.stack([lay.over_t(token_plane, k) for k in range(nt)])
    experts = jnp.arange(EXPERTS, dtype=jnp.int32)
    came_from = (me_t ^ (experts % nt)) * nz + (me_z ^ (experts // nt))
    probs_grad = lax.dot_general(
        token_home.reshape(EXPERTS, rows),
        (experts[:, None] == came_from[None, :]).astype(F32),
        (((0,), (0,)), ((), ())),
        precision=lax.Precision.HIGHEST,
        preferred_element_type=F32,
    )

    ffs = w_shared_out.shape[0]
    shared_in = jnp.swapaxes(shared_all[:, : 2 * ffs], 0, 1).reshape(2 * ffs, width)
    shared_out = jnp.swapaxes(shared_all[:, 2 * ffs :], 0, 1).reshape(ffs, width)
    shared_pre = dot_nt(ffn_low, shared_in)
    shared_gate, shared_up = shared_pre[:, :ffs], shared_pre[:, ffs:]
    shared_sig = jax.nn.sigmoid(shared_gate)
    shared_silu = shared_gate * shared_sig
    shared_act = (shared_silu * shared_up).astype(BF16)
    shared_part = scatter_t_direct(dot(shared_act, shared_out))
    shared_act_grad = dot_nt(cot_low, shared_out)
    shared_pre_grad = jnp.concatenate(
        [
            shared_act_grad * shared_up * shared_sig * (1.0 + shared_gate * (1.0 - shared_sig)),
            shared_act_grad * shared_silu,
        ],
        1,
    ).astype(BF16)
    grad_shared_in = dot_tn(shared_pre_grad, ffn_low)
    grad_shared_out = dot_tn(shared_act, cot_low)
    shared_grad = scatter_t_direct(dot(shared_pre_grad, shared_in))

    logits_grad = router_probs * (
        probs_grad - jnp.sum(router_probs * probs_grad, axis=-1, keepdims=True)
    )
    router_part = lax.dot_general(
        logits_grad,
        ffn_low.astype(F32),
        (((0,), (0,)), ((), ())),
        precision=lax.Precision.HIGHEST,
        preferred_element_type=F32,
    )
    router_slice = lax.dynamic_slice_in_dim(router_t, me_t * part, part, 1)
    ffn_grad = (
        shared_grad
        + routed_grad
        + lax.dot_general(
            logits_grad,
            router_slice.astype(F32),
            (((1,), (0,)), ((), ())),
            precision=lax.Precision.HIGHEST,
            preferred_element_type=F32,
        )
    )
    scaled = ffn_scale * ffn_grad
    ffn_gain_part = jnp.sum(ffn_grad * ffn_hat, axis=0)
    residual_grad = cot_part.astype(F32) + ffn_inverse * (
        scaled - ffn_hat * row_mean(ffn_hat * scaled)
    )
    residual_low = gather_t(residual_grad.astype(BF16))

    output = gather_t_direct((residual + routed + shared_part).astype(BF16))

    def sum_dp(values):
        return lax.psum_scatter(values, "dp", scatter_dimension=0, tiled=False).astype(F32)

    def by_owner(values):
        return jnp.swapaxes(values.astype(BF16).reshape(-1, ndp, d_loc), 0, 1)

    shared_grads = jnp.concatenate([by_owner(grad_shared_in), by_owner(grad_shared_out)], 1)
    residual_low, shared_grads, grad_plane = lax.optimization_barrier(
        (residual_low, shared_grads, grad_plane)
    )
    shared_sum = sum_dp(shared_grads)
    grad_out_w = dot_tn(attended_low, residual_low)
    attended_grad = dot_nt(residual_low, out_w).astype(BF16)
    query_nope_grad, query_turned_grad, kv_grad, rope_grad = attend_back(
        lengths,
        query_nope,
        query_rope,
        keys_values,
        key_rope,
        attended_grad,
        log_totals,
        heads,
        score_scale,
    )
    turned_first, turned_second = rotate_back(
        query_turned_grad[:, : heads * half], query_turned_grad[:, heads * half :], wide_cos, wide_sin
    )
    query_grad = jnp.concatenate(
        [query_nope_grad, turned_first.astype(BF16), turned_second.astype(BF16)], 1
    )
    rope_sum = rope_grad.reshape(rows, 2, heads, half).sum(2)
    key_rope_part = jnp.concatenate(
        rotate_back(
            rope_sum[:, 0], rope_sum[:, 1], wide_cos[:, :half], wide_sin[:, :half]
        ),
        1,
    )
    latent_part = dot_nt(kv_grad, up_w)
    grad_kv_gain = jnp.sum(latent_part * latent_hat, axis=0)
    scaled_kv = kv_scale * latent_part
    latent_back = kv_inverse * (
        scaled_kv - latent_hat * jnp.mean(latent_hat * scaled_kv, axis=-1, keepdims=True)
    )
    down_grad = jnp.concatenate([latent_back, key_rope_part], -1).astype(BF16)
    normed_grad = scatter_t_direct(dot(query_grad, query_t) + dot(down_grad, down_t))
    grad_home = swap_t(jnp.swapaxes(grad_plane, 0, 1)).reshape(EXPERTS, 3, f_loc, d_loc)
    normed_grad, grad_home = lax.optimization_barrier((normed_grad, grad_home))
    attn_hat = own_part(hidden).astype(F32) * attn_inverse
    scaled_in = lax.dynamic_slice_in_dim(attn_scale, me_t * part, part, 0) * normed_grad
    attn_gain_part = jnp.sum(normed_grad * attn_hat, axis=0)
    input_grad = residual_grad + attn_inverse * (
        scaled_in - attn_hat * row_mean(attn_hat * scaled_in)
    )
    grad_expert_in, grad_expert_out = home_gradients(lay, ids, grad_home, f_loc, d_loc)
    grad_hidden = gather_t_direct(input_grad.astype(BF16))

    def spread(values):
        return lax.dynamic_update_slice(
            jnp.zeros((1, width), F32), values[None], (jnp.int32(0), me_t * part)
        )

    kv_gain_row = jnp.pad(
        grad_kv_gain.reshape(ndp, lat_loc), ((0, 0), (0, d_loc - lat_loc))
    ).reshape(1, width)
    gain_grads = jnp.concatenate([spread(attn_gain_part), spread(ffn_gain_part), kv_gain_row], 0)
    front_sum = sum_dp(
        jnp.concatenate(
            [
                by_owner(dot_tn(down_grad, normed_low)),
                by_owner(jnp.pad(gain_grads, ((0, 13), (0, 0)))),
                by_owner(router_part),
                by_owner(dot_tn(query_grad, normed_low)),
                by_owner(grad_out_w),
                dot_tn(latent_low, kv_grad).astype(BF16).reshape(ndp, -1, d_loc),
            ],
            1,
        )
    )
    own_sum = lax.psum(front_sum[: down_rows + EXPERTS], "tensor")
    at = down_rows + 2 * EXPERTS
    return (
        output,
        grad_hidden,
        own_sum[down_rows],
        jnp.transpose(by_head(front_sum[at : at + q_rows])),
        jnp.transpose(own_sum[:down_rows]),
        own_sum[down_rows + 2, :lat_loc],
        front_sum[at + q_rows + out_rows :].reshape(w_kv_up.shape),
        front_sum[at + q_rows : at + q_rows + out_rows],
        own_sum[down_rows + 1],
        jnp.transpose(front_sum[down_rows + EXPERTS : at]),
        grad_expert_in,
        grad_expert_out,
        jnp.swapaxes(shared_sum[: 2 * ffs].reshape(2, ffs, d_loc), 1, 2),
        shared_sum[2 * ffs :],
    )


def solution(mesh):
    return jax.shard_map(
        functools.partial(body, Layout(mesh.shape["dp"], mesh.shape["tensor"])),
        mesh=mesh,
        in_specs=(
            P("dp", None),
            P("dp"),
            P("dp", None),
            P("dp"),
            P("dp", "tensor"),
            P("dp", None),
            P("dp"),
            P("dp", "tensor"),
            P("tensor", "dp"),
            P("dp"),
            P("dp", None),
            P(None, None, "dp", "tensor"),
            P(None, "tensor", "dp"),
            P(None, "dp", "tensor"),
            P("tensor", "dp"),
            P("dp", None),
        ),
        out_specs=(
            P("dp", None),
            P("dp", None),
            P("dp"),
            P("dp", "tensor"),
            P("dp", None),
            P("dp"),
            P("dp", "tensor"),
            P("tensor", "dp"),
            P("dp"),
            P("dp", None),
            P(None, None, "dp", "tensor"),
            P(None, "tensor", "dp"),
            P(None, "dp", "tensor"),
            P("tensor", "dp"),
        ),
        check_vma=False,
    )
```

```python
import functools
import math

import jax
import jax.numpy as jnp
from jax import lax
from jax.experimental import pallas as pl
from jax.experimental.pallas import tpu as pltpu
from jax.sharding import PartitionSpec as P

NOPE = 128
ROPE = 64
VDIM = 128
LATENT = 512
TOP = 6
EXPERTS = 16
CAP = 512

EPSILON = 1e-06
NEGATIVE = -1e30
F32 = jnp.float32
BF16 = jnp.bfloat16


def dot(a, b):
    return jnp.dot(a, b, preferred_element_type=F32)


def dot_nt(a, b):
    return lax.dot_general(a, b, (((1,), (1,)), ((), ())), preferred_element_type=F32)


def dot_tn(a, b):
    return lax.dot_general(a, b, (((0,), (0,)), ((), ())), preferred_element_type=F32)


def rotate(first, second, cosine, sine):
    return first * cosine - second * sine, second * cosine + first * sine


def rotate_back(first, second, cosine, sine):
    return first * cosine + second * sine, second * cosine - first * sine


def angle_tables(rows_count):
    positions = jnp.arange(rows_count, dtype=F32)
    freqs = jnp.exp(jnp.arange(ROPE // 2, dtype=F32) * (-2.0 * math.log(10000.0) / ROPE))
    angles = positions[:, None] * freqs[None, :]
    return (jnp.cos(angles), jnp.sin(angles))


def inverse_rms(values):
    return lax.rsqrt(jnp.mean(values * values, axis=-1, keepdims=True) + EPSILON)


class Layout:
    def __init__(self, n_dp, n_tensor):
        self.dp, self.t = n_dp, n_tensor
        self.q = n_dp * n_tensor // EXPERTS
        self.z = n_dp // self.q
        if self.z * self.t != EXPERTS or self.z * self.q != n_dp:
            raise ValueError("mesh")
        self.z_groups = [[c + self.q * z for z in range(self.z)] for c in range(self.q)]

    def over_t(self, values, k):
        if k == 0:
            return values
        return lax.ppermute(values, "tensor", [(i, i ^ k) for i in range(self.t)])

    def over_z(self, values, k):
        if k == 0:
            return values
        return lax.ppermute(values, "dp", [(d, d ^ (k * self.q)) for d in range(self.dp)])

    def over_c(self, values, k):
        if k == 0:
            return values
        return lax.ppermute(values, "dp", [(d, d ^ k) for d in range(self.dp)])


def lay_out_weights(lay, ids, stacks, f_loc, d_loc, width):
    ffe = f_loc * lay.t

    def kernel(ids_ref, *refs):
        sources, (in_ref, out_ref) = refs[: 3 * lay.q], refs[3 * lay.q :]
        for kc in range(lay.q):
            columns = pl.ds(pl.multiple_of((ids_ref[1] ^ kc) * d_loc, 128), d_loc)
            for g in range(2):
                in_ref[g, :, columns] = sources[3 * kc + g][0]
            out_ref[:, columns] = sources[3 * kc + 2][0]

    own_in, own_out = pl.pallas_call(
        kernel,
        out_shape=(
            jax.ShapeDtypeStruct((2, ffe, width), BF16),
            jax.ShapeDtypeStruct((ffe, width), BF16),
        ),
        grid_spec=pltpu.PrefetchScalarGridSpec(
            num_scalar_prefetch=1,
            grid=(lay.t, lay.z),
            in_specs=[
                pl.BlockSpec((1, f_loc, d_loc), lambda kt, kz, ids: (kz * lay.t + kt, 0, 0))
            ]
            * (3 * lay.q),
            out_specs=(
                pl.BlockSpec((2, f_loc, lay.q * d_loc), lambda kt, kz, ids: (0, kt, kz)),
                pl.BlockSpec((f_loc, lay.q * d_loc), lambda kt, kz, ids: (kt, kz)),
            ),
        ),
        cost_estimate=pl.CostEstimate(
            flops=0, bytes_accessed=12 * ffe * width, transcendentals=0
        ),
        compiler_params=pltpu.CompilerParams(vmem_limit_bytes=32 << 20),
        name="lay_out_weights",
    )(ids, *stacks)
    return own_in.reshape(2 * ffe, width), own_out


def take_apart(lay, ids, grad_in, grad_out, f_loc, d_loc, width):
    ffe = f_loc * lay.t

    def kernel(ids_ref, in_ref, out_ref, *targets):
        for kc in range(lay.q):
            columns = pl.ds(pl.multiple_of((ids_ref[1] ^ kc) * d_loc, 128), d_loc)
            for g in range(2):
                targets[3 * kc + g][0] = in_ref[g, :, columns]
            targets[3 * kc + 2][0] = out_ref[:, columns]

    shape = jax.ShapeDtypeStruct((lay.t * lay.z, f_loc, d_loc), BF16)
    spec = pl.BlockSpec((1, f_loc, d_loc), lambda kt, kz, ids: (kz * lay.t + kt, 0, 0))
    return pl.pallas_call(
        kernel,
        out_shape=(shape,) * (3 * lay.q),
        grid_spec=pltpu.PrefetchScalarGridSpec(
            num_scalar_prefetch=1,
            grid=(lay.t, lay.z),
            in_specs=[
                pl.BlockSpec((2, f_loc, lay.q * d_loc), lambda kt, kz, ids: (0, kt, kz)),
                pl.BlockSpec((f_loc, lay.q * d_loc), lambda kt, kz, ids: (kt, kz)),
            ],
            out_specs=(spec,) * (3 * lay.q),
        ),
        cost_estimate=pl.CostEstimate(
            flops=0, bytes_accessed=12 * ffe * width, transcendentals=0
        ),
        compiler_params=pltpu.CompilerParams(vmem_limit_bytes=32 << 20),
        name="take_apart",
    )(ids, grad_in.reshape(2, ffe, width), grad_out)


def home_gradients(lay, pieces, f_loc, d_loc):
    def kernel(gate_ref, up_ref, down_ref, in_ref, out_ref):
        in_ref[0, 0] = gate_ref[0].astype(F32)
        in_ref[0, 1] = up_ref[0].astype(F32)
        out_ref[0] = down_ref[0].astype(F32)

    spec = pl.BlockSpec((1, f_loc, d_loc), lambda e: (e % lay.t * lay.z + e // lay.t, 0, 0))
    grad_in, grad_out = pl.pallas_call(
        kernel,
        out_shape=(
            jax.ShapeDtypeStruct((EXPERTS, 2, f_loc, d_loc), F32),
            jax.ShapeDtypeStruct((EXPERTS, f_loc, d_loc), F32),
        ),
        grid=(EXPERTS,),
        in_specs=[spec] * 3,
        out_specs=(
            pl.BlockSpec((1, 2, f_loc, d_loc), lambda e: (e, 0, 0, 0)),
            pl.BlockSpec((1, f_loc, d_loc), lambda e: (e, 0, 0)),
        ),
        cost_estimate=pl.CostEstimate(
            flops=0, bytes_accessed=18 * EXPERTS * f_loc * d_loc, transcendentals=0
        ),
        name="home_gradients",
    )(*pieces)
    return jnp.swapaxes(grad_in, 2, 3), grad_out


def join_columns(parts, me, count):
    rows, part = parts[0].shape
    block = min(512, rows)

    def kernel(me_ref, *refs):
        for k in range(count):

            @pl.when(pl.program_id(1) == k)
            def _(k=k):
                refs[count][...] = refs[k][...]

    return pl.pallas_call(
        kernel,
        out_shape=jax.ShapeDtypeStruct((rows, count * part), parts[0].dtype),
        grid_spec=pltpu.PrefetchScalarGridSpec(
            num_scalar_prefetch=1,
            grid=(rows // block, count),
            in_specs=[pl.BlockSpec((block, part), lambda i, k, me: (i, 0))] * count,
            out_specs=pl.BlockSpec((block, part), lambda i, k, me: (i, me[0] ^ k)),
        ),
        cost_estimate=pl.CostEstimate(
            flops=0, bytes_accessed=4 * rows * part * count, transcendentals=0
        ),
        name="join_columns",
    )(me.reshape(1).astype(jnp.int32), *parts)


def score_block(q_ref, r_ref, k_ref, kr_ref, head, step, keys, block, length, scale):
    half = r_ref.shape[1] // 2
    lanes = lax.broadcasted_iota(jnp.int32, r_ref.shape, 1) % half // (ROPE // 2)
    turned = jnp.where(lanes == head, r_ref[...], jnp.zeros_like(r_ref))
    raw = lax.dot_general(
        q_ref[...], k_ref[:keys], (((1,), (1,)), ((), ())), preferred_element_type=F32
    ) + lax.dot_general(
        turned, kr_ref[:keys], (((1,), (1,)), ((), ())), preferred_element_type=F32
    )
    rows = lax.broadcasted_iota(jnp.int32, raw.shape, 0) + step * block
    cols = lax.broadcasted_iota(jnp.int32, raw.shape, 1)
    allowed = (cols <= rows) & (cols < length)
    return jnp.where(allowed, raw * scale, NEGATIVE), turned


def attend(length, query, query_rope, kv, key_rope, heads, scale):
    rows = query.shape[0]
    block = min(256, rows)
    steps = rows // block

    def kernel(len_ref, q_ref, r_ref, k_ref, v_ref, kr_ref, o_ref, total_ref):
        head, step = pl.program_id(0), pl.program_id(1)
        for n in range(steps):

            @pl.when(step == n)
            def _(n=n):
                keys = (n + 1) * block
                scores, _ = score_block(
                    q_ref, r_ref, k_ref, kr_ref, head, n, keys, block, len_ref[0], scale
                )
                highest = jnp.max(scores, axis=-1, keepdims=True)
                expo = jnp.exp(scores - highest)
                totals = jnp.sum(expo, axis=-1, keepdims=True)
                weights = (expo * (1.0 / totals)).astype(BF16)
                o_ref[...] = dot(weights, v_ref[:keys]).astype(BF16)
                total_ref[0] = jnp.broadcast_to(highest + jnp.log(totals), (block, 128))

    return pl.pallas_call(
        kernel,
        out_shape=(
            jax.ShapeDtypeStruct((rows, heads * VDIM), BF16),
            jax.ShapeDtypeStruct((heads, rows, 128), F32),
        ),
        grid_spec=pltpu.PrefetchScalarGridSpec(
            num_scalar_prefetch=1,
            grid=(heads, steps),
            in_specs=[
                pl.BlockSpec((block, NOPE), lambda h, i, n: (i, h)),
                pl.BlockSpec((block, query_rope.shape[1]), lambda h, i, n: (i, 0)),
                pl.BlockSpec((rows, NOPE), lambda h, i, n: (0, 2 * h)),
                pl.BlockSpec((rows, VDIM), lambda h, i, n: (0, 2 * h + 1)),
                pl.BlockSpec((rows, key_rope.shape[1]), lambda h, i, n: (0, 0)),
            ],
            out_specs=(
                pl.BlockSpec((block, VDIM), lambda h, i, n: (i, h)),
                pl.BlockSpec((1, block, 128), lambda h, i, n: (h, i, 0)),
            ),
        ),
        cost_estimate=pl.CostEstimate(
            flops=heads * rows * rows * 512,
            bytes_accessed=8 * rows * heads * 512,
            transcendentals=heads * rows * rows,
        ),
        compiler_params=pltpu.CompilerParams(vmem_limit_bytes=32 << 20),
        name="attend",
    )(length, query, query_rope, kv, kv, key_rope)


def attend_back(length, query, query_rope, kv, key_rope, out_grad, log_totals, heads, scale):
    rows = query.shape[0]
    block = min(256, rows)
    steps = rows // block
    turned_cols = query_rope.shape[1]

    def kernel(
        len_ref, q_ref, r_ref, k_ref, v_ref, kr_ref, do_ref, total_ref,
        dq_ref, dr_ref, dkv_ref, dkr_ref, dk_acc, dv_acc,
    ):
        head, step = pl.program_id(0), pl.program_id(1)

        @pl.when(step == 0)
        def _():
            dk_acc[...] = jnp.zeros_like(dk_acc)
            dv_acc[...] = jnp.zeros_like(dv_acc)

        @pl.when((step == 0) & (head == 0))
        def _():
            dr_ref[...] = jnp.zeros_like(dr_ref)
            dkr_ref[...] = jnp.zeros_like(dkr_ref)

        for n in range(steps):

            @pl.when(step == n)
            def _(n=n):
                keys = (n + 1) * block
                scores, turned = score_block(
                    q_ref, r_ref, k_ref, kr_ref, head, n, keys, block, len_ref[0], scale
                )
                probs = jnp.exp(scores - total_ref[0][:, :1])
                prob_grad = lax.dot_general(
                    do_ref[...], v_ref[:keys], (((1,), (1,)), ((), ())), preferred_element_type=F32
                )
                centre = jnp.sum(probs * prob_grad, axis=-1, keepdims=True)
                score_grad = (probs * (prob_grad - centre)).astype(BF16)
                probs_low = probs.astype(BF16)
                dq_ref[...] = (dot(score_grad, k_ref[:keys]) * scale).astype(BF16)
                half = turned_cols // 2
                lanes = lax.broadcasted_iota(jnp.int32, (block, turned_cols), 1)
                lanes = lanes % half // (ROPE // 2)
                turned_grad = dot(score_grad, kr_ref[:keys]) * scale
                dr_ref[n * block : keys] += jnp.where(lanes == head, turned_grad, 0.0)
                dk_acc[:keys] += dot_tn(score_grad, q_ref[...]) * scale
                dkr_ref[:keys] += dot_tn(score_grad, turned) * scale
                dv_acc[:keys] += dot_tn(probs_low, do_ref[...])

        @pl.when(step == steps - 1)
        def _():
            dkv_ref[:, :NOPE] = dk_acc[...].astype(BF16)
            dkv_ref[:, NOPE:] = dv_acc[...].astype(BF16)

    return pl.pallas_call(
        kernel,
        out_shape=(
            jax.ShapeDtypeStruct((rows, heads * NOPE), BF16),
            jax.ShapeDtypeStruct((rows, turned_cols), F32),
            jax.ShapeDtypeStruct((rows, heads * (NOPE + VDIM)), BF16),
            jax.ShapeDtypeStruct((rows, turned_cols), F32),
        ),
        grid_spec=pltpu.PrefetchScalarGridSpec(
            num_scalar_prefetch=1,
            grid=(heads, steps),
            in_specs=[
                pl.BlockSpec((block, NOPE), lambda h, i, n: (i, h)),
                pl.BlockSpec((block, turned_cols), lambda h, i, n: (i, 0)),
                pl.BlockSpec((rows, NOPE), lambda h, i, n: (0, 2 * h)),
                pl.BlockSpec((rows, VDIM), lambda h, i, n: (0, 2 * h + 1)),
                pl.BlockSpec((rows, turned_cols), lambda h, i, n: (0, 0)),
                pl.BlockSpec((block, VDIM), lambda h, i, n: (i, h)),
                pl.BlockSpec((1, block, 128), lambda h, i, n: (h, i, 0)),
            ],
            out_specs=(
                pl.BlockSpec((block, NOPE), lambda h, i, n: (i, h)),
                pl.BlockSpec((rows, turned_cols), lambda h, i, n: (0, 0)),
                pl.BlockSpec((rows, NOPE + VDIM), lambda h, i, n: (0, h)),
                pl.BlockSpec((rows, turned_cols), lambda h, i, n: (0, 0)),
            ),
            scratch_shapes=[pltpu.VMEM((rows, NOPE), F32), pltpu.VMEM((rows, VDIM), F32)],
        ),
        cost_estimate=pl.CostEstimate(
            flops=heads * rows * rows * 1600,
            bytes_accessed=16 * rows * heads * 512,
            transcendentals=heads * rows * rows,
        ),
        compiler_params=pltpu.CompilerParams(vmem_limit_bytes=40 << 20),
        name="attend_back",
    )(length, query, query_rope, kv, kv, key_rope, out_grad, log_totals)


def in_order(values, me, count):
    zero = jnp.zeros_like(values[0])
    ordered = []
    for j in range(count):
        total = zero
        for k in range(count):
            total = jnp.where((me ^ k) == j, values[k], total)
        ordered.append(total)
    return jnp.stack(ordered)


def body(
    lay,
    hidden,
    lengths,
    routes,
    attn_gain,
    w_query,
    w_kv_down,
    kv_gain,
    w_kv_up,
    w_out,
    ffn_gain,
    w_router,
    w_expert_in,
    w_expert_out,
    w_shared_in,
    w_shared_out,
    cotangent,
):
    rows, width = hidden.shape
    nz, nt, nq, ndp = lay.z, lay.t, lay.q, lay.dp
    me_dp = lax.axis_index("dp")
    me_t = lax.axis_index("tensor")
    me_z = me_dp // nq
    me_c = me_dp % nq
    part = width // nt
    d_loc = w_query.shape[0]
    f_loc = w_expert_out.shape[1]
    ffe = f_loc * nt
    heads = w_query.shape[1] // (NOPE + ROPE)
    score_scale = (NOPE + ROPE) ** (-0.5)

    def own_part(values):
        return lax.dynamic_slice_in_dim(values, me_t * part, part, 1)

    def gather_z(values):
        return lax.all_gather(values, "dp", axis=0, tiled=False, axis_index_groups=lay.z_groups)

    def scatter_z(values):
        return lax.psum_scatter(
            values, "dp", scatter_dimension=0, tiled=False, axis_index_groups=lay.z_groups
        )

    def gather_t(values):
        return lax.all_gather(values, "tensor", axis=1, tiled=True)

    def scatter_t(values):
        return lax.psum_scatter(
            values.astype(BF16), "tensor", scatter_dimension=1, tiled=True
        ).astype(F32)

    def swap_t(values):
        return lax.all_to_all(values, "tensor", split_axis=0, concat_axis=0, tiled=True)

    def swap_z(values):
        return lax.all_to_all(
            values,
            "dp",
            split_axis=0,
            concat_axis=0,
            axis_index_groups=lay.z_groups,
            tiled=True,
        )

    def gather_t_direct(values):
        return join_columns([lay.over_t(values, k) for k in range(nt)], me_t, nt)

    def part_for(values, k):
        return lax.dynamic_slice_in_dim(values, (me_t ^ k) * part, part, 1)

    def scatter_t_direct(values):
        total = part_for(values, 0)
        for k in range(1, nt):
            total = total + lay.over_t(part_for(values, k).astype(BF16), k).astype(F32)
        return total

    ids = jnp.stack([me_z, me_c, me_t]).astype(jnp.int32)

    packed = jnp.concatenate(
        [jnp.swapaxes(w_expert_in, 2, 3), w_expert_out[:, None]], 1
    ).reshape(nz, nt, 3, f_loc, d_loc)
    by_column = swap_t(jnp.swapaxes(packed, 0, 1))

    lat_loc = kv_gain.shape[0]
    q_rows, down_rows, out_rows = w_query.shape[1], w_kv_down.shape[1], w_out.shape[0]
    half = ROPE // 2

    def by_kind(turned):
        split = turned.reshape(heads, NOPE + ROPE, -1)
        return jnp.concatenate(
            [
                split[:, :NOPE].reshape(heads * NOPE, -1),
                split[:, NOPE : NOPE + half].reshape(heads * half, -1),
                split[:, NOPE + half :].reshape(heads * half, -1),
            ],
            0,
        )

    def by_head(rows_in):
        nope = rows_in[: heads * NOPE].reshape(heads, NOPE, -1)
        first = rows_in[heads * NOPE : heads * (NOPE + half)].reshape(heads, half, -1)
        second = rows_in[heads * (NOPE + half) :].reshape(heads, half, -1)
        return jnp.concatenate([nope, first, second], 1).reshape(heads * (NOPE + ROPE), -1)

    gains = jnp.stack([attn_gain, ffn_gain, jnp.pad(kv_gain, (0, d_loc - lat_loc))])
    front_pack = jnp.concatenate(
        [
            by_kind(jnp.transpose(w_query)),
            jnp.transpose(w_kv_down),
            jnp.transpose(w_router),
            jnp.pad(gains, ((0, 13), (0, 0))),
            w_out,
            w_kv_up.reshape(-1, d_loc),
        ],
        0,
    )
    front = lax.all_gather(front_pack, "dp", axis=0, tiled=False)

    valid_length = lengths[0]
    valid_rows = lax.broadcasted_iota(jnp.int32, (rows, 1), 0) < valid_length
    cot_low = jnp.where(valid_rows, cotangent, jnp.zeros_like(cotangent))
    cot_part = own_part(cot_low)
    route_own = jnp.pad(jnp.transpose(routes), ((0, -TOP % 8), (0, 0)), constant_values=-1)
    route_all = in_order([lay.over_z(route_own, k) for k in range(nz)], me_z, nz)
    inputs = hidden.astype(F32)
    attn_inverse = inverse_rms(inputs)
    cosine, sine = angle_tables(rows)
    wide_cos, wide_sin = jnp.tile(cosine, (1, heads)), jnp.tile(sine, (1, heads))
    front, attn_inverse, wide_cos, wide_sin = lax.optimization_barrier(
        (front, attn_inverse, wide_cos, wide_sin)
    )

    plane_ids = me_z * nt + jnp.arange(nt, dtype=jnp.int32)
    member = jnp.any(route_all[:, :, :, None] == plane_ids[None, None, None, :], axis=1)
    row_ids = lax.broadcasted_iota(jnp.int32, (rows, rows), 0)
    col_ids = lax.broadcasted_iota(jnp.int32, (rows, rows), 1)
    before = (col_ids < row_ids).astype(BF16)
    position = jnp.einsum("ij,sje->sei", before, member.astype(BF16), preferred_element_type=F32)
    key = jnp.where(jnp.swapaxes(member, 1, 2), position.astype(jnp.int32), -1)
    slots_iota = lax.broadcasted_iota(jnp.int32, (1, 1, CAP, 1), 2)

    def place_of(keys):
        return (keys[:, :, None, :] == slots_iota).astype(BF16)

    place = place_of(key)
    own_key = lax.dynamic_index_in_dim(key, me_t, 1, keepdims=False)
    own_place = own_key[:, None, :] == slots_iota[0]

    def pick_rows(values):
        picked = jnp.einsum("sepk,skd->espd", place, values, preferred_element_type=F32)
        return picked.astype(BF16).reshape(nt, nz * CAP, part)

    def send_out(picked):
        return jnp.swapaxes(swap_t(picked), 0, 1).reshape(nz * CAP, width)

    def send_back(values):
        return swap_t(jnp.swapaxes(values.reshape(nz * CAP, nt, part), 0, 1))

    def combine(parts):
        parts = parts.reshape(nt, nz, CAP, part)
        summed = jnp.einsum("sepk,espd->skd", place, parts, preferred_element_type=F32)
        return summed.astype(BF16)


    def rows_of(first, count):
        return jnp.swapaxes(front[:, first : first + count], 0, 1).reshape(count, width)

    query_t = rows_of(0, q_rows)
    down_t = rows_of(q_rows, down_rows)
    at = q_rows + down_rows
    router_t = rows_of(at, EXPERTS)
    gain_attn = front[:, at + EXPERTS].reshape(-1)
    gain_ffn = front[:, at + EXPERTS + 1].reshape(-1)
    gain_kv = front[:, at + EXPERTS + 2, :lat_loc].reshape(-1)
    at = at + 2 * EXPERTS
    out_w = rows_of(at, out_rows)
    up_w = front[:, at + out_rows :].reshape(LATENT, heads * (NOPE + VDIM))

    attn_scale = gain_attn.astype(F32)
    normed_low = (inputs * attn_inverse * attn_scale).astype(BF16)
    query = dot_nt(normed_low, query_t)
    nope_cols = heads * NOPE
    query_nope = query[:, :nope_cols].astype(BF16)
    query_rope = jnp.concatenate(
        rotate(
            query[:, nope_cols : nope_cols + heads * half],
            query[:, nope_cols + heads * half :],
            wide_cos,
            wide_sin,
        ),
        1,
    ).astype(BF16)
    turned_t = jnp.concatenate(
        [down_t[:LATENT]]
        + [down_t[LATENT : LATENT + half]] * heads
        + [down_t[LATENT + half :]] * heads,
        0,
    )
    latent_all = dot_nt(normed_low, turned_t)
    latent_all, by_column = lax.optimization_barrier((latent_all, by_column))
    by_column = jnp.transpose(by_column, (2, 1, 0, 3, 4))
    by_plane = [swap_z(by_column[g]) for g in range(3)]
    latent = latent_all[:, :LATENT]
    kv_inverse = inverse_rms(latent)
    latent_hat = latent * kv_inverse
    kv_scale = gain_kv.astype(F32)
    latent_low = (latent_hat * kv_scale).astype(BF16)
    key_rope = jnp.concatenate(
        rotate(
            latent_all[:, LATENT : LATENT + heads * half],
            latent_all[:, LATENT + heads * half :],
            wide_cos,
            wide_sin,
        ),
        1,
    ).astype(BF16)
    keys_values = dot(latent_low, up_w).astype(BF16)
    attended_low, log_totals = attend(
        lengths, query_nope, query_rope, keys_values, key_rope, heads, score_scale
    )
    attn_part, by_plane[0] = lax.optimization_barrier((dot(attended_low, out_w), by_plane[0]))
    attn_sum = scatter_t(attn_part)
    residual = own_part(hidden).astype(F32) + attn_sum

    def row_mean(values):
        partial = jnp.sum(values, axis=-1).reshape(-1, 128)
        return lax.psum(partial, "tensor").reshape(-1, 1) * (1.0 / width)

    ffn_inverse = lax.rsqrt(row_mean(residual * residual) + EPSILON)
    ffn_hat = residual * ffn_inverse
    ffn_scale = lax.dynamic_slice_in_dim(gain_ffn, me_t * part, part, 0).astype(F32)
    ffn_part = (ffn_hat * ffn_scale).astype(BF16)

    ffn_all = gather_z(ffn_part)
    ffn_low = gather_t_direct(ffn_part)
    ffn_all, ffn_low = lax.optimization_barrier((ffn_all, ffn_low))
    picked = pick_rows(ffn_all)
    picked, cot_ready = lax.optimization_barrier((picked, cot_part))
    expert_rows = send_out(picked)
    cot_picked = pick_rows(gather_z(cot_ready))
    shared_pack = jnp.concatenate(
        [jnp.swapaxes(w_shared_in, 1, 2).reshape(-1, d_loc), w_shared_out], 0
    )
    cot_picked, shared_pack = lax.optimization_barrier((cot_picked, shared_pack))
    cot_rows = send_out(cot_picked)
    shared_all = lax.all_gather(shared_pack, "dp", axis=0, tiled=False)
    pieces = [plane.reshape(nz * nt, f_loc, d_loc) for plane in by_plane]
    own_in, own_out = lay_out_weights(
        lay,
        ids,
        [lay.over_c(pieces[g], k) for k in range(nq) for g in range(3)],
        f_loc,
        d_loc,
        width,
    )
    router_probs = jax.nn.softmax(dot_nt(ffn_low, router_t), axis=-1)
    probs_turned = jnp.transpose(router_probs).reshape(EXPERTS, -1, 128)
    own_probs = in_order(
        [
            lay.over_z(
                lax.dynamic_index_in_dim(
                    probs_turned, (me_z ^ k) * nt + me_t, 0, keepdims=False
                ),
                k,
            )
            for k in range(nz)
        ],
        me_z,
        nz,
    ).reshape(nz, rows)
    gate_rows = jnp.sum(jnp.where(own_place, own_probs[:, None, :], 0.0), axis=-1).reshape(
        nz * CAP, 1
    )
    gate_up = dot_nt(expert_rows, own_in)
    gate_pre, up_pre = gate_up[:, :ffe], gate_up[:, ffe:]
    gate_sig = jax.nn.sigmoid(gate_pre)
    gate_silu = gate_pre * gate_sig
    active = (gate_silu * up_pre).astype(BF16)
    rows_out = (dot(active, own_out) * gate_rows).astype(BF16)
    rows_out, cot_rows = lax.optimization_barrier((rows_out, cot_rows))
    out_parts = send_back(rows_out)
    active_grad_raw = dot_nt(cot_rows, own_out)
    gate_grad = jnp.sum(active.astype(F32) * active_grad_raw, axis=-1).reshape(nz, CAP)
    active_grad = active_grad_raw * gate_rows
    pre_low = jnp.concatenate(
        [
            active_grad * up_pre * gate_sig * (1.0 + gate_pre * (1.0 - gate_sig)),
            active_grad * gate_silu,
        ],
        1,
    ).astype(BF16)
    gated_active = (active.astype(F32) * gate_rows).astype(BF16)
    rows_grad = dot(pre_low, own_in).astype(BF16)
    rows_grad, out_parts = lax.optimization_barrier((rows_grad, out_parts))
    grad_parts = send_back(rows_grad)
    routed, pre_low = lax.optimization_barrier((combine(out_parts), pre_low))
    routed = scatter_z(routed).astype(F32)
    grad_in_own = dot_tn(pre_low, expert_rows).astype(BF16)
    grad_out_own = dot_tn(gated_active, cot_rows).astype(BF16)
    grad_parts, grad_in_own, grad_out_own, routed = lax.optimization_barrier(
        (grad_parts, grad_in_own, grad_out_own, routed)
    )
    grad_pieces = take_apart(lay, ids, grad_in_own, grad_out_own, f_loc, d_loc, width)
    routed_grad = scatter_z(combine(grad_parts)).astype(F32)
    grad_class = [
        sum(lay.over_c(grad_pieces[3 * k + g], k).astype(F32) for k in range(nq)).astype(BF16)
        for g in range(3)
    ]
    routed_grad, grad_class = lax.optimization_barrier((routed_grad, grad_class))
    grad_plane = [swap_z(grad_class[g].reshape(nz, nt, f_loc, d_loc)) for g in range(3)]

    def to_columns(values):
        return swap_t(jnp.swapaxes(values, 0, 1)).reshape(EXPERTS, f_loc, d_loc)

    token_grad = jnp.sum(jnp.where(own_place, gate_grad[:, :, None], 0.0), axis=1)
    token_grad = token_grad.reshape(nz, -1, 128)
    token_plane = jnp.stack(
        [
            lay.over_z(lax.dynamic_index_in_dim(token_grad, me_z ^ k, 0, keepdims=False), k)
            for k in range(nz)
        ]
    )
    token_home = jnp.stack([lay.over_t(token_plane, k) for k in range(nt)])
    experts = jnp.arange(EXPERTS, dtype=jnp.int32)
    came_from = (me_t ^ (experts % nt)) * nz + (me_z ^ (experts // nt))
    probs_grad = lax.dot_general(
        token_home.reshape(EXPERTS, rows),
        (experts[:, None] == came_from[None, :]).astype(F32),
        (((0,), (0,)), ((), ())),
        precision=lax.Precision.HIGHEST,
        preferred_element_type=F32,
    )

    ffs = w_shared_out.shape[0]
    shared_in = jnp.swapaxes(shared_all[:, : 2 * ffs], 0, 1).reshape(2 * ffs, width)
    shared_out = jnp.swapaxes(shared_all[:, 2 * ffs :], 0, 1).reshape(ffs, width)
    shared_pre = dot_nt(ffn_low, shared_in)
    shared_gate, shared_up = shared_pre[:, :ffs], shared_pre[:, ffs:]
    shared_sig = jax.nn.sigmoid(shared_gate)
    shared_silu = shared_gate * shared_sig
    shared_act = (shared_silu * shared_up).astype(BF16)
    shared_part = scatter_t_direct(dot(shared_act, shared_out))
    shared_act_grad = dot_nt(cot_low, shared_out)
    shared_pre_grad = jnp.concatenate(
        [
            shared_act_grad * shared_up * shared_sig * (1.0 + shared_gate * (1.0 - shared_sig)),
            shared_act_grad * shared_silu,
        ],
        1,
    ).astype(BF16)
    grad_shared_in = dot_tn(shared_pre_grad, ffn_low)
    grad_shared_out = dot_tn(shared_act, cot_low)
    shared_grad = scatter_t_direct(dot(shared_pre_grad, shared_in))

    logits_grad = router_probs * (
        probs_grad - jnp.sum(router_probs * probs_grad, axis=-1, keepdims=True)
    )
    router_part = lax.dot_general(
        logits_grad,
        ffn_low.astype(F32),
        (((0,), (0,)), ((), ())),
        precision=lax.Precision.HIGHEST,
        preferred_element_type=F32,
    )
    router_slice = lax.dynamic_slice_in_dim(router_t, me_t * part, part, 1)
    ffn_grad = (
        shared_grad
        + routed_grad
        + lax.dot_general(
            logits_grad,
            router_slice.astype(F32),
            (((1,), (0,)), ((), ())),
            precision=lax.Precision.HIGHEST,
            preferred_element_type=F32,
        )
    )
    scaled = ffn_scale * ffn_grad
    ffn_gain_part = jnp.sum(ffn_grad * ffn_hat, axis=0)
    residual_grad = cot_part.astype(F32) + ffn_inverse * (
        scaled - ffn_hat * row_mean(ffn_hat * scaled)
    )
    residual_ready, grad_plane[0] = lax.optimization_barrier(
        (residual_grad.astype(BF16), grad_plane[0])
    )
    residual_low = gather_t(residual_ready)

    def sum_dp(values):
        return lax.psum_scatter(values, "dp", scatter_dimension=0, tiled=False).astype(F32)

    def by_owner(values):
        return jnp.swapaxes(values.astype(BF16).reshape(-1, ndp, d_loc), 0, 1)

    shared_grads = jnp.concatenate([by_owner(grad_shared_in), by_owner(grad_shared_out)], 1)
    residual_low, shared_grads, grad_plane[1] = lax.optimization_barrier(
        (residual_low, shared_grads, grad_plane[1])
    )
    shared_sum = sum_dp(shared_grads)
    grad_out_w = dot_tn(attended_low, residual_low)
    attended_grad = dot_nt(residual_low, out_w).astype(BF16)
    query_nope_grad, query_turned_grad, kv_grad, rope_grad = attend_back(
        lengths,
        query_nope,
        query_rope,
        keys_values,
        key_rope,
        attended_grad,
        log_totals,
        heads,
        score_scale,
    )
    grad_home = [to_columns(grad_plane[0]), None, None]
    query_turned_grad, routed, shared_part, grad_plane[2] = lax.optimization_barrier(
        (query_turned_grad, routed, shared_part, grad_plane[2])
    )
    grad_home[1] = to_columns(grad_plane[1])
    grad_home[2] = to_columns(grad_plane[2])
    output = gather_t_direct((residual + routed + shared_part).astype(BF16))
    turned_first, turned_second = rotate_back(
        query_turned_grad[:, : heads * half], query_turned_grad[:, heads * half :], wide_cos, wide_sin
    )
    query_grad = jnp.concatenate(
        [query_nope_grad, turned_first.astype(BF16), turned_second.astype(BF16)], 1
    )
    rope_sum = rope_grad.reshape(rows, 2, heads, half).sum(2)
    key_rope_part = jnp.concatenate(
        rotate_back(
            rope_sum[:, 0], rope_sum[:, 1], wide_cos[:, :half], wide_sin[:, :half]
        ),
        1,
    )
    latent_part = dot_nt(kv_grad, up_w)
    grad_kv_gain = jnp.sum(latent_part * latent_hat, axis=0)
    scaled_kv = kv_scale * latent_part
    latent_back = kv_inverse * (
        scaled_kv - latent_hat * jnp.mean(latent_hat * scaled_kv, axis=-1, keepdims=True)
    )
    down_grad = jnp.concatenate([latent_back, key_rope_part], -1).astype(BF16)
    normed_grad = scatter_t_direct(dot(query_grad, query_t) + dot(down_grad, down_t))
    normed_grad, grad_home = lax.optimization_barrier((normed_grad, grad_home))
    attn_hat = own_part(hidden).astype(F32) * attn_inverse
    scaled_in = lax.dynamic_slice_in_dim(attn_scale, me_t * part, part, 0) * normed_grad
    attn_gain_part = jnp.sum(normed_grad * attn_hat, axis=0)
    input_grad = residual_grad + attn_inverse * (
        scaled_in - attn_hat * row_mean(attn_hat * scaled_in)
    )
    grad_expert_in, grad_expert_out = home_gradients(lay, grad_home, f_loc, d_loc)
    grad_hidden = gather_t_direct(input_grad.astype(BF16))

    def spread(values):
        return lax.dynamic_update_slice(
            jnp.zeros((1, width), F32), values[None], (jnp.int32(0), me_t * part)
        )

    kv_gain_row = jnp.pad(
        grad_kv_gain.reshape(ndp, lat_loc), ((0, 0), (0, d_loc - lat_loc))
    ).reshape(1, width)
    gain_grads = jnp.concatenate([spread(attn_gain_part), spread(ffn_gain_part), kv_gain_row], 0)
    front_sum = sum_dp(
        jnp.concatenate(
            [
                by_owner(dot_tn(down_grad, normed_low)),
                by_owner(jnp.pad(gain_grads, ((0, 13), (0, 0)))),
                by_owner(router_part),
                by_owner(dot_tn(query_grad, normed_low)),
                by_owner(grad_out_w),
                dot_tn(latent_low, kv_grad).astype(BF16).reshape(ndp, -1, d_loc),
            ],
            1,
        )
    )
    own_sum = lax.psum(front_sum[: down_rows + EXPERTS], "tensor")
    at = down_rows + 2 * EXPERTS
    return (
        output,
        grad_hidden,
        own_sum[down_rows],
        jnp.transpose(by_head(front_sum[at : at + q_rows])),
        jnp.transpose(own_sum[:down_rows]),
        own_sum[down_rows + 2, :lat_loc],
        front_sum[at + q_rows + out_rows :].reshape(w_kv_up.shape),
        front_sum[at + q_rows : at + q_rows + out_rows],
        own_sum[down_rows + 1],
        jnp.transpose(front_sum[down_rows + EXPERTS : at]),
        grad_expert_in,
        grad_expert_out,
        jnp.swapaxes(shared_sum[: 2 * ffs].reshape(2, ffs, d_loc), 1, 2),
        shared_sum[2 * ffs :],
    )


def solution(mesh):
    return jax.shard_map(
        functools.partial(body, Layout(mesh.shape["dp"], mesh.shape["tensor"])),
        mesh=mesh,
        in_specs=(
            P("dp", None),
            P("dp"),
            P("dp", None),
            P("dp"),
            P("dp", "tensor"),
            P("dp", None),
            P("dp"),
            P("dp", "tensor"),
            P("tensor", "dp"),
            P("dp"),
            P("dp", None),
            P(None, None, "dp", "tensor"),
            P(None, "tensor", "dp"),
            P(None, "dp", "tensor"),
            P("tensor", "dp"),
            P("dp", None),
        ),
        out_specs=(
            P("dp", None),
            P("dp", None),
            P("dp"),
            P("dp", "tensor"),
            P("dp", None),
            P("dp"),
            P("dp", "tensor"),
            P("tensor", "dp"),
            P("dp"),
            P("dp", None),
            P(None, None, "dp", "tensor"),
            P(None, "tensor", "dp"),
            P(None, "dp", "tensor"),
            P("tensor", "dp"),
        ),
        check_vma=False,
    )
```

```python
import functools
import math

import jax
import jax.numpy as jnp
from jax import lax
from jax.experimental import pallas as pl
from jax.experimental.pallas import tpu as pltpu
from jax.sharding import PartitionSpec as P

NOPE = 128
ROPE = 64
VDIM = 128
LATENT = 512
TOP = 6
EXPERTS = 16
CAP = 512

EPSILON = 1e-06
NEGATIVE = -1e30
F32 = jnp.float32
BF16 = jnp.bfloat16


def dot(a, b):
    return jnp.dot(a, b, preferred_element_type=F32)


def dot_nt(a, b):
    return lax.dot_general(a, b, (((1,), (1,)), ((), ())), preferred_element_type=F32)


def dot_tn(a, b):
    return lax.dot_general(a, b, (((0,), (0,)), ((), ())), preferred_element_type=F32)


def rotate(first, second, cosine, sine):
    return first * cosine - second * sine, second * cosine + first * sine


def rotate_back(first, second, cosine, sine):
    return first * cosine + second * sine, second * cosine - first * sine


def angle_tables(rows_count):
    positions = jnp.arange(rows_count, dtype=F32)
    freqs = jnp.exp(jnp.arange(ROPE // 2, dtype=F32) * (-2.0 * math.log(10000.0) / ROPE))
    angles = positions[:, None] * freqs[None, :]
    return (jnp.cos(angles), jnp.sin(angles))


def inverse_rms(values):
    return lax.rsqrt(jnp.mean(values * values, axis=-1, keepdims=True) + EPSILON)


class Layout:
    def __init__(self, n_dp, n_tensor):
        self.dp, self.t = n_dp, n_tensor
        self.q = n_dp * n_tensor // EXPERTS
        self.z = n_dp // self.q
        if self.z * self.t != EXPERTS or self.z * self.q != n_dp:
            raise ValueError("mesh")
        self.z_groups = [[c + self.q * z for z in range(self.z)] for c in range(self.q)]

    def over_t(self, values, k):
        if k == 0:
            return values
        return lax.ppermute(values, "tensor", [(i, i ^ k) for i in range(self.t)])

    def over_z(self, values, k):
        if k == 0:
            return values
        return lax.ppermute(values, "dp", [(d, d ^ (k * self.q)) for d in range(self.dp)])

    def over_c(self, values, k):
        if k == 0:
            return values
        return lax.ppermute(values, "dp", [(d, d ^ k) for d in range(self.dp)])


def lay_out_weights(lay, ids, stacks, f_loc, d_loc, width):
    ffe = f_loc * lay.t

    def kernel(ids_ref, *refs):
        sources, (in_ref, out_ref) = refs[: 3 * lay.q], refs[3 * lay.q :]
        for kc in range(lay.q):
            columns = pl.ds(pl.multiple_of((ids_ref[1] ^ kc) * d_loc, 128), d_loc)
            for g in range(2):
                in_ref[g, :, columns] = sources[3 * kc + g][0]
            out_ref[:, columns] = sources[3 * kc + 2][0]

    own_in, own_out = pl.pallas_call(
        kernel,
        out_shape=(
            jax.ShapeDtypeStruct((2, ffe, width), BF16),
            jax.ShapeDtypeStruct((ffe, width), BF16),
        ),
        grid_spec=pltpu.PrefetchScalarGridSpec(
            num_scalar_prefetch=1,
            grid=(lay.t, lay.z),
            in_specs=[
                pl.BlockSpec((1, f_loc, d_loc), lambda kt, kz, ids: (kz * lay.t + kt, 0, 0))
            ]
            * (3 * lay.q),
            out_specs=(
                pl.BlockSpec((2, f_loc, lay.q * d_loc), lambda kt, kz, ids: (0, kt, kz)),
                pl.BlockSpec((f_loc, lay.q * d_loc), lambda kt, kz, ids: (kt, kz)),
            ),
        ),
        cost_estimate=pl.CostEstimate(
            flops=0, bytes_accessed=12 * ffe * width, transcendentals=0
        ),
        compiler_params=pltpu.CompilerParams(vmem_limit_bytes=32 << 20),
        name="lay_out_weights",
    )(ids, *stacks)
    return own_in.reshape(2 * ffe, width), own_out


def take_apart(lay, ids, grad_in, grad_out, f_loc, d_loc, width):
    ffe = f_loc * lay.t

    def kernel(ids_ref, in_ref, out_ref, *targets):
        for kc in range(lay.q):
            columns = pl.ds(pl.multiple_of((ids_ref[1] ^ kc) * d_loc, 128), d_loc)
            for g in range(2):
                targets[3 * kc + g][0] = in_ref[g, :, columns]
            targets[3 * kc + 2][0] = out_ref[:, columns]

    shape = jax.ShapeDtypeStruct((lay.t * lay.z, f_loc, d_loc), BF16)
    spec = pl.BlockSpec((1, f_loc, d_loc), lambda kt, kz, ids: (kz * lay.t + kt, 0, 0))
    return pl.pallas_call(
        kernel,
        out_shape=(shape,) * (3 * lay.q),
        grid_spec=pltpu.PrefetchScalarGridSpec(
            num_scalar_prefetch=1,
            grid=(lay.t, lay.z),
            in_specs=[
                pl.BlockSpec((2, f_loc, lay.q * d_loc), lambda kt, kz, ids: (0, kt, kz)),
                pl.BlockSpec((f_loc, lay.q * d_loc), lambda kt, kz, ids: (kt, kz)),
            ],
            out_specs=(spec,) * (3 * lay.q),
        ),
        cost_estimate=pl.CostEstimate(
            flops=0, bytes_accessed=12 * ffe * width, transcendentals=0
        ),
        compiler_params=pltpu.CompilerParams(vmem_limit_bytes=32 << 20),
        name="take_apart",
    )(ids, grad_in.reshape(2, ffe, width), grad_out)


def home_gradients(lay, pieces, f_loc, d_loc):
    def kernel(piece_ref, in_ref, out_ref):
        in_ref[0] = piece_ref[0, :2, 0].astype(F32)
        out_ref[0] = piece_ref[0, 2, 0].astype(F32)

    spec = pl.BlockSpec((1, 3, 1, f_loc, d_loc), lambda e: (e % lay.t, 0, e // lay.t, 0, 0))
    grad_in, grad_out = pl.pallas_call(
        kernel,
        out_shape=(
            jax.ShapeDtypeStruct((EXPERTS, 2, f_loc, d_loc), F32),
            jax.ShapeDtypeStruct((EXPERTS, f_loc, d_loc), F32),
        ),
        grid=(EXPERTS,),
        in_specs=[spec],
        out_specs=(
            pl.BlockSpec((1, 2, f_loc, d_loc), lambda e: (e, 0, 0, 0)),
            pl.BlockSpec((1, f_loc, d_loc), lambda e: (e, 0, 0)),
        ),
        cost_estimate=pl.CostEstimate(
            flops=0, bytes_accessed=18 * EXPERTS * f_loc * d_loc, transcendentals=0
        ),
        name="home_gradients",
    )(pieces)
    return jnp.swapaxes(grad_in, 2, 3), grad_out


def join_columns(parts, me, count):
    rows, part = parts[0].shape
    block = min(512, rows)

    def kernel(me_ref, *refs):
        for k in range(count):

            @pl.when(pl.program_id(1) == k)
            def _(k=k):
                refs[count][...] = refs[k][...]

    return pl.pallas_call(
        kernel,
        out_shape=jax.ShapeDtypeStruct((rows, count * part), parts[0].dtype),
        grid_spec=pltpu.PrefetchScalarGridSpec(
            num_scalar_prefetch=1,
            grid=(rows // block, count),
            in_specs=[pl.BlockSpec((block, part), lambda i, k, me: (i, 0))] * count,
            out_specs=pl.BlockSpec((block, part), lambda i, k, me: (i, me[0] ^ k)),
        ),
        cost_estimate=pl.CostEstimate(
            flops=0, bytes_accessed=4 * rows * part * count, transcendentals=0
        ),
        name="join_columns",
    )(me.reshape(1).astype(jnp.int32), *parts)


def score_block(q_ref, r_ref, k_ref, kr_ref, head, step, keys, block, length, scale):
    half = r_ref.shape[1] // 2
    lanes = lax.broadcasted_iota(jnp.int32, r_ref.shape, 1) % half // (ROPE // 2)
    turned = jnp.where(lanes == head, r_ref[...], jnp.zeros_like(r_ref))
    raw = lax.dot_general(
        q_ref[...], k_ref[:keys], (((1,), (1,)), ((), ())), preferred_element_type=F32
    ) + lax.dot_general(
        turned, kr_ref[:keys], (((1,), (1,)), ((), ())), preferred_element_type=F32
    )
    rows = lax.broadcasted_iota(jnp.int32, raw.shape, 0) + step * block
    cols = lax.broadcasted_iota(jnp.int32, raw.shape, 1)
    allowed = (cols <= rows) & (cols < length)
    return jnp.where(allowed, raw * scale, NEGATIVE), turned


def attend(length, query, query_rope, kv, key_rope, heads, scale):
    rows = query.shape[0]
    block = min(256, rows)
    steps = rows // block

    def kernel(len_ref, q_ref, r_ref, k_ref, v_ref, kr_ref, o_ref, total_ref):
        head, step = pl.program_id(0), pl.program_id(1)
        for n in range(steps):

            @pl.when(step == n)
            def _(n=n):
                keys = (n + 1) * block
                scores, _ = score_block(
                    q_ref, r_ref, k_ref, kr_ref, head, n, keys, block, len_ref[0], scale
                )
                highest = jnp.max(scores, axis=-1, keepdims=True)
                expo = jnp.exp(scores - highest)
                totals = jnp.sum(expo, axis=-1, keepdims=True)
                weights = (expo * (1.0 / totals)).astype(BF16)
                o_ref[...] = dot(weights, v_ref[:keys]).astype(BF16)
                total_ref[0] = jnp.broadcast_to(highest + jnp.log(totals), (block, 128))

    return pl.pallas_call(
        kernel,
        out_shape=(
            jax.ShapeDtypeStruct((rows, heads * VDIM), BF16),
            jax.ShapeDtypeStruct((heads, rows, 128), F32),
        ),
        grid_spec=pltpu.PrefetchScalarGridSpec(
            num_scalar_prefetch=1,
            grid=(heads, steps),
            in_specs=[
                pl.BlockSpec((block, NOPE), lambda h, i, n: (i, h)),
                pl.BlockSpec((block, query_rope.shape[1]), lambda h, i, n: (i, 0)),
                pl.BlockSpec((rows, NOPE), lambda h, i, n: (0, 2 * h)),
                pl.BlockSpec((rows, VDIM), lambda h, i, n: (0, 2 * h + 1)),
                pl.BlockSpec((rows, key_rope.shape[1]), lambda h, i, n: (0, 0)),
            ],
            out_specs=(
                pl.BlockSpec((block, VDIM), lambda h, i, n: (i, h)),
                pl.BlockSpec((1, block, 128), lambda h, i, n: (h, i, 0)),
            ),
        ),
        cost_estimate=pl.CostEstimate(
            flops=heads * rows * rows * 512,
            bytes_accessed=8 * rows * heads * 512,
            transcendentals=heads * rows * rows,
        ),
        compiler_params=pltpu.CompilerParams(vmem_limit_bytes=32 << 20),
        name="attend",
    )(length, query, query_rope, kv, kv, key_rope)


def attend_back(length, query, query_rope, kv, key_rope, out_grad, log_totals, heads, scale):
    rows = query.shape[0]
    block = min(256, rows)
    steps = rows // block
    turned_cols = query_rope.shape[1]

    def kernel(
        len_ref, q_ref, r_ref, k_ref, v_ref, kr_ref, do_ref, total_ref,
        dq_ref, dr_ref, dkv_ref, dkr_ref, dk_acc, dv_acc,
    ):
        head, step = pl.program_id(0), pl.program_id(1)

        @pl.when(step == 0)
        def _():
            dk_acc[...] = jnp.zeros_like(dk_acc)
            dv_acc[...] = jnp.zeros_like(dv_acc)

        @pl.when((step == 0) & (head == 0))
        def _():
            dr_ref[...] = jnp.zeros_like(dr_ref)
            dkr_ref[...] = jnp.zeros_like(dkr_ref)

        for n in range(steps):

            @pl.when(step == n)
            def _(n=n):
                keys = (n + 1) * block
                scores, turned = score_block(
                    q_ref, r_ref, k_ref, kr_ref, head, n, keys, block, len_ref[0], scale
                )
                probs = jnp.exp(scores - total_ref[0][:, :1])
                prob_grad = lax.dot_general(
                    do_ref[...], v_ref[:keys], (((1,), (1,)), ((), ())), preferred_element_type=F32
                )
                centre = jnp.sum(probs * prob_grad, axis=-1, keepdims=True)
                score_grad = (probs * (prob_grad - centre)).astype(BF16)
                probs_low = probs.astype(BF16)
                dq_ref[...] = (dot(score_grad, k_ref[:keys]) * scale).astype(BF16)
                half = turned_cols // 2
                lanes = lax.broadcasted_iota(jnp.int32, (block, turned_cols), 1)
                lanes = lanes % half // (ROPE // 2)
                turned_grad = dot(score_grad, kr_ref[:keys]) * scale
                dr_ref[n * block : keys] += jnp.where(lanes == head, turned_grad, 0.0)
                dk_acc[:keys] += dot_tn(score_grad, q_ref[...]) * scale
                dkr_ref[:keys] += dot_tn(score_grad, turned) * scale
                dv_acc[:keys] += dot_tn(probs_low, do_ref[...])

        @pl.when(step == steps - 1)
        def _():
            dkv_ref[:, :NOPE] = dk_acc[...].astype(BF16)
            dkv_ref[:, NOPE:] = dv_acc[...].astype(BF16)

    return pl.pallas_call(
        kernel,
        out_shape=(
            jax.ShapeDtypeStruct((rows, heads * NOPE), BF16),
            jax.ShapeDtypeStruct((rows, turned_cols), F32),
            jax.ShapeDtypeStruct((rows, heads * (NOPE + VDIM)), BF16),
            jax.ShapeDtypeStruct((rows, turned_cols), F32),
        ),
        grid_spec=pltpu.PrefetchScalarGridSpec(
            num_scalar_prefetch=1,
            grid=(heads, steps),
            in_specs=[
                pl.BlockSpec((block, NOPE), lambda h, i, n: (i, h)),
                pl.BlockSpec((block, turned_cols), lambda h, i, n: (i, 0)),
                pl.BlockSpec((rows, NOPE), lambda h, i, n: (0, 2 * h)),
                pl.BlockSpec((rows, VDIM), lambda h, i, n: (0, 2 * h + 1)),
                pl.BlockSpec((rows, turned_cols), lambda h, i, n: (0, 0)),
                pl.BlockSpec((block, VDIM), lambda h, i, n: (i, h)),
                pl.BlockSpec((1, block, 128), lambda h, i, n: (h, i, 0)),
            ],
            out_specs=(
                pl.BlockSpec((block, NOPE), lambda h, i, n: (i, h)),
                pl.BlockSpec((rows, turned_cols), lambda h, i, n: (0, 0)),
                pl.BlockSpec((rows, NOPE + VDIM), lambda h, i, n: (0, h)),
                pl.BlockSpec((rows, turned_cols), lambda h, i, n: (0, 0)),
            ),
            scratch_shapes=[pltpu.VMEM((rows, NOPE), F32), pltpu.VMEM((rows, VDIM), F32)],
        ),
        cost_estimate=pl.CostEstimate(
            flops=heads * rows * rows * 1600,
            bytes_accessed=16 * rows * heads * 512,
            transcendentals=heads * rows * rows,
        ),
        compiler_params=pltpu.CompilerParams(vmem_limit_bytes=40 << 20),
        name="attend_back",
    )(length, query, query_rope, kv, kv, key_rope, out_grad, log_totals)


def in_order(values, me, count):
    zero = jnp.zeros_like(values[0])
    ordered = []
    for j in range(count):
        total = zero
        for k in range(count):
            total = jnp.where((me ^ k) == j, values[k], total)
        ordered.append(total)
    return jnp.stack(ordered)


def body(
    lay,
    hidden,
    lengths,
    routes,
    attn_gain,
    w_query,
    w_kv_down,
    kv_gain,
    w_kv_up,
    w_out,
    ffn_gain,
    w_router,
    w_expert_in,
    w_expert_out,
    w_shared_in,
    w_shared_out,
    cotangent,
):
    rows, width = hidden.shape
    nz, nt, nq, ndp = lay.z, lay.t, lay.q, lay.dp
    me_dp = lax.axis_index("dp")
    me_t = lax.axis_index("tensor")
    me_z = me_dp // nq
    me_c = me_dp % nq
    part = width // nt
    d_loc = w_query.shape[0]
    f_loc = w_expert_out.shape[1]
    ffe = f_loc * nt
    heads = w_query.shape[1] // (NOPE + ROPE)
    score_scale = (NOPE + ROPE) ** (-0.5)

    def own_part(values):
        return lax.dynamic_slice_in_dim(values, me_t * part, part, 1)

    def gather_z(values):
        return lax.all_gather(values, "dp", axis=0, tiled=False, axis_index_groups=lay.z_groups)

    def scatter_z(values):
        return lax.psum_scatter(
            values, "dp", scatter_dimension=0, tiled=False, axis_index_groups=lay.z_groups
        )

    def gather_t(values):
        return lax.all_gather(values, "tensor", axis=1, tiled=True)

    def scatter_t(values):
        return lax.psum_scatter(
            values.astype(BF16), "tensor", scatter_dimension=1, tiled=True
        ).astype(F32)

    def swap_t(values):
        return lax.all_to_all(values, "tensor", split_axis=0, concat_axis=0, tiled=True)

    def swap_z(values):
        return lax.all_to_all(
            values,
            "dp",
            split_axis=0,
            concat_axis=0,
            axis_index_groups=lay.z_groups,
            tiled=True,
        )

    def gather_t_direct(values):
        return join_columns([lay.over_t(values, k) for k in range(nt)], me_t, nt)

    def part_for(values, k):
        return lax.dynamic_slice_in_dim(values, (me_t ^ k) * part, part, 1)

    def scatter_t_direct(values):
        total = part_for(values, 0)
        for k in range(1, nt):
            total = total + lay.over_t(part_for(values, k).astype(BF16), k).astype(F32)
        return total

    ids = jnp.stack([me_z, me_c, me_t]).astype(jnp.int32)

    packed = jnp.concatenate(
        [jnp.swapaxes(w_expert_in, 2, 3), w_expert_out[:, None]], 1
    ).reshape(nz, nt, 3, f_loc, d_loc)
    by_column = swap_t(jnp.swapaxes(packed, 0, 1))

    lat_loc = kv_gain.shape[0]
    q_rows, down_rows, out_rows = w_query.shape[1], w_kv_down.shape[1], w_out.shape[0]
    half = ROPE // 2

    def by_kind(turned):
        split = turned.reshape(heads, NOPE + ROPE, -1)
        return jnp.concatenate(
            [
                split[:, :NOPE].reshape(heads * NOPE, -1),
                split[:, NOPE : NOPE + half].reshape(heads * half, -1),
                split[:, NOPE + half :].reshape(heads * half, -1),
            ],
            0,
        )

    def by_head(rows_in):
        nope = rows_in[: heads * NOPE].reshape(heads, NOPE, -1)
        first = rows_in[heads * NOPE : heads * (NOPE + half)].reshape(heads, half, -1)
        second = rows_in[heads * (NOPE + half) :].reshape(heads, half, -1)
        return jnp.concatenate([nope, first, second], 1).reshape(heads * (NOPE + ROPE), -1)

    gains = jnp.stack([attn_gain, ffn_gain, jnp.pad(kv_gain, (0, d_loc - lat_loc))])
    front_pack = jnp.concatenate(
        [
            by_kind(jnp.transpose(w_query)),
            jnp.transpose(w_kv_down),
            jnp.transpose(w_router),
            jnp.pad(gains, ((0, 13), (0, 0))),
            w_out,
            w_kv_up.reshape(-1, d_loc),
        ],
        0,
    )
    front = lax.all_gather(front_pack, "dp", axis=0, tiled=False)

    valid_length = lengths[0]
    valid_rows = lax.broadcasted_iota(jnp.int32, (rows, 1), 0) < valid_length
    cot_low = jnp.where(valid_rows, cotangent, jnp.zeros_like(cotangent))
    cot_part = own_part(cot_low)
    route_own = jnp.pad(jnp.transpose(routes), ((0, -TOP % 8), (0, 0)), constant_values=-1)
    route_all = in_order([lay.over_z(route_own, k) for k in range(nz)], me_z, nz)
    inputs = hidden.astype(F32)
    attn_inverse = inverse_rms(inputs)
    cosine, sine = angle_tables(rows)
    wide_cos, wide_sin = jnp.tile(cosine, (1, heads)), jnp.tile(sine, (1, heads))
    front, attn_inverse, wide_cos, wide_sin, route_all = lax.optimization_barrier(
        (front, attn_inverse, wide_cos, wide_sin, route_all)
    )

    plane_ids = me_z * nt + jnp.arange(nt, dtype=jnp.int32)
    member = jnp.any(route_all[:, :, :, None] == plane_ids[None, None, None, :], axis=1)
    row_ids = lax.broadcasted_iota(jnp.int32, (rows, rows), 0)
    col_ids = lax.broadcasted_iota(jnp.int32, (rows, rows), 1)
    before = (col_ids < row_ids).astype(BF16)
    position = jnp.einsum("ij,sje->sei", before, member.astype(BF16), preferred_element_type=F32)
    key = jnp.where(jnp.swapaxes(member, 1, 2), position.astype(jnp.int32), -1)
    slots_iota = lax.broadcasted_iota(jnp.int32, (1, 1, CAP, 1), 2)

    def place_of(keys):
        return (keys[:, :, None, :] == slots_iota).astype(BF16)

    place = place_of(key)
    own_key = lax.dynamic_index_in_dim(key, me_t, 1, keepdims=False)
    own_place = own_key[:, None, :] == slots_iota[0]

    def pick_rows(values):
        picked = jnp.einsum("sepk,skd->espd", place, values, preferred_element_type=F32)
        return picked.astype(BF16).reshape(nt, nz * CAP, part)

    def send_out(picked):
        return jnp.swapaxes(swap_t(picked), 0, 1).reshape(nz * CAP, width)

    def send_back(values):
        return swap_t(jnp.swapaxes(values.reshape(nz * CAP, nt, part), 0, 1))

    def combine(parts):
        parts = parts.reshape(nt, nz, CAP, part)
        summed = jnp.einsum("sepk,espd->skd", place, parts, preferred_element_type=F32)
        return summed.astype(BF16)


    def rows_of(first, count):
        return jnp.swapaxes(front[:, first : first + count], 0, 1).reshape(count, width)

    query_t = rows_of(0, q_rows)
    down_t = rows_of(q_rows, down_rows)
    at = q_rows + down_rows
    router_t = rows_of(at, EXPERTS)
    gain_attn = front[:, at + EXPERTS].reshape(-1)
    gain_ffn = front[:, at + EXPERTS + 1].reshape(-1)
    gain_kv = front[:, at + EXPERTS + 2, :lat_loc].reshape(-1)
    at = at + 2 * EXPERTS
    out_w = rows_of(at, out_rows)
    up_w = front[:, at + out_rows :].reshape(LATENT, heads * (NOPE + VDIM))

    attn_scale = gain_attn.astype(F32)
    normed_low = (inputs * attn_inverse * attn_scale).astype(BF16)
    query = dot_nt(normed_low, query_t)
    nope_cols = heads * NOPE
    query_nope = query[:, :nope_cols].astype(BF16)
    query_rope = jnp.concatenate(
        rotate(
            query[:, nope_cols : nope_cols + heads * half],
            query[:, nope_cols + heads * half :],
            wide_cos,
            wide_sin,
        ),
        1,
    ).astype(BF16)
    latent_all = dot_nt(normed_low, down_t)
    latent_all, by_column = lax.optimization_barrier((latent_all, by_column))
    by_column = jnp.transpose(by_column, (2, 1, 0, 3, 4))
    by_plane = [swap_z(by_column[g]) for g in range(3)]
    latent = latent_all[:, :LATENT]
    kv_inverse = inverse_rms(latent)
    latent_hat = latent * kv_inverse
    kv_scale = gain_kv.astype(F32)
    latent_low = (latent_hat * kv_scale).astype(BF16)
    key_turned = jnp.concatenate(
        rotate(
            latent_all[:, LATENT : LATENT + half],
            latent_all[:, LATENT + half :],
            wide_cos[:, :half],
            wide_sin[:, :half],
        ),
        1,
    ).astype(BF16)
    copies = (2 * half, 2 * heads * half)
    to_col = lax.broadcasted_iota(jnp.int32, copies, 1)
    from_col = to_col // (heads * half) * half + to_col % half
    repeat = (lax.broadcasted_iota(jnp.int32, copies, 0) == from_col).astype(BF16)
    key_rope = dot(key_turned, repeat).astype(BF16)
    keys_values = dot(latent_low, up_w).astype(BF16)
    attended_low, log_totals = attend(
        lengths, query_nope, query_rope, keys_values, key_rope, heads, score_scale
    )
    attn_part, by_plane[0] = lax.optimization_barrier((dot(attended_low, out_w), by_plane[0]))
    attn_sum = scatter_t(attn_part)
    residual = own_part(hidden).astype(F32) + attn_sum

    def row_mean(values):
        partial = jnp.sum(values, axis=-1).reshape(-1, 128)
        return lax.psum(partial, "tensor").reshape(-1, 1) * (1.0 / width)

    ffn_inverse = lax.rsqrt(row_mean(residual * residual) + EPSILON)
    ffn_hat = residual * ffn_inverse
    ffn_scale = lax.dynamic_slice_in_dim(gain_ffn, me_t * part, part, 0).astype(F32)
    ffn_part = (ffn_hat * ffn_scale).astype(BF16)

    ffn_part, by_plane[1] = lax.optimization_barrier((ffn_part, by_plane[1]))
    ffn_all = gather_z(ffn_part)
    ffn_low = gather_t_direct(ffn_part)
    ffn_all, ffn_low, cot_ready = lax.optimization_barrier((ffn_all, ffn_low, cot_part))
    picked = pick_rows(ffn_all)
    expert_rows = send_out(picked)
    cot_picked = pick_rows(gather_z(cot_ready))
    shared_pack = jnp.concatenate(
        [jnp.swapaxes(w_shared_in, 1, 2).reshape(-1, d_loc), w_shared_out], 0
    )
    cot_picked, shared_pack = lax.optimization_barrier((cot_picked, shared_pack))
    cot_rows = send_out(cot_picked)
    shared_all = lax.all_gather(shared_pack, "dp", axis=0, tiled=False)
    pieces = [plane.reshape(nz * nt, f_loc, d_loc) for plane in by_plane]
    own_in, own_out = lay_out_weights(
        lay,
        ids,
        [lay.over_c(pieces[g], k) for k in range(nq) for g in range(3)],
        f_loc,
        d_loc,
        width,
    )
    router_probs = jax.nn.softmax(dot_nt(ffn_low, router_t), axis=-1)
    probs_turned = jnp.transpose(router_probs).reshape(EXPERTS, -1, 128)
    own_probs = in_order(
        [
            lay.over_z(
                lax.dynamic_index_in_dim(
                    probs_turned, (me_z ^ k) * nt + me_t, 0, keepdims=False
                ),
                k,
            )
            for k in range(nz)
        ],
        me_z,
        nz,
    ).reshape(nz, rows)
    gate_rows = jnp.sum(jnp.where(own_place, own_probs[:, None, :], 0.0), axis=-1).reshape(
        nz * CAP, 1
    )
    gate_up = dot_nt(expert_rows, own_in)
    gate_pre, up_pre = gate_up[:, :ffe], gate_up[:, ffe:]
    gate_sig = jax.nn.sigmoid(gate_pre)
    gate_silu = gate_pre * gate_sig
    active = (gate_silu * up_pre).astype(BF16)
    rows_out = (dot(active, own_out) * gate_rows).astype(BF16)
    rows_out, cot_rows, shared_all = lax.optimization_barrier((rows_out, cot_rows, shared_all))
    out_parts = send_back(rows_out)
    active_grad_raw = dot_nt(cot_rows, own_out)
    gate_grad = jnp.sum(active.astype(F32) * active_grad_raw, axis=-1).reshape(nz, CAP)
    active_grad = active_grad_raw * gate_rows
    pre_low = jnp.concatenate(
        [
            active_grad * up_pre * gate_sig * (1.0 + gate_pre * (1.0 - gate_sig)),
            active_grad * gate_silu,
        ],
        1,
    ).astype(BF16)
    gated_active = (active.astype(F32) * gate_rows).astype(BF16)
    rows_grad = dot(pre_low, own_in).astype(BF16)
    rows_grad, out_parts = lax.optimization_barrier((rows_grad, out_parts))
    grad_parts = send_back(rows_grad)
    routed, pre_low, gated_active = lax.optimization_barrier(
        (combine(out_parts), pre_low, gated_active)
    )
    routed = scatter_z(routed).astype(F32)
    token_grad = jnp.sum(jnp.where(own_place, gate_grad[:, :, None], 0.0), axis=1)
    token_grad = token_grad.reshape(nz, -1, 128)
    token_plane = jnp.stack(
        [
            lay.over_z(lax.dynamic_index_in_dim(token_grad, me_z ^ k, 0, keepdims=False), k)
            for k in range(nz)
        ]
    )
    token_home = jnp.stack([lay.over_t(token_plane, k) for k in range(nt)])
    experts = jnp.arange(EXPERTS, dtype=jnp.int32)
    came_from = (me_t ^ (experts % nt)) * nz + (me_z ^ (experts // nt))
    probs_grad = lax.dot_general(
        token_home.reshape(EXPERTS, rows),
        (experts[:, None] == came_from[None, :]).astype(F32),
        (((0,), (0,)), ((), ())),
        precision=lax.Precision.HIGHEST,
        preferred_element_type=F32,
    )

    grad_in_own = dot_tn(pre_low, expert_rows).astype(BF16)
    grad_out_own = dot_tn(gated_active, cot_rows).astype(BF16)
    ffs = w_shared_out.shape[0]
    shared_in = jnp.swapaxes(shared_all[:, : 2 * ffs], 0, 1).reshape(2 * ffs, width)
    shared_out = jnp.swapaxes(shared_all[:, 2 * ffs :], 0, 1).reshape(ffs, width)
    shared_pre = dot_nt(ffn_low, shared_in)
    shared_gate, shared_up = shared_pre[:, :ffs], shared_pre[:, ffs:]
    shared_sig = jax.nn.sigmoid(shared_gate)
    shared_silu = shared_gate * shared_sig
    shared_act = (shared_silu * shared_up).astype(BF16)
    shared_full = dot(shared_act, shared_out)
    shared_act_grad = dot_nt(cot_low, shared_out)
    shared_pre_grad = jnp.concatenate(
        [
            shared_act_grad * shared_up * shared_sig * (1.0 + shared_gate * (1.0 - shared_sig)),
            shared_act_grad * shared_silu,
        ],
        1,
    ).astype(BF16)
    grad_shared_in = dot_tn(shared_pre_grad, ffn_low)
    grad_shared_out = dot_tn(shared_act, cot_low)
    shared_grad_full = dot(shared_pre_grad, shared_in)

    (
        grad_parts,
        grad_in_own,
        grad_out_own,
        routed,
        probs_grad,
        shared_full,
        shared_grad_full,
    ) = lax.optimization_barrier(
        (
            grad_parts,
            grad_in_own,
            grad_out_own,
            routed,
            probs_grad,
            shared_full,
            shared_grad_full,
        )
    )
    shared_both = jnp.concatenate([shared_grad_full, shared_full], 0).astype(BF16)
    shared_both = swap_t(jnp.swapaxes(shared_both.reshape(2 * rows, nt, part), 0, 1))
    shared_both = jnp.sum(shared_both.astype(F32), axis=0)
    shared_grad, shared_part = shared_both[:rows], shared_both[rows:]
    grad_pieces = take_apart(lay, ids, grad_in_own, grad_out_own, f_loc, d_loc, width)
    routed_grad = scatter_z(combine(grad_parts)).astype(F32)
    grad_class = [
        sum(lay.over_c(grad_pieces[3 * k + g], k).astype(F32) for k in range(nq)).astype(BF16)
        for g in range(3)
    ]
    routed_grad, grad_class = lax.optimization_barrier((routed_grad, grad_class))
    grad_plane = [swap_z(grad_class[g].reshape(nz, nt, f_loc, d_loc)) for g in range(3)]

    logits_grad = router_probs * (
        probs_grad - jnp.sum(router_probs * probs_grad, axis=-1, keepdims=True)
    )
    router_part = lax.dot_general(
        logits_grad,
        ffn_low.astype(F32),
        (((0,), (0,)), ((), ())),
        precision=lax.Precision.HIGHEST,
        preferred_element_type=F32,
    )
    router_slice = lax.dynamic_slice_in_dim(router_t, me_t * part, part, 1)
    ffn_grad = (
        shared_grad
        + routed_grad
        + lax.dot_general(
            logits_grad,
            router_slice.astype(F32),
            (((1,), (0,)), ((), ())),
            precision=lax.Precision.HIGHEST,
            preferred_element_type=F32,
        )
    )
    scaled = ffn_scale * ffn_grad
    ffn_gain_part = jnp.sum(ffn_grad * ffn_hat, axis=0)
    residual_grad = cot_part.astype(F32) + ffn_inverse * (
        scaled - ffn_hat * row_mean(ffn_hat * scaled)
    )
    residual_low = gather_t(residual_grad.astype(BF16))

    def sum_dp(values):
        return lax.psum_scatter(values, "dp", scatter_dimension=0, tiled=False).astype(F32)

    def by_owner(values):
        return jnp.swapaxes(values.astype(BF16).reshape(-1, ndp, d_loc), 0, 1)

    shared_grads = jnp.concatenate([by_owner(grad_shared_in), by_owner(grad_shared_out)], 1)
    residual_low, shared_grads, grad_plane[0] = lax.optimization_barrier(
        (residual_low, shared_grads, grad_plane[0])
    )
    shared_sum = sum_dp(shared_grads)
    grad_out_w = dot_tn(attended_low, residual_low)
    attended_grad = dot_nt(residual_low, out_w).astype(BF16)
    query_nope_grad, query_turned_grad, kv_grad, rope_grad = attend_back(
        lengths,
        query_nope,
        query_rope,
        keys_values,
        key_rope,
        attended_grad,
        log_totals,
        heads,
        score_scale,
    )
    output_part = lax.optimization_barrier((residual + routed + shared_part).astype(BF16))
    query_turned_grad, output_parts = lax.optimization_barrier(
        (query_turned_grad, [lay.over_t(output_part, k) for k in range(nt)])
    )
    output = join_columns(output_parts, me_t, nt)
    turned_first, turned_second = rotate_back(
        query_turned_grad[:, : heads * half], query_turned_grad[:, heads * half :], wide_cos, wide_sin
    )
    query_grad = jnp.concatenate(
        [query_nope_grad, turned_first.astype(BF16), turned_second.astype(BF16)], 1
    )
    rope_sum = rope_grad.reshape(rows, 2, heads, half).sum(2)
    key_rope_part = jnp.concatenate(
        rotate_back(
            rope_sum[:, 0], rope_sum[:, 1], wide_cos[:, :half], wide_sin[:, :half]
        ),
        1,
    )
    latent_part = dot_nt(kv_grad, up_w)
    grad_kv_gain = jnp.sum(latent_part * latent_hat, axis=0)
    scaled_kv = kv_scale * latent_part
    latent_back = kv_inverse * (
        scaled_kv - latent_hat * jnp.mean(latent_hat * scaled_kv, axis=-1, keepdims=True)
    )
    down_grad = jnp.concatenate([latent_back, key_rope_part], -1).astype(BF16)
    normed_full, grad_plane[1] = lax.optimization_barrier(
        (dot(query_grad, query_t) + dot(down_grad, down_t), grad_plane[1])
    )
    normed_grad = scatter_t_direct(normed_full)
    normed_grad, grad_plane[2] = lax.optimization_barrier((normed_grad, grad_plane[2]))
    grad_home = swap_t(jnp.transpose(jnp.stack(grad_plane), (2, 0, 1, 3, 4)))
    attn_hat = own_part(hidden).astype(F32) * attn_inverse
    scaled_in = lax.dynamic_slice_in_dim(attn_scale, me_t * part, part, 0) * normed_grad
    attn_gain_part = jnp.sum(normed_grad * attn_hat, axis=0)
    input_grad = residual_grad + attn_inverse * (
        scaled_in - attn_hat * row_mean(attn_hat * scaled_in)
    )
    grad_expert_in, grad_expert_out = home_gradients(lay, grad_home, f_loc, d_loc)
    grad_hidden = gather_t_direct(input_grad.astype(BF16))

    def spread(values):
        return lax.dynamic_update_slice(
            jnp.zeros((1, width), F32), values[None], (jnp.int32(0), me_t * part)
        )

    kv_gain_row = jnp.pad(
        grad_kv_gain.reshape(ndp, lat_loc), ((0, 0), (0, d_loc - lat_loc))
    ).reshape(1, width)
    gain_grads = jnp.concatenate([spread(attn_gain_part), spread(ffn_gain_part), kv_gain_row], 0)
    front_sum = sum_dp(
        jnp.concatenate(
            [
                by_owner(dot_tn(down_grad, normed_low)),
                by_owner(jnp.pad(gain_grads, ((0, 13), (0, 0)))),
                by_owner(router_part),
                by_owner(dot_tn(query_grad, normed_low)),
                by_owner(grad_out_w),
                dot_tn(latent_low, kv_grad).astype(BF16).reshape(ndp, -1, d_loc),
            ],
            1,
        )
    )
    own_sum = front_sum[: down_rows + EXPERTS]
    own_low = own_sum.astype(BF16)
    for k in range(1, nt):
        own_sum = own_sum + lay.over_t(own_low, k).astype(F32)
    at = down_rows + 2 * EXPERTS
    return (
        output,
        grad_hidden,
        own_sum[down_rows],
        jnp.transpose(by_head(front_sum[at : at + q_rows])),
        jnp.transpose(own_sum[:down_rows]),
        own_sum[down_rows + 2, :lat_loc],
        front_sum[at + q_rows + out_rows :].reshape(w_kv_up.shape),
        front_sum[at + q_rows : at + q_rows + out_rows],
        own_sum[down_rows + 1],
        jnp.transpose(front_sum[down_rows + EXPERTS : at]),
        grad_expert_in,
        grad_expert_out,
        jnp.swapaxes(shared_sum[: 2 * ffs].reshape(2, ffs, d_loc), 1, 2),
        shared_sum[2 * ffs :],
    )


def solution(mesh):
    return jax.shard_map(
        functools.partial(body, Layout(mesh.shape["dp"], mesh.shape["tensor"])),
        mesh=mesh,
        in_specs=(
            P("dp", None),
            P("dp"),
            P("dp", None),
            P("dp"),
            P("dp", "tensor"),
            P("dp", None),
            P("dp"),
            P("dp", "tensor"),
            P("tensor", "dp"),
            P("dp"),
            P("dp", None),
            P(None, None, "dp", "tensor"),
            P(None, "tensor", "dp"),
            P(None, "dp", "tensor"),
            P("tensor", "dp"),
            P("dp", None),
        ),
        out_specs=(
            P("dp", None),
            P("dp", None),
            P("dp"),
            P("dp", "tensor"),
            P("dp", None),
            P("dp"),
            P("dp", "tensor"),
            P("tensor", "dp"),
            P("dp"),
            P("dp", None),
            P(None, None, "dp", "tensor"),
            P(None, "tensor", "dp"),
            P(None, "dp", "tensor"),
            P("tensor", "dp"),
        ),
        check_vma=False,
    )
```

```python
import functools
import math

import jax
import jax.numpy as jnp
from jax import lax
from jax.experimental import pallas as pl
from jax.experimental.pallas import tpu as pltpu
from jax.sharding import PartitionSpec as P

NOPE = 128
ROPE = 64
VDIM = 128
LATENT = 512
TOP = 6
EXPERTS = 16
CAP = 512

EPSILON = 1e-06
NEGATIVE = -1e30
F32 = jnp.float32
BF16 = jnp.bfloat16


def dot(a, b):
    return jnp.dot(a, b, preferred_element_type=F32)


def dot_nt(a, b):
    return lax.dot_general(a, b, (((1,), (1,)), ((), ())), preferred_element_type=F32)


def dot_tn(a, b):
    return lax.dot_general(a, b, (((0,), (0,)), ((), ())), preferred_element_type=F32)


def rotate(first, second, cosine, sine):
    return first * cosine - second * sine, second * cosine + first * sine


def rotate_back(first, second, cosine, sine):
    return first * cosine + second * sine, second * cosine - first * sine


def angle_tables(rows_count):
    positions = jnp.arange(rows_count, dtype=F32)
    freqs = jnp.exp(jnp.arange(ROPE // 2, dtype=F32) * (-2.0 * math.log(10000.0) / ROPE))
    angles = positions[:, None] * freqs[None, :]
    return (jnp.cos(angles), jnp.sin(angles))


def inverse_rms(values):
    return lax.rsqrt(jnp.mean(values * values, axis=-1, keepdims=True) + EPSILON)


class Layout:
    def __init__(self, n_dp, n_tensor):
        self.dp, self.t = n_dp, n_tensor
        self.q = n_dp * n_tensor // EXPERTS
        self.z = n_dp // self.q
        if self.z * self.t != EXPERTS or self.z * self.q != n_dp:
            raise ValueError("mesh")
        self.z_groups = [[c + self.q * z for z in range(self.z)] for c in range(self.q)]

    def over_t(self, values, k):
        if k == 0:
            return values
        return lax.ppermute(values, "tensor", [(i, i ^ k) for i in range(self.t)])

    def over_z(self, values, k):
        if k == 0:
            return values
        return lax.ppermute(values, "dp", [(d, d ^ (k * self.q)) for d in range(self.dp)])

    def over_c(self, values, k):
        if k == 0:
            return values
        return lax.ppermute(values, "dp", [(d, d ^ k) for d in range(self.dp)])


def lay_out_weights(lay, ids, stacks, f_loc, d_loc, width):
    ffe = f_loc * lay.t
    count = len(stacks) // lay.q

    def kernel(ids_ref, *refs):
        for kc in range(lay.q):
            columns = pl.ds(pl.multiple_of((ids_ref[1] ^ kc) * d_loc, 128), d_loc)
            for g in range(count):
                refs[-1][g, :, columns] = refs[count * kc + g][0]

    own = pl.pallas_call(
        kernel,
        out_shape=jax.ShapeDtypeStruct((count, ffe, width), BF16),
        grid_spec=pltpu.PrefetchScalarGridSpec(
            num_scalar_prefetch=1,
            grid=(lay.t, lay.z),
            in_specs=[
                pl.BlockSpec(
                    (1, f_loc, d_loc), lambda kt, kz, ids: ((kz ^ ids[0]) * lay.t + kt, 0, 0)
                )
            ]
            * len(stacks),
            out_specs=pl.BlockSpec(
                (count, f_loc, lay.q * d_loc), lambda kt, kz, ids: (0, kt, kz)
            ),
        ),
        cost_estimate=pl.CostEstimate(
            flops=0, bytes_accessed=4 * count * ffe * width, transcendentals=0
        ),
        compiler_params=pltpu.CompilerParams(vmem_limit_bytes=32 << 20),
        name="lay_out_weights",
    )(ids, *stacks)
    return own.reshape(count * ffe, width)


def take_apart(lay, ids, grad_in, grad_out, f_loc, d_loc, width):
    ffe = f_loc * lay.t

    def kernel(ids_ref, in_ref, out_ref, *targets):
        for kc in range(lay.q):
            columns = pl.ds(pl.multiple_of((ids_ref[1] ^ kc) * d_loc, 128), d_loc)
            for g in range(2):
                targets[3 * kc + g][0] = in_ref[g, :, columns]
            targets[3 * kc + 2][0] = out_ref[:, columns]

    shape = jax.ShapeDtypeStruct((lay.t * lay.z, f_loc, d_loc), BF16)
    spec = pl.BlockSpec((1, f_loc, d_loc), lambda kt, kz, ids: (kz * lay.t + kt, 0, 0))
    return pl.pallas_call(
        kernel,
        out_shape=(shape,) * (3 * lay.q),
        grid_spec=pltpu.PrefetchScalarGridSpec(
            num_scalar_prefetch=1,
            grid=(lay.t, lay.z),
            in_specs=[
                pl.BlockSpec((2, f_loc, lay.q * d_loc), lambda kt, kz, ids: (0, kt, kz)),
                pl.BlockSpec((f_loc, lay.q * d_loc), lambda kt, kz, ids: (kt, kz)),
            ],
            out_specs=(spec,) * (3 * lay.q),
        ),
        cost_estimate=pl.CostEstimate(
            flops=0, bytes_accessed=12 * ffe * width, transcendentals=0
        ),
        compiler_params=pltpu.CompilerParams(vmem_limit_bytes=32 << 20),
        name="take_apart",
    )(ids, grad_in.reshape(2, ffe, width), grad_out)


def home_gradients(lay, pieces, f_loc, d_loc):
    def kernel(piece_ref, in_ref, out_ref):
        in_ref[0] = piece_ref[0, :2, 0].astype(F32)
        out_ref[0] = piece_ref[0, 2, 0].astype(F32)

    spec = pl.BlockSpec((1, 3, 1, f_loc, d_loc), lambda e: (e % lay.t, 0, e // lay.t, 0, 0))
    grad_in, grad_out = pl.pallas_call(
        kernel,
        out_shape=(
            jax.ShapeDtypeStruct((EXPERTS, 2, f_loc, d_loc), F32),
            jax.ShapeDtypeStruct((EXPERTS, f_loc, d_loc), F32),
        ),
        grid=(EXPERTS,),
        in_specs=[spec],
        out_specs=(
            pl.BlockSpec((1, 2, f_loc, d_loc), lambda e: (e, 0, 0, 0)),
            pl.BlockSpec((1, f_loc, d_loc), lambda e: (e, 0, 0)),
        ),
        cost_estimate=pl.CostEstimate(
            flops=0, bytes_accessed=18 * EXPERTS * f_loc * d_loc, transcendentals=0
        ),
        name="home_gradients",
    )(pieces)
    return jnp.swapaxes(grad_in, 2, 3), grad_out


def join_columns(parts, me, count):
    rows, part = parts[0].shape
    block = min(512, rows)

    def kernel(me_ref, *refs):
        for k in range(count):

            @pl.when(pl.program_id(1) == k)
            def _(k=k):
                refs[count][...] = refs[k][...]

    return pl.pallas_call(
        kernel,
        out_shape=jax.ShapeDtypeStruct((rows, count * part), parts[0].dtype),
        grid_spec=pltpu.PrefetchScalarGridSpec(
            num_scalar_prefetch=1,
            grid=(rows // block, count),
            in_specs=[pl.BlockSpec((block, part), lambda i, k, me: (i, 0))] * count,
            out_specs=pl.BlockSpec((block, part), lambda i, k, me: (i, me[0] ^ k)),
        ),
        cost_estimate=pl.CostEstimate(
            flops=0, bytes_accessed=4 * rows * part * count, transcendentals=0
        ),
        name="join_columns",
    )(me.reshape(1).astype(jnp.int32), *parts)


def score_block(q_ref, r_ref, k_ref, kr_ref, head, step, keys, block, length, scale):
    half = r_ref.shape[1] // 2
    lanes = lax.broadcasted_iota(jnp.int32, r_ref.shape, 1) % half // (ROPE // 2)
    turned = jnp.where(lanes == head, r_ref[...], jnp.zeros_like(r_ref))
    raw = lax.dot_general(
        q_ref[...], k_ref[:keys], (((1,), (1,)), ((), ())), preferred_element_type=F32
    ) + lax.dot_general(
        turned, kr_ref[:keys], (((1,), (1,)), ((), ())), preferred_element_type=F32
    )
    rows = lax.broadcasted_iota(jnp.int32, raw.shape, 0) + step * block
    cols = lax.broadcasted_iota(jnp.int32, raw.shape, 1)
    allowed = (cols <= rows) & (cols < length)
    return jnp.where(allowed, raw * scale, NEGATIVE), turned


def attend(length, query, query_rope, kv, key_rope, heads, scale):
    rows = query.shape[0]
    block = min(256, rows)
    steps = rows // block

    def kernel(len_ref, q_ref, r_ref, k_ref, v_ref, kr_ref, o_ref, total_ref):
        head, step = pl.program_id(0), pl.program_id(1)
        for n in range(steps):

            @pl.when(step == n)
            def _(n=n):
                keys = (n + 1) * block
                scores, _ = score_block(
                    q_ref, r_ref, k_ref, kr_ref, head, n, keys, block, len_ref[0], scale
                )
                highest = jnp.max(scores, axis=-1, keepdims=True)
                expo = jnp.exp(scores - highest)
                totals = jnp.sum(expo, axis=-1, keepdims=True)
                weights = (expo * (1.0 / totals)).astype(BF16)
                o_ref[...] = dot(weights, v_ref[:keys]).astype(BF16)
                total_ref[0] = jnp.broadcast_to(highest + jnp.log(totals), (block, 128))

    return pl.pallas_call(
        kernel,
        out_shape=(
            jax.ShapeDtypeStruct((rows, heads * VDIM), BF16),
            jax.ShapeDtypeStruct((heads, rows, 128), F32),
        ),
        grid_spec=pltpu.PrefetchScalarGridSpec(
            num_scalar_prefetch=1,
            grid=(heads, steps),
            in_specs=[
                pl.BlockSpec((block, NOPE), lambda h, i, n: (i, h)),
                pl.BlockSpec((block, query_rope.shape[1]), lambda h, i, n: (i, 0)),
                pl.BlockSpec((rows, NOPE), lambda h, i, n: (0, 2 * h)),
                pl.BlockSpec((rows, VDIM), lambda h, i, n: (0, 2 * h + 1)),
                pl.BlockSpec((rows, key_rope.shape[1]), lambda h, i, n: (0, 0)),
            ],
            out_specs=(
                pl.BlockSpec((block, VDIM), lambda h, i, n: (i, h)),
                pl.BlockSpec((1, block, 128), lambda h, i, n: (h, i, 0)),
            ),
        ),
        cost_estimate=pl.CostEstimate(
            flops=heads * rows * rows * 512,
            bytes_accessed=8 * rows * heads * 512,
            transcendentals=heads * rows * rows,
        ),
        compiler_params=pltpu.CompilerParams(vmem_limit_bytes=32 << 20),
        name="attend",
    )(length, query, query_rope, kv, kv, key_rope)


def attend_back(length, query, query_rope, kv, key_rope, out_grad, log_totals, heads, scale):
    rows = query.shape[0]
    block = min(256, rows)
    steps = rows // block
    turned_cols = query_rope.shape[1]

    def kernel(
        len_ref, q_ref, r_ref, k_ref, v_ref, kr_ref, do_ref, total_ref,
        dq_ref, dr_ref, dkv_ref, dkr_ref, dk_acc, dv_acc,
    ):
        head, step = pl.program_id(0), pl.program_id(1)

        @pl.when(step == 0)
        def _():
            dk_acc[...] = jnp.zeros_like(dk_acc)
            dv_acc[...] = jnp.zeros_like(dv_acc)

        @pl.when((step == 0) & (head == 0))
        def _():
            dr_ref[...] = jnp.zeros_like(dr_ref)
            dkr_ref[...] = jnp.zeros_like(dkr_ref)

        for n in range(steps):

            @pl.when(step == n)
            def _(n=n):
                keys = (n + 1) * block
                scores, turned = score_block(
                    q_ref, r_ref, k_ref, kr_ref, head, n, keys, block, len_ref[0], scale
                )
                probs = jnp.exp(scores - total_ref[0][:, :1])
                prob_grad = lax.dot_general(
                    do_ref[...], v_ref[:keys], (((1,), (1,)), ((), ())), preferred_element_type=F32
                )
                centre = jnp.sum(probs * prob_grad, axis=-1, keepdims=True)
                score_grad = (probs * (prob_grad - centre)).astype(BF16)
                probs_low = probs.astype(BF16)
                dq_ref[...] = (dot(score_grad, k_ref[:keys]) * scale).astype(BF16)
                half = turned_cols // 2
                lanes = lax.broadcasted_iota(jnp.int32, (block, turned_cols), 1)
                lanes = lanes % half // (ROPE // 2)
                turned_grad = dot(score_grad, kr_ref[:keys]) * scale
                dr_ref[n * block : keys] += jnp.where(lanes == head, turned_grad, 0.0)
                dk_acc[:keys] += dot_tn(score_grad, q_ref[...]) * scale
                dkr_ref[:keys] += dot_tn(score_grad, turned) * scale
                dv_acc[:keys] += dot_tn(probs_low, do_ref[...])

        @pl.when(step == steps - 1)
        def _():
            dkv_ref[:, :NOPE] = dk_acc[...].astype(BF16)
            dkv_ref[:, NOPE:] = dv_acc[...].astype(BF16)

    return pl.pallas_call(
        kernel,
        out_shape=(
            jax.ShapeDtypeStruct((rows, heads * NOPE), BF16),
            jax.ShapeDtypeStruct((rows, turned_cols), F32),
            jax.ShapeDtypeStruct((rows, heads * (NOPE + VDIM)), BF16),
            jax.ShapeDtypeStruct((rows, turned_cols), F32),
        ),
        grid_spec=pltpu.PrefetchScalarGridSpec(
            num_scalar_prefetch=1,
            grid=(heads, steps),
            in_specs=[
                pl.BlockSpec((block, NOPE), lambda h, i, n: (i, h)),
                pl.BlockSpec((block, turned_cols), lambda h, i, n: (i, 0)),
                pl.BlockSpec((rows, NOPE), lambda h, i, n: (0, 2 * h)),
                pl.BlockSpec((rows, VDIM), lambda h, i, n: (0, 2 * h + 1)),
                pl.BlockSpec((rows, turned_cols), lambda h, i, n: (0, 0)),
                pl.BlockSpec((block, VDIM), lambda h, i, n: (i, h)),
                pl.BlockSpec((1, block, 128), lambda h, i, n: (h, i, 0)),
            ],
            out_specs=(
                pl.BlockSpec((block, NOPE), lambda h, i, n: (i, h)),
                pl.BlockSpec((rows, turned_cols), lambda h, i, n: (0, 0)),
                pl.BlockSpec((rows, NOPE + VDIM), lambda h, i, n: (0, h)),
                pl.BlockSpec((rows, turned_cols), lambda h, i, n: (0, 0)),
            ),
            scratch_shapes=[pltpu.VMEM((rows, NOPE), F32), pltpu.VMEM((rows, VDIM), F32)],
        ),
        cost_estimate=pl.CostEstimate(
            flops=heads * rows * rows * 1600,
            bytes_accessed=16 * rows * heads * 512,
            transcendentals=heads * rows * rows,
        ),
        compiler_params=pltpu.CompilerParams(vmem_limit_bytes=40 << 20),
        name="attend_back",
    )(length, query, query_rope, kv, kv, key_rope, out_grad, log_totals)


def in_order(values, me, count):
    zero = jnp.zeros_like(values[0])
    ordered = []
    for j in range(count):
        total = zero
        for k in range(count):
            total = jnp.where((me ^ k) == j, values[k], total)
        ordered.append(total)
    return jnp.stack(ordered)


def body(
    lay,
    hidden,
    lengths,
    routes,
    attn_gain,
    w_query,
    w_kv_down,
    kv_gain,
    w_kv_up,
    w_out,
    ffn_gain,
    w_router,
    w_expert_in,
    w_expert_out,
    w_shared_in,
    w_shared_out,
    cotangent,
):
    rows, width = hidden.shape
    nz, nt, nq, ndp = lay.z, lay.t, lay.q, lay.dp
    me_dp = lax.axis_index("dp")
    me_t = lax.axis_index("tensor")
    me_z = me_dp // nq
    me_c = me_dp % nq
    part = width // nt
    d_loc = w_query.shape[0]
    f_loc = w_expert_out.shape[1]
    ffe = f_loc * nt
    heads = w_query.shape[1] // (NOPE + ROPE)
    score_scale = (NOPE + ROPE) ** (-0.5)

    def own_part(values):
        return lax.dynamic_slice_in_dim(values, me_t * part, part, 1)

    def gather_z(values):
        return lax.all_gather(values, "dp", axis=0, tiled=False, axis_index_groups=lay.z_groups)

    def scatter_z(values):
        return lax.psum_scatter(
            values, "dp", scatter_dimension=0, tiled=False, axis_index_groups=lay.z_groups
        )

    def gather_t(values):
        return lax.all_gather(values, "tensor", axis=1, tiled=True)

    def scatter_t(values):
        return lax.psum_scatter(
            values.astype(BF16), "tensor", scatter_dimension=1, tiled=True
        ).astype(F32)

    def swap_t(values):
        return lax.all_to_all(values, "tensor", split_axis=0, concat_axis=0, tiled=True)

    def swap_z(values):
        return lax.all_to_all(
            values,
            "dp",
            split_axis=0,
            concat_axis=0,
            axis_index_groups=lay.z_groups,
            tiled=True,
        )

    def gather_t_direct(values):
        return join_columns([lay.over_t(values, k) for k in range(nt)], me_t, nt)

    def part_for(values, k):
        return lax.dynamic_slice_in_dim(values, (me_t ^ k) * part, part, 1)

    def scatter_t_direct(values):
        total = part_for(values, 0)
        for k in range(1, nt):
            total = total + lay.over_t(part_for(values, k).astype(BF16), k).astype(F32)
        return total

    ids = jnp.stack([me_z, me_c, me_t]).astype(jnp.int32)

    packed = jnp.concatenate(
        [jnp.swapaxes(w_expert_in, 2, 3), w_expert_out[:, None]], 1
    ).reshape(nz, nt, 3, f_loc, d_loc)
    by_column = swap_t(jnp.swapaxes(packed, 0, 1))

    lat_loc = kv_gain.shape[0]
    q_rows, down_rows, out_rows = w_query.shape[1], w_kv_down.shape[1], w_out.shape[0]
    half = ROPE // 2

    def by_kind(turned):
        split = turned.reshape(heads, NOPE + ROPE, -1)
        return jnp.concatenate(
            [
                split[:, :NOPE].reshape(heads * NOPE, -1),
                split[:, NOPE : NOPE + half].reshape(heads * half, -1),
                split[:, NOPE + half :].reshape(heads * half, -1),
            ],
            0,
        )

    def by_head(rows_in):
        nope = rows_in[: heads * NOPE].reshape(heads, NOPE, -1)
        first = rows_in[heads * NOPE : heads * (NOPE + half)].reshape(heads, half, -1)
        second = rows_in[heads * (NOPE + half) :].reshape(heads, half, -1)
        return jnp.concatenate([nope, first, second], 1).reshape(heads * (NOPE + ROPE), -1)

    gains = jnp.stack([attn_gain, ffn_gain, jnp.pad(kv_gain, (0, d_loc - lat_loc))])
    front_pack = jnp.concatenate(
        [
            by_kind(jnp.transpose(w_query)),
            jnp.transpose(w_kv_down),
            jnp.transpose(w_router),
            jnp.pad(gains, ((0, 13), (0, 0))),
            w_out,
            w_kv_up.reshape(-1, d_loc),
        ],
        0,
    )
    front = lax.all_gather(front_pack, "dp", axis=0, tiled=False)

    valid_length = lengths[0]
    valid_rows = lax.broadcasted_iota(jnp.int32, (rows, 1), 0) < valid_length
    cot_low = jnp.where(valid_rows, cotangent, jnp.zeros_like(cotangent))
    cot_part = own_part(cot_low)
    route_own = jnp.pad(jnp.transpose(routes), ((0, -TOP % 8), (0, 0)), constant_values=-1)
    route_all = in_order([lay.over_z(route_own, k) for k in range(nz)], me_z, nz)
    inputs = hidden.astype(F32)
    attn_inverse = inverse_rms(inputs)
    cosine, sine = angle_tables(rows)
    wide_cos, wide_sin = jnp.tile(cosine, (1, heads)), jnp.tile(sine, (1, heads))
    front, attn_inverse, wide_cos, wide_sin, route_all = lax.optimization_barrier(
        (front, attn_inverse, wide_cos, wide_sin, route_all)
    )

    plane_ids = me_z * nt + jnp.arange(nt, dtype=jnp.int32)
    member = jnp.any(route_all[:, :, :, None] == plane_ids[None, None, None, :], axis=1)
    row_ids = lax.broadcasted_iota(jnp.int32, (rows, rows), 0)
    col_ids = lax.broadcasted_iota(jnp.int32, (rows, rows), 1)
    before = (col_ids < row_ids).astype(BF16)
    position = jnp.einsum("ij,sje->sei", before, member.astype(BF16), preferred_element_type=F32)
    key = jnp.where(jnp.swapaxes(member, 1, 2), position.astype(jnp.int32), -1)
    slots_iota = lax.broadcasted_iota(jnp.int32, (1, 1, CAP, 1), 2)

    def place_of(keys):
        return (keys[:, :, None, :] == slots_iota).astype(BF16)

    place = place_of(key)
    own_key = lax.dynamic_index_in_dim(key, me_t, 1, keepdims=False)
    own_place = own_key[:, None, :] == slots_iota[0]

    def pick_rows(values):
        picked = jnp.einsum("sepk,skd->espd", place, values, preferred_element_type=F32)
        return picked.astype(BF16).reshape(nt, nz * CAP, part)

    def send_out(picked):
        return jnp.swapaxes(swap_t(picked), 0, 1).reshape(nz * CAP, width)

    def send_back(values):
        return swap_t(jnp.swapaxes(values.reshape(nz * CAP, nt, part), 0, 1))

    def combine(parts):
        parts = parts.reshape(nt, nz, CAP, part)
        summed = jnp.einsum("sepk,espd->skd", place, parts, preferred_element_type=F32)
        return summed.astype(BF16)


    def rows_of(first, count):
        return jnp.swapaxes(front[:, first : first + count], 0, 1).reshape(count, width)

    query_t = rows_of(0, q_rows)
    down_t = rows_of(q_rows, down_rows)
    at = q_rows + down_rows
    router_t = rows_of(at, EXPERTS)
    gain_attn = front[:, at + EXPERTS].reshape(-1)
    gain_ffn = front[:, at + EXPERTS + 1].reshape(-1)
    gain_kv = front[:, at + EXPERTS + 2, :lat_loc].reshape(-1)
    at = at + 2 * EXPERTS
    out_w = rows_of(at, out_rows)
    up_w = front[:, at + out_rows :].reshape(LATENT, heads * (NOPE + VDIM))

    attn_scale = gain_attn.astype(F32)
    normed_low = (inputs * attn_inverse * attn_scale).astype(BF16)
    query = dot_nt(normed_low, query_t)
    nope_cols = heads * NOPE
    query_nope = query[:, :nope_cols].astype(BF16)
    query_rope = jnp.concatenate(
        rotate(
            query[:, nope_cols : nope_cols + heads * half],
            query[:, nope_cols + heads * half :],
            wide_cos,
            wide_sin,
        ),
        1,
    ).astype(BF16)
    latent_all = dot_nt(normed_low, down_t)
    latent_all, by_column = lax.optimization_barrier((latent_all, by_column))
    by_column = jnp.transpose(by_column, (2, 1, 0, 3, 4))
    by_plane = [swap_z(by_column[g]) for g in range(2)]
    latent = latent_all[:, :LATENT]
    kv_inverse = inverse_rms(latent)
    latent_hat = latent * kv_inverse
    kv_scale = gain_kv.astype(F32)
    latent_low = (latent_hat * kv_scale).astype(BF16)
    key_turned = jnp.concatenate(
        rotate(
            latent_all[:, LATENT : LATENT + half],
            latent_all[:, LATENT + half :],
            wide_cos[:, :half],
            wide_sin[:, :half],
        ),
        1,
    ).astype(BF16)
    copies = (2 * half, 2 * heads * half)
    to_col = lax.broadcasted_iota(jnp.int32, copies, 1)
    from_col = to_col // (heads * half) * half + to_col % half
    repeat = (lax.broadcasted_iota(jnp.int32, copies, 0) == from_col).astype(BF16)
    key_rope = dot(key_turned, repeat).astype(BF16)
    keys_values = dot(latent_low, up_w).astype(BF16)
    attended_low, log_totals = attend(
        lengths, query_nope, query_rope, keys_values, key_rope, heads, score_scale
    )
    attn_part, by_plane[0] = lax.optimization_barrier((dot(attended_low, out_w), by_plane[0]))
    attn_sum = scatter_t(attn_part)
    residual = own_part(hidden).astype(F32) + attn_sum

    def row_mean(values):
        partial = jnp.sum(values, axis=-1).reshape(-1, 128)
        return lax.psum(partial, "tensor").reshape(-1, 1) * (1.0 / width)

    ffn_inverse = lax.rsqrt(row_mean(residual * residual) + EPSILON)
    ffn_hat = residual * ffn_inverse
    ffn_scale = lax.dynamic_slice_in_dim(gain_ffn, me_t * part, part, 0).astype(F32)
    ffn_part = (ffn_hat * ffn_scale).astype(BF16)

    ffn_part, by_plane[1] = lax.optimization_barrier((ffn_part, by_plane[1]))
    ffn_all = gather_z(ffn_part)
    ffn_low = gather_t_direct(ffn_part)
    ffn_all, ffn_low, cot_ready = lax.optimization_barrier((ffn_all, ffn_low, cot_part))
    picked = pick_rows(ffn_all)
    expert_rows = send_out(picked)
    shared_pack = jnp.concatenate(
        [jnp.swapaxes(w_shared_in, 1, 2).reshape(-1, d_loc), w_shared_out], 0
    )
    cot_all, last_column = lax.optimization_barrier((gather_z(cot_ready), by_column[2]))
    by_plane.append(
        jnp.stack(
            [
                lay.over_z(lax.dynamic_index_in_dim(last_column, me_z ^ k, 0, keepdims=False), k)
                for k in range(nz)
            ]
        )
    )
    cot_picked, shared_pack = lax.optimization_barrier((pick_rows(cot_all), shared_pack))
    cot_rows = send_out(cot_picked)
    shared_all = lax.all_gather(shared_pack, "dp", axis=0, tiled=False)

    def own_weights(matrices, order):
        pieces = [by_plane[g].reshape(nz * nt, f_loc, d_loc) for g in matrices]
        stacks = [lay.over_c(piece, k) for k in range(nq) for piece in pieces]
        return lay_out_weights(lay, order, stacks, f_loc, d_loc, width)

    own_in = own_weights((0, 1), ids * jnp.array([0, 1, 1], jnp.int32))
    own_out = own_weights((2,), ids)
    router_probs = jax.nn.softmax(dot_nt(ffn_low, router_t), axis=-1)
    probs_turned = jnp.transpose(router_probs).reshape(EXPERTS, -1, 128)
    own_probs = in_order(
        [
            lay.over_z(
                lax.dynamic_index_in_dim(
                    probs_turned, (me_z ^ k) * nt + me_t, 0, keepdims=False
                ),
                k,
            )
            for k in range(nz)
        ],
        me_z,
        nz,
    ).reshape(nz, rows)
    gate_rows = jnp.sum(jnp.where(own_place, own_probs[:, None, :], 0.0), axis=-1).reshape(
        nz * CAP, 1
    )
    gate_up = dot_nt(expert_rows, own_in)
    gate_pre, up_pre = gate_up[:, :ffe], gate_up[:, ffe:]
    gate_sig = jax.nn.sigmoid(gate_pre)
    gate_silu = gate_pre * gate_sig
    active = (gate_silu * up_pre).astype(BF16)
    rows_out = (dot(active, own_out) * gate_rows).astype(BF16)
    rows_out, cot_rows, shared_all = lax.optimization_barrier((rows_out, cot_rows, shared_all))
    out_parts = send_back(rows_out)
    active_grad_raw = dot_nt(cot_rows, own_out)
    gate_grad = jnp.sum(active.astype(F32) * active_grad_raw, axis=-1).reshape(nz, CAP)
    active_grad = active_grad_raw * gate_rows
    pre_low = jnp.concatenate(
        [
            active_grad * up_pre * gate_sig * (1.0 + gate_pre * (1.0 - gate_sig)),
            active_grad * gate_silu,
        ],
        1,
    ).astype(BF16)
    gated_active = (active.astype(F32) * gate_rows).astype(BF16)
    rows_grad = dot(pre_low, own_in).astype(BF16)
    rows_grad, out_parts = lax.optimization_barrier((rows_grad, out_parts))
    grad_parts = send_back(rows_grad)
    routed, pre_low, gated_active = lax.optimization_barrier(
        (combine(out_parts), pre_low, gated_active)
    )
    routed = scatter_z(routed).astype(F32)
    token_grad = jnp.sum(jnp.where(own_place, gate_grad[:, :, None], 0.0), axis=1)
    token_grad = token_grad.reshape(nz, -1, 128)
    token_plane = jnp.stack(
        [
            lay.over_z(lax.dynamic_index_in_dim(token_grad, me_z ^ k, 0, keepdims=False), k)
            for k in range(nz)
        ]
    )
    token_home = jnp.stack([lay.over_t(token_plane, k) for k in range(nt)])
    experts = jnp.arange(EXPERTS, dtype=jnp.int32)
    came_from = (me_t ^ (experts % nt)) * nz + (me_z ^ (experts // nt))
    probs_grad = lax.dot_general(
        token_home.reshape(EXPERTS, rows),
        (experts[:, None] == came_from[None, :]).astype(F32),
        (((0,), (0,)), ((), ())),
        precision=lax.Precision.HIGHEST,
        preferred_element_type=F32,
    )

    grad_in_own = dot_tn(pre_low, expert_rows).astype(BF16)
    grad_out_own = dot_tn(gated_active, cot_rows).astype(BF16)
    ffs = w_shared_out.shape[0]
    shared_in = jnp.swapaxes(shared_all[:, : 2 * ffs], 0, 1).reshape(2 * ffs, width)
    shared_out = jnp.swapaxes(shared_all[:, 2 * ffs :], 0, 1).reshape(ffs, width)
    shared_pre = dot_nt(ffn_low, shared_in)
    shared_gate, shared_up = shared_pre[:, :ffs], shared_pre[:, ffs:]
    shared_sig = jax.nn.sigmoid(shared_gate)
    shared_silu = shared_gate * shared_sig
    shared_act = (shared_silu * shared_up).astype(BF16)
    shared_full = dot(shared_act, shared_out)
    shared_act_grad = dot_nt(cot_low, shared_out)
    shared_pre_grad = jnp.concatenate(
        [
            shared_act_grad * shared_up * shared_sig * (1.0 + shared_gate * (1.0 - shared_sig)),
            shared_act_grad * shared_silu,
        ],
        1,
    ).astype(BF16)
    grad_shared_in = dot_tn(shared_pre_grad, ffn_low)
    grad_shared_out = dot_tn(shared_act, cot_low)
    shared_grad_full = dot(shared_pre_grad, shared_in)

    (
        grad_parts,
        grad_in_own,
        grad_out_own,
        routed,
        probs_grad,
        shared_full,
        shared_grad_full,
    ) = lax.optimization_barrier(
        (
            grad_parts,
            grad_in_own,
            grad_out_own,
            routed,
            probs_grad,
            shared_full,
            shared_grad_full,
        )
    )
    shared_grad = swap_t(
        jnp.swapaxes(shared_grad_full.astype(BF16).reshape(rows, nt, part), 0, 1)
    )
    shared_grad = jnp.sum(shared_grad.astype(F32), axis=0)
    grad_pieces = take_apart(lay, ids, grad_in_own, grad_out_own, f_loc, d_loc, width)
    routed_grad = scatter_z(combine(grad_parts)).astype(F32)
    grad_class = [
        sum(lay.over_c(grad_pieces[3 * k + g], k).astype(F32) for k in range(nq)).astype(BF16)
        for g in range(3)
    ]
    routed_grad, grad_class = lax.optimization_barrier((routed_grad, grad_class))
    grad_plane = [swap_z(grad_class[g].reshape(nz, nt, f_loc, d_loc)) for g in range(3)]

    logits_grad = router_probs * (
        probs_grad - jnp.sum(router_probs * probs_grad, axis=-1, keepdims=True)
    )
    router_part = lax.dot_general(
        logits_grad,
        ffn_low.astype(F32),
        (((0,), (0,)), ((), ())),
        precision=lax.Precision.HIGHEST,
        preferred_element_type=F32,
    )
    router_slice = lax.dynamic_slice_in_dim(router_t, me_t * part, part, 1)
    ffn_grad = (
        shared_grad
        + routed_grad
        + lax.dot_general(
            logits_grad,
            router_slice.astype(F32),
            (((1,), (0,)), ((), ())),
            precision=lax.Precision.HIGHEST,
            preferred_element_type=F32,
        )
    )
    scaled = ffn_scale * ffn_grad
    ffn_gain_part = jnp.sum(ffn_grad * ffn_hat, axis=0)
    residual_grad = cot_part.astype(F32) + ffn_inverse * (
        scaled - ffn_hat * row_mean(ffn_hat * scaled)
    )
    residual_low = gather_t(residual_grad.astype(BF16))

    def sum_dp(values):
        return lax.psum_scatter(values, "dp", scatter_dimension=0, tiled=False).astype(F32)

    def by_owner(values):
        return jnp.swapaxes(values.astype(BF16).reshape(-1, ndp, d_loc), 0, 1)

    shared_grads = jnp.concatenate([by_owner(grad_shared_in), by_owner(grad_shared_out)], 1)
    residual_low, shared_grads, grad_plane[0] = lax.optimization_barrier(
        (residual_low, shared_grads, grad_plane[0])
    )
    shared_sum = sum_dp(shared_grads)
    grad_out_w = dot_tn(attended_low, residual_low)
    attended_grad = dot_nt(residual_low, out_w).astype(BF16)
    query_nope_grad, query_turned_grad, kv_grad, rope_grad = attend_back(
        lengths,
        query_nope,
        query_rope,
        keys_values,
        key_rope,
        attended_grad,
        log_totals,
        heads,
        score_scale,
    )
    query_turned_grad, grad_plane[1], shared_full = lax.optimization_barrier(
        (query_turned_grad, grad_plane[1], shared_full)
    )
    turned_first, turned_second = rotate_back(
        query_turned_grad[:, : heads * half], query_turned_grad[:, heads * half :], wide_cos, wide_sin
    )
    query_grad = jnp.concatenate(
        [query_nope_grad, turned_first.astype(BF16), turned_second.astype(BF16)], 1
    )
    rope_sum = rope_grad.reshape(rows, 2, heads, half).sum(2)
    key_rope_part = jnp.concatenate(
        rotate_back(
            rope_sum[:, 0], rope_sum[:, 1], wide_cos[:, :half], wide_sin[:, :half]
        ),
        1,
    )
    latent_part = dot_nt(kv_grad, up_w)
    grad_kv_gain = jnp.sum(latent_part * latent_hat, axis=0)
    scaled_kv = kv_scale * latent_part
    latent_back = kv_inverse * (
        scaled_kv - latent_hat * jnp.mean(latent_hat * scaled_kv, axis=-1, keepdims=True)
    )
    down_grad = jnp.concatenate([latent_back, key_rope_part], -1).astype(BF16)
    normed_full, shared_part = lax.optimization_barrier(
        (dot(query_grad, query_t) + dot(down_grad, down_t), scatter_t_direct(shared_full))
    )
    output = gather_t_direct((residual + routed + shared_part).astype(BF16))
    normed_grad, shared_sum, grad_plane[2] = lax.optimization_barrier(
        (scatter_t_direct(normed_full), shared_sum, grad_plane[2])
    )
    attn_hat = own_part(hidden).astype(F32) * attn_inverse
    scaled_in = lax.dynamic_slice_in_dim(attn_scale, me_t * part, part, 0) * normed_grad
    attn_gain_part = jnp.sum(normed_grad * attn_hat, axis=0)
    input_grad = residual_grad + attn_inverse * (
        scaled_in - attn_hat * row_mean(attn_hat * scaled_in)
    )
    input_low, grad_plane = lax.optimization_barrier((input_grad.astype(BF16), grad_plane))
    grad_home = swap_t(jnp.transpose(jnp.stack(grad_plane), (2, 0, 1, 3, 4)))
    grad_expert_in, grad_expert_out = home_gradients(lay, grad_home, f_loc, d_loc)
    grad_hidden = gather_t_direct(input_low)

    def spread(values):
        return lax.dynamic_update_slice(
            jnp.zeros((1, width), F32), values[None], (jnp.int32(0), me_t * part)
        )

    kv_gain_row = jnp.pad(
        grad_kv_gain.reshape(ndp, lat_loc), ((0, 0), (0, d_loc - lat_loc))
    ).reshape(1, width)
    gain_grads = jnp.concatenate([spread(attn_gain_part), spread(ffn_gain_part), kv_gain_row], 0)
    front_sum = sum_dp(
        jnp.concatenate(
            [
                by_owner(dot_tn(down_grad, normed_low)),
                by_owner(jnp.pad(gain_grads, ((0, 13), (0, 0)))),
                by_owner(router_part),
                by_owner(dot_tn(query_grad, normed_low)),
                by_owner(grad_out_w),
                dot_tn(latent_low, kv_grad).astype(BF16).reshape(ndp, -1, d_loc),
            ],
            1,
        )
    )
    own_sum = front_sum[: down_rows + EXPERTS]
    own_low = own_sum.astype(BF16)
    for k in range(1, nt):
        own_sum = own_sum + lay.over_t(own_low, k).astype(F32)
    at = down_rows + 2 * EXPERTS
    return (
        output,
        grad_hidden,
        own_sum[down_rows],
        jnp.transpose(by_head(front_sum[at : at + q_rows])),
        jnp.transpose(own_sum[:down_rows]),
        own_sum[down_rows + 2, :lat_loc],
        front_sum[at + q_rows + out_rows :].reshape(w_kv_up.shape),
        front_sum[at + q_rows : at + q_rows + out_rows],
        own_sum[down_rows + 1],
        jnp.transpose(front_sum[down_rows + EXPERTS : at]),
        grad_expert_in,
        grad_expert_out,
        jnp.swapaxes(shared_sum[: 2 * ffs].reshape(2, ffs, d_loc), 1, 2),
        shared_sum[2 * ffs :],
    )


def solution(mesh):
    return jax.shard_map(
        functools.partial(body, Layout(mesh.shape["dp"], mesh.shape["tensor"])),
        mesh=mesh,
        in_specs=(
            P("dp", None),
            P("dp"),
            P("dp", None),
            P("dp"),
            P("dp", "tensor"),
            P("dp", None),
            P("dp"),
            P("dp", "tensor"),
            P("tensor", "dp"),
            P("dp"),
            P("dp", None),
            P(None, None, "dp", "tensor"),
            P(None, "tensor", "dp"),
            P(None, "dp", "tensor"),
            P("tensor", "dp"),
            P("dp", None),
        ),
        out_specs=(
            P("dp", None),
            P("dp", None),
            P("dp"),
            P("dp", "tensor"),
            P("dp", None),
            P("dp"),
            P("dp", "tensor"),
            P("tensor", "dp"),
            P("dp"),
            P("dp", None),
            P(None, None, "dp", "tensor"),
            P(None, "tensor", "dp"),
            P(None, "dp", "tensor"),
            P("tensor", "dp"),
        ),
        check_vma=False,
    )
```

```python
import functools
import math

import jax
import jax.numpy as jnp
from jax import lax
from jax.experimental import pallas as pl
from jax.experimental.pallas import tpu as pltpu
from jax.sharding import PartitionSpec as P

NOPE = 128
ROPE = 64
VDIM = 128
LATENT = 512
TOP = 6
EXPERTS = 16
CAP = 512

EPSILON = 1e-06
NEGATIVE = -1e30
F32 = jnp.float32
BF16 = jnp.bfloat16


def dot(a, b):
    return jnp.dot(a, b, preferred_element_type=F32)


def dot_nt(a, b):
    return lax.dot_general(a, b, (((1,), (1,)), ((), ())), preferred_element_type=F32)


def dot_tn(a, b):
    return lax.dot_general(a, b, (((0,), (0,)), ((), ())), preferred_element_type=F32)


def rotate(first, second, cosine, sine):
    return first * cosine - second * sine, second * cosine + first * sine


def rotate_back(first, second, cosine, sine):
    return first * cosine + second * sine, second * cosine - first * sine


def angle_tables(rows_count):
    positions = jnp.arange(rows_count, dtype=F32)
    freqs = jnp.exp(jnp.arange(ROPE // 2, dtype=F32) * (-2.0 * math.log(10000.0) / ROPE))
    angles = positions[:, None] * freqs[None, :]
    return (jnp.cos(angles), jnp.sin(angles))


def inverse_rms(values):
    return lax.rsqrt(jnp.mean(values * values, axis=-1, keepdims=True) + EPSILON)


class Layout:
    def __init__(self, n_dp, n_tensor):
        self.dp, self.t = n_dp, n_tensor
        self.q = n_dp * n_tensor // EXPERTS
        self.z = n_dp // self.q
        if self.z * self.t != EXPERTS or self.z * self.q != n_dp:
            raise ValueError("mesh")
        self.z_groups = [[c + self.q * z for z in range(self.z)] for c in range(self.q)]

    def over_t(self, values, k):
        if k == 0:
            return values
        return lax.ppermute(values, "tensor", [(i, i ^ k) for i in range(self.t)])

    def over_z(self, values, k):
        if k == 0:
            return values
        return lax.ppermute(values, "dp", [(d, d ^ (k * self.q)) for d in range(self.dp)])

    def over_c(self, values, k):
        if k == 0:
            return values
        return lax.ppermute(values, "dp", [(d, d ^ k) for d in range(self.dp)])


def lay_out_weights(lay, ids, stacks, f_loc, d_loc, width):
    ffe = f_loc * lay.t
    count = len(stacks) // lay.q

    def kernel(ids_ref, *refs):
        for kc in range(lay.q):
            columns = pl.ds(pl.multiple_of((ids_ref[1] ^ kc) * d_loc, 128), d_loc)
            for g in range(count):
                refs[-1][g, :, columns] = refs[count * kc + g][0]

    own = pl.pallas_call(
        kernel,
        out_shape=jax.ShapeDtypeStruct((count, ffe, width), BF16),
        grid_spec=pltpu.PrefetchScalarGridSpec(
            num_scalar_prefetch=1,
            grid=(lay.t, lay.z),
            in_specs=[
                pl.BlockSpec(
                    (1, f_loc, d_loc), lambda kt, kz, ids: ((kz ^ ids[0]) * lay.t + kt, 0, 0)
                )
            ]
            * len(stacks),
            out_specs=pl.BlockSpec(
                (count, f_loc, lay.q * d_loc), lambda kt, kz, ids: (0, kt, kz)
            ),
        ),
        cost_estimate=pl.CostEstimate(
            flops=0, bytes_accessed=4 * count * ffe * width, transcendentals=0
        ),
        compiler_params=pltpu.CompilerParams(vmem_limit_bytes=32 << 20),
        name="lay_out_weights",
    )(ids, *stacks)
    return own.reshape(count * ffe, width)


def take_apart(lay, ids, grad_in, grad_out, f_loc, d_loc, width):
    ffe = f_loc * lay.t

    def kernel(ids_ref, in_ref, out_ref, *targets):
        for kc in range(lay.q):
            columns = pl.ds(pl.multiple_of((ids_ref[1] ^ kc) * d_loc, 128), d_loc)
            for g in range(2):
                targets[3 * kc + g][0] = in_ref[g, :, columns]
            targets[3 * kc + 2][0] = out_ref[:, columns]

    shape = jax.ShapeDtypeStruct((lay.t * lay.z, f_loc, d_loc), BF16)
    spec = pl.BlockSpec((1, f_loc, d_loc), lambda kt, kz, ids: (kz * lay.t + kt, 0, 0))
    return pl.pallas_call(
        kernel,
        out_shape=(shape,) * (3 * lay.q),
        grid_spec=pltpu.PrefetchScalarGridSpec(
            num_scalar_prefetch=1,
            grid=(lay.t, lay.z),
            in_specs=[
                pl.BlockSpec((2, f_loc, lay.q * d_loc), lambda kt, kz, ids: (0, kt, kz)),
                pl.BlockSpec((f_loc, lay.q * d_loc), lambda kt, kz, ids: (kt, kz)),
            ],
            out_specs=(spec,) * (3 * lay.q),
        ),
        cost_estimate=pl.CostEstimate(
            flops=0, bytes_accessed=12 * ffe * width, transcendentals=0
        ),
        compiler_params=pltpu.CompilerParams(vmem_limit_bytes=32 << 20),
        name="take_apart",
    )(ids, grad_in.reshape(2, ffe, width), grad_out)


def home_gradients(lay, pieces, f_loc, d_loc):
    def kernel(piece_ref, in_ref, out_ref):
        in_ref[0] = piece_ref[0, :2, 0].astype(F32)
        out_ref[0] = piece_ref[0, 2, 0].astype(F32)

    spec = pl.BlockSpec((1, 3, 1, f_loc, d_loc), lambda e: (e % lay.t, 0, e // lay.t, 0, 0))
    grad_in, grad_out = pl.pallas_call(
        kernel,
        out_shape=(
            jax.ShapeDtypeStruct((EXPERTS, 2, f_loc, d_loc), F32),
            jax.ShapeDtypeStruct((EXPERTS, f_loc, d_loc), F32),
        ),
        grid=(EXPERTS,),
        in_specs=[spec],
        out_specs=(
            pl.BlockSpec((1, 2, f_loc, d_loc), lambda e: (e, 0, 0, 0)),
            pl.BlockSpec((1, f_loc, d_loc), lambda e: (e, 0, 0)),
        ),
        cost_estimate=pl.CostEstimate(
            flops=0, bytes_accessed=18 * EXPERTS * f_loc * d_loc, transcendentals=0
        ),
        name="home_gradients",
    )(pieces)
    return jnp.swapaxes(grad_in, 2, 3), grad_out


def join_columns(parts, me, count):
    rows, part = parts[0].shape
    block = min(512, rows)

    def kernel(me_ref, *refs):
        for k in range(count):

            @pl.when(pl.program_id(1) == k)
            def _(k=k):
                refs[count][...] = refs[k][...]

    return pl.pallas_call(
        kernel,
        out_shape=jax.ShapeDtypeStruct((rows, count * part), parts[0].dtype),
        grid_spec=pltpu.PrefetchScalarGridSpec(
            num_scalar_prefetch=1,
            grid=(rows // block, count),
            in_specs=[pl.BlockSpec((block, part), lambda i, k, me: (i, 0))] * count,
            out_specs=pl.BlockSpec((block, part), lambda i, k, me: (i, me[0] ^ k)),
        ),
        cost_estimate=pl.CostEstimate(
            flops=0, bytes_accessed=4 * rows * part * count, transcendentals=0
        ),
        name="join_columns",
    )(me.reshape(1).astype(jnp.int32), *parts)


def score_block(q_ref, r_ref, k_ref, kr_ref, head, step, keys, block, length, scale):
    half = r_ref.shape[1] // 2
    lanes = lax.broadcasted_iota(jnp.int32, r_ref.shape, 1) % half // (ROPE // 2)
    turned = jnp.where(lanes == head, r_ref[...], jnp.zeros_like(r_ref))
    raw = lax.dot_general(
        q_ref[...], k_ref[:keys], (((1,), (1,)), ((), ())), preferred_element_type=F32
    ) + lax.dot_general(
        turned, kr_ref[:keys], (((1,), (1,)), ((), ())), preferred_element_type=F32
    )
    rows = lax.broadcasted_iota(jnp.int32, raw.shape, 0) + step * block
    cols = lax.broadcasted_iota(jnp.int32, raw.shape, 1)
    allowed = (cols <= rows) & (cols < length)
    return jnp.where(allowed, raw * scale, NEGATIVE), turned


def attend(length, query, query_rope, kv, key_rope, heads, scale):
    rows = query.shape[0]
    block = min(256, rows)
    steps = rows // block

    def kernel(len_ref, q_ref, r_ref, k_ref, v_ref, kr_ref, o_ref, total_ref):
        head, step = pl.program_id(0), pl.program_id(1)
        for n in range(steps):

            @pl.when(step == n)
            def _(n=n):
                keys = (n + 1) * block
                scores, _ = score_block(
                    q_ref, r_ref, k_ref, kr_ref, head, n, keys, block, len_ref[0], scale
                )
                highest = jnp.max(scores, axis=-1, keepdims=True)
                expo = jnp.exp(scores - highest)
                totals = jnp.sum(expo, axis=-1, keepdims=True)
                weights = (expo * (1.0 / totals)).astype(BF16)
                o_ref[...] = dot(weights, v_ref[:keys]).astype(BF16)
                total_ref[0] = jnp.broadcast_to(highest + jnp.log(totals), (block, 128))

    return pl.pallas_call(
        kernel,
        out_shape=(
            jax.ShapeDtypeStruct((rows, heads * VDIM), BF16),
            jax.ShapeDtypeStruct((heads, rows, 128), F32),
        ),
        grid_spec=pltpu.PrefetchScalarGridSpec(
            num_scalar_prefetch=1,
            grid=(heads, steps),
            in_specs=[
                pl.BlockSpec((block, NOPE), lambda h, i, n: (i, h)),
                pl.BlockSpec((block, query_rope.shape[1]), lambda h, i, n: (i, 0)),
                pl.BlockSpec((rows, NOPE), lambda h, i, n: (0, 2 * h)),
                pl.BlockSpec((rows, VDIM), lambda h, i, n: (0, 2 * h + 1)),
                pl.BlockSpec((rows, key_rope.shape[1]), lambda h, i, n: (0, 0)),
            ],
            out_specs=(
                pl.BlockSpec((block, VDIM), lambda h, i, n: (i, h)),
                pl.BlockSpec((1, block, 128), lambda h, i, n: (h, i, 0)),
            ),
        ),
        cost_estimate=pl.CostEstimate(
            flops=heads * rows * rows * 512,
            bytes_accessed=8 * rows * heads * 512,
            transcendentals=heads * rows * rows,
        ),
        compiler_params=pltpu.CompilerParams(vmem_limit_bytes=32 << 20),
        name="attend",
    )(length, query, query_rope, kv, kv, key_rope)


def attend_back(length, query, query_rope, kv, key_rope, out_grad, log_totals, heads, scale):
    rows = query.shape[0]
    block = min(256, rows)
    steps = rows // block
    turned_cols = query_rope.shape[1]

    def kernel(
        len_ref, q_ref, r_ref, k_ref, v_ref, kr_ref, do_ref, total_ref,
        dq_ref, dr_ref, dkv_ref, dkr_ref, dk_acc, dv_acc,
    ):
        head, step = pl.program_id(0), pl.program_id(1)

        @pl.when(step == 0)
        def _():
            dk_acc[...] = jnp.zeros_like(dk_acc)
            dv_acc[...] = jnp.zeros_like(dv_acc)

        @pl.when((step == 0) & (head == 0))
        def _():
            dr_ref[...] = jnp.zeros_like(dr_ref)
            dkr_ref[...] = jnp.zeros_like(dkr_ref)

        for n in range(steps):

            @pl.when(step == n)
            def _(n=n):
                keys = (n + 1) * block
                scores, turned = score_block(
                    q_ref, r_ref, k_ref, kr_ref, head, n, keys, block, len_ref[0], scale
                )
                probs = jnp.exp(scores - total_ref[0][:, :1])
                prob_grad = lax.dot_general(
                    do_ref[...], v_ref[:keys], (((1,), (1,)), ((), ())), preferred_element_type=F32
                )
                centre = jnp.sum(probs * prob_grad, axis=-1, keepdims=True)
                score_grad = (probs * (prob_grad - centre)).astype(BF16)
                probs_low = probs.astype(BF16)
                dq_ref[...] = (dot(score_grad, k_ref[:keys]) * scale).astype(BF16)
                half = turned_cols // 2
                lanes = lax.broadcasted_iota(jnp.int32, (block, turned_cols), 1)
                lanes = lanes % half // (ROPE // 2)
                turned_grad = dot(score_grad, kr_ref[:keys]) * scale
                dr_ref[n * block : keys] += jnp.where(lanes == head, turned_grad, 0.0)
                dk_acc[:keys] += dot_tn(score_grad, q_ref[...]) * scale
                dkr_ref[:keys] += dot_tn(score_grad, turned) * scale
                dv_acc[:keys] += dot_tn(probs_low, do_ref[...])

        @pl.when(step == steps - 1)
        def _():
            dkv_ref[:, :NOPE] = dk_acc[...].astype(BF16)
            dkv_ref[:, NOPE:] = dv_acc[...].astype(BF16)

    return pl.pallas_call(
        kernel,
        out_shape=(
            jax.ShapeDtypeStruct((rows, heads * NOPE), BF16),
            jax.ShapeDtypeStruct((rows, turned_cols), F32),
            jax.ShapeDtypeStruct((rows, heads * (NOPE + VDIM)), BF16),
            jax.ShapeDtypeStruct((rows, turned_cols), F32),
        ),
        grid_spec=pltpu.PrefetchScalarGridSpec(
            num_scalar_prefetch=1,
            grid=(heads, steps),
            in_specs=[
                pl.BlockSpec((block, NOPE), lambda h, i, n: (i, h)),
                pl.BlockSpec((block, turned_cols), lambda h, i, n: (i, 0)),
                pl.BlockSpec((rows, NOPE), lambda h, i, n: (0, 2 * h)),
                pl.BlockSpec((rows, VDIM), lambda h, i, n: (0, 2 * h + 1)),
                pl.BlockSpec((rows, turned_cols), lambda h, i, n: (0, 0)),
                pl.BlockSpec((block, VDIM), lambda h, i, n: (i, h)),
                pl.BlockSpec((1, block, 128), lambda h, i, n: (h, i, 0)),
            ],
            out_specs=(
                pl.BlockSpec((block, NOPE), lambda h, i, n: (i, h)),
                pl.BlockSpec((rows, turned_cols), lambda h, i, n: (0, 0)),
                pl.BlockSpec((rows, NOPE + VDIM), lambda h, i, n: (0, h)),
                pl.BlockSpec((rows, turned_cols), lambda h, i, n: (0, 0)),
            ),
            scratch_shapes=[pltpu.VMEM((rows, NOPE), F32), pltpu.VMEM((rows, VDIM), F32)],
        ),
        cost_estimate=pl.CostEstimate(
            flops=heads * rows * rows * 1600,
            bytes_accessed=16 * rows * heads * 512,
            transcendentals=heads * rows * rows,
        ),
        compiler_params=pltpu.CompilerParams(vmem_limit_bytes=40 << 20),
        name="attend_back",
    )(length, query, query_rope, kv, kv, key_rope, out_grad, log_totals)


def in_order(values, me, count):
    zero = jnp.zeros_like(values[0])
    ordered = []
    for j in range(count):
        total = zero
        for k in range(count):
            total = jnp.where((me ^ k) == j, values[k], total)
        ordered.append(total)
    return jnp.stack(ordered)


def body(
    lay,
    hidden,
    lengths,
    routes,
    attn_gain,
    w_query,
    w_kv_down,
    kv_gain,
    w_kv_up,
    w_out,
    ffn_gain,
    w_router,
    w_expert_in,
    w_expert_out,
    w_shared_in,
    w_shared_out,
    cotangent,
):
    rows, width = hidden.shape
    nz, nt, nq, ndp = lay.z, lay.t, lay.q, lay.dp
    me_dp = lax.axis_index("dp")
    me_t = lax.axis_index("tensor")
    me_z = me_dp // nq
    me_c = me_dp % nq
    part = width // nt
    d_loc = w_query.shape[0]
    f_loc = w_expert_out.shape[1]
    ffe = f_loc * nt
    heads = w_query.shape[1] // (NOPE + ROPE)
    score_scale = (NOPE + ROPE) ** (-0.5)

    def own_part(values):
        return lax.dynamic_slice_in_dim(values, me_t * part, part, 1)

    def gather_z(values):
        return lax.all_gather(values, "dp", axis=0, tiled=False, axis_index_groups=lay.z_groups)

    def scatter_z(values):
        return lax.psum_scatter(
            values, "dp", scatter_dimension=0, tiled=False, axis_index_groups=lay.z_groups
        )

    def gather_t(values):
        return lax.all_gather(values, "tensor", axis=1, tiled=True)

    def scatter_t(values):
        return lax.psum_scatter(
            values.astype(BF16), "tensor", scatter_dimension=1, tiled=True
        ).astype(F32)

    def swap_t(values):
        return lax.all_to_all(values, "tensor", split_axis=0, concat_axis=0, tiled=True)

    def swap_z(values):
        return lax.all_to_all(
            values,
            "dp",
            split_axis=0,
            concat_axis=0,
            axis_index_groups=lay.z_groups,
            tiled=True,
        )

    def gather_t_direct(values):
        return join_columns([lay.over_t(values, k) for k in range(nt)], me_t, nt)

    def part_for(values, k):
        return lax.dynamic_slice_in_dim(values, (me_t ^ k) * part, part, 1)

    def scatter_t_direct(values):
        total = part_for(values, 0)
        for k in range(1, nt):
            total = total + lay.over_t(part_for(values, k).astype(BF16), k).astype(F32)
        return total

    ids = jnp.stack([me_z, me_c, me_t]).astype(jnp.int32)

    packed = jnp.concatenate(
        [jnp.swapaxes(w_expert_in, 2, 3), w_expert_out[:, None]], 1
    ).reshape(nz, nt, 3, f_loc, d_loc)
    by_column = swap_t(jnp.swapaxes(packed, 0, 1))

    lat_loc = kv_gain.shape[0]
    q_rows, down_rows, out_rows = w_query.shape[1], w_kv_down.shape[1], w_out.shape[0]
    half = ROPE // 2

    def by_kind(turned):
        split = turned.reshape(heads, NOPE + ROPE, -1)
        return jnp.concatenate(
            [
                split[:, :NOPE].reshape(heads * NOPE, -1),
                split[:, NOPE : NOPE + half].reshape(heads * half, -1),
                split[:, NOPE + half :].reshape(heads * half, -1),
            ],
            0,
        )

    def by_head(rows_in):
        nope = rows_in[: heads * NOPE].reshape(heads, NOPE, -1)
        first = rows_in[heads * NOPE : heads * (NOPE + half)].reshape(heads, half, -1)
        second = rows_in[heads * (NOPE + half) :].reshape(heads, half, -1)
        return jnp.concatenate([nope, first, second], 1).reshape(heads * (NOPE + ROPE), -1)

    gains = jnp.stack([attn_gain, ffn_gain, jnp.pad(kv_gain, (0, d_loc - lat_loc))])
    front_pack = jnp.concatenate(
        [
            by_kind(jnp.transpose(w_query)),
            jnp.transpose(w_kv_down),
            jnp.transpose(w_router),
            jnp.pad(gains, ((0, 13), (0, 0))),
            w_out,
            w_kv_up.reshape(-1, d_loc),
        ],
        0,
    )
    front = lax.all_gather(front_pack, "dp", axis=0, tiled=False)

    valid_length = lengths[0]
    valid_rows = lax.broadcasted_iota(jnp.int32, (rows, 1), 0) < valid_length
    cot_low = jnp.where(valid_rows, cotangent, jnp.zeros_like(cotangent))
    cot_part = own_part(cot_low)
    route_own = jnp.pad(jnp.transpose(routes), ((0, -TOP % 8), (0, 0)), constant_values=-1)
    route_all = in_order([lay.over_z(route_own, k) for k in range(nz)], me_z, nz)
    inputs = hidden.astype(F32)
    attn_inverse = inverse_rms(inputs)
    cosine, sine = angle_tables(rows)
    wide_cos, wide_sin = jnp.tile(cosine, (1, heads)), jnp.tile(sine, (1, heads))
    front, attn_inverse, wide_cos, wide_sin, route_all = lax.optimization_barrier(
        (front, attn_inverse, wide_cos, wide_sin, route_all)
    )

    plane_ids = me_z * nt + jnp.arange(nt, dtype=jnp.int32)
    member = jnp.any(route_all[:, :, :, None] == plane_ids[None, None, None, :], axis=1)
    row_ids = lax.broadcasted_iota(jnp.int32, (rows, rows), 0)
    col_ids = lax.broadcasted_iota(jnp.int32, (rows, rows), 1)
    before = (col_ids < row_ids).astype(BF16)
    position = jnp.einsum("ij,sje->sei", before, member.astype(BF16), preferred_element_type=F32)
    key = jnp.where(jnp.swapaxes(member, 1, 2), position.astype(jnp.int32), -1)
    slots_iota = lax.broadcasted_iota(jnp.int32, (1, 1, CAP, 1), 2)

    def place_of(keys):
        return (keys[:, :, None, :] == slots_iota).astype(BF16)

    place = place_of(key)
    own_key = lax.dynamic_index_in_dim(key, me_t, 1, keepdims=False)
    own_place = own_key[:, None, :] == slots_iota[0]

    def pick_rows(values):
        picked = jnp.einsum("sepk,skd->espd", place, values, preferred_element_type=F32)
        return picked.astype(BF16).reshape(nt, nz * CAP, part)

    def send_out(picked):
        return jnp.swapaxes(swap_t(picked), 0, 1).reshape(nz * CAP, width)

    def send_back(values):
        return swap_t(jnp.swapaxes(values.reshape(nz * CAP, nt, part), 0, 1))

    def combine(parts):
        parts = parts.reshape(nt, nz, CAP, part)
        summed = jnp.einsum("sepk,espd->skd", place, parts, preferred_element_type=F32)
        return summed.astype(BF16)


    def rows_of(first, count):
        return jnp.swapaxes(front[:, first : first + count], 0, 1).reshape(count, width)

    query_t = rows_of(0, q_rows)
    down_t = rows_of(q_rows, down_rows)
    at = q_rows + down_rows
    router_t = rows_of(at, EXPERTS)
    gain_attn = front[:, at + EXPERTS].reshape(-1)
    gain_ffn = front[:, at + EXPERTS + 1].reshape(-1)
    gain_kv = front[:, at + EXPERTS + 2, :lat_loc].reshape(-1)
    at = at + 2 * EXPERTS
    out_w = rows_of(at, out_rows)
    up_w = front[:, at + out_rows :].reshape(LATENT, heads * (NOPE + VDIM))

    attn_scale = gain_attn.astype(F32)
    normed_low = (inputs * attn_inverse * attn_scale).astype(BF16)
    query = dot_nt(normed_low, query_t)
    nope_cols = heads * NOPE
    query_nope = query[:, :nope_cols].astype(BF16)
    query_rope = jnp.concatenate(
        rotate(
            query[:, nope_cols : nope_cols + heads * half],
            query[:, nope_cols + heads * half :],
            wide_cos,
            wide_sin,
        ),
        1,
    ).astype(BF16)
    latent_all = dot_nt(normed_low, down_t)
    latent_all, by_column = lax.optimization_barrier((latent_all, by_column))
    by_column = jnp.transpose(by_column, (2, 1, 0, 3, 4))
    by_plane = [swap_z(by_column[g]) for g in range(2)]
    latent = latent_all[:, :LATENT]
    kv_inverse = inverse_rms(latent)
    latent_hat = latent * kv_inverse
    kv_scale = gain_kv.astype(F32)
    latent_low = (latent_hat * kv_scale).astype(BF16)
    key_turned = jnp.concatenate(
        rotate(
            latent_all[:, LATENT : LATENT + half],
            latent_all[:, LATENT + half :],
            wide_cos[:, :half],
            wide_sin[:, :half],
        ),
        1,
    ).astype(BF16)
    copies = (2 * half, 2 * heads * half)
    to_col = lax.broadcasted_iota(jnp.int32, copies, 1)
    from_col = to_col // (heads * half) * half + to_col % half
    repeat = (lax.broadcasted_iota(jnp.int32, copies, 0) == from_col).astype(BF16)
    key_rope = dot(key_turned, repeat).astype(BF16)
    keys_values = dot(latent_low, up_w).astype(BF16)
    attended_low, log_totals = attend(
        lengths, query_nope, query_rope, keys_values, key_rope, heads, score_scale
    )
    attn_part, by_plane[0] = lax.optimization_barrier((dot(attended_low, out_w), by_plane[0]))
    attn_sum = scatter_t(attn_part)
    residual = own_part(hidden).astype(F32) + attn_sum

    def row_mean(values):
        partial = jnp.sum(values, axis=-1).reshape(-1, 128)
        return lax.psum(partial, "tensor").reshape(-1, 1) * (1.0 / width)

    ffn_inverse = lax.rsqrt(row_mean(residual * residual) + EPSILON)
    ffn_hat = residual * ffn_inverse
    ffn_scale = lax.dynamic_slice_in_dim(gain_ffn, me_t * part, part, 0).astype(F32)
    ffn_part = (ffn_hat * ffn_scale).astype(BF16)

    ffn_part, by_plane[1] = lax.optimization_barrier((ffn_part, by_plane[1]))
    ffn_all = gather_z(ffn_part)
    ffn_low = gather_t_direct(ffn_part)
    ffn_all, ffn_low, cot_ready = lax.optimization_barrier((ffn_all, ffn_low, cot_part))
    picked = pick_rows(ffn_all)
    expert_rows = send_out(picked)
    shared_pack = jnp.concatenate(
        [jnp.swapaxes(w_shared_in, 1, 2).reshape(-1, d_loc), w_shared_out], 0
    )
    cot_all, last_column = lax.optimization_barrier((gather_z(cot_ready), by_column[2]))
    by_plane.append(
        jnp.stack(
            [
                lay.over_z(lax.dynamic_index_in_dim(last_column, me_z ^ k, 0, keepdims=False), k)
                for k in range(nz)
            ]
        )
    )

    def own_weights(matrices, order):
        pieces = [by_plane[g].reshape(nz * nt, f_loc, d_loc) for g in matrices]
        stacks = [lay.over_c(piece, k) for k in range(nq) for piece in pieces]
        return lay_out_weights(lay, order, stacks, f_loc, d_loc, width)

    own_in = own_weights((0, 1), ids * jnp.array([0, 1, 1], jnp.int32))
    by_plane[2], shared_pack, cot_picked = lax.optimization_barrier(
        (by_plane[2], shared_pack, pick_rows(cot_all))
    )
    cot_rows = send_out(cot_picked)
    shared_all = lax.all_gather(shared_pack, "dp", axis=0, tiled=False)
    own_out = own_weights((2,), ids)
    router_probs = jax.nn.softmax(dot_nt(ffn_low, router_t), axis=-1)
    probs_turned = jnp.transpose(router_probs).reshape(EXPERTS, -1, 128)
    own_probs = in_order(
        [
            lay.over_z(
                lax.dynamic_index_in_dim(
                    probs_turned, (me_z ^ k) * nt + me_t, 0, keepdims=False
                ),
                k,
            )
            for k in range(nz)
        ],
        me_z,
        nz,
    ).reshape(nz, rows)
    gate_rows = jnp.sum(jnp.where(own_place, own_probs[:, None, :], 0.0), axis=-1).reshape(
        nz * CAP, 1
    )
    gate_up = dot_nt(expert_rows, own_in)
    gate_pre, up_pre = gate_up[:, :ffe], gate_up[:, ffe:]
    gate_sig = jax.nn.sigmoid(gate_pre)
    gate_silu = gate_pre * gate_sig
    active = (gate_silu * up_pre).astype(BF16)
    rows_out = (dot(active, own_out) * gate_rows).astype(BF16)
    rows_out, cot_rows, shared_all = lax.optimization_barrier((rows_out, cot_rows, shared_all))
    out_parts = send_back(rows_out)
    active_grad_raw = dot_nt(cot_rows, own_out)
    gate_grad = jnp.sum(active.astype(F32) * active_grad_raw, axis=-1).reshape(nz, CAP)
    active_grad = active_grad_raw * gate_rows
    pre_low = jnp.concatenate(
        [
            active_grad * up_pre * gate_sig * (1.0 + gate_pre * (1.0 - gate_sig)),
            active_grad * gate_silu,
        ],
        1,
    ).astype(BF16)
    gated_active = (active.astype(F32) * gate_rows).astype(BF16)
    rows_grad = dot(pre_low, own_in).astype(BF16)
    rows_grad, out_parts = lax.optimization_barrier((rows_grad, out_parts))
    grad_parts = send_back(rows_grad)
    routed, pre_low, gated_active = lax.optimization_barrier(
        (combine(out_parts), pre_low, gated_active)
    )
    routed = scatter_z(routed).astype(F32)
    token_grad = jnp.sum(jnp.where(own_place, gate_grad[:, :, None], 0.0), axis=1)
    token_grad = token_grad.reshape(nz, -1, 128)
    token_plane = jnp.stack(
        [
            lay.over_z(lax.dynamic_index_in_dim(token_grad, me_z ^ k, 0, keepdims=False), k)
            for k in range(nz)
        ]
    )
    token_home = jnp.stack([lay.over_t(token_plane, k) for k in range(nt)])
    experts = jnp.arange(EXPERTS, dtype=jnp.int32)
    came_from = (me_t ^ (experts % nt)) * nz + (me_z ^ (experts // nt))
    probs_grad = lax.dot_general(
        token_home.reshape(EXPERTS, rows),
        (experts[:, None] == came_from[None, :]).astype(F32),
        (((0,), (0,)), ((), ())),
        precision=lax.Precision.HIGHEST,
        preferred_element_type=F32,
    )

    grad_in_own = dot_tn(pre_low, expert_rows).astype(BF16)
    grad_out_own = dot_tn(gated_active, cot_rows).astype(BF16)
    ffs = w_shared_out.shape[0]
    shared_in = jnp.swapaxes(shared_all[:, : 2 * ffs], 0, 1).reshape(2 * ffs, width)
    shared_out = jnp.swapaxes(shared_all[:, 2 * ffs :], 0, 1).reshape(ffs, width)
    shared_pre = dot_nt(ffn_low, shared_in)
    shared_gate, shared_up = shared_pre[:, :ffs], shared_pre[:, ffs:]
    shared_sig = jax.nn.sigmoid(shared_gate)
    shared_silu = shared_gate * shared_sig
    shared_act = (shared_silu * shared_up).astype(BF16)
    shared_full = dot(shared_act, shared_out)
    shared_act_grad = dot_nt(cot_low, shared_out)
    shared_pre_grad = jnp.concatenate(
        [
            shared_act_grad * shared_up * shared_sig * (1.0 + shared_gate * (1.0 - shared_sig)),
            shared_act_grad * shared_silu,
        ],
        1,
    ).astype(BF16)
    grad_shared_in = dot_tn(shared_pre_grad, ffn_low)
    grad_shared_out = dot_tn(shared_act, cot_low)
    shared_grad_full = dot(shared_pre_grad, shared_in)

    (
        grad_parts,
        grad_in_own,
        grad_out_own,
        routed,
        probs_grad,
        shared_full,
        shared_grad_full,
    ) = lax.optimization_barrier(
        (
            grad_parts,
            grad_in_own,
            grad_out_own,
            routed,
            probs_grad,
            shared_full,
            shared_grad_full,
        )
    )
    shared_grad = swap_t(
        jnp.swapaxes(shared_grad_full.astype(BF16).reshape(rows, nt, part), 0, 1)
    )
    shared_grad = jnp.sum(shared_grad.astype(F32), axis=0)
    grad_pieces = take_apart(lay, ids, grad_in_own, grad_out_own, f_loc, d_loc, width)
    routed_grad = scatter_z(combine(grad_parts)).astype(F32)
    grad_class = [
        sum(lay.over_c(grad_pieces[3 * k + g], k).astype(F32) for k in range(nq)).astype(BF16)
        for g in range(3)
    ]
    routed_grad, grad_class = lax.optimization_barrier((routed_grad, grad_class))
    grad_plane = [swap_z(grad_class[g].reshape(nz, nt, f_loc, d_loc)) for g in range(3)]

    logits_grad = router_probs * (
        probs_grad - jnp.sum(router_probs * probs_grad, axis=-1, keepdims=True)
    )
    router_part = lax.dot_general(
        logits_grad,
        ffn_low.astype(F32),
        (((0,), (0,)), ((), ())),
        precision=lax.Precision.HIGHEST,
        preferred_element_type=F32,
    )
    router_slice = lax.dynamic_slice_in_dim(router_t, me_t * part, part, 1)
    ffn_grad = (
        shared_grad
        + routed_grad
        + lax.dot_general(
            logits_grad,
            router_slice.astype(F32),
            (((1,), (0,)), ((), ())),
            precision=lax.Precision.HIGHEST,
            preferred_element_type=F32,
        )
    )
    scaled = ffn_scale * ffn_grad
    ffn_gain_part = jnp.sum(ffn_grad * ffn_hat, axis=0)
    residual_grad = cot_part.astype(F32) + ffn_inverse * (
        scaled - ffn_hat * row_mean(ffn_hat * scaled)
    )
    residual_low = gather_t(residual_grad.astype(BF16))

    def sum_dp(values):
        return lax.psum_scatter(values, "dp", scatter_dimension=0, tiled=False).astype(F32)

    def by_owner(values):
        return jnp.swapaxes(values.astype(BF16).reshape(-1, ndp, d_loc), 0, 1)

    shared_grads = jnp.concatenate([by_owner(grad_shared_in), by_owner(grad_shared_out)], 1)
    residual_low, shared_grads, grad_plane[0] = lax.optimization_barrier(
        (residual_low, shared_grads, grad_plane[0])
    )
    grad_out_w = dot_tn(attended_low, residual_low)
    attended_grad = dot_nt(residual_low, out_w).astype(BF16)
    query_nope_grad, query_turned_grad, kv_grad, rope_grad = attend_back(
        lengths,
        query_nope,
        query_rope,
        keys_values,
        key_rope,
        attended_grad,
        log_totals,
        heads,
        score_scale,
    )
    query_turned_grad, grad_plane[1], shared_full, shared_grads = lax.optimization_barrier(
        (query_turned_grad, grad_plane[1], shared_full, shared_grads)
    )
    shared_sum = sum_dp(shared_grads)
    turned_first, turned_second = rotate_back(
        query_turned_grad[:, : heads * half], query_turned_grad[:, heads * half :], wide_cos, wide_sin
    )
    query_grad = jnp.concatenate(
        [query_nope_grad, turned_first.astype(BF16), turned_second.astype(BF16)], 1
    )
    rope_sum = rope_grad.reshape(rows, 2, heads, half).sum(2)
    key_rope_part = jnp.concatenate(
        rotate_back(
            rope_sum[:, 0], rope_sum[:, 1], wide_cos[:, :half], wide_sin[:, :half]
        ),
        1,
    )
    latent_part = dot_nt(kv_grad, up_w)
    grad_kv_gain = jnp.sum(latent_part * latent_hat, axis=0)
    scaled_kv = kv_scale * latent_part
    latent_back = kv_inverse * (
        scaled_kv - latent_hat * jnp.mean(latent_hat * scaled_kv, axis=-1, keepdims=True)
    )
    down_grad = jnp.concatenate([latent_back, key_rope_part], -1).astype(BF16)
    normed_full, shared_part = lax.optimization_barrier(
        (dot(query_grad, query_t) + dot(down_grad, down_t), scatter_t_direct(shared_full))
    )
    output = gather_t_direct((residual + routed + shared_part).astype(BF16))
    normed_grad, grad_plane[2] = lax.optimization_barrier(
        (scatter_t_direct(normed_full), grad_plane[2])
    )
    attn_hat = own_part(hidden).astype(F32) * attn_inverse
    scaled_in = lax.dynamic_slice_in_dim(attn_scale, me_t * part, part, 0) * normed_grad
    attn_gain_part = jnp.sum(normed_grad * attn_hat, axis=0)
    input_grad = residual_grad + attn_inverse * (
        scaled_in - attn_hat * row_mean(attn_hat * scaled_in)
    )
    input_low, grad_plane = lax.optimization_barrier((input_grad.astype(BF16), grad_plane))
    grad_home = swap_t(jnp.transpose(jnp.stack(grad_plane), (2, 0, 1, 3, 4)))
    grad_expert_in, grad_expert_out = home_gradients(lay, grad_home, f_loc, d_loc)
    grad_hidden = gather_t_direct(input_low)

    def spread(values):
        return lax.dynamic_update_slice(
            jnp.zeros((1, width), F32), values[None], (jnp.int32(0), me_t * part)
        )

    kv_gain_row = jnp.pad(
        grad_kv_gain.reshape(ndp, lat_loc), ((0, 0), (0, d_loc - lat_loc))
    ).reshape(1, width)
    gain_grads = jnp.concatenate([spread(attn_gain_part), spread(ffn_gain_part), kv_gain_row], 0)
    front_sum = sum_dp(
        jnp.concatenate(
            [
                by_owner(dot_tn(down_grad, normed_low)),
                by_owner(jnp.pad(gain_grads, ((0, 13), (0, 0)))),
                by_owner(router_part),
                by_owner(dot_tn(query_grad, normed_low)),
                by_owner(grad_out_w),
                dot_tn(latent_low, kv_grad).astype(BF16).reshape(ndp, -1, d_loc),
            ],
            1,
        )
    )
    own_sum = front_sum[: down_rows + EXPERTS]
    own_low = own_sum.astype(BF16)
    for k in range(1, nt):
        own_sum = own_sum + lay.over_t(own_low, k).astype(F32)
    at = down_rows + 2 * EXPERTS
    return (
        output,
        grad_hidden,
        own_sum[down_rows],
        jnp.transpose(by_head(front_sum[at : at + q_rows])),
        jnp.transpose(own_sum[:down_rows]),
        own_sum[down_rows + 2, :lat_loc],
        front_sum[at + q_rows + out_rows :].reshape(w_kv_up.shape),
        front_sum[at + q_rows : at + q_rows + out_rows],
        own_sum[down_rows + 1],
        jnp.transpose(front_sum[down_rows + EXPERTS : at]),
        grad_expert_in,
        grad_expert_out,
        jnp.swapaxes(shared_sum[: 2 * ffs].reshape(2, ffs, d_loc), 1, 2),
        shared_sum[2 * ffs :],
    )


def solution(mesh):
    return jax.shard_map(
        functools.partial(body, Layout(mesh.shape["dp"], mesh.shape["tensor"])),
        mesh=mesh,
        in_specs=(
            P("dp", None),
            P("dp"),
            P("dp", None),
            P("dp"),
            P("dp", "tensor"),
            P("dp", None),
            P("dp"),
            P("dp", "tensor"),
            P("tensor", "dp"),
            P("dp"),
            P("dp", None),
            P(None, None, "dp", "tensor"),
            P(None, "tensor", "dp"),
            P(None, "dp", "tensor"),
            P("tensor", "dp"),
            P("dp", None),
        ),
        out_specs=(
            P("dp", None),
            P("dp", None),
            P("dp"),
            P("dp", "tensor"),
            P("dp", None),
            P("dp"),
            P("dp", "tensor"),
            P("tensor", "dp"),
            P("dp"),
            P("dp", None),
            P(None, None, "dp", "tensor"),
            P(None, "tensor", "dp"),
            P(None, "dp", "tensor"),
            P("tensor", "dp"),
        ),
        check_vma=False,
    )
```

```python
import functools
import math

import jax
import jax.numpy as jnp
from jax import lax
from jax.experimental import pallas as pl
from jax.experimental.pallas import tpu as pltpu
from jax.sharding import PartitionSpec as P

NOPE = 128
ROPE = 64
VDIM = 128
LATENT = 512
TOP = 6
EXPERTS = 16
CAP = 512

EPSILON = 1e-06
NEGATIVE = -1e30
F32 = jnp.float32
BF16 = jnp.bfloat16


def dot(a, b):
    return jnp.dot(a, b, preferred_element_type=F32)


def dot_nt(a, b):
    return lax.dot_general(a, b, (((1,), (1,)), ((), ())), preferred_element_type=F32)


def dot_tn(a, b):
    return lax.dot_general(a, b, (((0,), (0,)), ((), ())), preferred_element_type=F32)


def rotate(first, second, cosine, sine):
    return first * cosine - second * sine, second * cosine + first * sine


def rotate_back(first, second, cosine, sine):
    return first * cosine + second * sine, second * cosine - first * sine


def angle_tables(rows_count):
    positions = jnp.arange(rows_count, dtype=F32)
    freqs = jnp.exp(jnp.arange(ROPE // 2, dtype=F32) * (-2.0 * math.log(10000.0) / ROPE))
    angles = positions[:, None] * freqs[None, :]
    return (jnp.cos(angles), jnp.sin(angles))


def inverse_rms(values):
    return lax.rsqrt(jnp.mean(values * values, axis=-1, keepdims=True) + EPSILON)


class Layout:
    def __init__(self, n_dp, n_tensor):
        self.dp, self.t = n_dp, n_tensor
        self.q = n_dp * n_tensor // EXPERTS
        self.z = n_dp // self.q
        if self.z * self.t != EXPERTS or self.z * self.q != n_dp:
            raise ValueError("mesh")
        self.z_groups = [[c + self.q * z for z in range(self.z)] for c in range(self.q)]

    def over_t(self, values, k):
        if k == 0:
            return values
        return lax.ppermute(values, "tensor", [(i, i ^ k) for i in range(self.t)])

    def over_z(self, values, k):
        if k == 0:
            return values
        return lax.ppermute(values, "dp", [(d, d ^ (k * self.q)) for d in range(self.dp)])

    def over_c(self, values, k):
        if k == 0:
            return values
        return lax.ppermute(values, "dp", [(d, d ^ k) for d in range(self.dp)])


def lay_out_weights(lay, ids, stacks, f_loc, d_loc, width):
    ffe = f_loc * lay.t
    count = len(stacks) // lay.q

    def kernel(ids_ref, *refs):
        for kc in range(lay.q):
            columns = pl.ds(pl.multiple_of((ids_ref[1] ^ kc) * d_loc, 128), d_loc)
            for g in range(count):
                refs[-1][g, :, columns] = refs[count * kc + g][0]

    own = pl.pallas_call(
        kernel,
        out_shape=jax.ShapeDtypeStruct((count, ffe, width), BF16),
        grid_spec=pltpu.PrefetchScalarGridSpec(
            num_scalar_prefetch=1,
            grid=(lay.t, lay.z),
            in_specs=[
                pl.BlockSpec(
                    (1, f_loc, d_loc), lambda kt, kz, ids: ((kz ^ ids[0]) * lay.t + kt, 0, 0)
                )
            ]
            * len(stacks),
            out_specs=pl.BlockSpec(
                (count, f_loc, lay.q * d_loc), lambda kt, kz, ids: (0, kt, kz)
            ),
        ),
        cost_estimate=pl.CostEstimate(
            flops=0, bytes_accessed=4 * count * ffe * width, transcendentals=0
        ),
        compiler_params=pltpu.CompilerParams(vmem_limit_bytes=32 << 20),
        name="lay_out_weights",
    )(ids, *stacks)
    return own.reshape(count * ffe, width)


def take_apart(lay, ids, grad_in, grad_out, f_loc, d_loc, width):
    ffe = f_loc * lay.t

    def kernel(ids_ref, in_ref, out_ref, *targets):
        for kc in range(lay.q):
            columns = pl.ds(pl.multiple_of((ids_ref[1] ^ kc) * d_loc, 128), d_loc)
            for g in range(2):
                targets[3 * kc + g][0] = in_ref[g, :, columns]
            targets[3 * kc + 2][0] = out_ref[:, columns]

    shape = jax.ShapeDtypeStruct((lay.t * lay.z, f_loc, d_loc), BF16)
    spec = pl.BlockSpec((1, f_loc, d_loc), lambda kt, kz, ids: (kz * lay.t + kt, 0, 0))
    return pl.pallas_call(
        kernel,
        out_shape=(shape,) * (3 * lay.q),
        grid_spec=pltpu.PrefetchScalarGridSpec(
            num_scalar_prefetch=1,
            grid=(lay.t, lay.z),
            in_specs=[
                pl.BlockSpec((2, f_loc, lay.q * d_loc), lambda kt, kz, ids: (0, kt, kz)),
                pl.BlockSpec((f_loc, lay.q * d_loc), lambda kt, kz, ids: (kt, kz)),
            ],
            out_specs=(spec,) * (3 * lay.q),
        ),
        cost_estimate=pl.CostEstimate(
            flops=0, bytes_accessed=12 * ffe * width, transcendentals=0
        ),
        compiler_params=pltpu.CompilerParams(vmem_limit_bytes=32 << 20),
        name="take_apart",
    )(ids, grad_in.reshape(2, ffe, width), grad_out)


def home_gradients(lay, ids, parts, f_loc, d_loc):
    def kernel(ids_ref, *refs):
        sources, (in_ref, out_ref) = refs[: 3 * lay.t], refs[3 * lay.t :]
        for k in range(lay.t):

            @pl.when((pl.program_id(1) ^ ids_ref[2]) == k)
            def _(k=k):
                for g in range(2):
                    in_ref[0, g] = sources[g * lay.t + k][0].astype(F32)
                out_ref[0] = sources[2 * lay.t + k][0].astype(F32)

    grad_in, grad_out = pl.pallas_call(
        kernel,
        out_shape=(
            jax.ShapeDtypeStruct((EXPERTS, 2, f_loc, d_loc), F32),
            jax.ShapeDtypeStruct((EXPERTS, f_loc, d_loc), F32),
        ),
        grid_spec=pltpu.PrefetchScalarGridSpec(
            num_scalar_prefetch=1,
            grid=(lay.z, lay.t),
            in_specs=[pl.BlockSpec((1, f_loc, d_loc), lambda z, t, ids: (z, 0, 0))] * (3 * lay.t),
            out_specs=(
                pl.BlockSpec((1, 2, f_loc, d_loc), lambda z, t, ids: (z * lay.t + t, 0, 0, 0)),
                pl.BlockSpec((1, f_loc, d_loc), lambda z, t, ids: (z * lay.t + t, 0, 0)),
            ),
        ),
        cost_estimate=pl.CostEstimate(
            flops=0, bytes_accessed=18 * EXPERTS * f_loc * d_loc, transcendentals=0
        ),
        compiler_params=pltpu.CompilerParams(vmem_limit_bytes=32 << 20),
        name="home_gradients",
    )(ids, *[piece for part in parts for piece in part])
    return jnp.swapaxes(grad_in, 2, 3), grad_out


def join_columns(parts, me, count):
    rows, part = parts[0].shape
    block = min(512, rows)

    def kernel(me_ref, *refs):
        for k in range(count):

            @pl.when(pl.program_id(1) == k)
            def _(k=k):
                refs[count][...] = refs[k][...]

    return pl.pallas_call(
        kernel,
        out_shape=jax.ShapeDtypeStruct((rows, count * part), parts[0].dtype),
        grid_spec=pltpu.PrefetchScalarGridSpec(
            num_scalar_prefetch=1,
            grid=(rows // block, count),
            in_specs=[pl.BlockSpec((block, part), lambda i, k, me: (i, 0))] * count,
            out_specs=pl.BlockSpec((block, part), lambda i, k, me: (i, me[0] ^ k)),
        ),
        cost_estimate=pl.CostEstimate(
            flops=0, bytes_accessed=4 * rows * part * count, transcendentals=0
        ),
        name="join_columns",
    )(me.reshape(1).astype(jnp.int32), *parts)


def score_block(q_ref, r_ref, k_ref, kr_ref, head, step, keys, block, length, scale):
    half = r_ref.shape[1] // 2
    lanes = lax.broadcasted_iota(jnp.int32, r_ref.shape, 1) % half // (ROPE // 2)
    turned = jnp.where(lanes == head, r_ref[...], jnp.zeros_like(r_ref))
    raw = lax.dot_general(
        q_ref[...], k_ref[:keys], (((1,), (1,)), ((), ())), preferred_element_type=F32
    ) + lax.dot_general(
        turned, kr_ref[:keys], (((1,), (1,)), ((), ())), preferred_element_type=F32
    )
    rows = lax.broadcasted_iota(jnp.int32, raw.shape, 0) + step * block
    cols = lax.broadcasted_iota(jnp.int32, raw.shape, 1)
    allowed = (cols <= rows) & (cols < length)
    return jnp.where(allowed, raw * scale, NEGATIVE), turned


def attend(length, query, query_rope, kv, key_rope, heads, scale):
    rows = query.shape[0]
    block = min(256, rows)
    steps = rows // block

    def kernel(len_ref, q_ref, r_ref, k_ref, v_ref, kr_ref, o_ref, total_ref):
        head, step = pl.program_id(0), pl.program_id(1)
        for n in range(steps):

            @pl.when(step == n)
            def _(n=n):
                keys = (n + 1) * block
                scores, _ = score_block(
                    q_ref, r_ref, k_ref, kr_ref, head, n, keys, block, len_ref[0], scale
                )
                highest = jnp.max(scores, axis=-1, keepdims=True)
                expo = jnp.exp(scores - highest)
                totals = jnp.sum(expo, axis=-1, keepdims=True)
                weights = (expo * (1.0 / totals)).astype(BF16)
                o_ref[...] = dot(weights, v_ref[:keys]).astype(BF16)
                total_ref[0] = jnp.broadcast_to(highest + jnp.log(totals), (block, 128))

    return pl.pallas_call(
        kernel,
        out_shape=(
            jax.ShapeDtypeStruct((rows, heads * VDIM), BF16),
            jax.ShapeDtypeStruct((heads, rows, 128), F32),
        ),
        grid_spec=pltpu.PrefetchScalarGridSpec(
            num_scalar_prefetch=1,
            grid=(heads, steps),
            in_specs=[
                pl.BlockSpec((block, NOPE), lambda h, i, n: (i, h)),
                pl.BlockSpec((block, query_rope.shape[1]), lambda h, i, n: (i, 0)),
                pl.BlockSpec((rows, NOPE), lambda h, i, n: (0, 2 * h)),
                pl.BlockSpec((rows, VDIM), lambda h, i, n: (0, 2 * h + 1)),
                pl.BlockSpec((rows, key_rope.shape[1]), lambda h, i, n: (0, 0)),
            ],
            out_specs=(
                pl.BlockSpec((block, VDIM), lambda h, i, n: (i, h)),
                pl.BlockSpec((1, block, 128), lambda h, i, n: (h, i, 0)),
            ),
        ),
        cost_estimate=pl.CostEstimate(
            flops=heads * rows * rows * 512,
            bytes_accessed=8 * rows * heads * 512,
            transcendentals=heads * rows * rows,
        ),
        compiler_params=pltpu.CompilerParams(vmem_limit_bytes=32 << 20),
        name="attend",
    )(length, query, query_rope, kv, kv, key_rope)


def attend_back(length, query, query_rope, kv, key_rope, out_grad, log_totals, heads, scale):
    rows = query.shape[0]
    block = min(256, rows)
    steps = rows // block
    turned_cols = query_rope.shape[1]

    def kernel(
        len_ref, q_ref, r_ref, k_ref, v_ref, kr_ref, do_ref, total_ref,
        dq_ref, dr_ref, dkv_ref, dkr_ref, dk_acc, dv_acc,
    ):
        head, step = pl.program_id(0), pl.program_id(1)

        @pl.when(step == 0)
        def _():
            dk_acc[...] = jnp.zeros_like(dk_acc)
            dv_acc[...] = jnp.zeros_like(dv_acc)

        @pl.when((step == 0) & (head == 0))
        def _():
            dr_ref[...] = jnp.zeros_like(dr_ref)
            dkr_ref[...] = jnp.zeros_like(dkr_ref)

        for n in range(steps):

            @pl.when(step == n)
            def _(n=n):
                keys = (n + 1) * block
                scores, turned = score_block(
                    q_ref, r_ref, k_ref, kr_ref, head, n, keys, block, len_ref[0], scale
                )
                probs = jnp.exp(scores - total_ref[0][:, :1])
                prob_grad = lax.dot_general(
                    do_ref[...], v_ref[:keys], (((1,), (1,)), ((), ())), preferred_element_type=F32
                )
                centre = jnp.sum(probs * prob_grad, axis=-1, keepdims=True)
                score_grad = (probs * (prob_grad - centre)).astype(BF16)
                probs_low = probs.astype(BF16)
                dq_ref[...] = (dot(score_grad, k_ref[:keys]) * scale).astype(BF16)
                half = turned_cols // 2
                lanes = lax.broadcasted_iota(jnp.int32, (block, turned_cols), 1)
                lanes = lanes % half // (ROPE // 2)
                turned_grad = dot(score_grad, kr_ref[:keys]) * scale
                dr_ref[n * block : keys] += jnp.where(lanes == head, turned_grad, 0.0)
                dk_acc[:keys] += dot_tn(score_grad, q_ref[...]) * scale
                dkr_ref[:keys] += dot_tn(score_grad, turned) * scale
                dv_acc[:keys] += dot_tn(probs_low, do_ref[...])

        @pl.when(step == steps - 1)
        def _():
            dkv_ref[:, :NOPE] = dk_acc[...].astype(BF16)
            dkv_ref[:, NOPE:] = dv_acc[...].astype(BF16)

    return pl.pallas_call(
        kernel,
        out_shape=(
            jax.ShapeDtypeStruct((rows, heads * NOPE), BF16),
            jax.ShapeDtypeStruct((rows, turned_cols), F32),
            jax.ShapeDtypeStruct((rows, heads * (NOPE + VDIM)), BF16),
            jax.ShapeDtypeStruct((rows, turned_cols), F32),
        ),
        grid_spec=pltpu.PrefetchScalarGridSpec(
            num_scalar_prefetch=1,
            grid=(heads, steps),
            in_specs=[
                pl.BlockSpec((block, NOPE), lambda h, i, n: (i, h)),
                pl.BlockSpec((block, turned_cols), lambda h, i, n: (i, 0)),
                pl.BlockSpec((rows, NOPE), lambda h, i, n: (0, 2 * h)),
                pl.BlockSpec((rows, VDIM), lambda h, i, n: (0, 2 * h + 1)),
                pl.BlockSpec((rows, turned_cols), lambda h, i, n: (0, 0)),
                pl.BlockSpec((block, VDIM), lambda h, i, n: (i, h)),
                pl.BlockSpec((1, block, 128), lambda h, i, n: (h, i, 0)),
            ],
            out_specs=(
                pl.BlockSpec((block, NOPE), lambda h, i, n: (i, h)),
                pl.BlockSpec((rows, turned_cols), lambda h, i, n: (0, 0)),
                pl.BlockSpec((rows, NOPE + VDIM), lambda h, i, n: (0, h)),
                pl.BlockSpec((rows, turned_cols), lambda h, i, n: (0, 0)),
            ),
            scratch_shapes=[pltpu.VMEM((rows, NOPE), F32), pltpu.VMEM((rows, VDIM), F32)],
        ),
        cost_estimate=pl.CostEstimate(
            flops=heads * rows * rows * 1600,
            bytes_accessed=16 * rows * heads * 512,
            transcendentals=heads * rows * rows,
        ),
        compiler_params=pltpu.CompilerParams(vmem_limit_bytes=40 << 20),
        name="attend_back",
    )(length, query, query_rope, kv, kv, key_rope, out_grad, log_totals)


def in_order(values, me, count):
    zero = jnp.zeros_like(values[0])
    ordered = []
    for j in range(count):
        total = zero
        for k in range(count):
            total = jnp.where((me ^ k) == j, values[k], total)
        ordered.append(total)
    return jnp.stack(ordered)


def body(
    lay,
    hidden,
    lengths,
    routes,
    attn_gain,
    w_query,
    w_kv_down,
    kv_gain,
    w_kv_up,
    w_out,
    ffn_gain,
    w_router,
    w_expert_in,
    w_expert_out,
    w_shared_in,
    w_shared_out,
    cotangent,
):
    rows, width = hidden.shape
    nz, nt, nq, ndp = lay.z, lay.t, lay.q, lay.dp
    me_dp = lax.axis_index("dp")
    me_t = lax.axis_index("tensor")
    me_z = me_dp // nq
    me_c = me_dp % nq
    part = width // nt
    d_loc = w_query.shape[0]
    f_loc = w_expert_out.shape[1]
    ffe = f_loc * nt
    heads = w_query.shape[1] // (NOPE + ROPE)
    score_scale = (NOPE + ROPE) ** (-0.5)

    def own_part(values):
        return lax.dynamic_slice_in_dim(values, me_t * part, part, 1)

    def gather_z(values):
        return lax.all_gather(values, "dp", axis=0, tiled=False, axis_index_groups=lay.z_groups)

    def scatter_z(values):
        return lax.psum_scatter(
            values, "dp", scatter_dimension=0, tiled=False, axis_index_groups=lay.z_groups
        )

    def gather_t(values):
        return lax.all_gather(values, "tensor", axis=1, tiled=True)

    def scatter_t(values):
        return lax.psum_scatter(
            values.astype(BF16), "tensor", scatter_dimension=1, tiled=True
        ).astype(F32)

    def swap_t(values):
        return lax.all_to_all(values, "tensor", split_axis=0, concat_axis=0, tiled=True)

    def swap_z(values):
        return lax.all_to_all(
            values,
            "dp",
            split_axis=0,
            concat_axis=0,
            axis_index_groups=lay.z_groups,
            tiled=True,
        )

    def gather_t_direct(values):
        return join_columns([lay.over_t(values, k) for k in range(nt)], me_t, nt)

    def part_for(values, k):
        return lax.dynamic_slice_in_dim(values, (me_t ^ k) * part, part, 1)

    def scatter_t_direct(values):
        total = part_for(values, 0)
        for k in range(1, nt):
            total = total + lay.over_t(part_for(values, k).astype(BF16), k).astype(F32)
        return total

    ids = jnp.stack([me_z, me_c, me_t]).astype(jnp.int32)

    packed = jnp.concatenate(
        [jnp.swapaxes(w_expert_in, 2, 3), w_expert_out[:, None]], 1
    ).reshape(nz, nt, 3, f_loc, d_loc)
    by_column = swap_t(jnp.swapaxes(packed, 0, 1))

    lat_loc = kv_gain.shape[0]
    q_rows, down_rows, out_rows = w_query.shape[1], w_kv_down.shape[1], w_out.shape[0]
    half = ROPE // 2

    def by_kind(turned):
        split = turned.reshape(heads, NOPE + ROPE, -1)
        return jnp.concatenate(
            [
                split[:, :NOPE].reshape(heads * NOPE, -1),
                split[:, NOPE : NOPE + half].reshape(heads * half, -1),
                split[:, NOPE + half :].reshape(heads * half, -1),
            ],
            0,
        )

    def by_head(rows_in):
        nope = rows_in[: heads * NOPE].reshape(heads, NOPE, -1)
        first = rows_in[heads * NOPE : heads * (NOPE + half)].reshape(heads, half, -1)
        second = rows_in[heads * (NOPE + half) :].reshape(heads, half, -1)
        return jnp.concatenate([nope, first, second], 1).reshape(heads * (NOPE + ROPE), -1)

    gains = jnp.stack([attn_gain, ffn_gain, jnp.pad(kv_gain, (0, d_loc - lat_loc))])
    front_pack = jnp.concatenate(
        [
            by_kind(jnp.transpose(w_query)),
            jnp.transpose(w_kv_down),
            jnp.transpose(w_router),
            jnp.pad(gains, ((0, 13), (0, 0))),
            w_out,
            w_kv_up.reshape(-1, d_loc),
        ],
        0,
    )
    front = lax.all_gather(front_pack, "dp", axis=0, tiled=False)

    valid_length = lengths[0]
    valid_rows = lax.broadcasted_iota(jnp.int32, (rows, 1), 0) < valid_length
    cot_low = jnp.where(valid_rows, cotangent, jnp.zeros_like(cotangent))
    cot_part = own_part(cot_low)
    route_own = jnp.pad(jnp.transpose(routes), ((0, -TOP % 8), (0, 0)), constant_values=-1)
    route_all = in_order([lay.over_z(route_own, k) for k in range(nz)], me_z, nz)
    inputs = hidden.astype(F32)
    attn_inverse = inverse_rms(inputs)
    cosine, sine = angle_tables(rows)
    wide_cos, wide_sin = jnp.tile(cosine, (1, heads)), jnp.tile(sine, (1, heads))
    front, attn_inverse, wide_cos, wide_sin, route_all = lax.optimization_barrier(
        (front, attn_inverse, wide_cos, wide_sin, route_all)
    )

    plane_ids = me_z * nt + jnp.arange(nt, dtype=jnp.int32)
    member = jnp.any(route_all[:, :, :, None] == plane_ids[None, None, None, :], axis=1)
    row_ids = lax.broadcasted_iota(jnp.int32, (rows, rows), 0)
    col_ids = lax.broadcasted_iota(jnp.int32, (rows, rows), 1)
    before = (col_ids < row_ids).astype(BF16)
    position = jnp.einsum("ij,sje->sei", before, member.astype(BF16), preferred_element_type=F32)
    key = jnp.where(jnp.swapaxes(member, 1, 2), position.astype(jnp.int32), -1)
    slots_iota = lax.broadcasted_iota(jnp.int32, (1, 1, CAP, 1), 2)

    def place_of(keys):
        return (keys[:, :, None, :] == slots_iota).astype(BF16)

    place = place_of(key)
    own_key = lax.dynamic_index_in_dim(key, me_t, 1, keepdims=False)
    own_place = own_key[:, None, :] == slots_iota[0]

    def pick_rows(values):
        picked = jnp.einsum("sepk,skd->espd", place, values, preferred_element_type=F32)
        return picked.astype(BF16).reshape(nt, nz * CAP, part)

    def send_out(picked):
        return jnp.swapaxes(swap_t(picked), 0, 1).reshape(nz * CAP, width)

    def send_back(values):
        return swap_t(jnp.swapaxes(values.reshape(nz * CAP, nt, part), 0, 1))

    def combine(parts):
        parts = parts.reshape(nt, nz, CAP, part)
        summed = jnp.einsum("sepk,espd->skd", place, parts, preferred_element_type=F32)
        return summed.astype(BF16)


    def rows_of(first, count):
        return jnp.swapaxes(front[:, first : first + count], 0, 1).reshape(count, width)

    query_t = rows_of(0, q_rows)
    down_t = rows_of(q_rows, down_rows)
    at = q_rows + down_rows
    router_t = rows_of(at, EXPERTS)
    gain_attn = front[:, at + EXPERTS].reshape(-1)
    gain_ffn = front[:, at + EXPERTS + 1].reshape(-1)
    gain_kv = front[:, at + EXPERTS + 2, :lat_loc].reshape(-1)
    at = at + 2 * EXPERTS
    out_w = rows_of(at, out_rows)
    up_w = front[:, at + out_rows :].reshape(LATENT, heads * (NOPE + VDIM))

    attn_scale = gain_attn.astype(F32)
    normed_low = (inputs * attn_inverse * attn_scale).astype(BF16)
    query = dot_nt(normed_low, query_t)
    nope_cols = heads * NOPE
    query_nope = query[:, :nope_cols].astype(BF16)
    query_rope = jnp.concatenate(
        rotate(
            query[:, nope_cols : nope_cols + heads * half],
            query[:, nope_cols + heads * half :],
            wide_cos,
            wide_sin,
        ),
        1,
    ).astype(BF16)
    latent_all = dot_nt(normed_low, down_t)
    latent_all, by_column = lax.optimization_barrier((latent_all, by_column))
    by_column = jnp.transpose(by_column, (2, 1, 0, 3, 4))
    by_plane = [swap_z(by_column[g]) for g in range(2)]
    latent = latent_all[:, :LATENT]
    kv_inverse = inverse_rms(latent)
    latent_hat = latent * kv_inverse
    kv_scale = gain_kv.astype(F32)
    latent_low = (latent_hat * kv_scale).astype(BF16)
    key_turned = jnp.concatenate(
        rotate(
            latent_all[:, LATENT : LATENT + half],
            latent_all[:, LATENT + half :],
            wide_cos[:, :half],
            wide_sin[:, :half],
        ),
        1,
    ).astype(BF16)
    copies = (2 * half, 2 * heads * half)
    to_col = lax.broadcasted_iota(jnp.int32, copies, 1)
    from_col = to_col // (heads * half) * half + to_col % half
    repeat = (lax.broadcasted_iota(jnp.int32, copies, 0) == from_col).astype(BF16)
    key_rope = dot(key_turned, repeat).astype(BF16)
    keys_values = dot(latent_low, up_w).astype(BF16)
    attended_low, log_totals = attend(
        lengths, query_nope, query_rope, keys_values, key_rope, heads, score_scale
    )
    attn_part, by_plane[0] = lax.optimization_barrier((dot(attended_low, out_w), by_plane[0]))
    attn_sum = scatter_t(attn_part)
    residual = own_part(hidden).astype(F32) + attn_sum

    def row_mean(values):
        partial = jnp.sum(values, axis=-1).reshape(-1, 128)
        return lax.psum(partial, "tensor").reshape(-1, 1) * (1.0 / width)

    ffn_inverse = lax.rsqrt(row_mean(residual * residual) + EPSILON)
    ffn_hat = residual * ffn_inverse
    ffn_scale = lax.dynamic_slice_in_dim(gain_ffn, me_t * part, part, 0).astype(F32)
    ffn_part = (ffn_hat * ffn_scale).astype(BF16)

    ffn_part, by_plane[1] = lax.optimization_barrier((ffn_part, by_plane[1]))
    ffn_all = gather_z(ffn_part)
    ffn_low = gather_t_direct(ffn_part)
    ffn_all, ffn_low, cot_ready = lax.optimization_barrier((ffn_all, ffn_low, cot_part))
    picked, by_plane[0], by_plane[1] = lax.optimization_barrier(
        (pick_rows(ffn_all), by_plane[0], by_plane[1])
    )
    expert_rows = send_out(picked)
    shared_pack = jnp.concatenate(
        [jnp.swapaxes(w_shared_in, 1, 2).reshape(-1, d_loc), w_shared_out], 0
    )
    def own_weights(matrices, order):
        pieces = [by_plane[g].reshape(nz * nt, f_loc, d_loc) for g in matrices]
        stacks = [lay.over_c(piece, k) for k in range(nq) for piece in pieces]
        return lay_out_weights(lay, order, stacks, f_loc, d_loc, width)

    own_in = own_weights((0, 1), ids * jnp.array([0, 1, 1], jnp.int32))
    cot_all, last_column, own_in = lax.optimization_barrier(
        (gather_z(cot_ready), by_column[2], own_in)
    )
    by_plane.append(
        jnp.stack(
            [
                lay.over_z(lax.dynamic_index_in_dim(last_column, me_z ^ k, 0, keepdims=False), k)
                for k in range(nz)
            ]
        )
    )

    by_plane[2], shared_pack, cot_picked = lax.optimization_barrier(
        (by_plane[2], shared_pack, pick_rows(cot_all))
    )
    cot_rows = send_out(cot_picked)
    shared_all = lax.all_gather(shared_pack, "dp", axis=0, tiled=False)
    own_out = own_weights((2,), ids)
    router_probs = jax.nn.softmax(dot_nt(ffn_low, router_t), axis=-1)
    probs_turned = jnp.transpose(router_probs).reshape(EXPERTS, -1, 128)
    own_probs = in_order(
        [
            lay.over_z(
                lax.dynamic_index_in_dim(
                    probs_turned, (me_z ^ k) * nt + me_t, 0, keepdims=False
                ),
                k,
            )
            for k in range(nz)
        ],
        me_z,
        nz,
    ).reshape(nz, rows)
    gate_rows = jnp.sum(jnp.where(own_place, own_probs[:, None, :], 0.0), axis=-1).reshape(
        nz * CAP, 1
    )
    gate_up = dot_nt(expert_rows, own_in)
    gate_pre, up_pre = gate_up[:, :ffe], gate_up[:, ffe:]
    gate_sig = jax.nn.sigmoid(gate_pre)
    gate_silu = gate_pre * gate_sig
    active = (gate_silu * up_pre).astype(BF16)
    rows_out = (dot(active, own_out) * gate_rows).astype(BF16)
    rows_out, cot_rows, shared_all = lax.optimization_barrier((rows_out, cot_rows, shared_all))
    out_parts = send_back(rows_out)
    active_grad_raw = dot_nt(cot_rows, own_out)
    gate_grad = jnp.sum(active.astype(F32) * active_grad_raw, axis=-1).reshape(nz, CAP)
    active_grad = active_grad_raw * gate_rows
    pre_low = jnp.concatenate(
        [
            active_grad * up_pre * gate_sig * (1.0 + gate_pre * (1.0 - gate_sig)),
            active_grad * gate_silu,
        ],
        1,
    ).astype(BF16)
    gated_active = (active.astype(F32) * gate_rows).astype(BF16)
    out_parts, pre_low = lax.optimization_barrier((out_parts, pre_low))
    rows_grad = dot(pre_low, own_in).astype(BF16)
    rows_grad, out_parts = lax.optimization_barrier((rows_grad, out_parts))
    grad_parts = send_back(rows_grad)
    routed, pre_low, gated_active = lax.optimization_barrier(
        (combine(out_parts), pre_low, gated_active)
    )
    routed = scatter_z(routed).astype(F32)
    token_grad = jnp.sum(jnp.where(own_place, gate_grad[:, :, None], 0.0), axis=1)
    token_grad = token_grad.reshape(nz, -1, 128)
    token_plane = jnp.stack(
        [
            lay.over_z(lax.dynamic_index_in_dim(token_grad, me_z ^ k, 0, keepdims=False), k)
            for k in range(nz)
        ]
    )
    token_home = jnp.stack([lay.over_t(token_plane, k) for k in range(nt)])
    experts = jnp.arange(EXPERTS, dtype=jnp.int32)
    came_from = (me_t ^ (experts % nt)) * nz + (me_z ^ (experts // nt))
    probs_grad = lax.dot_general(
        token_home.reshape(EXPERTS, rows),
        (experts[:, None] == came_from[None, :]).astype(F32),
        (((0,), (0,)), ((), ())),
        precision=lax.Precision.HIGHEST,
        preferred_element_type=F32,
    )

    grad_in_own = dot_tn(pre_low, expert_rows).astype(BF16)
    grad_out_own = dot_tn(gated_active, cot_rows).astype(BF16)
    ffs = w_shared_out.shape[0]
    shared_in = jnp.swapaxes(shared_all[:, : 2 * ffs], 0, 1).reshape(2 * ffs, width)
    shared_out = jnp.swapaxes(shared_all[:, 2 * ffs :], 0, 1).reshape(ffs, width)
    shared_pre = dot_nt(ffn_low, shared_in)
    shared_gate, shared_up = shared_pre[:, :ffs], shared_pre[:, ffs:]
    shared_sig = jax.nn.sigmoid(shared_gate)
    shared_silu = shared_gate * shared_sig
    shared_act = (shared_silu * shared_up).astype(BF16)
    shared_full = dot(shared_act, shared_out)
    shared_act_grad = dot_nt(cot_low, shared_out)
    shared_pre_grad = jnp.concatenate(
        [
            shared_act_grad * shared_up * shared_sig * (1.0 + shared_gate * (1.0 - shared_sig)),
            shared_act_grad * shared_silu,
        ],
        1,
    ).astype(BF16)
    grad_shared_in = dot_tn(shared_pre_grad, ffn_low)
    grad_shared_out = dot_tn(shared_act, cot_low)
    shared_grad_full = dot(shared_pre_grad, shared_in)

    (
        grad_parts,
        grad_in_own,
        grad_out_own,
        routed,
        probs_grad,
        shared_full,
        shared_grad_full,
    ) = lax.optimization_barrier(
        (
            grad_parts,
            grad_in_own,
            grad_out_own,
            routed,
            probs_grad,
            shared_full,
            shared_grad_full,
        )
    )
    shared_grad = swap_t(
        jnp.swapaxes(shared_grad_full.astype(BF16).reshape(rows, nt, part), 0, 1)
    )
    shared_grad = jnp.sum(shared_grad.astype(F32), axis=0)
    grad_pieces = take_apart(lay, ids, grad_in_own, grad_out_own, f_loc, d_loc, width)
    routed_grad = scatter_z(combine(grad_parts)).astype(F32)
    grad_class = [
        sum(lay.over_c(grad_pieces[3 * k + g], k).astype(F32) for k in range(nq)).astype(BF16)
        for g in range(3)
    ]
    routed_grad, grad_class = lax.optimization_barrier((routed_grad, grad_class))
    grad_plane = [swap_z(grad_class[g].reshape(nz, nt, f_loc, d_loc)) for g in range(3)]

    logits_grad = router_probs * (
        probs_grad - jnp.sum(router_probs * probs_grad, axis=-1, keepdims=True)
    )
    router_part = lax.dot_general(
        logits_grad,
        ffn_low.astype(F32),
        (((0,), (0,)), ((), ())),
        precision=lax.Precision.HIGHEST,
        preferred_element_type=F32,
    )
    router_slice = lax.dynamic_slice_in_dim(router_t, me_t * part, part, 1)
    ffn_grad = (
        shared_grad
        + routed_grad
        + lax.dot_general(
            logits_grad,
            router_slice.astype(F32),
            (((1,), (0,)), ((), ())),
            precision=lax.Precision.HIGHEST,
            preferred_element_type=F32,
        )
    )
    scaled = ffn_scale * ffn_grad
    ffn_gain_part = jnp.sum(ffn_grad * ffn_hat, axis=0)
    residual_grad = cot_part.astype(F32) + ffn_inverse * (
        scaled - ffn_hat * row_mean(ffn_hat * scaled)
    )
    residual_low = gather_t(residual_grad.astype(BF16))

    def sum_dp(values):
        return lax.psum_scatter(values, "dp", scatter_dimension=0, tiled=False).astype(F32)

    def by_owner(values):
        return jnp.swapaxes(values.astype(BF16).reshape(-1, ndp, d_loc), 0, 1)

    shared_grads = jnp.concatenate([by_owner(grad_shared_in), by_owner(grad_shared_out)], 1)
    residual_low, shared_grads, grad_plane[0] = lax.optimization_barrier(
        (residual_low, shared_grads, grad_plane[0])
    )
    grad_out_w = dot_tn(attended_low, residual_low)
    attended_grad = dot_nt(residual_low, out_w).astype(BF16)
    query_nope_grad, query_turned_grad, kv_grad, rope_grad = attend_back(
        lengths,
        query_nope,
        query_rope,
        keys_values,
        key_rope,
        attended_grad,
        log_totals,
        heads,
        score_scale,
    )
    def to_columns(values):
        return [
            lay.over_t(lax.dynamic_index_in_dim(values, me_t ^ k, 1, keepdims=False), k)
            for k in range(nt)
        ]

    grad_home = [to_columns(grad_plane[0]), None, None]
    (
        query_turned_grad,
        grad_plane[1],
        grad_home[0],
        shared_full,
        shared_grads,
    ) = lax.optimization_barrier(
        (query_turned_grad, grad_plane[1], grad_home[0], shared_full, shared_grads)
    )
    shared_sum = sum_dp(shared_grads)
    turned_first, turned_second = rotate_back(
        query_turned_grad[:, : heads * half], query_turned_grad[:, heads * half :], wide_cos, wide_sin
    )
    query_grad = jnp.concatenate(
        [query_nope_grad, turned_first.astype(BF16), turned_second.astype(BF16)], 1
    )
    rope_sum = rope_grad.reshape(rows, 2, heads, half).sum(2)
    key_rope_part = jnp.concatenate(
        rotate_back(
            rope_sum[:, 0], rope_sum[:, 1], wide_cos[:, :half], wide_sin[:, :half]
        ),
        1,
    )
    latent_part = dot_nt(kv_grad, up_w)
    grad_kv_gain = jnp.sum(latent_part * latent_hat, axis=0)
    scaled_kv = kv_scale * latent_part
    latent_back = kv_inverse * (
        scaled_kv - latent_hat * jnp.mean(latent_hat * scaled_kv, axis=-1, keepdims=True)
    )
    down_grad = jnp.concatenate([latent_back, key_rope_part], -1).astype(BF16)
    normed_full, shared_part = lax.optimization_barrier(
        (dot(query_grad, query_t) + dot(down_grad, down_t), scatter_t_direct(shared_full))
    )
    output = gather_t_direct((residual + routed + shared_part).astype(BF16))
    normed_grad, grad_plane[2], grad_home[1] = lax.optimization_barrier(
        (scatter_t_direct(normed_full), grad_plane[2], to_columns(grad_plane[1]))
    )
    attn_hat = own_part(hidden).astype(F32) * attn_inverse
    scaled_in = lax.dynamic_slice_in_dim(attn_scale, me_t * part, part, 0) * normed_grad
    attn_gain_part = jnp.sum(normed_grad * attn_hat, axis=0)
    input_grad = residual_grad + attn_inverse * (
        scaled_in - attn_hat * row_mean(attn_hat * scaled_in)
    )
    input_low, grad_plane[2] = lax.optimization_barrier((input_grad.astype(BF16), grad_plane[2]))
    grad_home[2] = to_columns(grad_plane[2])
    grad_expert_in, grad_expert_out = home_gradients(lay, ids, grad_home, f_loc, d_loc)
    grad_hidden = gather_t_direct(input_low)

    def spread(values):
        return lax.dynamic_update_slice(
            jnp.zeros((1, width), F32), values[None], (jnp.int32(0), me_t * part)
        )

    kv_gain_row = jnp.pad(
        grad_kv_gain.reshape(ndp, lat_loc), ((0, 0), (0, d_loc - lat_loc))
    ).reshape(1, width)
    gain_grads = jnp.concatenate([spread(attn_gain_part), spread(ffn_gain_part), kv_gain_row], 0)
    front_sum = sum_dp(
        jnp.concatenate(
            [
                by_owner(dot_tn(down_grad, normed_low)),
                by_owner(jnp.pad(gain_grads, ((0, 13), (0, 0)))),
                by_owner(router_part),
                by_owner(dot_tn(query_grad, normed_low)),
                by_owner(grad_out_w),
                dot_tn(latent_low, kv_grad).astype(BF16).reshape(ndp, -1, d_loc),
            ],
            1,
        )
    )
    own_sum = front_sum[: down_rows + EXPERTS]
    own_low = own_sum.astype(BF16)
    for k in range(1, nt):
        own_sum = own_sum + lay.over_t(own_low, k).astype(F32)
    at = down_rows + 2 * EXPERTS
    return (
        output,
        grad_hidden,
        own_sum[down_rows],
        jnp.transpose(by_head(front_sum[at : at + q_rows])),
        jnp.transpose(own_sum[:down_rows]),
        own_sum[down_rows + 2, :lat_loc],
        front_sum[at + q_rows + out_rows :].reshape(w_kv_up.shape),
        front_sum[at + q_rows : at + q_rows + out_rows],
        own_sum[down_rows + 1],
        jnp.transpose(front_sum[down_rows + EXPERTS : at]),
        grad_expert_in,
        grad_expert_out,
        jnp.swapaxes(shared_sum[: 2 * ffs].reshape(2, ffs, d_loc), 1, 2),
        shared_sum[2 * ffs :],
    )


def solution(mesh):
    return jax.shard_map(
        functools.partial(body, Layout(mesh.shape["dp"], mesh.shape["tensor"])),
        mesh=mesh,
        in_specs=(
            P("dp", None),
            P("dp"),
            P("dp", None),
            P("dp"),
            P("dp", "tensor"),
            P("dp", None),
            P("dp"),
            P("dp", "tensor"),
            P("tensor", "dp"),
            P("dp"),
            P("dp", None),
            P(None, None, "dp", "tensor"),
            P(None, "tensor", "dp"),
            P(None, "dp", "tensor"),
            P("tensor", "dp"),
            P("dp", None),
        ),
        out_specs=(
            P("dp", None),
            P("dp", None),
            P("dp"),
            P("dp", "tensor"),
            P("dp", None),
            P("dp"),
            P("dp", "tensor"),
            P("tensor", "dp"),
            P("dp"),
            P("dp", None),
            P(None, None, "dp", "tensor"),
            P(None, "tensor", "dp"),
            P(None, "dp", "tensor"),
            P("tensor", "dp"),
        ),
        check_vma=False,
    )
```

```python
import functools
import math

import jax
import jax.numpy as jnp
from jax import lax
from jax.experimental import pallas as pl
from jax.experimental.pallas import tpu as pltpu
from jax.sharding import PartitionSpec as P

NOPE = 128
ROPE = 64
VDIM = 128
LATENT = 512
TOP = 6
EXPERTS = 16
CAP = 512

EPSILON = 1e-06
NEGATIVE = -1e30
F32 = jnp.float32
BF16 = jnp.bfloat16


def dot(a, b):
    return jnp.dot(a, b, preferred_element_type=F32)


def dot_nt(a, b):
    return lax.dot_general(a, b, (((1,), (1,)), ((), ())), preferred_element_type=F32)


def dot_tn(a, b):
    return lax.dot_general(a, b, (((0,), (0,)), ((), ())), preferred_element_type=F32)


def rotate(first, second, cosine, sine):
    return first * cosine - second * sine, second * cosine + first * sine


def rotate_back(first, second, cosine, sine):
    return first * cosine + second * sine, second * cosine - first * sine


def angle_tables(rows_count):
    positions = jnp.arange(rows_count, dtype=F32)
    freqs = jnp.exp(jnp.arange(ROPE // 2, dtype=F32) * (-2.0 * math.log(10000.0) / ROPE))
    angles = positions[:, None] * freqs[None, :]
    return (jnp.cos(angles), jnp.sin(angles))


def inverse_rms(values):
    return lax.rsqrt(jnp.mean(values * values, axis=-1, keepdims=True) + EPSILON)


class Layout:
    def __init__(self, n_dp, n_tensor):
        self.dp, self.t = n_dp, n_tensor
        self.q = n_dp * n_tensor // EXPERTS
        self.z = n_dp // self.q
        if self.z * self.t != EXPERTS or self.z * self.q != n_dp:
            raise ValueError("mesh")
        self.z_groups = [[c + self.q * z for z in range(self.z)] for c in range(self.q)]

    def over_t(self, values, k):
        if k == 0:
            return values
        return lax.ppermute(values, "tensor", [(i, i ^ k) for i in range(self.t)])

    def over_z(self, values, k):
        if k == 0:
            return values
        return lax.ppermute(values, "dp", [(d, d ^ (k * self.q)) for d in range(self.dp)])

    def over_c(self, values, k):
        if k == 0:
            return values
        return lax.ppermute(values, "dp", [(d, d ^ k) for d in range(self.dp)])


def lay_out_weights(lay, ids, stacks, f_loc, d_loc, width):
    ffe = f_loc * lay.t
    count = len(stacks) // lay.q

    def kernel(ids_ref, *refs):
        for kc in range(lay.q):
            columns = pl.ds(pl.multiple_of((ids_ref[1] ^ kc) * d_loc, 128), d_loc)
            for g in range(count):
                refs[-1][g, :, columns] = refs[count * kc + g][0]

    own = pl.pallas_call(
        kernel,
        out_shape=jax.ShapeDtypeStruct((count, ffe, width), BF16),
        grid_spec=pltpu.PrefetchScalarGridSpec(
            num_scalar_prefetch=1,
            grid=(lay.t, lay.z),
            in_specs=[
                pl.BlockSpec(
                    (1, f_loc, d_loc), lambda kt, kz, ids: ((kz ^ ids[0]) * lay.t + kt, 0, 0)
                )
            ]
            * len(stacks),
            out_specs=pl.BlockSpec(
                (count, f_loc, lay.q * d_loc), lambda kt, kz, ids: (0, kt, kz)
            ),
        ),
        cost_estimate=pl.CostEstimate(
            flops=0, bytes_accessed=4 * count * ffe * width, transcendentals=0
        ),
        compiler_params=pltpu.CompilerParams(vmem_limit_bytes=32 << 20),
        name="lay_out_weights",
    )(ids, *stacks)
    return own.reshape(count * ffe, width)


def take_apart(lay, ids, grad_in, grad_out, f_loc, d_loc, width):
    ffe = f_loc * lay.t

    def kernel(ids_ref, in_ref, out_ref, *targets):
        for kc in range(lay.q):
            columns = pl.ds(pl.multiple_of((ids_ref[1] ^ kc) * d_loc, 128), d_loc)
            for g in range(2):
                targets[3 * kc + g][0] = in_ref[g, :, columns]
            targets[3 * kc + 2][0] = out_ref[:, columns]

    shape = jax.ShapeDtypeStruct((lay.t * lay.z, f_loc, d_loc), BF16)
    spec = pl.BlockSpec((1, f_loc, d_loc), lambda kt, kz, ids: (kz * lay.t + kt, 0, 0))
    return pl.pallas_call(
        kernel,
        out_shape=(shape,) * (3 * lay.q),
        grid_spec=pltpu.PrefetchScalarGridSpec(
            num_scalar_prefetch=1,
            grid=(lay.t, lay.z),
            in_specs=[
                pl.BlockSpec((2, f_loc, lay.q * d_loc), lambda kt, kz, ids: (0, kt, kz)),
                pl.BlockSpec((f_loc, lay.q * d_loc), lambda kt, kz, ids: (kt, kz)),
            ],
            out_specs=(spec,) * (3 * lay.q),
        ),
        cost_estimate=pl.CostEstimate(
            flops=0, bytes_accessed=12 * ffe * width, transcendentals=0
        ),
        compiler_params=pltpu.CompilerParams(vmem_limit_bytes=32 << 20),
        name="take_apart",
    )(ids, grad_in.reshape(2, ffe, width), grad_out)


def home_gradients(lay, ids, parts, f_loc, d_loc):
    def kernel(ids_ref, *refs):
        sources, (in_ref, out_ref) = refs[: 3 * lay.t], refs[3 * lay.t :]
        for k in range(lay.t):

            @pl.when((pl.program_id(1) ^ ids_ref[2]) == k)
            def _(k=k):
                for g in range(2):
                    in_ref[0, g] = sources[g * lay.t + k][0].astype(F32)
                out_ref[0] = sources[2 * lay.t + k][0].astype(F32)

    grad_in, grad_out = pl.pallas_call(
        kernel,
        out_shape=(
            jax.ShapeDtypeStruct((EXPERTS, 2, f_loc, d_loc), F32),
            jax.ShapeDtypeStruct((EXPERTS, f_loc, d_loc), F32),
        ),
        grid_spec=pltpu.PrefetchScalarGridSpec(
            num_scalar_prefetch=1,
            grid=(lay.z, lay.t),
            in_specs=[pl.BlockSpec((1, f_loc, d_loc), lambda z, t, ids: (z, 0, 0))] * (3 * lay.t),
            out_specs=(
                pl.BlockSpec((1, 2, f_loc, d_loc), lambda z, t, ids: (z * lay.t + t, 0, 0, 0)),
                pl.BlockSpec((1, f_loc, d_loc), lambda z, t, ids: (z * lay.t + t, 0, 0)),
            ),
        ),
        cost_estimate=pl.CostEstimate(
            flops=0, bytes_accessed=18 * EXPERTS * f_loc * d_loc, transcendentals=0
        ),
        compiler_params=pltpu.CompilerParams(vmem_limit_bytes=32 << 20),
        name="home_gradients",
    )(ids, *[piece for part in parts for piece in part])
    return jnp.swapaxes(grad_in, 2, 3), grad_out


def join_columns(parts, me, count):
    rows, part = parts[0].shape
    block = min(512, rows)

    def kernel(me_ref, *refs):
        for k in range(count):

            @pl.when(pl.program_id(1) == k)
            def _(k=k):
                refs[count][...] = refs[k][...]

    return pl.pallas_call(
        kernel,
        out_shape=jax.ShapeDtypeStruct((rows, count * part), parts[0].dtype),
        grid_spec=pltpu.PrefetchScalarGridSpec(
            num_scalar_prefetch=1,
            grid=(rows // block, count),
            in_specs=[pl.BlockSpec((block, part), lambda i, k, me: (i, 0))] * count,
            out_specs=pl.BlockSpec((block, part), lambda i, k, me: (i, me[0] ^ k)),
        ),
        cost_estimate=pl.CostEstimate(
            flops=0, bytes_accessed=4 * rows * part * count, transcendentals=0
        ),
        name="join_columns",
    )(me.reshape(1).astype(jnp.int32), *parts)


def score_block(q_ref, r_ref, k_ref, kr_ref, head, step, keys, block, length, scale):
    half = r_ref.shape[1] // 2
    lanes = lax.broadcasted_iota(jnp.int32, r_ref.shape, 1) % half // (ROPE // 2)
    turned = jnp.where(lanes == head, r_ref[...], jnp.zeros_like(r_ref))
    raw = lax.dot_general(
        q_ref[...], k_ref[:keys], (((1,), (1,)), ((), ())), preferred_element_type=F32
    ) + lax.dot_general(
        turned, kr_ref[:keys], (((1,), (1,)), ((), ())), preferred_element_type=F32
    )
    rows = lax.broadcasted_iota(jnp.int32, raw.shape, 0) + step * block
    cols = lax.broadcasted_iota(jnp.int32, raw.shape, 1)
    allowed = (cols <= rows) & (cols < length)
    return jnp.where(allowed, raw * scale, NEGATIVE), turned


def attend(length, query, query_rope, kv, key_rope, heads, scale):
    rows = query.shape[0]
    block = min(256, rows)
    steps = rows // block

    def kernel(len_ref, q_ref, r_ref, k_ref, v_ref, kr_ref, o_ref, total_ref):
        head, step = pl.program_id(0), pl.program_id(1)
        for n in range(steps):

            @pl.when(step == n)
            def _(n=n):
                keys = (n + 1) * block
                scores, _ = score_block(
                    q_ref, r_ref, k_ref, kr_ref, head, n, keys, block, len_ref[0], scale
                )
                highest = jnp.max(scores, axis=-1, keepdims=True)
                expo = jnp.exp(scores - highest)
                totals = jnp.sum(expo, axis=-1, keepdims=True)
                weights = (expo * (1.0 / totals)).astype(BF16)
                o_ref[...] = dot(weights, v_ref[:keys]).astype(BF16)
                total_ref[0] = jnp.broadcast_to(highest + jnp.log(totals), (block, 128))

    return pl.pallas_call(
        kernel,
        out_shape=(
            jax.ShapeDtypeStruct((rows, heads * VDIM), BF16),
            jax.ShapeDtypeStruct((heads, rows, 128), F32),
        ),
        grid_spec=pltpu.PrefetchScalarGridSpec(
            num_scalar_prefetch=1,
            grid=(heads, steps),
            in_specs=[
                pl.BlockSpec((block, NOPE), lambda h, i, n: (i, h)),
                pl.BlockSpec((block, query_rope.shape[1]), lambda h, i, n: (i, 0)),
                pl.BlockSpec((rows, NOPE), lambda h, i, n: (0, 2 * h)),
                pl.BlockSpec((rows, VDIM), lambda h, i, n: (0, 2 * h + 1)),
                pl.BlockSpec((rows, key_rope.shape[1]), lambda h, i, n: (0, 0)),
            ],
            out_specs=(
                pl.BlockSpec((block, VDIM), lambda h, i, n: (i, h)),
                pl.BlockSpec((1, block, 128), lambda h, i, n: (h, i, 0)),
            ),
        ),
        cost_estimate=pl.CostEstimate(
            flops=heads * rows * rows * 512,
            bytes_accessed=8 * rows * heads * 512,
            transcendentals=heads * rows * rows,
        ),
        compiler_params=pltpu.CompilerParams(vmem_limit_bytes=32 << 20),
        name="attend",
    )(length, query, query_rope, kv, kv, key_rope)


def attend_back(length, query, query_rope, kv, key_rope, out_grad, log_totals, heads, scale):
    rows = query.shape[0]
    block = min(256, rows)
    steps = rows // block
    turned_cols = query_rope.shape[1]

    def kernel(
        len_ref, q_ref, r_ref, k_ref, v_ref, kr_ref, do_ref, total_ref,
        dq_ref, dr_ref, dkv_ref, dkr_ref, dk_acc, dv_acc,
    ):
        head, step = pl.program_id(0), pl.program_id(1)

        @pl.when(step == 0)
        def _():
            dk_acc[...] = jnp.zeros_like(dk_acc)
            dv_acc[...] = jnp.zeros_like(dv_acc)

        @pl.when((step == 0) & (head == 0))
        def _():
            dr_ref[...] = jnp.zeros_like(dr_ref)
            dkr_ref[...] = jnp.zeros_like(dkr_ref)

        for n in range(steps):

            @pl.when(step == n)
            def _(n=n):
                keys = (n + 1) * block
                scores, turned = score_block(
                    q_ref, r_ref, k_ref, kr_ref, head, n, keys, block, len_ref[0], scale
                )
                probs = jnp.exp(scores - total_ref[0][:, :1])
                prob_grad = lax.dot_general(
                    do_ref[...], v_ref[:keys], (((1,), (1,)), ((), ())), preferred_element_type=F32
                )
                centre = jnp.sum(probs * prob_grad, axis=-1, keepdims=True)
                score_grad = (probs * (prob_grad - centre)).astype(BF16)
                probs_low = probs.astype(BF16)
                dq_ref[...] = (dot(score_grad, k_ref[:keys]) * scale).astype(BF16)
                half = turned_cols // 2
                lanes = lax.broadcasted_iota(jnp.int32, (block, turned_cols), 1)
                lanes = lanes % half // (ROPE // 2)
                turned_grad = dot(score_grad, kr_ref[:keys]) * scale
                dr_ref[n * block : keys] += jnp.where(lanes == head, turned_grad, 0.0)
                dk_acc[:keys] += dot_tn(score_grad, q_ref[...]) * scale
                dkr_ref[:keys] += dot_tn(score_grad, turned) * scale
                dv_acc[:keys] += dot_tn(probs_low, do_ref[...])

        @pl.when(step == steps - 1)
        def _():
            dkv_ref[:, :NOPE] = dk_acc[...].astype(BF16)
            dkv_ref[:, NOPE:] = dv_acc[...].astype(BF16)

    return pl.pallas_call(
        kernel,
        out_shape=(
            jax.ShapeDtypeStruct((rows, heads * NOPE), BF16),
            jax.ShapeDtypeStruct((rows, turned_cols), F32),
            jax.ShapeDtypeStruct((rows, heads * (NOPE + VDIM)), BF16),
            jax.ShapeDtypeStruct((rows, turned_cols), F32),
        ),
        grid_spec=pltpu.PrefetchScalarGridSpec(
            num_scalar_prefetch=1,
            grid=(heads, steps),
            in_specs=[
                pl.BlockSpec((block, NOPE), lambda h, i, n: (i, h)),
                pl.BlockSpec((block, turned_cols), lambda h, i, n: (i, 0)),
                pl.BlockSpec((rows, NOPE), lambda h, i, n: (0, 2 * h)),
                pl.BlockSpec((rows, VDIM), lambda h, i, n: (0, 2 * h + 1)),
                pl.BlockSpec((rows, turned_cols), lambda h, i, n: (0, 0)),
                pl.BlockSpec((block, VDIM), lambda h, i, n: (i, h)),
                pl.BlockSpec((1, block, 128), lambda h, i, n: (h, i, 0)),
            ],
            out_specs=(
                pl.BlockSpec((block, NOPE), lambda h, i, n: (i, h)),
                pl.BlockSpec((rows, turned_cols), lambda h, i, n: (0, 0)),
                pl.BlockSpec((rows, NOPE + VDIM), lambda h, i, n: (0, h)),
                pl.BlockSpec((rows, turned_cols), lambda h, i, n: (0, 0)),
            ),
            scratch_shapes=[pltpu.VMEM((rows, NOPE), F32), pltpu.VMEM((rows, VDIM), F32)],
        ),
        cost_estimate=pl.CostEstimate(
            flops=heads * rows * rows * 1600,
            bytes_accessed=16 * rows * heads * 512,
            transcendentals=heads * rows * rows,
        ),
        compiler_params=pltpu.CompilerParams(vmem_limit_bytes=40 << 20),
        name="attend_back",
    )(length, query, query_rope, kv, kv, key_rope, out_grad, log_totals)


def in_order(values, me, count):
    zero = jnp.zeros_like(values[0])
    ordered = []
    for j in range(count):
        total = zero
        for k in range(count):
            total = jnp.where((me ^ k) == j, values[k], total)
        ordered.append(total)
    return jnp.stack(ordered)


def body(
    lay,
    hidden,
    lengths,
    routes,
    attn_gain,
    w_query,
    w_kv_down,
    kv_gain,
    w_kv_up,
    w_out,
    ffn_gain,
    w_router,
    w_expert_in,
    w_expert_out,
    w_shared_in,
    w_shared_out,
    cotangent,
):
    rows, width = hidden.shape
    nz, nt, nq, ndp = lay.z, lay.t, lay.q, lay.dp
    me_dp = lax.axis_index("dp")
    me_t = lax.axis_index("tensor")
    me_z = me_dp // nq
    me_c = me_dp % nq
    part = width // nt
    d_loc = w_query.shape[0]
    f_loc = w_expert_out.shape[1]
    ffe = f_loc * nt
    heads = w_query.shape[1] // (NOPE + ROPE)
    score_scale = (NOPE + ROPE) ** (-0.5)

    def own_part(values):
        return lax.dynamic_slice_in_dim(values, me_t * part, part, 1)

    def gather_z(values):
        return lax.all_gather(values, "dp", axis=0, tiled=False, axis_index_groups=lay.z_groups)

    def scatter_z(values):
        return lax.psum_scatter(
            values, "dp", scatter_dimension=0, tiled=False, axis_index_groups=lay.z_groups
        )

    def gather_t(values):
        return lax.all_gather(values, "tensor", axis=1, tiled=True)

    def scatter_t(values):
        return lax.psum_scatter(
            values.astype(BF16), "tensor", scatter_dimension=1, tiled=True
        ).astype(F32)

    def swap_t(values):
        return lax.all_to_all(values, "tensor", split_axis=0, concat_axis=0, tiled=True)

    def swap_z(values):
        return lax.all_to_all(
            values,
            "dp",
            split_axis=0,
            concat_axis=0,
            axis_index_groups=lay.z_groups,
            tiled=True,
        )

    def gather_t_direct(values):
        return join_columns([lay.over_t(values, k) for k in range(nt)], me_t, nt)

    def part_for(values, k):
        return lax.dynamic_slice_in_dim(values, (me_t ^ k) * part, part, 1)

    def scatter_t_direct(values):
        total = part_for(values, 0)
        for k in range(1, nt):
            total = total + lay.over_t(part_for(values, k).astype(BF16), k).astype(F32)
        return total

    ids = jnp.stack([me_z, me_c, me_t]).astype(jnp.int32)

    packed = jnp.concatenate(
        [jnp.swapaxes(w_expert_in, 2, 3), w_expert_out[:, None]], 1
    ).reshape(nz, nt, 3, f_loc, d_loc)
    by_column = swap_t(jnp.swapaxes(packed, 0, 1))

    lat_loc = kv_gain.shape[0]
    q_rows, down_rows, out_rows = w_query.shape[1], w_kv_down.shape[1], w_out.shape[0]
    half = ROPE // 2

    def by_kind(turned):
        split = turned.reshape(heads, NOPE + ROPE, -1)
        return jnp.concatenate(
            [
                split[:, :NOPE].reshape(heads * NOPE, -1),
                split[:, NOPE : NOPE + half].reshape(heads * half, -1),
                split[:, NOPE + half :].reshape(heads * half, -1),
            ],
            0,
        )

    def by_head(rows_in):
        nope = rows_in[: heads * NOPE].reshape(heads, NOPE, -1)
        first = rows_in[heads * NOPE : heads * (NOPE + half)].reshape(heads, half, -1)
        second = rows_in[heads * (NOPE + half) :].reshape(heads, half, -1)
        return jnp.concatenate([nope, first, second], 1).reshape(heads * (NOPE + ROPE), -1)

    gains = jnp.stack([attn_gain, ffn_gain, jnp.pad(kv_gain, (0, d_loc - lat_loc))])
    front_pack = jnp.concatenate(
        [
            by_kind(jnp.transpose(w_query)),
            jnp.transpose(w_kv_down),
            jnp.transpose(w_router),
            jnp.pad(gains, ((0, 13), (0, 0))),
            w_out,
            w_kv_up.reshape(-1, d_loc),
        ],
        0,
    )
    front = lax.all_gather(front_pack, "dp", axis=0, tiled=False)

    valid_length = lengths[0]
    valid_rows = lax.broadcasted_iota(jnp.int32, (rows, 1), 0) < valid_length
    cot_low = jnp.where(valid_rows, cotangent, jnp.zeros_like(cotangent))
    cot_part = own_part(cot_low)
    route_own = jnp.pad(jnp.transpose(routes), ((0, -TOP % 8), (0, 0)), constant_values=-1)
    route_all = in_order([lay.over_z(route_own, k) for k in range(nz)], me_z, nz)
    inputs = hidden.astype(F32)
    attn_inverse = inverse_rms(inputs)
    cosine, sine = angle_tables(rows)
    wide_cos, wide_sin = jnp.tile(cosine, (1, heads)), jnp.tile(sine, (1, heads))
    front, attn_inverse, wide_cos, wide_sin, route_all = lax.optimization_barrier(
        (front, attn_inverse, wide_cos, wide_sin, route_all)
    )

    plane_ids = me_z * nt + jnp.arange(nt, dtype=jnp.int32)
    member = jnp.any(route_all[:, :, :, None] == plane_ids[None, None, None, :], axis=1)
    row_ids = lax.broadcasted_iota(jnp.int32, (rows, rows), 0)
    col_ids = lax.broadcasted_iota(jnp.int32, (rows, rows), 1)
    before = (col_ids < row_ids).astype(BF16)
    position = jnp.einsum("ij,sje->sei", before, member.astype(BF16), preferred_element_type=F32)
    key = jnp.where(jnp.swapaxes(member, 1, 2), position.astype(jnp.int32), -1)
    slots_iota = lax.broadcasted_iota(jnp.int32, (1, 1, CAP, 1), 2)

    def place_of(keys):
        return (keys[:, :, None, :] == slots_iota).astype(BF16)

    place = place_of(key)
    own_key = lax.dynamic_index_in_dim(key, me_t, 1, keepdims=False)
    own_place = own_key[:, None, :] == slots_iota[0]

    def pick_rows(values):
        picked = jnp.einsum("sepk,skd->espd", place, values, preferred_element_type=F32)
        return picked.astype(BF16).reshape(nt, nz * CAP, part)

    def send_out(picked):
        return jnp.swapaxes(swap_t(picked), 0, 1).reshape(nz * CAP, width)

    def send_back(values):
        return swap_t(jnp.swapaxes(values.reshape(nz * CAP, nt, part), 0, 1))

    def combine(parts):
        parts = parts.reshape(nt, nz, CAP, part)
        summed = jnp.einsum("sepk,espd->skd", place, parts, preferred_element_type=F32)
        return summed.astype(BF16)


    def rows_of(first, count):
        return jnp.swapaxes(front[:, first : first + count], 0, 1).reshape(count, width)

    query_t = rows_of(0, q_rows)
    down_t = rows_of(q_rows, down_rows)
    at = q_rows + down_rows
    router_t = rows_of(at, EXPERTS)
    gain_attn = front[:, at + EXPERTS].reshape(-1)
    gain_ffn = front[:, at + EXPERTS + 1].reshape(-1)
    gain_kv = front[:, at + EXPERTS + 2, :lat_loc].reshape(-1)
    at = at + 2 * EXPERTS
    out_w = rows_of(at, out_rows)
    up_w = front[:, at + out_rows :].reshape(LATENT, heads * (NOPE + VDIM))

    attn_scale = gain_attn.astype(F32)
    normed_low = (inputs * attn_inverse * attn_scale).astype(BF16)
    query = dot_nt(normed_low, query_t)
    nope_cols = heads * NOPE
    query_nope = query[:, :nope_cols].astype(BF16)
    query_rope = jnp.concatenate(
        rotate(
            query[:, nope_cols : nope_cols + heads * half],
            query[:, nope_cols + heads * half :],
            wide_cos,
            wide_sin,
        ),
        1,
    ).astype(BF16)
    latent_all = dot_nt(normed_low, down_t)
    latent_all, by_column = lax.optimization_barrier((latent_all, by_column))
    by_column = jnp.transpose(by_column, (2, 1, 0, 3, 4))
    by_plane = [swap_z(by_column[g]) for g in range(2)]
    latent = latent_all[:, :LATENT]
    kv_inverse = inverse_rms(latent)
    latent_hat = latent * kv_inverse
    kv_scale = gain_kv.astype(F32)
    latent_low = (latent_hat * kv_scale).astype(BF16)
    key_turned = jnp.concatenate(
        rotate(
            latent_all[:, LATENT : LATENT + half],
            latent_all[:, LATENT + half :],
            wide_cos[:, :half],
            wide_sin[:, :half],
        ),
        1,
    ).astype(BF16)
    copies = (2 * half, 2 * heads * half)
    to_col = lax.broadcasted_iota(jnp.int32, copies, 1)
    from_col = to_col // (heads * half) * half + to_col % half
    repeat = (lax.broadcasted_iota(jnp.int32, copies, 0) == from_col).astype(BF16)
    key_rope = dot(key_turned, repeat).astype(BF16)
    keys_values = dot(latent_low, up_w).astype(BF16)
    attended_low, log_totals = attend(
        lengths, query_nope, query_rope, keys_values, key_rope, heads, score_scale
    )
    attn_part, by_plane[0] = lax.optimization_barrier((dot(attended_low, out_w), by_plane[0]))
    attn_sum = scatter_t(attn_part)
    residual = own_part(hidden).astype(F32) + attn_sum

    def row_mean(values):
        partial = jnp.sum(values, axis=-1).reshape(-1, 128)
        return lax.psum(partial, "tensor").reshape(-1, 1) * (1.0 / width)

    ffn_inverse = lax.rsqrt(row_mean(residual * residual) + EPSILON)
    ffn_hat = residual * ffn_inverse
    ffn_scale = lax.dynamic_slice_in_dim(gain_ffn, me_t * part, part, 0).astype(F32)
    ffn_part = (ffn_hat * ffn_scale).astype(BF16)

    ffn_part, by_plane[1] = lax.optimization_barrier((ffn_part, by_plane[1]))
    ffn_all = gather_z(ffn_part)
    ffn_low = gather_t_direct(ffn_part)
    ffn_all, ffn_low, cot_ready = lax.optimization_barrier((ffn_all, ffn_low, cot_part))
    picked, by_plane[0], by_plane[1] = lax.optimization_barrier(
        (pick_rows(ffn_all), by_plane[0], by_plane[1])
    )
    expert_rows = send_out(picked)
    shared_pack = jnp.concatenate(
        [jnp.swapaxes(w_shared_in, 1, 2).reshape(-1, d_loc), w_shared_out], 0
    )
    def own_weights(matrices, order):
        pieces = [by_plane[g].reshape(nz * nt, f_loc, d_loc) for g in matrices]
        stacks = [lay.over_c(piece, k) for k in range(nq) for piece in pieces]
        return lay_out_weights(lay, order, stacks, f_loc, d_loc, width)

    own_in = own_weights((0, 1), ids * jnp.array([0, 1, 1], jnp.int32))
    cot_all, last_column, own_in = lax.optimization_barrier(
        (gather_z(cot_ready), by_column[2], own_in)
    )
    by_plane.append(
        jnp.stack(
            [
                lay.over_z(lax.dynamic_index_in_dim(last_column, me_z ^ k, 0, keepdims=False), k)
                for k in range(nz)
            ]
        )
    )

    by_plane[2], shared_pack, cot_picked = lax.optimization_barrier(
        (by_plane[2], shared_pack, pick_rows(cot_all))
    )
    cot_rows = send_out(cot_picked)
    shared_all = lax.all_gather(shared_pack, "dp", axis=0, tiled=False)
    own_out = own_weights((2,), ids)
    router_probs = jax.nn.softmax(dot_nt(ffn_low, router_t), axis=-1)
    probs_turned = jnp.transpose(router_probs).reshape(EXPERTS, -1, 128)
    own_probs = in_order(
        [
            lay.over_z(
                lax.dynamic_index_in_dim(
                    probs_turned, (me_z ^ k) * nt + me_t, 0, keepdims=False
                ),
                k,
            )
            for k in range(nz)
        ],
        me_z,
        nz,
    ).reshape(nz, rows)
    gate_rows = jnp.sum(jnp.where(own_place, own_probs[:, None, :], 0.0), axis=-1).reshape(
        nz * CAP, 1
    )
    gate_up = dot_nt(expert_rows, own_in)
    gate_pre, up_pre = gate_up[:, :ffe], gate_up[:, ffe:]
    gate_sig = jax.nn.sigmoid(gate_pre)
    gate_silu = gate_pre * gate_sig
    active = (gate_silu * up_pre).astype(BF16)
    rows_out = (dot(active, own_out) * gate_rows).astype(BF16)
    rows_out, cot_rows, shared_all = lax.optimization_barrier((rows_out, cot_rows, shared_all))
    out_parts = send_back(rows_out)
    active_grad_raw = dot_nt(cot_rows, own_out)
    gate_grad = jnp.sum(active.astype(F32) * active_grad_raw, axis=-1).reshape(nz, CAP)
    active_grad = active_grad_raw * gate_rows
    pre_low = jnp.concatenate(
        [
            active_grad * up_pre * gate_sig * (1.0 + gate_pre * (1.0 - gate_sig)),
            active_grad * gate_silu,
        ],
        1,
    ).astype(BF16)
    gated_active = (active.astype(F32) * gate_rows).astype(BF16)
    ffs = w_shared_out.shape[0]
    shared_in = jnp.swapaxes(shared_all[:, : 2 * ffs], 0, 1).reshape(2 * ffs, width)
    shared_out = jnp.swapaxes(shared_all[:, 2 * ffs :], 0, 1).reshape(ffs, width)
    shared_pre = dot_nt(ffn_low, shared_in)
    shared_gate, shared_up = shared_pre[:, :ffs], shared_pre[:, ffs:]
    shared_sig = jax.nn.sigmoid(shared_gate)
    shared_silu = shared_gate * shared_sig
    shared_act = (shared_silu * shared_up).astype(BF16)
    shared_full = dot(shared_act, shared_out)
    shared_act_grad = dot_nt(cot_low, shared_out)
    shared_pre_grad = jnp.concatenate(
        [
            shared_act_grad * shared_up * shared_sig * (1.0 + shared_gate * (1.0 - shared_sig)),
            shared_act_grad * shared_silu,
        ],
        1,
    ).astype(BF16)
    grad_shared_in = dot_tn(shared_pre_grad, ffn_low)
    grad_shared_out = dot_tn(shared_act, cot_low)
    shared_grad_full = dot(shared_pre_grad, shared_in)

    out_parts, pre_low, shared_full = lax.optimization_barrier((out_parts, pre_low, shared_full))
    rows_grad = dot(pre_low, own_in).astype(BF16)
    rows_grad, out_parts = lax.optimization_barrier((rows_grad, out_parts))
    grad_parts = send_back(rows_grad)
    routed, pre_low, gated_active, shared_part = lax.optimization_barrier(
        (combine(out_parts), pre_low, gated_active, scatter_t(shared_full))
    )
    routed = scatter_z(routed).astype(F32)
    token_grad = jnp.sum(jnp.where(own_place, gate_grad[:, :, None], 0.0), axis=1)
    token_grad = token_grad.reshape(nz, -1, 128)
    token_plane = jnp.stack(
        [
            lay.over_z(lax.dynamic_index_in_dim(token_grad, me_z ^ k, 0, keepdims=False), k)
            for k in range(nz)
        ]
    )
    token_home = jnp.stack([lay.over_t(token_plane, k) for k in range(nt)])
    experts = jnp.arange(EXPERTS, dtype=jnp.int32)
    came_from = (me_t ^ (experts % nt)) * nz + (me_z ^ (experts // nt))
    probs_grad = lax.dot_general(
        token_home.reshape(EXPERTS, rows),
        (experts[:, None] == came_from[None, :]).astype(F32),
        (((0,), (0,)), ((), ())),
        precision=lax.Precision.HIGHEST,
        preferred_element_type=F32,
    )

    grad_in_own = dot_tn(pre_low, expert_rows).astype(BF16)
    grad_out_own = dot_tn(gated_active, cot_rows).astype(BF16)
    (
        grad_parts,
        grad_in_own,
        grad_out_own,
        routed,
        probs_grad,
        shared_grad_full,
    ) = lax.optimization_barrier(
        (grad_parts, grad_in_own, grad_out_own, routed, probs_grad, shared_grad_full)
    )
    shared_grad = swap_t(
        jnp.swapaxes(shared_grad_full.astype(BF16).reshape(rows, nt, part), 0, 1)
    )
    shared_grad = jnp.sum(shared_grad.astype(F32), axis=0)
    grad_pieces = take_apart(lay, ids, grad_in_own, grad_out_own, f_loc, d_loc, width)
    routed_grad = scatter_z(combine(grad_parts)).astype(F32)
    grad_class = [
        sum(lay.over_c(grad_pieces[3 * k + g], k).astype(F32) for k in range(nq)).astype(BF16)
        for g in range(3)
    ]
    routed_grad, grad_class = lax.optimization_barrier((routed_grad, grad_class))
    grad_plane = [swap_z(grad_class[g].reshape(nz, nt, f_loc, d_loc)) for g in range(3)]

    logits_grad = router_probs * (
        probs_grad - jnp.sum(router_probs * probs_grad, axis=-1, keepdims=True)
    )
    router_part = lax.dot_general(
        logits_grad,
        ffn_low.astype(F32),
        (((0,), (0,)), ((), ())),
        precision=lax.Precision.HIGHEST,
        preferred_element_type=F32,
    )
    router_slice = lax.dynamic_slice_in_dim(router_t, me_t * part, part, 1)
    ffn_grad = (
        shared_grad
        + routed_grad
        + lax.dot_general(
            logits_grad,
            router_slice.astype(F32),
            (((1,), (0,)), ((), ())),
            precision=lax.Precision.HIGHEST,
            preferred_element_type=F32,
        )
    )
    scaled = ffn_scale * ffn_grad
    ffn_gain_part = jnp.sum(ffn_grad * ffn_hat, axis=0)
    residual_grad = cot_part.astype(F32) + ffn_inverse * (
        scaled - ffn_hat * row_mean(ffn_hat * scaled)
    )
    residual_low = gather_t(residual_grad.astype(BF16))

    def sum_dp(values):
        return lax.psum_scatter(values, "dp", scatter_dimension=0, tiled=False).astype(F32)

    def by_owner(values):
        return jnp.swapaxes(values.astype(BF16).reshape(-1, ndp, d_loc), 0, 1)

    shared_grads = jnp.concatenate([by_owner(grad_shared_in), by_owner(grad_shared_out)], 1)
    output_part = lax.optimization_barrier((residual + routed + shared_part).astype(BF16))
    residual_low, shared_grads, grad_plane[0], output_part = lax.optimization_barrier(
        (residual_low, shared_grads, grad_plane[0], output_part)
    )
    grad_out_w = dot_tn(attended_low, residual_low)
    attended_grad = dot_nt(residual_low, out_w).astype(BF16)
    query_nope_grad, query_turned_grad, kv_grad, rope_grad = attend_back(
        lengths,
        query_nope,
        query_rope,
        keys_values,
        key_rope,
        attended_grad,
        log_totals,
        heads,
        score_scale,
    )
    def to_columns(values):
        return [
            lay.over_t(lax.dynamic_index_in_dim(values, me_t ^ k, 1, keepdims=False), k)
            for k in range(nt)
        ]

    grad_home = [to_columns(grad_plane[0]), None, None]
    query_turned_grad, grad_plane[1], grad_home[0], shared_grads = lax.optimization_barrier(
        (query_turned_grad, grad_plane[1], grad_home[0], shared_grads)
    )
    shared_sum = sum_dp(shared_grads)
    turned_first, turned_second = rotate_back(
        query_turned_grad[:, : heads * half], query_turned_grad[:, heads * half :], wide_cos, wide_sin
    )
    query_grad = jnp.concatenate(
        [query_nope_grad, turned_first.astype(BF16), turned_second.astype(BF16)], 1
    )
    rope_sum = rope_grad.reshape(rows, 2, heads, half).sum(2)
    key_rope_part = jnp.concatenate(
        rotate_back(
            rope_sum[:, 0], rope_sum[:, 1], wide_cos[:, :half], wide_sin[:, :half]
        ),
        1,
    )
    latent_part = dot_nt(kv_grad, up_w)
    grad_kv_gain = jnp.sum(latent_part * latent_hat, axis=0)
    scaled_kv = kv_scale * latent_part
    latent_back = kv_inverse * (
        scaled_kv - latent_hat * jnp.mean(latent_hat * scaled_kv, axis=-1, keepdims=True)
    )
    down_grad = jnp.concatenate([latent_back, key_rope_part], -1).astype(BF16)
    normed_full, output = lax.optimization_barrier(
        (dot(query_grad, query_t) + dot(down_grad, down_t), gather_t(output_part))
    )
    normed_grad, grad_plane[2], grad_home[1] = lax.optimization_barrier(
        (scatter_t_direct(normed_full), grad_plane[2], to_columns(grad_plane[1]))
    )
    attn_hat = own_part(hidden).astype(F32) * attn_inverse
    scaled_in = lax.dynamic_slice_in_dim(attn_scale, me_t * part, part, 0) * normed_grad
    attn_gain_part = jnp.sum(normed_grad * attn_hat, axis=0)
    input_grad = residual_grad + attn_inverse * (
        scaled_in - attn_hat * row_mean(attn_hat * scaled_in)
    )
    input_low, grad_plane[2], query_grad, kv_grad, down_grad = lax.optimization_barrier(
        (input_grad.astype(BF16), grad_plane[2], query_grad, kv_grad, down_grad)
    )
    grad_home[2] = to_columns(grad_plane[2])
    grad_expert_in, grad_expert_out = home_gradients(lay, ids, grad_home, f_loc, d_loc)
    grad_hidden = gather_t_direct(input_low)

    def spread(values):
        return lax.dynamic_update_slice(
            jnp.zeros((1, width), F32), values[None], (jnp.int32(0), me_t * part)
        )

    kv_gain_row = jnp.pad(
        grad_kv_gain.reshape(ndp, lat_loc), ((0, 0), (0, d_loc - lat_loc))
    ).reshape(1, width)
    gain_grads = jnp.concatenate([spread(ffn_gain_part), kv_gain_row], 0)
    attn_sum_all = lax.psum(spread(attn_gain_part).reshape(-1, 128), ("dp", "tensor"))
    attn_gain_grad = lax.dynamic_slice_in_dim(attn_sum_all.reshape(-1), me_dp * d_loc, d_loc, 0)
    front_sum = sum_dp(
        jnp.concatenate(
            [
                by_owner(dot_tn(down_grad, normed_low)),
                by_owner(jnp.pad(gain_grads, ((0, 14), (0, 0)))),
                by_owner(router_part),
                by_owner(dot_tn(query_grad, normed_low)),
                by_owner(grad_out_w),
                dot_tn(latent_low, kv_grad).astype(BF16).reshape(ndp, -1, d_loc),
            ],
            1,
        )
    )
    own_sum = front_sum[: down_rows + EXPERTS]
    own_low = own_sum.astype(BF16)
    for k in range(1, nt):
        own_sum = own_sum + lay.over_t(own_low, k).astype(F32)
    at = down_rows + 2 * EXPERTS
    return (
        output,
        grad_hidden,
        attn_gain_grad,
        jnp.transpose(by_head(front_sum[at : at + q_rows])),
        jnp.transpose(own_sum[:down_rows]),
        own_sum[down_rows + 1, :lat_loc],
        front_sum[at + q_rows + out_rows :].reshape(w_kv_up.shape),
        front_sum[at + q_rows : at + q_rows + out_rows],
        own_sum[down_rows],
        jnp.transpose(front_sum[down_rows + EXPERTS : at]),
        grad_expert_in,
        grad_expert_out,
        jnp.swapaxes(shared_sum[: 2 * ffs].reshape(2, ffs, d_loc), 1, 2),
        shared_sum[2 * ffs :],
    )


def solution(mesh):
    return jax.shard_map(
        functools.partial(body, Layout(mesh.shape["dp"], mesh.shape["tensor"])),
        mesh=mesh,
        in_specs=(
            P("dp", None),
            P("dp"),
            P("dp", None),
            P("dp"),
            P("dp", "tensor"),
            P("dp", None),
            P("dp"),
            P("dp", "tensor"),
            P("tensor", "dp"),
            P("dp"),
            P("dp", None),
            P(None, None, "dp", "tensor"),
            P(None, "tensor", "dp"),
            P(None, "dp", "tensor"),
            P("tensor", "dp"),
            P("dp", None),
        ),
        out_specs=(
            P("dp", None),
            P("dp", None),
            P("dp"),
            P("dp", "tensor"),
            P("dp", None),
            P("dp"),
            P("dp", "tensor"),
            P("tensor", "dp"),
            P("dp"),
            P("dp", None),
            P(None, None, "dp", "tensor"),
            P(None, "tensor", "dp"),
            P(None, "dp", "tensor"),
            P("tensor", "dp"),
        ),
        check_vma=False,
    )
```

```python
import functools
import math

import jax
import jax.numpy as jnp
from jax import lax
from jax.experimental import pallas as pl
from jax.experimental.pallas import tpu as pltpu
from jax.sharding import PartitionSpec as P

NOPE = 128
ROPE = 64
VDIM = 128
LATENT = 512
TOP = 6
EXPERTS = 16
CAP = 512

EPSILON = 1e-06
NEGATIVE = -1e30
F32 = jnp.float32
BF16 = jnp.bfloat16


def dot(a, b):
    return jnp.dot(a, b, preferred_element_type=F32)


def dot_nt(a, b):
    return lax.dot_general(a, b, (((1,), (1,)), ((), ())), preferred_element_type=F32)


def dot_tn(a, b):
    return lax.dot_general(a, b, (((0,), (0,)), ((), ())), preferred_element_type=F32)


def rotate(first, second, cosine, sine):
    return first * cosine - second * sine, second * cosine + first * sine


def rotate_back(first, second, cosine, sine):
    return first * cosine + second * sine, second * cosine - first * sine


def angle_tables(rows_count):
    positions = jnp.arange(rows_count, dtype=F32)
    freqs = jnp.exp(jnp.arange(ROPE // 2, dtype=F32) * (-2.0 * math.log(10000.0) / ROPE))
    angles = positions[:, None] * freqs[None, :]
    return (jnp.cos(angles), jnp.sin(angles))


def inverse_rms(values):
    return lax.rsqrt(jnp.mean(values * values, axis=-1, keepdims=True) + EPSILON)


class Layout:
    def __init__(self, n_dp, n_tensor):
        self.dp, self.t = n_dp, n_tensor
        self.q = n_dp * n_tensor // EXPERTS
        self.z = n_dp // self.q
        if self.z * self.t != EXPERTS or self.z * self.q != n_dp:
            raise ValueError("mesh")
        self.z_groups = [[c + self.q * z for z in range(self.z)] for c in range(self.q)]

    def over_t(self, values, k):
        if k == 0:
            return values
        return lax.ppermute(values, "tensor", [(i, i ^ k) for i in range(self.t)])

    def over_z(self, values, k):
        if k == 0:
            return values
        return lax.ppermute(values, "dp", [(d, d ^ (k * self.q)) for d in range(self.dp)])

    def over_c(self, values, k):
        if k == 0:
            return values
        return lax.ppermute(values, "dp", [(d, d ^ k) for d in range(self.dp)])


def lay_out_weights(lay, ids, stacks, f_loc, d_loc, width):
    ffe = f_loc * lay.t
    count = len(stacks) // lay.q

    def kernel(ids_ref, *refs):
        for kc in range(lay.q):
            columns = pl.ds(pl.multiple_of((ids_ref[1] ^ kc) * d_loc, 128), d_loc)
            for g in range(count):
                refs[-1][g, :, columns] = refs[count * kc + g][0]

    own = pl.pallas_call(
        kernel,
        out_shape=jax.ShapeDtypeStruct((count, ffe, width), BF16),
        grid_spec=pltpu.PrefetchScalarGridSpec(
            num_scalar_prefetch=1,
            grid=(lay.t, lay.z),
            in_specs=[
                pl.BlockSpec(
                    (1, f_loc, d_loc), lambda kt, kz, ids: ((kz ^ ids[0]) * lay.t + kt, 0, 0)
                )
            ]
            * len(stacks),
            out_specs=pl.BlockSpec(
                (count, f_loc, lay.q * d_loc), lambda kt, kz, ids: (0, kt, kz)
            ),
        ),
        cost_estimate=pl.CostEstimate(
            flops=0, bytes_accessed=4 * count * ffe * width, transcendentals=0
        ),
        compiler_params=pltpu.CompilerParams(vmem_limit_bytes=32 << 20),
        name="lay_out_weights",
    )(ids, *stacks)
    return own.reshape(count * ffe, width)


def take_apart(lay, ids, grad_in, grad_out, f_loc, d_loc, width):
    ffe = f_loc * lay.t

    def kernel(ids_ref, in_ref, out_ref, *targets):
        for kc in range(lay.q):
            columns = pl.ds(pl.multiple_of((ids_ref[1] ^ kc) * d_loc, 128), d_loc)
            for g in range(2):
                targets[3 * kc + g][0] = in_ref[g, :, columns]
            targets[3 * kc + 2][0] = out_ref[:, columns]

    shape = jax.ShapeDtypeStruct((lay.t * lay.z, f_loc, d_loc), BF16)
    spec = pl.BlockSpec((1, f_loc, d_loc), lambda kt, kz, ids: (kz * lay.t + kt, 0, 0))
    return pl.pallas_call(
        kernel,
        out_shape=(shape,) * (3 * lay.q),
        grid_spec=pltpu.PrefetchScalarGridSpec(
            num_scalar_prefetch=1,
            grid=(lay.t, lay.z),
            in_specs=[
                pl.BlockSpec((2, f_loc, lay.q * d_loc), lambda kt, kz, ids: (0, kt, kz)),
                pl.BlockSpec((f_loc, lay.q * d_loc), lambda kt, kz, ids: (kt, kz)),
            ],
            out_specs=(spec,) * (3 * lay.q),
        ),
        cost_estimate=pl.CostEstimate(
            flops=0, bytes_accessed=12 * ffe * width, transcendentals=0
        ),
        compiler_params=pltpu.CompilerParams(vmem_limit_bytes=32 << 20),
        name="take_apart",
    )(ids, grad_in.reshape(2, ffe, width), grad_out)


def home_gradients(lay, ids, parts, f_loc, d_loc):
    def kernel(ids_ref, *refs):
        sources, (in_ref, out_ref) = refs[: 3 * lay.t], refs[3 * lay.t :]
        for k in range(lay.t):

            @pl.when((pl.program_id(1) ^ ids_ref[2]) == k)
            def _(k=k):
                for g in range(2):
                    in_ref[0, g] = sources[g * lay.t + k][0].astype(F32)
                out_ref[0] = sources[2 * lay.t + k][0].astype(F32)

    grad_in, grad_out = pl.pallas_call(
        kernel,
        out_shape=(
            jax.ShapeDtypeStruct((EXPERTS, 2, f_loc, d_loc), F32),
            jax.ShapeDtypeStruct((EXPERTS, f_loc, d_loc), F32),
        ),
        grid_spec=pltpu.PrefetchScalarGridSpec(
            num_scalar_prefetch=1,
            grid=(lay.z, lay.t),
            in_specs=[pl.BlockSpec((1, f_loc, d_loc), lambda z, t, ids: (z, 0, 0))] * (3 * lay.t),
            out_specs=(
                pl.BlockSpec((1, 2, f_loc, d_loc), lambda z, t, ids: (z * lay.t + t, 0, 0, 0)),
                pl.BlockSpec((1, f_loc, d_loc), lambda z, t, ids: (z * lay.t + t, 0, 0)),
            ),
        ),
        cost_estimate=pl.CostEstimate(
            flops=0, bytes_accessed=18 * EXPERTS * f_loc * d_loc, transcendentals=0
        ),
        compiler_params=pltpu.CompilerParams(vmem_limit_bytes=32 << 20),
        name="home_gradients",
    )(ids, *[piece for part in parts for piece in part])
    return jnp.swapaxes(grad_in, 2, 3), grad_out


def join_columns(parts, me, count):
    rows, part = parts[0].shape
    block = min(512, rows)

    def kernel(me_ref, *refs):
        for k in range(count):

            @pl.when(pl.program_id(1) == k)
            def _(k=k):
                refs[count][...] = refs[k][...]

    return pl.pallas_call(
        kernel,
        out_shape=jax.ShapeDtypeStruct((rows, count * part), parts[0].dtype),
        grid_spec=pltpu.PrefetchScalarGridSpec(
            num_scalar_prefetch=1,
            grid=(rows // block, count),
            in_specs=[pl.BlockSpec((block, part), lambda i, k, me: (i, 0))] * count,
            out_specs=pl.BlockSpec((block, part), lambda i, k, me: (i, me[0] ^ k)),
        ),
        cost_estimate=pl.CostEstimate(
            flops=0, bytes_accessed=4 * rows * part * count, transcendentals=0
        ),
        name="join_columns",
    )(me.reshape(1).astype(jnp.int32), *parts)


def score_block(q_ref, r_ref, k_ref, kr_ref, head, step, keys, block, length, scale):
    half = r_ref.shape[1] // 2
    lanes = lax.broadcasted_iota(jnp.int32, r_ref.shape, 1) % half // (ROPE // 2)
    turned = jnp.where(lanes == head, r_ref[...], jnp.zeros_like(r_ref))
    raw = lax.dot_general(
        q_ref[...], k_ref[:keys], (((1,), (1,)), ((), ())), preferred_element_type=F32
    ) + lax.dot_general(
        turned, kr_ref[:keys], (((1,), (1,)), ((), ())), preferred_element_type=F32
    )
    rows = lax.broadcasted_iota(jnp.int32, raw.shape, 0) + step * block
    cols = lax.broadcasted_iota(jnp.int32, raw.shape, 1)
    allowed = (cols <= rows) & (cols < length)
    return jnp.where(allowed, raw * scale, NEGATIVE), turned


def attend(length, query, query_rope, kv, key_rope, heads, scale):
    rows = query.shape[0]
    block = min(256, rows)
    steps = rows // block

    def kernel(len_ref, q_ref, r_ref, k_ref, v_ref, kr_ref, o_ref, total_ref):
        head, step = pl.program_id(0), pl.program_id(1)
        for n in range(steps):

            @pl.when(step == n)
            def _(n=n):
                keys = (n + 1) * block
                scores, _ = score_block(
                    q_ref, r_ref, k_ref, kr_ref, head, n, keys, block, len_ref[0], scale
                )
                highest = jnp.max(scores, axis=-1, keepdims=True)
                expo = jnp.exp(scores - highest)
                totals = jnp.sum(expo, axis=-1, keepdims=True)
                weights = (expo * (1.0 / totals)).astype(BF16)
                o_ref[...] = dot(weights, v_ref[:keys]).astype(BF16)
                total_ref[0] = jnp.broadcast_to(highest + jnp.log(totals), (block, 128))

    return pl.pallas_call(
        kernel,
        out_shape=(
            jax.ShapeDtypeStruct((rows, heads * VDIM), BF16),
            jax.ShapeDtypeStruct((heads, rows, 128), F32),
        ),
        grid_spec=pltpu.PrefetchScalarGridSpec(
            num_scalar_prefetch=1,
            grid=(heads, steps),
            in_specs=[
                pl.BlockSpec((block, NOPE), lambda h, i, n: (i, h)),
                pl.BlockSpec((block, query_rope.shape[1]), lambda h, i, n: (i, 0)),
                pl.BlockSpec((rows, NOPE), lambda h, i, n: (0, 2 * h)),
                pl.BlockSpec((rows, VDIM), lambda h, i, n: (0, 2 * h + 1)),
                pl.BlockSpec((rows, key_rope.shape[1]), lambda h, i, n: (0, 0)),
            ],
            out_specs=(
                pl.BlockSpec((block, VDIM), lambda h, i, n: (i, h)),
                pl.BlockSpec((1, block, 128), lambda h, i, n: (h, i, 0)),
            ),
        ),
        cost_estimate=pl.CostEstimate(
            flops=heads * rows * rows * 512,
            bytes_accessed=8 * rows * heads * 512,
            transcendentals=heads * rows * rows,
        ),
        compiler_params=pltpu.CompilerParams(vmem_limit_bytes=32 << 20),
        name="attend",
    )(length, query, query_rope, kv, kv, key_rope)


def attend_back(length, query, query_rope, kv, key_rope, out_grad, log_totals, heads, scale):
    rows = query.shape[0]
    block = min(256, rows)
    steps = rows // block
    turned_cols = query_rope.shape[1]

    def kernel(
        len_ref, q_ref, r_ref, k_ref, v_ref, kr_ref, do_ref, total_ref,
        dq_ref, dr_ref, dkv_ref, dkr_ref, dk_acc, dv_acc,
    ):
        head, step = pl.program_id(0), pl.program_id(1)

        @pl.when(step == 0)
        def _():
            dk_acc[...] = jnp.zeros_like(dk_acc)
            dv_acc[...] = jnp.zeros_like(dv_acc)

        @pl.when((step == 0) & (head == 0))
        def _():
            dr_ref[...] = jnp.zeros_like(dr_ref)
            dkr_ref[...] = jnp.zeros_like(dkr_ref)

        for n in range(steps):

            @pl.when(step == n)
            def _(n=n):
                keys = (n + 1) * block
                scores, turned = score_block(
                    q_ref, r_ref, k_ref, kr_ref, head, n, keys, block, len_ref[0], scale
                )
                probs = jnp.exp(scores - total_ref[0][:, :1])
                prob_grad = lax.dot_general(
                    do_ref[...], v_ref[:keys], (((1,), (1,)), ((), ())), preferred_element_type=F32
                )
                centre = jnp.sum(probs * prob_grad, axis=-1, keepdims=True)
                score_grad = (probs * (prob_grad - centre)).astype(BF16)
                probs_low = probs.astype(BF16)
                dq_ref[...] = (dot(score_grad, k_ref[:keys]) * scale).astype(BF16)
                half = turned_cols // 2
                lanes = lax.broadcasted_iota(jnp.int32, (block, turned_cols), 1)
                lanes = lanes % half // (ROPE // 2)
                turned_grad = dot(score_grad, kr_ref[:keys]) * scale
                dr_ref[n * block : keys] += jnp.where(lanes == head, turned_grad, 0.0)
                dk_acc[:keys] += dot_tn(score_grad, q_ref[...]) * scale
                dkr_ref[:keys] += dot_tn(score_grad, turned) * scale
                dv_acc[:keys] += dot_tn(probs_low, do_ref[...])

        @pl.when(step == steps - 1)
        def _():
            dkv_ref[:, :NOPE] = dk_acc[...].astype(BF16)
            dkv_ref[:, NOPE:] = dv_acc[...].astype(BF16)

    return pl.pallas_call(
        kernel,
        out_shape=(
            jax.ShapeDtypeStruct((rows, heads * NOPE), BF16),
            jax.ShapeDtypeStruct((rows, turned_cols), F32),
            jax.ShapeDtypeStruct((rows, heads * (NOPE + VDIM)), BF16),
            jax.ShapeDtypeStruct((rows, turned_cols), F32),
        ),
        grid_spec=pltpu.PrefetchScalarGridSpec(
            num_scalar_prefetch=1,
            grid=(heads, steps),
            in_specs=[
                pl.BlockSpec((block, NOPE), lambda h, i, n: (i, h)),
                pl.BlockSpec((block, turned_cols), lambda h, i, n: (i, 0)),
                pl.BlockSpec((rows, NOPE), lambda h, i, n: (0, 2 * h)),
                pl.BlockSpec((rows, VDIM), lambda h, i, n: (0, 2 * h + 1)),
                pl.BlockSpec((rows, turned_cols), lambda h, i, n: (0, 0)),
                pl.BlockSpec((block, VDIM), lambda h, i, n: (i, h)),
                pl.BlockSpec((1, block, 128), lambda h, i, n: (h, i, 0)),
            ],
            out_specs=(
                pl.BlockSpec((block, NOPE), lambda h, i, n: (i, h)),
                pl.BlockSpec((rows, turned_cols), lambda h, i, n: (0, 0)),
                pl.BlockSpec((rows, NOPE + VDIM), lambda h, i, n: (0, h)),
                pl.BlockSpec((rows, turned_cols), lambda h, i, n: (0, 0)),
            ),
            scratch_shapes=[pltpu.VMEM((rows, NOPE), F32), pltpu.VMEM((rows, VDIM), F32)],
        ),
        cost_estimate=pl.CostEstimate(
            flops=heads * rows * rows * 1600,
            bytes_accessed=16 * rows * heads * 512,
            transcendentals=heads * rows * rows,
        ),
        compiler_params=pltpu.CompilerParams(vmem_limit_bytes=40 << 20),
        name="attend_back",
    )(length, query, query_rope, kv, kv, key_rope, out_grad, log_totals)


def in_order(values, me, count):
    zero = jnp.zeros_like(values[0])
    ordered = []
    for j in range(count):
        total = zero
        for k in range(count):
            total = jnp.where((me ^ k) == j, values[k], total)
        ordered.append(total)
    return jnp.stack(ordered)


def body(
    lay,
    hidden,
    lengths,
    routes,
    attn_gain,
    w_query,
    w_kv_down,
    kv_gain,
    w_kv_up,
    w_out,
    ffn_gain,
    w_router,
    w_expert_in,
    w_expert_out,
    w_shared_in,
    w_shared_out,
    cotangent,
):
    rows, width = hidden.shape
    nz, nt, nq, ndp = lay.z, lay.t, lay.q, lay.dp
    me_dp = lax.axis_index("dp")
    me_t = lax.axis_index("tensor")
    me_z = me_dp // nq
    me_c = me_dp % nq
    part = width // nt
    d_loc = w_query.shape[0]
    f_loc = w_expert_out.shape[1]
    ffe = f_loc * nt
    heads = w_query.shape[1] // (NOPE + ROPE)
    score_scale = (NOPE + ROPE) ** (-0.5)

    def own_part(values):
        return lax.dynamic_slice_in_dim(values, me_t * part, part, 1)

    def gather_z(values):
        return lax.all_gather(values, "dp", axis=0, tiled=False, axis_index_groups=lay.z_groups)

    def scatter_z(values):
        return lax.psum_scatter(
            values, "dp", scatter_dimension=0, tiled=False, axis_index_groups=lay.z_groups
        )

    def gather_t(values):
        return lax.all_gather(values, "tensor", axis=1, tiled=True)

    def scatter_t(values):
        return lax.psum_scatter(
            values.astype(BF16), "tensor", scatter_dimension=1, tiled=True
        ).astype(F32)

    def swap_t(values):
        return lax.all_to_all(values, "tensor", split_axis=0, concat_axis=0, tiled=True)

    def swap_z(values):
        return lax.all_to_all(
            values,
            "dp",
            split_axis=0,
            concat_axis=0,
            axis_index_groups=lay.z_groups,
            tiled=True,
        )

    def gather_t_direct(values):
        return join_columns([lay.over_t(values, k) for k in range(nt)], me_t, nt)

    def part_for(values, k):
        return lax.dynamic_slice_in_dim(values, (me_t ^ k) * part, part, 1)

    def scatter_t_direct(values):
        total = part_for(values, 0)
        for k in range(1, nt):
            total = total + lay.over_t(part_for(values, k).astype(BF16), k).astype(F32)
        return total

    ids = jnp.stack([me_z, me_c, me_t]).astype(jnp.int32)

    packed = jnp.concatenate(
        [jnp.swapaxes(w_expert_in, 2, 3), w_expert_out[:, None]], 1
    ).reshape(nz, nt, 3, f_loc, d_loc)
    by_column = swap_t(jnp.swapaxes(packed, 0, 1))

    lat_loc = kv_gain.shape[0]
    q_rows, down_rows, out_rows = w_query.shape[1], w_kv_down.shape[1], w_out.shape[0]
    half = ROPE // 2

    def by_kind(turned):
        split = turned.reshape(heads, NOPE + ROPE, -1)
        return jnp.concatenate(
            [
                split[:, :NOPE].reshape(heads * NOPE, -1),
                split[:, NOPE : NOPE + half].reshape(heads * half, -1),
                split[:, NOPE + half :].reshape(heads * half, -1),
            ],
            0,
        )

    def by_head(rows_in):
        nope = rows_in[: heads * NOPE].reshape(heads, NOPE, -1)
        first = rows_in[heads * NOPE : heads * (NOPE + half)].reshape(heads, half, -1)
        second = rows_in[heads * (NOPE + half) :].reshape(heads, half, -1)
        return jnp.concatenate([nope, first, second], 1).reshape(heads * (NOPE + ROPE), -1)

    gains = jnp.stack([attn_gain, ffn_gain, jnp.pad(kv_gain, (0, d_loc - lat_loc))])
    front_pack = jnp.concatenate(
        [
            by_kind(jnp.transpose(w_query)),
            jnp.transpose(w_kv_down),
            jnp.transpose(w_router),
            jnp.pad(gains, ((0, 13), (0, 0))),
            w_out,
            w_kv_up.reshape(-1, d_loc),
        ],
        0,
    )
    front = lax.all_gather(front_pack, "dp", axis=0, tiled=False)

    valid_length = lengths[0]
    valid_rows = lax.broadcasted_iota(jnp.int32, (rows, 1), 0) < valid_length
    cot_low = jnp.where(valid_rows, cotangent, jnp.zeros_like(cotangent))
    cot_part = own_part(cot_low)
    route_own = jnp.pad(jnp.transpose(routes), ((0, -TOP % 8), (0, 0)), constant_values=-1)
    route_all = in_order([lay.over_z(route_own, k) for k in range(nz)], me_z, nz)
    inputs = hidden.astype(F32)
    attn_inverse = inverse_rms(inputs)
    cosine, sine = angle_tables(rows)
    wide_cos, wide_sin = jnp.tile(cosine, (1, heads)), jnp.tile(sine, (1, heads))
    front, attn_inverse, wide_cos, wide_sin, route_all = lax.optimization_barrier(
        (front, attn_inverse, wide_cos, wide_sin, route_all)
    )

    plane_ids = me_z * nt + jnp.arange(nt, dtype=jnp.int32)
    member = jnp.any(route_all[:, :, :, None] == plane_ids[None, None, None, :], axis=1)
    row_ids = lax.broadcasted_iota(jnp.int32, (rows, rows), 0)
    col_ids = lax.broadcasted_iota(jnp.int32, (rows, rows), 1)
    before = (col_ids < row_ids).astype(BF16)
    position = jnp.einsum("ij,sje->sei", before, member.astype(BF16), preferred_element_type=F32)
    key = jnp.where(jnp.swapaxes(member, 1, 2), position.astype(jnp.int32), -1)
    slots_iota = lax.broadcasted_iota(jnp.int32, (1, 1, CAP, 1), 2)

    def place_of(keys):
        return (keys[:, :, None, :] == slots_iota).astype(BF16)

    place = place_of(key)
    own_key = lax.dynamic_index_in_dim(key, me_t, 1, keepdims=False)
    own_place = own_key[:, None, :] == slots_iota[0]

    def pick_rows(values):
        picked = jnp.einsum("sepk,skd->espd", place, values, preferred_element_type=F32)
        return picked.astype(BF16).reshape(nt, nz * CAP, part)

    def send_out(picked):
        return jnp.swapaxes(swap_t(picked), 0, 1).reshape(nz * CAP, width)

    def send_back(values):
        return swap_t(jnp.swapaxes(values.reshape(nz * CAP, nt, part), 0, 1))

    def combine(parts):
        parts = parts.reshape(nt, nz, CAP, part)
        summed = jnp.einsum("sepk,espd->skd", place, parts, preferred_element_type=F32)
        return summed.astype(BF16)


    def rows_of(first, count):
        return jnp.swapaxes(front[:, first : first + count], 0, 1).reshape(count, width)

    query_t = rows_of(0, q_rows)
    down_t = rows_of(q_rows, down_rows)
    at = q_rows + down_rows
    router_t = rows_of(at, EXPERTS)
    gain_attn = front[:, at + EXPERTS].reshape(-1)
    gain_ffn = front[:, at + EXPERTS + 1].reshape(-1)
    gain_kv = front[:, at + EXPERTS + 2, :lat_loc].reshape(-1)
    at = at + 2 * EXPERTS
    out_w = rows_of(at, out_rows)
    up_w = front[:, at + out_rows :].reshape(LATENT, heads * (NOPE + VDIM))

    attn_scale = gain_attn.astype(F32)
    normed_low = (inputs * attn_inverse * attn_scale).astype(BF16)
    query = dot_nt(normed_low, query_t)
    nope_cols = heads * NOPE
    query_nope = query[:, :nope_cols].astype(BF16)
    query_rope = jnp.concatenate(
        rotate(
            query[:, nope_cols : nope_cols + heads * half],
            query[:, nope_cols + heads * half :],
            wide_cos,
            wide_sin,
        ),
        1,
    ).astype(BF16)
    latent_all = dot_nt(normed_low, down_t)
    latent_all, by_column = lax.optimization_barrier((latent_all, by_column))
    by_column = jnp.transpose(by_column, (2, 1, 0, 3, 4))
    by_plane = [swap_z(by_column[g]) for g in range(2)]
    latent = latent_all[:, :LATENT]
    kv_inverse = inverse_rms(latent)
    latent_hat = latent * kv_inverse
    kv_scale = gain_kv.astype(F32)
    latent_low = (latent_hat * kv_scale).astype(BF16)
    key_turned = jnp.concatenate(
        rotate(
            latent_all[:, LATENT : LATENT + half],
            latent_all[:, LATENT + half :],
            wide_cos[:, :half],
            wide_sin[:, :half],
        ),
        1,
    ).astype(BF16)
    copies = (2 * half, 2 * heads * half)
    to_col = lax.broadcasted_iota(jnp.int32, copies, 1)
    from_col = to_col // (heads * half) * half + to_col % half
    repeat = (lax.broadcasted_iota(jnp.int32, copies, 0) == from_col).astype(BF16)
    key_rope = dot(key_turned, repeat).astype(BF16)
    keys_values = dot(latent_low, up_w).astype(BF16)
    attended_low, log_totals = attend(
        lengths, query_nope, query_rope, keys_values, key_rope, heads, score_scale
    )
    attn_part, by_plane[0] = lax.optimization_barrier((dot(attended_low, out_w), by_plane[0]))
    attn_sum = scatter_t(attn_part)
    residual = own_part(hidden).astype(F32) + attn_sum

    def row_mean(values):
        partial = jnp.sum(values, axis=-1).reshape(-1, 128)
        return lax.psum(partial, "tensor").reshape(-1, 1) * (1.0 / width)

    ffn_inverse = lax.rsqrt(row_mean(residual * residual) + EPSILON)
    ffn_hat = residual * ffn_inverse
    ffn_scale = lax.dynamic_slice_in_dim(gain_ffn, me_t * part, part, 0).astype(F32)
    ffn_part = (ffn_hat * ffn_scale).astype(BF16)

    ffn_part, by_plane[1] = lax.optimization_barrier((ffn_part, by_plane[1]))
    ffn_all = gather_z(ffn_part)
    ffn_low = gather_t_direct(ffn_part)
    ffn_all, ffn_low, cot_ready = lax.optimization_barrier((ffn_all, ffn_low, cot_part))
    picked, by_plane[0], by_plane[1] = lax.optimization_barrier(
        (pick_rows(ffn_all), by_plane[0], by_plane[1])
    )
    expert_rows = send_out(picked)
    shared_pack = jnp.concatenate(
        [jnp.swapaxes(w_shared_in, 1, 2).reshape(-1, d_loc), w_shared_out], 0
    )
    def own_weights(matrices, order):
        pieces = [by_plane[g].reshape(nz * nt, f_loc, d_loc) for g in matrices]
        stacks = [lay.over_c(piece, k) for k in range(nq) for piece in pieces]
        return lay_out_weights(lay, order, stacks, f_loc, d_loc, width)

    own_in = own_weights((0, 1), ids * jnp.array([0, 1, 1], jnp.int32))
    cot_all, last_column, own_in = lax.optimization_barrier(
        (gather_z(cot_ready), by_column[2], own_in)
    )
    by_plane.append(
        jnp.stack(
            [
                lay.over_z(lax.dynamic_index_in_dim(last_column, me_z ^ k, 0, keepdims=False), k)
                for k in range(nz)
            ]
        )
    )

    by_plane[2], shared_pack, cot_picked = lax.optimization_barrier(
        (by_plane[2], shared_pack, pick_rows(cot_all))
    )
    cot_rows = send_out(cot_picked)
    shared_all = lax.all_gather(shared_pack, "dp", axis=0, tiled=False)
    own_out = own_weights((2,), ids)
    router_probs = jax.nn.softmax(dot_nt(ffn_low, router_t), axis=-1)
    probs_turned = jnp.transpose(router_probs).reshape(EXPERTS, -1, 128)
    own_probs = in_order(
        [
            lay.over_z(
                lax.dynamic_index_in_dim(
                    probs_turned, (me_z ^ k) * nt + me_t, 0, keepdims=False
                ),
                k,
            )
            for k in range(nz)
        ],
        me_z,
        nz,
    ).reshape(nz, rows)
    gate_rows = jnp.sum(jnp.where(own_place, own_probs[:, None, :], 0.0), axis=-1).reshape(
        nz * CAP, 1
    )
    gate_up = dot_nt(expert_rows, own_in)
    gate_pre, up_pre = gate_up[:, :ffe], gate_up[:, ffe:]
    gate_sig = jax.nn.sigmoid(gate_pre)
    gate_silu = gate_pre * gate_sig
    active = (gate_silu * up_pre).astype(BF16)
    rows_out = (dot(active, own_out) * gate_rows).astype(BF16)
    rows_out, cot_rows, shared_all = lax.optimization_barrier((rows_out, cot_rows, shared_all))
    out_parts = send_back(rows_out)
    active_grad_raw = dot_nt(cot_rows, own_out)
    gate_grad = jnp.sum(active.astype(F32) * active_grad_raw, axis=-1).reshape(nz, CAP)
    active_grad = active_grad_raw * gate_rows
    pre_low = jnp.concatenate(
        [
            active_grad * up_pre * gate_sig * (1.0 + gate_pre * (1.0 - gate_sig)),
            active_grad * gate_silu,
        ],
        1,
    ).astype(BF16)
    gated_active = (active.astype(F32) * gate_rows).astype(BF16)
    ffs = w_shared_out.shape[0]
    shared_in = jnp.swapaxes(shared_all[:, : 2 * ffs], 0, 1).reshape(2 * ffs, width)
    shared_out = jnp.swapaxes(shared_all[:, 2 * ffs :], 0, 1).reshape(ffs, width)
    shared_pre = dot_nt(ffn_low, shared_in)
    shared_gate, shared_up = shared_pre[:, :ffs], shared_pre[:, ffs:]
    shared_sig = jax.nn.sigmoid(shared_gate)
    shared_silu = shared_gate * shared_sig
    shared_act = (shared_silu * shared_up).astype(BF16)
    shared_full = dot(shared_act, shared_out)
    shared_act_grad = dot_nt(cot_low, shared_out)
    shared_pre_grad = jnp.concatenate(
        [
            shared_act_grad * shared_up * shared_sig * (1.0 + shared_gate * (1.0 - shared_sig)),
            shared_act_grad * shared_silu,
        ],
        1,
    ).astype(BF16)
    grad_shared_in = dot_tn(shared_pre_grad, ffn_low)
    grad_shared_out = dot_tn(shared_act, cot_low)
    shared_grad_full = dot(shared_pre_grad, shared_in)

    out_parts, pre_low, shared_full = lax.optimization_barrier((out_parts, pre_low, shared_full))
    rows_grad = dot(pre_low, own_in).astype(BF16)
    rows_grad, out_parts = lax.optimization_barrier((rows_grad, out_parts))
    grad_parts = send_back(rows_grad)
    routed, pre_low, gated_active, shared_part = lax.optimization_barrier(
        (combine(out_parts), pre_low, gated_active, scatter_t(shared_full))
    )
    routed = scatter_z(routed).astype(F32)
    token_grad = jnp.sum(jnp.where(own_place, gate_grad[:, :, None], 0.0), axis=1)
    token_grad = token_grad.reshape(nz, -1, 128)
    token_plane = jnp.stack(
        [
            lay.over_z(lax.dynamic_index_in_dim(token_grad, me_z ^ k, 0, keepdims=False), k)
            for k in range(nz)
        ]
    )
    token_home = jnp.stack([lay.over_t(token_plane, k) for k in range(nt)])
    experts = jnp.arange(EXPERTS, dtype=jnp.int32)
    came_from = (me_t ^ (experts % nt)) * nz + (me_z ^ (experts // nt))
    probs_grad = lax.dot_general(
        token_home.reshape(EXPERTS, rows),
        (experts[:, None] == came_from[None, :]).astype(F32),
        (((0,), (0,)), ((), ())),
        precision=lax.Precision.HIGHEST,
        preferred_element_type=F32,
    )

    grad_in_own = dot_tn(pre_low, expert_rows).astype(BF16)
    grad_out_own = dot_tn(gated_active, cot_rows).astype(BF16)
    (
        grad_parts,
        grad_in_own,
        grad_out_own,
        routed,
        probs_grad,
        shared_grad_full,
    ) = lax.optimization_barrier(
        (grad_parts, grad_in_own, grad_out_own, routed, probs_grad, shared_grad_full)
    )
    shared_grad = swap_t(
        jnp.swapaxes(shared_grad_full.astype(BF16).reshape(rows, nt, part), 0, 1)
    )
    shared_grad = jnp.sum(shared_grad.astype(F32), axis=0)
    grad_pieces = take_apart(lay, ids, grad_in_own, grad_out_own, f_loc, d_loc, width)
    routed_grad = scatter_z(combine(grad_parts)).astype(F32)
    grad_class = [
        sum(lay.over_c(grad_pieces[3 * k + g], k).astype(F32) for k in range(nq)).astype(BF16)
        for g in range(3)
    ]
    routed_grad, grad_class = lax.optimization_barrier((routed_grad, grad_class))
    grad_plane = [swap_z(grad_class[g].reshape(nz, nt, f_loc, d_loc)) for g in range(3)]

    logits_grad = router_probs * (
        probs_grad - jnp.sum(router_probs * probs_grad, axis=-1, keepdims=True)
    )
    router_part = lax.dot_general(
        logits_grad,
        ffn_low.astype(F32),
        (((0,), (0,)), ((), ())),
        precision=lax.Precision.HIGHEST,
        preferred_element_type=F32,
    )
    router_slice = lax.dynamic_slice_in_dim(router_t, me_t * part, part, 1)
    ffn_grad = (
        shared_grad
        + routed_grad
        + lax.dot_general(
            logits_grad,
            router_slice.astype(F32),
            (((1,), (0,)), ((), ())),
            precision=lax.Precision.HIGHEST,
            preferred_element_type=F32,
        )
    )
    scaled = ffn_scale * ffn_grad
    ffn_gain_part = jnp.sum(ffn_grad * ffn_hat, axis=0)
    residual_grad = cot_part.astype(F32) + ffn_inverse * (
        scaled - ffn_hat * row_mean(ffn_hat * scaled)
    )
    residual_low = gather_t(residual_grad.astype(BF16))

    def sum_dp(values):
        return lax.psum_scatter(values, "dp", scatter_dimension=0, tiled=False).astype(F32)

    def by_owner(values):
        return jnp.swapaxes(values.astype(BF16).reshape(-1, ndp, d_loc), 0, 1)

    shared_grads = jnp.concatenate([by_owner(grad_shared_in), by_owner(grad_shared_out)], 1)
    output_part = lax.optimization_barrier((residual + routed + shared_part).astype(BF16))
    residual_low, shared_grads, grad_plane[0], output_part = lax.optimization_barrier(
        (residual_low, shared_grads, grad_plane[0], output_part)
    )
    grad_out_w = dot_tn(attended_low, residual_low)
    attended_grad = dot_nt(residual_low, out_w).astype(BF16)
    query_nope_grad, query_turned_grad, kv_grad, rope_grad = attend_back(
        lengths,
        query_nope,
        query_rope,
        keys_values,
        key_rope,
        attended_grad,
        log_totals,
        heads,
        score_scale,
    )
    def to_columns(values):
        return [
            lay.over_t(lax.dynamic_index_in_dim(values, me_t ^ k, 1, keepdims=False), k)
            for k in range(nt)
        ]

    grad_home = [to_columns(grad_plane[0]), None, None]
    query_turned_grad, grad_plane[1], grad_home[0], shared_grads = lax.optimization_barrier(
        (query_turned_grad, grad_plane[1], grad_home[0], shared_grads)
    )
    shared_sum = sum_dp(shared_grads)
    turned_first, turned_second = rotate_back(
        query_turned_grad[:, : heads * half], query_turned_grad[:, heads * half :], wide_cos, wide_sin
    )
    query_grad = jnp.concatenate(
        [query_nope_grad, turned_first.astype(BF16), turned_second.astype(BF16)], 1
    )
    rope_sum = rope_grad.reshape(rows, 2, heads, half).sum(2)
    key_rope_part = jnp.concatenate(
        rotate_back(
            rope_sum[:, 0], rope_sum[:, 1], wide_cos[:, :half], wide_sin[:, :half]
        ),
        1,
    )
    latent_part = dot_nt(kv_grad, up_w)
    grad_kv_gain = jnp.sum(latent_part * latent_hat, axis=0)
    scaled_kv = kv_scale * latent_part
    latent_back = kv_inverse * (
        scaled_kv - latent_hat * jnp.mean(latent_hat * scaled_kv, axis=-1, keepdims=True)
    )
    down_grad = jnp.concatenate([latent_back, key_rope_part], -1).astype(BF16)
    normed_full, output = lax.optimization_barrier(
        (dot(query_grad, query_t) + dot(down_grad, down_t), gather_t(output_part))
    )
    pieces = [lay.over_t(part_for(normed_full, k).astype(BF16), k) for k in range(1, nt)]
    pieces[0], query_grad, kv_grad, down_grad = lax.optimization_barrier(
        (pieces[0], query_grad, kv_grad, down_grad)
    )
    normed_grad = part_for(normed_full, 0) + sum(piece.astype(F32) for piece in pieces)
    normed_grad, grad_plane[2], grad_home[1] = lax.optimization_barrier(
        (normed_grad, grad_plane[2], to_columns(grad_plane[1]))
    )
    attn_hat = own_part(hidden).astype(F32) * attn_inverse
    scaled_in = lax.dynamic_slice_in_dim(attn_scale, me_t * part, part, 0) * normed_grad
    attn_gain_part = jnp.sum(normed_grad * attn_hat, axis=0)
    input_grad = residual_grad + attn_inverse * (
        scaled_in - attn_hat * row_mean(attn_hat * scaled_in)
    )
    input_low, grad_plane[2] = lax.optimization_barrier((input_grad.astype(BF16), grad_plane[2]))
    grad_home[2] = to_columns(grad_plane[2])
    grad_expert_in, grad_expert_out = home_gradients(lay, ids, grad_home, f_loc, d_loc)
    grad_hidden = gather_t_direct(input_low)

    def spread(values):
        return lax.dynamic_update_slice(
            jnp.zeros((1, width), F32), values[None], (jnp.int32(0), me_t * part)
        )

    kv_gain_row = jnp.pad(
        grad_kv_gain.reshape(ndp, lat_loc), ((0, 0), (0, d_loc - lat_loc))
    ).reshape(1, width)
    gain_grads = jnp.concatenate([spread(attn_gain_part), spread(ffn_gain_part), kv_gain_row], 0)
    front_sum = sum_dp(
        jnp.concatenate(
            [
                by_owner(dot_tn(down_grad, normed_low)),
                by_owner(jnp.pad(gain_grads, ((0, 13), (0, 0)))),
                by_owner(router_part),
                by_owner(dot_tn(query_grad, normed_low)),
                by_owner(grad_out_w),
                dot_tn(latent_low, kv_grad).astype(BF16).reshape(ndp, -1, d_loc),
            ],
            1,
        )
    )
    own_sum = front_sum[: down_rows + EXPERTS]
    own_low = own_sum.astype(BF16)
    for k in range(1, nt):
        own_sum = own_sum + lay.over_t(own_low, k).astype(F32)
    at = down_rows + 2 * EXPERTS
    return (
        output,
        grad_hidden,
        own_sum[down_rows],
        jnp.transpose(by_head(front_sum[at : at + q_rows])),
        jnp.transpose(own_sum[:down_rows]),
        own_sum[down_rows + 2, :lat_loc],
        front_sum[at + q_rows + out_rows :].reshape(w_kv_up.shape),
        front_sum[at + q_rows : at + q_rows + out_rows],
        own_sum[down_rows + 1],
        jnp.transpose(front_sum[down_rows + EXPERTS : at]),
        grad_expert_in,
        grad_expert_out,
        jnp.swapaxes(shared_sum[: 2 * ffs].reshape(2, ffs, d_loc), 1, 2),
        shared_sum[2 * ffs :],
    )


def solution(mesh):
    return jax.shard_map(
        functools.partial(body, Layout(mesh.shape["dp"], mesh.shape["tensor"])),
        mesh=mesh,
        in_specs=(
            P("dp", None),
            P("dp"),
            P("dp", None),
            P("dp"),
            P("dp", "tensor"),
            P("dp", None),
            P("dp"),
            P("dp", "tensor"),
            P("tensor", "dp"),
            P("dp"),
            P("dp", None),
            P(None, None, "dp", "tensor"),
            P(None, "tensor", "dp"),
            P(None, "dp", "tensor"),
            P("tensor", "dp"),
            P("dp", None),
        ),
        out_specs=(
            P("dp", None),
            P("dp", None),
            P("dp"),
            P("dp", "tensor"),
            P("dp", None),
            P("dp"),
            P("dp", "tensor"),
            P("tensor", "dp"),
            P("dp"),
            P("dp", None),
            P(None, None, "dp", "tensor"),
            P(None, "tensor", "dp"),
            P(None, "dp", "tensor"),
            P("tensor", "dp"),
        ),
        check_vma=False,
    )
```

```python
import functools
import math

import jax
import jax.numpy as jnp
from jax import lax
from jax.experimental import pallas as pl
from jax.experimental.pallas import tpu as pltpu
from jax.sharding import PartitionSpec as P

NOPE = 128
ROPE = 64
VDIM = 128
LATENT = 512
TOP = 6
EXPERTS = 16
CAP = 512

EPSILON = 1e-06
NEGATIVE = -1e30
F32 = jnp.float32
BF16 = jnp.bfloat16


def dot(a, b):
    return jnp.dot(a, b, preferred_element_type=F32)


def dot_nt(a, b):
    return lax.dot_general(a, b, (((1,), (1,)), ((), ())), preferred_element_type=F32)


def dot_tn(a, b):
    return lax.dot_general(a, b, (((0,), (0,)), ((), ())), preferred_element_type=F32)


def rotate(first, second, cosine, sine):
    return first * cosine - second * sine, second * cosine + first * sine


def rotate_back(first, second, cosine, sine):
    return first * cosine + second * sine, second * cosine - first * sine


def angle_tables(rows_count):
    positions = jnp.arange(rows_count, dtype=F32)
    freqs = jnp.exp(jnp.arange(ROPE // 2, dtype=F32) * (-2.0 * math.log(10000.0) / ROPE))
    angles = positions[:, None] * freqs[None, :]
    return (jnp.cos(angles), jnp.sin(angles))


def inverse_rms(values):
    return lax.rsqrt(jnp.mean(values * values, axis=-1, keepdims=True) + EPSILON)


class Layout:
    def __init__(self, n_dp, n_tensor):
        self.dp, self.t = n_dp, n_tensor
        self.q = n_dp * n_tensor // EXPERTS
        self.z = n_dp // self.q
        if self.z * self.t != EXPERTS or self.z * self.q != n_dp:
            raise ValueError("mesh")
        self.z_groups = [[c + self.q * z for z in range(self.z)] for c in range(self.q)]

    def over_t(self, values, k):
        if k == 0:
            return values
        return lax.ppermute(values, "tensor", [(i, i ^ k) for i in range(self.t)])

    def over_z(self, values, k):
        if k == 0:
            return values
        return lax.ppermute(values, "dp", [(d, d ^ (k * self.q)) for d in range(self.dp)])

    def over_c(self, values, k):
        if k == 0:
            return values
        return lax.ppermute(values, "dp", [(d, d ^ k) for d in range(self.dp)])


def lay_out_weights(lay, ids, stacks, f_loc, d_loc, width):
    ffe = f_loc * lay.t
    count = len(stacks) // lay.q

    def kernel(ids_ref, *refs):
        for kc in range(lay.q):
            columns = pl.ds(pl.multiple_of((ids_ref[1] ^ kc) * d_loc, 128), d_loc)
            for g in range(count):
                refs[-1][g, :, columns] = refs[count * kc + g][0]

    own = pl.pallas_call(
        kernel,
        out_shape=jax.ShapeDtypeStruct((count, ffe, width), BF16),
        grid_spec=pltpu.PrefetchScalarGridSpec(
            num_scalar_prefetch=1,
            grid=(lay.t, lay.z),
            in_specs=[
                pl.BlockSpec(
                    (1, f_loc, d_loc), lambda kt, kz, ids: ((kz ^ ids[0]) * lay.t + kt, 0, 0)
                )
            ]
            * len(stacks),
            out_specs=pl.BlockSpec(
                (count, f_loc, lay.q * d_loc), lambda kt, kz, ids: (0, kt, kz)
            ),
        ),
        cost_estimate=pl.CostEstimate(
            flops=0, bytes_accessed=4 * count * ffe * width, transcendentals=0
        ),
        compiler_params=pltpu.CompilerParams(vmem_limit_bytes=32 << 20),
        name="lay_out_weights",
    )(ids, *stacks)
    return own.reshape(count * ffe, width)


def take_apart(lay, ids, grad_in, grad_out, f_loc, d_loc, width):
    ffe = f_loc * lay.t

    def kernel(ids_ref, in_ref, out_ref, *targets):
        for kc in range(lay.q):
            columns = pl.ds(pl.multiple_of((ids_ref[1] ^ kc) * d_loc, 128), d_loc)
            for g in range(2):
                targets[3 * kc + g][0] = in_ref[g, :, columns]
            targets[3 * kc + 2][0] = out_ref[:, columns]

    shape = jax.ShapeDtypeStruct((lay.t * lay.z, f_loc, d_loc), BF16)
    spec = pl.BlockSpec((1, f_loc, d_loc), lambda kt, kz, ids: (kz * lay.t + kt, 0, 0))
    return pl.pallas_call(
        kernel,
        out_shape=(shape,) * (3 * lay.q),
        grid_spec=pltpu.PrefetchScalarGridSpec(
            num_scalar_prefetch=1,
            grid=(lay.t, lay.z),
            in_specs=[
                pl.BlockSpec((2, f_loc, lay.q * d_loc), lambda kt, kz, ids: (0, kt, kz)),
                pl.BlockSpec((f_loc, lay.q * d_loc), lambda kt, kz, ids: (kt, kz)),
            ],
            out_specs=(spec,) * (3 * lay.q),
        ),
        cost_estimate=pl.CostEstimate(
            flops=0, bytes_accessed=12 * ffe * width, transcendentals=0
        ),
        compiler_params=pltpu.CompilerParams(vmem_limit_bytes=32 << 20),
        name="take_apart",
    )(ids, grad_in.reshape(2, ffe, width), grad_out)


def home_gradients(lay, ids, parts, f_loc, d_loc):
    def kernel(ids_ref, *refs):
        sources, (in_ref, out_ref) = refs[: 3 * lay.t], refs[3 * lay.t :]
        for k in range(lay.t):

            @pl.when((pl.program_id(1) ^ ids_ref[2]) == k)
            def _(k=k):
                for g in range(2):
                    in_ref[0, g] = sources[g * lay.t + k][0].astype(F32)
                out_ref[0] = sources[2 * lay.t + k][0].astype(F32)

    grad_in, grad_out = pl.pallas_call(
        kernel,
        out_shape=(
            jax.ShapeDtypeStruct((EXPERTS, 2, f_loc, d_loc), F32),
            jax.ShapeDtypeStruct((EXPERTS, f_loc, d_loc), F32),
        ),
        grid_spec=pltpu.PrefetchScalarGridSpec(
            num_scalar_prefetch=1,
            grid=(lay.z, lay.t),
            in_specs=[pl.BlockSpec((1, f_loc, d_loc), lambda z, t, ids: (z, 0, 0))] * (3 * lay.t),
            out_specs=(
                pl.BlockSpec((1, 2, f_loc, d_loc), lambda z, t, ids: (z * lay.t + t, 0, 0, 0)),
                pl.BlockSpec((1, f_loc, d_loc), lambda z, t, ids: (z * lay.t + t, 0, 0)),
            ),
        ),
        cost_estimate=pl.CostEstimate(
            flops=0, bytes_accessed=18 * EXPERTS * f_loc * d_loc, transcendentals=0
        ),
        compiler_params=pltpu.CompilerParams(vmem_limit_bytes=32 << 20),
        name="home_gradients",
    )(ids, *[piece for part in parts for piece in part])
    return jnp.swapaxes(grad_in, 2, 3), grad_out


def join_columns(parts, me, count):
    rows, part = parts[0].shape
    block = min(512, rows)

    def kernel(me_ref, *refs):
        for k in range(count):

            @pl.when(pl.program_id(1) == k)
            def _(k=k):
                refs[count][...] = refs[k][...]

    return pl.pallas_call(
        kernel,
        out_shape=jax.ShapeDtypeStruct((rows, count * part), parts[0].dtype),
        grid_spec=pltpu.PrefetchScalarGridSpec(
            num_scalar_prefetch=1,
            grid=(rows // block, count),
            in_specs=[pl.BlockSpec((block, part), lambda i, k, me: (i, 0))] * count,
            out_specs=pl.BlockSpec((block, part), lambda i, k, me: (i, me[0] ^ k)),
        ),
        cost_estimate=pl.CostEstimate(
            flops=0, bytes_accessed=4 * rows * part * count, transcendentals=0
        ),
        name="join_columns",
    )(me.reshape(1).astype(jnp.int32), *parts)


def score_block(q_ref, r_ref, k_ref, kr_ref, head, step, keys, block, length, scale):
    half = r_ref.shape[1] // 2
    lanes = lax.broadcasted_iota(jnp.int32, r_ref.shape, 1) % half // (ROPE // 2)
    turned = jnp.where(lanes == head, r_ref[...], jnp.zeros_like(r_ref))
    raw = lax.dot_general(
        q_ref[...], k_ref[:keys], (((1,), (1,)), ((), ())), preferred_element_type=F32
    ) + lax.dot_general(
        turned, kr_ref[:keys], (((1,), (1,)), ((), ())), preferred_element_type=F32
    )
    rows = lax.broadcasted_iota(jnp.int32, raw.shape, 0) + step * block
    cols = lax.broadcasted_iota(jnp.int32, raw.shape, 1)
    allowed = (cols <= rows) & (cols < length)
    return jnp.where(allowed, raw * scale, NEGATIVE), turned


def attend(length, query, query_rope, kv, key_rope, heads, scale):
    rows = query.shape[0]
    block = min(256, rows)
    steps = rows // block

    def kernel(len_ref, q_ref, r_ref, k_ref, v_ref, kr_ref, o_ref, total_ref):
        head, step = pl.program_id(0), pl.program_id(1)
        for n in range(steps):

            @pl.when(step == n)
            def _(n=n):
                keys = (n + 1) * block
                scores, _ = score_block(
                    q_ref, r_ref, k_ref, kr_ref, head, n, keys, block, len_ref[0], scale
                )
                highest = jnp.max(scores, axis=-1, keepdims=True)
                expo = jnp.exp(scores - highest)
                totals = jnp.sum(expo, axis=-1, keepdims=True)
                weights = (expo * (1.0 / totals)).astype(BF16)
                o_ref[...] = dot(weights, v_ref[:keys]).astype(BF16)
                total_ref[0] = jnp.broadcast_to(highest + jnp.log(totals), (block, 128))

    return pl.pallas_call(
        kernel,
        out_shape=(
            jax.ShapeDtypeStruct((rows, heads * VDIM), BF16),
            jax.ShapeDtypeStruct((heads, rows, 128), F32),
        ),
        grid_spec=pltpu.PrefetchScalarGridSpec(
            num_scalar_prefetch=1,
            grid=(heads, steps),
            in_specs=[
                pl.BlockSpec((block, NOPE), lambda h, i, n: (i, h)),
                pl.BlockSpec((block, query_rope.shape[1]), lambda h, i, n: (i, 0)),
                pl.BlockSpec((rows, NOPE), lambda h, i, n: (0, 2 * h)),
                pl.BlockSpec((rows, VDIM), lambda h, i, n: (0, 2 * h + 1)),
                pl.BlockSpec((rows, key_rope.shape[1]), lambda h, i, n: (0, 0)),
            ],
            out_specs=(
                pl.BlockSpec((block, VDIM), lambda h, i, n: (i, h)),
                pl.BlockSpec((1, block, 128), lambda h, i, n: (h, i, 0)),
            ),
        ),
        cost_estimate=pl.CostEstimate(
            flops=heads * rows * rows * 512,
            bytes_accessed=8 * rows * heads * 512,
            transcendentals=heads * rows * rows,
        ),
        compiler_params=pltpu.CompilerParams(vmem_limit_bytes=32 << 20),
        name="attend",
    )(length, query, query_rope, kv, kv, key_rope)


def attend_back(length, query, query_rope, kv, key_rope, out_grad, log_totals, heads, scale):
    rows = query.shape[0]
    block = min(256, rows)
    steps = rows // block
    turned_cols = query_rope.shape[1]

    def kernel(
        len_ref, q_ref, r_ref, k_ref, v_ref, kr_ref, do_ref, total_ref,
        dq_ref, dr_ref, dkv_ref, dkr_ref, dk_acc, dv_acc,
    ):
        head, step = pl.program_id(0), pl.program_id(1)

        @pl.when(step == 0)
        def _():
            dk_acc[...] = jnp.zeros_like(dk_acc)
            dv_acc[...] = jnp.zeros_like(dv_acc)

        @pl.when((step == 0) & (head == 0))
        def _():
            dr_ref[...] = jnp.zeros_like(dr_ref)
            dkr_ref[...] = jnp.zeros_like(dkr_ref)

        for n in range(steps):

            @pl.when(step == n)
            def _(n=n):
                keys = (n + 1) * block
                scores, turned = score_block(
                    q_ref, r_ref, k_ref, kr_ref, head, n, keys, block, len_ref[0], scale
                )
                probs = jnp.exp(scores - total_ref[0][:, :1])
                prob_grad = lax.dot_general(
                    do_ref[...], v_ref[:keys], (((1,), (1,)), ((), ())), preferred_element_type=F32
                )
                centre = jnp.sum(probs * prob_grad, axis=-1, keepdims=True)
                score_grad = (probs * (prob_grad - centre)).astype(BF16)
                probs_low = probs.astype(BF16)
                dq_ref[...] = (dot(score_grad, k_ref[:keys]) * scale).astype(BF16)
                half = turned_cols // 2
                lanes = lax.broadcasted_iota(jnp.int32, (block, turned_cols), 1)
                lanes = lanes % half // (ROPE // 2)
                turned_grad = dot(score_grad, kr_ref[:keys]) * scale
                dr_ref[n * block : keys] += jnp.where(lanes == head, turned_grad, 0.0)
                dk_acc[:keys] += dot_tn(score_grad, q_ref[...]) * scale
                dkr_ref[:keys] += dot_tn(score_grad, turned) * scale
                dv_acc[:keys] += dot_tn(probs_low, do_ref[...])

        @pl.when(step == steps - 1)
        def _():
            dkv_ref[:, :NOPE] = dk_acc[...].astype(BF16)
            dkv_ref[:, NOPE:] = dv_acc[...].astype(BF16)

    return pl.pallas_call(
        kernel,
        out_shape=(
            jax.ShapeDtypeStruct((rows, heads * NOPE), BF16),
            jax.ShapeDtypeStruct((rows, turned_cols), F32),
            jax.ShapeDtypeStruct((rows, heads * (NOPE + VDIM)), BF16),
            jax.ShapeDtypeStruct((rows, turned_cols), F32),
        ),
        grid_spec=pltpu.PrefetchScalarGridSpec(
            num_scalar_prefetch=1,
            grid=(heads, steps),
            in_specs=[
                pl.BlockSpec((block, NOPE), lambda h, i, n: (i, h)),
                pl.BlockSpec((block, turned_cols), lambda h, i, n: (i, 0)),
                pl.BlockSpec((rows, NOPE), lambda h, i, n: (0, 2 * h)),
                pl.BlockSpec((rows, VDIM), lambda h, i, n: (0, 2 * h + 1)),
                pl.BlockSpec((rows, turned_cols), lambda h, i, n: (0, 0)),
                pl.BlockSpec((block, VDIM), lambda h, i, n: (i, h)),
                pl.BlockSpec((1, block, 128), lambda h, i, n: (h, i, 0)),
            ],
            out_specs=(
                pl.BlockSpec((block, NOPE), lambda h, i, n: (i, h)),
                pl.BlockSpec((rows, turned_cols), lambda h, i, n: (0, 0)),
                pl.BlockSpec((rows, NOPE + VDIM), lambda h, i, n: (0, h)),
                pl.BlockSpec((rows, turned_cols), lambda h, i, n: (0, 0)),
            ),
            scratch_shapes=[pltpu.VMEM((rows, NOPE), F32), pltpu.VMEM((rows, VDIM), F32)],
        ),
        cost_estimate=pl.CostEstimate(
            flops=heads * rows * rows * 1600,
            bytes_accessed=16 * rows * heads * 512,
            transcendentals=heads * rows * rows,
        ),
        compiler_params=pltpu.CompilerParams(vmem_limit_bytes=40 << 20),
        name="attend_back",
    )(length, query, query_rope, kv, kv, key_rope, out_grad, log_totals)


def in_order(values, me, count):
    zero = jnp.zeros_like(values[0])
    ordered = []
    for j in range(count):
        total = zero
        for k in range(count):
            total = jnp.where((me ^ k) == j, values[k], total)
        ordered.append(total)
    return jnp.stack(ordered)


def body(
    lay,
    hidden,
    lengths,
    routes,
    attn_gain,
    w_query,
    w_kv_down,
    kv_gain,
    w_kv_up,
    w_out,
    ffn_gain,
    w_router,
    w_expert_in,
    w_expert_out,
    w_shared_in,
    w_shared_out,
    cotangent,
):
    rows, width = hidden.shape
    nz, nt, nq, ndp = lay.z, lay.t, lay.q, lay.dp
    me_dp = lax.axis_index("dp")
    me_t = lax.axis_index("tensor")
    me_z = me_dp // nq
    me_c = me_dp % nq
    part = width // nt
    d_loc = w_query.shape[0]
    f_loc = w_expert_out.shape[1]
    ffe = f_loc * nt
    heads = w_query.shape[1] // (NOPE + ROPE)
    score_scale = (NOPE + ROPE) ** (-0.5)

    def own_part(values):
        return lax.dynamic_slice_in_dim(values, me_t * part, part, 1)

    def gather_z(values):
        return lax.all_gather(values, "dp", axis=0, tiled=False, axis_index_groups=lay.z_groups)

    def scatter_z(values):
        return lax.psum_scatter(
            values, "dp", scatter_dimension=0, tiled=False, axis_index_groups=lay.z_groups
        )

    def sum_dp(values):
        return lax.psum_scatter(values, "dp", scatter_dimension=0, tiled=False).astype(F32)

    def by_owner(values):
        return jnp.swapaxes(values.astype(BF16).reshape(-1, ndp, d_loc), 0, 1)

    def gather_t(values):
        return lax.all_gather(values, "tensor", axis=1, tiled=True)

    def scatter_t(values):
        return lax.psum_scatter(
            values.astype(BF16), "tensor", scatter_dimension=1, tiled=True
        ).astype(F32)

    def swap_t(values):
        return lax.all_to_all(values, "tensor", split_axis=0, concat_axis=0, tiled=True)

    def swap_z(values):
        return lax.all_to_all(
            values,
            "dp",
            split_axis=0,
            concat_axis=0,
            axis_index_groups=lay.z_groups,
            tiled=True,
        )

    def gather_t_direct(values):
        return join_columns([lay.over_t(values, k) for k in range(nt)], me_t, nt)

    def part_for(values, k):
        return lax.dynamic_slice_in_dim(values, (me_t ^ k) * part, part, 1)

    def scatter_t_direct(values):
        total = part_for(values, 0)
        for k in range(1, nt):
            total = total + lay.over_t(part_for(values, k).astype(BF16), k).astype(F32)
        return total

    ids = jnp.stack([me_z, me_c, me_t]).astype(jnp.int32)

    packed = jnp.concatenate(
        [jnp.swapaxes(w_expert_in, 2, 3), w_expert_out[:, None]], 1
    ).reshape(nz, nt, 3, f_loc, d_loc)
    by_column = swap_t(jnp.swapaxes(packed, 0, 1))

    lat_loc = kv_gain.shape[0]
    q_rows, down_rows, out_rows = w_query.shape[1], w_kv_down.shape[1], w_out.shape[0]
    half = ROPE // 2

    def by_kind(turned):
        split = turned.reshape(heads, NOPE + ROPE, -1)
        return jnp.concatenate(
            [
                split[:, :NOPE].reshape(heads * NOPE, -1),
                split[:, NOPE : NOPE + half].reshape(heads * half, -1),
                split[:, NOPE + half :].reshape(heads * half, -1),
            ],
            0,
        )

    def by_head(rows_in):
        nope = rows_in[: heads * NOPE].reshape(heads, NOPE, -1)
        first = rows_in[heads * NOPE : heads * (NOPE + half)].reshape(heads, half, -1)
        second = rows_in[heads * (NOPE + half) :].reshape(heads, half, -1)
        return jnp.concatenate([nope, first, second], 1).reshape(heads * (NOPE + ROPE), -1)

    gains = jnp.stack([attn_gain, ffn_gain, jnp.pad(kv_gain, (0, d_loc - lat_loc))])
    front_pack = jnp.concatenate(
        [
            by_kind(jnp.transpose(w_query)),
            jnp.transpose(w_kv_down),
            jnp.transpose(w_router),
            jnp.pad(gains, ((0, 13), (0, 0))),
            w_out,
            w_kv_up.reshape(-1, d_loc),
        ],
        0,
    )
    front = lax.all_gather(front_pack, "dp", axis=0, tiled=False)

    valid_length = lengths[0]
    valid_rows = lax.broadcasted_iota(jnp.int32, (rows, 1), 0) < valid_length
    cot_low = jnp.where(valid_rows, cotangent, jnp.zeros_like(cotangent))
    cot_part = own_part(cot_low)
    route_own = jnp.pad(jnp.transpose(routes), ((0, -TOP % 8), (0, 0)), constant_values=-1)
    route_all = in_order([lay.over_z(route_own, k) for k in range(nz)], me_z, nz)
    inputs = hidden.astype(F32)
    attn_inverse = inverse_rms(inputs)
    cosine, sine = angle_tables(rows)
    wide_cos, wide_sin = jnp.tile(cosine, (1, heads)), jnp.tile(sine, (1, heads))
    front, attn_inverse, wide_cos, wide_sin, route_all = lax.optimization_barrier(
        (front, attn_inverse, wide_cos, wide_sin, route_all)
    )

    plane_ids = me_z * nt + jnp.arange(nt, dtype=jnp.int32)
    member = jnp.any(route_all[:, :, :, None] == plane_ids[None, None, None, :], axis=1)
    row_ids = lax.broadcasted_iota(jnp.int32, (rows, rows), 0)
    col_ids = lax.broadcasted_iota(jnp.int32, (rows, rows), 1)
    before = (col_ids < row_ids).astype(BF16)
    position = jnp.einsum("ij,sje->sei", before, member.astype(BF16), preferred_element_type=F32)
    key = jnp.where(jnp.swapaxes(member, 1, 2), position.astype(jnp.int32), -1)
    slots_iota = lax.broadcasted_iota(jnp.int32, (1, 1, CAP, 1), 2)

    def place_of(keys):
        return (keys[:, :, None, :] == slots_iota).astype(BF16)

    place = place_of(key)
    own_key = lax.dynamic_index_in_dim(key, me_t, 1, keepdims=False)
    own_place = own_key[:, None, :] == slots_iota[0]

    def pick_rows(values):
        picked = jnp.einsum("sepk,skd->espd", place, values, preferred_element_type=F32)
        return picked.astype(BF16).reshape(nt, nz * CAP, part)

    def send_out(picked):
        return jnp.swapaxes(swap_t(picked), 0, 1).reshape(nz * CAP, width)

    def send_back(values):
        return swap_t(jnp.swapaxes(values.reshape(nz * CAP, nt, part), 0, 1))

    def combine(parts):
        parts = parts.reshape(nt, nz, CAP, part)
        summed = jnp.einsum("sepk,espd->skd", place, parts, preferred_element_type=F32)
        return summed.astype(BF16)


    def rows_of(first, count):
        return jnp.swapaxes(front[:, first : first + count], 0, 1).reshape(count, width)

    query_t = rows_of(0, q_rows)
    down_t = rows_of(q_rows, down_rows)
    at = q_rows + down_rows
    router_t = rows_of(at, EXPERTS)
    gain_attn = front[:, at + EXPERTS].reshape(-1)
    gain_ffn = front[:, at + EXPERTS + 1].reshape(-1)
    gain_kv = front[:, at + EXPERTS + 2, :lat_loc].reshape(-1)
    at = at + 2 * EXPERTS
    out_w = rows_of(at, out_rows)
    up_w = front[:, at + out_rows :].reshape(LATENT, heads * (NOPE + VDIM))

    attn_scale = gain_attn.astype(F32)
    normed_low = (inputs * attn_inverse * attn_scale).astype(BF16)
    query = dot_nt(normed_low, query_t)
    nope_cols = heads * NOPE
    query_nope = query[:, :nope_cols].astype(BF16)
    query_rope = jnp.concatenate(
        rotate(
            query[:, nope_cols : nope_cols + heads * half],
            query[:, nope_cols + heads * half :],
            wide_cos,
            wide_sin,
        ),
        1,
    ).astype(BF16)
    latent_all = dot_nt(normed_low, down_t)
    latent_all, by_column = lax.optimization_barrier((latent_all, by_column))
    by_column = jnp.transpose(by_column, (2, 1, 0, 3, 4))
    by_plane = [swap_z(by_column[g]) for g in range(2)]
    latent = latent_all[:, :LATENT]
    kv_inverse = inverse_rms(latent)
    latent_hat = latent * kv_inverse
    kv_scale = gain_kv.astype(F32)
    latent_low = (latent_hat * kv_scale).astype(BF16)
    key_turned = jnp.concatenate(
        rotate(
            latent_all[:, LATENT : LATENT + half],
            latent_all[:, LATENT + half :],
            wide_cos[:, :half],
            wide_sin[:, :half],
        ),
        1,
    ).astype(BF16)
    copies = (2 * half, 2 * heads * half)
    to_col = lax.broadcasted_iota(jnp.int32, copies, 1)
    from_col = to_col // (heads * half) * half + to_col % half
    repeat = (lax.broadcasted_iota(jnp.int32, copies, 0) == from_col).astype(BF16)
    key_rope = dot(key_turned, repeat).astype(BF16)
    keys_values = dot(latent_low, up_w).astype(BF16)
    attended_low, log_totals = attend(
        lengths, query_nope, query_rope, keys_values, key_rope, heads, score_scale
    )
    attn_part, by_plane[0] = lax.optimization_barrier((dot(attended_low, out_w), by_plane[0]))
    attn_sum = scatter_t(attn_part)
    residual = own_part(hidden).astype(F32) + attn_sum

    def row_mean(values):
        partial = jnp.sum(values, axis=-1).reshape(-1, 128)
        return lax.psum(partial, "tensor").reshape(-1, 1) * (1.0 / width)

    ffn_inverse = lax.rsqrt(row_mean(residual * residual) + EPSILON)
    ffn_hat = residual * ffn_inverse
    ffn_scale = lax.dynamic_slice_in_dim(gain_ffn, me_t * part, part, 0).astype(F32)
    ffn_part = (ffn_hat * ffn_scale).astype(BF16)

    ffn_part, by_plane[1] = lax.optimization_barrier((ffn_part, by_plane[1]))
    ffn_all = gather_z(ffn_part)
    ffn_low = gather_t_direct(ffn_part)
    ffn_all, ffn_low, cot_ready = lax.optimization_barrier((ffn_all, ffn_low, cot_part))
    picked, by_plane[0], by_plane[1] = lax.optimization_barrier(
        (pick_rows(ffn_all), by_plane[0], by_plane[1])
    )
    expert_rows = send_out(picked)
    shared_pack = jnp.concatenate(
        [jnp.swapaxes(w_shared_in, 1, 2).reshape(-1, d_loc), w_shared_out], 0
    )
    def own_weights(matrices, order):
        pieces = [by_plane[g].reshape(nz * nt, f_loc, d_loc) for g in matrices]
        stacks = [lay.over_c(piece, k) for k in range(nq) for piece in pieces]
        return lay_out_weights(lay, order, stacks, f_loc, d_loc, width)

    own_in = own_weights((0, 1), ids * jnp.array([0, 1, 1], jnp.int32))
    cot_all, last_column, own_in = lax.optimization_barrier(
        (gather_z(cot_ready), by_column[2], own_in)
    )
    by_plane.append(
        jnp.stack(
            [
                lay.over_z(lax.dynamic_index_in_dim(last_column, me_z ^ k, 0, keepdims=False), k)
                for k in range(nz)
            ]
        )
    )

    by_plane[2], shared_pack, cot_picked = lax.optimization_barrier(
        (by_plane[2], shared_pack, pick_rows(cot_all))
    )
    cot_rows = send_out(cot_picked)
    shared_all = lax.all_gather(shared_pack, "dp", axis=0, tiled=False)
    own_out = own_weights((2,), ids)
    router_probs = jax.nn.softmax(dot_nt(ffn_low, router_t), axis=-1)
    probs_turned = jnp.transpose(router_probs).reshape(EXPERTS, -1, 128)
    own_probs = in_order(
        [
            lay.over_z(
                lax.dynamic_index_in_dim(
                    probs_turned, (me_z ^ k) * nt + me_t, 0, keepdims=False
                ),
                k,
            )
            for k in range(nz)
        ],
        me_z,
        nz,
    ).reshape(nz, rows)
    gate_rows = jnp.sum(jnp.where(own_place, own_probs[:, None, :], 0.0), axis=-1).reshape(
        nz * CAP, 1
    )
    gate_up = dot_nt(expert_rows, own_in)
    gate_pre, up_pre = gate_up[:, :ffe], gate_up[:, ffe:]
    gate_sig = jax.nn.sigmoid(gate_pre)
    gate_silu = gate_pre * gate_sig
    active = (gate_silu * up_pre).astype(BF16)
    rows_out = (dot(active, own_out) * gate_rows).astype(BF16)
    rows_out, cot_rows, shared_all = lax.optimization_barrier((rows_out, cot_rows, shared_all))
    out_parts = send_back(rows_out)
    ffs = w_shared_out.shape[0]
    shared_in = jnp.swapaxes(shared_all[:, : 2 * ffs], 0, 1).reshape(2 * ffs, width)
    shared_out = jnp.swapaxes(shared_all[:, 2 * ffs :], 0, 1).reshape(ffs, width)
    shared_pre = dot_nt(ffn_low, shared_in)
    shared_gate, shared_up = shared_pre[:, :ffs], shared_pre[:, ffs:]
    shared_sig = jax.nn.sigmoid(shared_gate)
    shared_silu = shared_gate * shared_sig
    shared_act = (shared_silu * shared_up).astype(BF16)
    shared_full = dot(shared_act, shared_out)
    shared_act_grad = dot_nt(cot_low, shared_out)
    shared_pre_grad = jnp.concatenate(
        [
            shared_act_grad * shared_up * shared_sig * (1.0 + shared_gate * (1.0 - shared_sig)),
            shared_act_grad * shared_silu,
        ],
        1,
    ).astype(BF16)
    grad_shared_in = dot_tn(shared_pre_grad, ffn_low)
    grad_shared_out = dot_tn(shared_act, cot_low)
    shared_grad_full = dot(shared_pre_grad, shared_in)
    shared_pack, cot_rows = lax.optimization_barrier(
        (jnp.concatenate([by_owner(grad_shared_in), by_owner(grad_shared_out)], 1), cot_rows)
    )
    shared_full, shared_sum = lax.optimization_barrier((shared_full, sum_dp(shared_pack)))

    active_grad_raw = dot_nt(cot_rows, own_out)
    gate_grad = jnp.sum(active.astype(F32) * active_grad_raw, axis=-1).reshape(nz, CAP)
    active_grad = active_grad_raw * gate_rows
    pre_low = jnp.concatenate(
        [
            active_grad * up_pre * gate_sig * (1.0 + gate_pre * (1.0 - gate_sig)),
            active_grad * gate_silu,
        ],
        1,
    ).astype(BF16)
    gated_active = (active.astype(F32) * gate_rows).astype(BF16)
    out_parts, pre_low, shared_full = lax.optimization_barrier((out_parts, pre_low, shared_full))
    rows_grad = dot(pre_low, own_in).astype(BF16)
    rows_grad, out_parts = lax.optimization_barrier((rows_grad, out_parts))
    grad_parts = send_back(rows_grad)
    routed, pre_low, gated_active = lax.optimization_barrier(
        (combine(out_parts), pre_low, gated_active)
    )
    routed = scatter_z(routed).astype(F32)
    token_grad = jnp.sum(jnp.where(own_place, gate_grad[:, :, None], 0.0), axis=1)
    token_grad = token_grad.reshape(nz, -1, 128)
    token_plane = jnp.stack(
        [
            lay.over_z(lax.dynamic_index_in_dim(token_grad, me_z ^ k, 0, keepdims=False), k)
            for k in range(nz)
        ]
    )
    token_home = jnp.stack([lay.over_t(token_plane, k) for k in range(nt)])
    experts = jnp.arange(EXPERTS, dtype=jnp.int32)
    came_from = (me_t ^ (experts % nt)) * nz + (me_z ^ (experts // nt))
    probs_grad = lax.dot_general(
        token_home.reshape(EXPERTS, rows),
        (experts[:, None] == came_from[None, :]).astype(F32),
        (((0,), (0,)), ((), ())),
        precision=lax.Precision.HIGHEST,
        preferred_element_type=F32,
    )

    grad_in_own = dot_tn(pre_low, expert_rows).astype(BF16)
    grad_out_own = dot_tn(gated_active, cot_rows).astype(BF16)
    grad_parts, grad_in_own, grad_out_own, probs_grad = lax.optimization_barrier(
        (grad_parts, grad_in_own, grad_out_own, probs_grad)
    )
    routed, shared_part, shared_grad_full = lax.optimization_barrier(
        (routed, scatter_t(shared_full), shared_grad_full)
    )
    shared_grad = swap_t(
        jnp.swapaxes(shared_grad_full.astype(BF16).reshape(rows, nt, part), 0, 1)
    )
    shared_grad = jnp.sum(shared_grad.astype(F32), axis=0)
    grad_pieces = take_apart(lay, ids, grad_in_own, grad_out_own, f_loc, d_loc, width)
    routed_grad = scatter_z(combine(grad_parts)).astype(F32)
    grad_class = [
        sum(lay.over_c(grad_pieces[3 * k + g], k).astype(F32) for k in range(nq)).astype(BF16)
        for g in range(3)
    ]
    routed_grad, grad_class = lax.optimization_barrier((routed_grad, grad_class))
    grad_plane = [swap_z(grad_class[g].reshape(nz, nt, f_loc, d_loc)) for g in range(3)]

    logits_grad = router_probs * (
        probs_grad - jnp.sum(router_probs * probs_grad, axis=-1, keepdims=True)
    )
    router_part = lax.dot_general(
        logits_grad,
        ffn_low.astype(F32),
        (((0,), (0,)), ((), ())),
        precision=lax.Precision.HIGHEST,
        preferred_element_type=F32,
    )
    router_slice = lax.dynamic_slice_in_dim(router_t, me_t * part, part, 1)
    ffn_grad = (
        shared_grad
        + routed_grad
        + lax.dot_general(
            logits_grad,
            router_slice.astype(F32),
            (((1,), (0,)), ((), ())),
            precision=lax.Precision.HIGHEST,
            preferred_element_type=F32,
        )
    )
    scaled = ffn_scale * ffn_grad
    ffn_gain_part = jnp.sum(ffn_grad * ffn_hat, axis=0)
    residual_grad = cot_part.astype(F32) + ffn_inverse * (
        scaled - ffn_hat * row_mean(ffn_hat * scaled)
    )
    residual_low = gather_t(residual_grad.astype(BF16))

    output_part = lax.optimization_barrier((residual + routed + shared_part).astype(BF16))
    residual_low, grad_plane[0], output_part = lax.optimization_barrier(
        (residual_low, grad_plane[0], output_part)
    )
    grad_out_w = dot_tn(attended_low, residual_low)
    attended_grad = dot_nt(residual_low, out_w).astype(BF16)
    query_nope_grad, query_turned_grad, kv_grad, rope_grad = attend_back(
        lengths,
        query_nope,
        query_rope,
        keys_values,
        key_rope,
        attended_grad,
        log_totals,
        heads,
        score_scale,
    )
    def to_columns(values):
        return [
            lay.over_t(lax.dynamic_index_in_dim(values, me_t ^ k, 1, keepdims=False), k)
            for k in range(nt)
        ]

    grad_home = [to_columns(grad_plane[0]), None, None]
    query_turned_grad, grad_plane[1], grad_home[0] = lax.optimization_barrier(
        (query_turned_grad, grad_plane[1], grad_home[0])
    )
    turned_first, turned_second = rotate_back(
        query_turned_grad[:, : heads * half], query_turned_grad[:, heads * half :], wide_cos, wide_sin
    )
    query_grad = jnp.concatenate(
        [query_nope_grad, turned_first.astype(BF16), turned_second.astype(BF16)], 1
    )
    rope_sum = rope_grad.reshape(rows, 2, heads, half).sum(2)
    key_rope_part = jnp.concatenate(
        rotate_back(
            rope_sum[:, 0], rope_sum[:, 1], wide_cos[:, :half], wide_sin[:, :half]
        ),
        1,
    )
    latent_part = dot_nt(kv_grad, up_w)
    grad_kv_gain = jnp.sum(latent_part * latent_hat, axis=0)
    scaled_kv = kv_scale * latent_part
    latent_back = kv_inverse * (
        scaled_kv - latent_hat * jnp.mean(latent_hat * scaled_kv, axis=-1, keepdims=True)
    )
    down_grad = jnp.concatenate([latent_back, key_rope_part], -1).astype(BF16)
    normed_full, output = lax.optimization_barrier(
        (dot(query_grad, query_t) + dot(down_grad, down_t), gather_t(output_part))
    )
    pieces = [lay.over_t(part_for(normed_full, k).astype(BF16), k) for k in range(1, nt)]
    pieces[0], query_grad, kv_grad, down_grad = lax.optimization_barrier(
        (pieces[0], query_grad, kv_grad, down_grad)
    )
    normed_grad = part_for(normed_full, 0) + sum(piece.astype(F32) for piece in pieces)
    normed_grad, grad_plane[2], grad_home[1] = lax.optimization_barrier(
        (normed_grad, grad_plane[2], to_columns(grad_plane[1]))
    )
    attn_hat = own_part(hidden).astype(F32) * attn_inverse
    scaled_in = lax.dynamic_slice_in_dim(attn_scale, me_t * part, part, 0) * normed_grad
    attn_gain_part = jnp.sum(normed_grad * attn_hat, axis=0)
    input_grad = residual_grad + attn_inverse * (
        scaled_in - attn_hat * row_mean(attn_hat * scaled_in)
    )
    input_low, grad_plane[2] = lax.optimization_barrier((input_grad.astype(BF16), grad_plane[2]))
    grad_home[2] = to_columns(grad_plane[2])
    grad_expert_in, grad_expert_out = home_gradients(lay, ids, grad_home, f_loc, d_loc)
    grad_hidden = gather_t_direct(input_low)

    def spread(values):
        return lax.dynamic_update_slice(
            jnp.zeros((1, width), F32), values[None], (jnp.int32(0), me_t * part)
        )

    kv_gain_row = jnp.pad(
        grad_kv_gain.reshape(ndp, lat_loc), ((0, 0), (0, d_loc - lat_loc))
    ).reshape(1, width)
    gain_grads = jnp.concatenate([spread(attn_gain_part), spread(ffn_gain_part), kv_gain_row], 0)
    front_sum = sum_dp(
        jnp.concatenate(
            [
                by_owner(dot_tn(down_grad, normed_low)),
                by_owner(jnp.pad(gain_grads, ((0, 13), (0, 0)))),
                by_owner(router_part),
                by_owner(dot_tn(query_grad, normed_low)),
                by_owner(grad_out_w),
                dot_tn(latent_low, kv_grad).astype(BF16).reshape(ndp, -1, d_loc),
            ],
            1,
        )
    )
    own_sum = front_sum[: down_rows + EXPERTS]
    own_low = own_sum.astype(BF16)
    for k in range(1, nt):
        own_sum = own_sum + lay.over_t(own_low, k).astype(F32)
    at = down_rows + 2 * EXPERTS
    return (
        output,
        grad_hidden,
        own_sum[down_rows],
        jnp.transpose(by_head(front_sum[at : at + q_rows])),
        jnp.transpose(own_sum[:down_rows]),
        own_sum[down_rows + 2, :lat_loc],
        front_sum[at + q_rows + out_rows :].reshape(w_kv_up.shape),
        front_sum[at + q_rows : at + q_rows + out_rows],
        own_sum[down_rows + 1],
        jnp.transpose(front_sum[down_rows + EXPERTS : at]),
        grad_expert_in,
        grad_expert_out,
        jnp.swapaxes(shared_sum[: 2 * ffs].reshape(2, ffs, d_loc), 1, 2),
        shared_sum[2 * ffs :],
    )


def solution(mesh):
    return jax.shard_map(
        functools.partial(body, Layout(mesh.shape["dp"], mesh.shape["tensor"])),
        mesh=mesh,
        in_specs=(
            P("dp", None),
            P("dp"),
            P("dp", None),
            P("dp"),
            P("dp", "tensor"),
            P("dp", None),
            P("dp"),
            P("dp", "tensor"),
            P("tensor", "dp"),
            P("dp"),
            P("dp", None),
            P(None, None, "dp", "tensor"),
            P(None, "tensor", "dp"),
            P(None, "dp", "tensor"),
            P("tensor", "dp"),
            P("dp", None),
        ),
        out_specs=(
            P("dp", None),
            P("dp", None),
            P("dp"),
            P("dp", "tensor"),
            P("dp", None),
            P("dp"),
            P("dp", "tensor"),
            P("tensor", "dp"),
            P("dp"),
            P("dp", None),
            P(None, None, "dp", "tensor"),
            P(None, "tensor", "dp"),
            P(None, "dp", "tensor"),
            P("tensor", "dp"),
        ),
        check_vma=False,
    )
```

```python
import functools
import math

import jax
import jax.numpy as jnp
from jax import lax
from jax.experimental import pallas as pl
from jax.experimental.pallas import tpu as pltpu
from jax.sharding import PartitionSpec as P

NOPE = 128
ROPE = 64
VDIM = 128
LATENT = 512
TOP = 6
EXPERTS = 16
CAP = 512

EPSILON = 1e-06
NEGATIVE = -1e30
F32 = jnp.float32
BF16 = jnp.bfloat16


def dot(a, b):
    return jnp.dot(a, b, preferred_element_type=F32)


def dot_nt(a, b):
    return lax.dot_general(a, b, (((1,), (1,)), ((), ())), preferred_element_type=F32)


def dot_tn(a, b):
    return lax.dot_general(a, b, (((0,), (0,)), ((), ())), preferred_element_type=F32)


def rotate(first, second, cosine, sine):
    return first * cosine - second * sine, second * cosine + first * sine


def rotate_back(first, second, cosine, sine):
    return first * cosine + second * sine, second * cosine - first * sine


def angle_tables(rows_count):
    positions = jnp.arange(rows_count, dtype=F32)
    freqs = jnp.exp(jnp.arange(ROPE // 2, dtype=F32) * (-2.0 * math.log(10000.0) / ROPE))
    angles = positions[:, None] * freqs[None, :]
    return (jnp.cos(angles), jnp.sin(angles))


def inverse_rms(values):
    return lax.rsqrt(jnp.mean(values * values, axis=-1, keepdims=True) + EPSILON)


class Layout:
    def __init__(self, n_dp, n_tensor):
        self.dp, self.t = n_dp, n_tensor
        self.q = n_dp * n_tensor // EXPERTS
        self.z = n_dp // self.q
        if self.z * self.t != EXPERTS or self.z * self.q != n_dp:
            raise ValueError("mesh")
        self.z_groups = [[c + self.q * z for z in range(self.z)] for c in range(self.q)]

    def over_t(self, values, k):
        if k == 0:
            return values
        return lax.ppermute(values, "tensor", [(i, i ^ k) for i in range(self.t)])

    def over_z(self, values, k):
        if k == 0:
            return values
        return lax.ppermute(values, "dp", [(d, d ^ (k * self.q)) for d in range(self.dp)])

    def over_c(self, values, k):
        if k == 0:
            return values
        return lax.ppermute(values, "dp", [(d, d ^ k) for d in range(self.dp)])


def lay_out_weights(lay, ids, stacks, f_loc, d_loc, width):
    ffe = f_loc * lay.t
    count = len(stacks) // lay.q

    def kernel(ids_ref, *refs):
        for kc in range(lay.q):
            columns = pl.ds(pl.multiple_of((ids_ref[1] ^ kc) * d_loc, 128), d_loc)
            for g in range(count):
                refs[-1][g, :, columns] = refs[count * kc + g][0]

    own = pl.pallas_call(
        kernel,
        out_shape=jax.ShapeDtypeStruct((count, ffe, width), BF16),
        grid_spec=pltpu.PrefetchScalarGridSpec(
            num_scalar_prefetch=1,
            grid=(lay.t, lay.z),
            in_specs=[
                pl.BlockSpec(
                    (1, f_loc, d_loc), lambda kt, kz, ids: ((kz ^ ids[0]) * lay.t + kt, 0, 0)
                )
            ]
            * len(stacks),
            out_specs=pl.BlockSpec(
                (count, f_loc, lay.q * d_loc), lambda kt, kz, ids: (0, kt, kz)
            ),
        ),
        cost_estimate=pl.CostEstimate(
            flops=0, bytes_accessed=4 * count * ffe * width, transcendentals=0
        ),
        compiler_params=pltpu.CompilerParams(vmem_limit_bytes=32 << 20),
        name="lay_out_weights",
    )(ids, *stacks)
    return own.reshape(count * ffe, width)


def take_apart(lay, ids, grad_in, grad_out, f_loc, d_loc, width):
    ffe = f_loc * lay.t

    def kernel(ids_ref, in_ref, out_ref, *targets):
        for kc in range(lay.q):
            columns = pl.ds(pl.multiple_of((ids_ref[1] ^ kc) * d_loc, 128), d_loc)
            for g in range(2):
                targets[3 * kc + g][0] = in_ref[g, :, columns]
            targets[3 * kc + 2][0] = out_ref[:, columns]

    shape = jax.ShapeDtypeStruct((lay.t * lay.z, f_loc, d_loc), BF16)
    spec = pl.BlockSpec((1, f_loc, d_loc), lambda kt, kz, ids: (kz * lay.t + kt, 0, 0))
    return pl.pallas_call(
        kernel,
        out_shape=(shape,) * (3 * lay.q),
        grid_spec=pltpu.PrefetchScalarGridSpec(
            num_scalar_prefetch=1,
            grid=(lay.t, lay.z),
            in_specs=[
                pl.BlockSpec((2, f_loc, lay.q * d_loc), lambda kt, kz, ids: (0, kt, kz)),
                pl.BlockSpec((f_loc, lay.q * d_loc), lambda kt, kz, ids: (kt, kz)),
            ],
            out_specs=(spec,) * (3 * lay.q),
        ),
        cost_estimate=pl.CostEstimate(
            flops=0, bytes_accessed=12 * ffe * width, transcendentals=0
        ),
        compiler_params=pltpu.CompilerParams(vmem_limit_bytes=32 << 20),
        name="take_apart",
    )(ids, grad_in.reshape(2, ffe, width), grad_out)


def home_gradients(lay, ids, parts, f_loc, d_loc):
    def kernel(ids_ref, *refs):
        sources, (in_ref, out_ref) = refs[: 3 * lay.t], refs[3 * lay.t :]
        for k in range(lay.t):

            @pl.when((pl.program_id(1) ^ ids_ref[2]) == k)
            def _(k=k):
                for g in range(2):
                    in_ref[0, g] = sources[g * lay.t + k][0].astype(F32)
                out_ref[0] = sources[2 * lay.t + k][0].astype(F32)

    grad_in, grad_out = pl.pallas_call(
        kernel,
        out_shape=(
            jax.ShapeDtypeStruct((EXPERTS, 2, f_loc, d_loc), F32),
            jax.ShapeDtypeStruct((EXPERTS, f_loc, d_loc), F32),
        ),
        grid_spec=pltpu.PrefetchScalarGridSpec(
            num_scalar_prefetch=1,
            grid=(lay.z, lay.t),
            in_specs=[pl.BlockSpec((1, f_loc, d_loc), lambda z, t, ids: (z, 0, 0))] * (3 * lay.t),
            out_specs=(
                pl.BlockSpec((1, 2, f_loc, d_loc), lambda z, t, ids: (z * lay.t + t, 0, 0, 0)),
                pl.BlockSpec((1, f_loc, d_loc), lambda z, t, ids: (z * lay.t + t, 0, 0)),
            ),
        ),
        cost_estimate=pl.CostEstimate(
            flops=0, bytes_accessed=18 * EXPERTS * f_loc * d_loc, transcendentals=0
        ),
        compiler_params=pltpu.CompilerParams(vmem_limit_bytes=32 << 20),
        name="home_gradients",
    )(ids, *[piece for part in parts for piece in part])
    return jnp.swapaxes(grad_in, 2, 3), grad_out


def join_columns(parts, me, count):
    rows, part = parts[0].shape
    block = min(512, rows)

    def kernel(me_ref, *refs):
        for k in range(count):

            @pl.when(pl.program_id(1) == k)
            def _(k=k):
                refs[count][...] = refs[k][...]

    return pl.pallas_call(
        kernel,
        out_shape=jax.ShapeDtypeStruct((rows, count * part), parts[0].dtype),
        grid_spec=pltpu.PrefetchScalarGridSpec(
            num_scalar_prefetch=1,
            grid=(rows // block, count),
            in_specs=[pl.BlockSpec((block, part), lambda i, k, me: (i, 0))] * count,
            out_specs=pl.BlockSpec((block, part), lambda i, k, me: (i, me[0] ^ k)),
        ),
        cost_estimate=pl.CostEstimate(
            flops=0, bytes_accessed=4 * rows * part * count, transcendentals=0
        ),
        name="join_columns",
    )(me.reshape(1).astype(jnp.int32), *parts)


def score_block(q_ref, r_ref, k_ref, kr_ref, head, step, keys, block, length, scale):
    half = r_ref.shape[1] // 2
    lanes = lax.broadcasted_iota(jnp.int32, r_ref.shape, 1) % half // (ROPE // 2)
    turned = jnp.where(lanes == head, r_ref[...], jnp.zeros_like(r_ref))
    raw = lax.dot_general(
        q_ref[...], k_ref[:keys], (((1,), (1,)), ((), ())), preferred_element_type=F32
    ) + lax.dot_general(
        turned, kr_ref[:keys], (((1,), (1,)), ((), ())), preferred_element_type=F32
    )
    rows = lax.broadcasted_iota(jnp.int32, raw.shape, 0) + step * block
    cols = lax.broadcasted_iota(jnp.int32, raw.shape, 1)
    allowed = (cols <= rows) & (cols < length)
    return jnp.where(allowed, raw * scale, NEGATIVE), turned


def attend(length, query, query_rope, kv, key_rope, heads, scale):
    rows = query.shape[0]
    block = min(256, rows)
    steps = rows // block

    def kernel(len_ref, q_ref, r_ref, k_ref, v_ref, kr_ref, o_ref, total_ref):
        head, step = pl.program_id(0), pl.program_id(1)
        for n in range(steps):

            @pl.when(step == n)
            def _(n=n):
                keys = (n + 1) * block
                scores, _ = score_block(
                    q_ref, r_ref, k_ref, kr_ref, head, n, keys, block, len_ref[0], scale
                )
                highest = jnp.max(scores, axis=-1, keepdims=True)
                expo = jnp.exp(scores - highest)
                totals = jnp.sum(expo, axis=-1, keepdims=True)
                weights = (expo * (1.0 / totals)).astype(BF16)
                o_ref[...] = dot(weights, v_ref[:keys]).astype(BF16)
                total_ref[0] = jnp.broadcast_to(highest + jnp.log(totals), (block, 128))

    return pl.pallas_call(
        kernel,
        out_shape=(
            jax.ShapeDtypeStruct((rows, heads * VDIM), BF16),
            jax.ShapeDtypeStruct((heads, rows, 128), F32),
        ),
        grid_spec=pltpu.PrefetchScalarGridSpec(
            num_scalar_prefetch=1,
            grid=(heads, steps),
            in_specs=[
                pl.BlockSpec((block, NOPE), lambda h, i, n: (i, h)),
                pl.BlockSpec((block, query_rope.shape[1]), lambda h, i, n: (i, 0)),
                pl.BlockSpec((rows, NOPE), lambda h, i, n: (0, 2 * h)),
                pl.BlockSpec((rows, VDIM), lambda h, i, n: (0, 2 * h + 1)),
                pl.BlockSpec((rows, key_rope.shape[1]), lambda h, i, n: (0, 0)),
            ],
            out_specs=(
                pl.BlockSpec((block, VDIM), lambda h, i, n: (i, h)),
                pl.BlockSpec((1, block, 128), lambda h, i, n: (h, i, 0)),
            ),
        ),
        cost_estimate=pl.CostEstimate(
            flops=heads * rows * rows * 512,
            bytes_accessed=8 * rows * heads * 512,
            transcendentals=heads * rows * rows,
        ),
        compiler_params=pltpu.CompilerParams(vmem_limit_bytes=32 << 20),
        name="attend",
    )(length, query, query_rope, kv, kv, key_rope)


def attend_back(length, query, query_rope, kv, key_rope, out_grad, log_totals, heads, scale):
    rows = query.shape[0]
    block = min(256, rows)
    steps = rows // block
    turned_cols = query_rope.shape[1]

    def kernel(
        len_ref, q_ref, r_ref, k_ref, v_ref, kr_ref, do_ref, total_ref,
        dq_ref, dr_ref, dkv_ref, dkr_ref, dk_acc, dv_acc,
    ):
        head, step = pl.program_id(0), pl.program_id(1)

        @pl.when(step == 0)
        def _():
            dk_acc[...] = jnp.zeros_like(dk_acc)
            dv_acc[...] = jnp.zeros_like(dv_acc)

        @pl.when((step == 0) & (head == 0))
        def _():
            dr_ref[...] = jnp.zeros_like(dr_ref)
            dkr_ref[...] = jnp.zeros_like(dkr_ref)

        for n in range(steps):

            @pl.when(step == n)
            def _(n=n):
                keys = (n + 1) * block
                scores, turned = score_block(
                    q_ref, r_ref, k_ref, kr_ref, head, n, keys, block, len_ref[0], scale
                )
                probs = jnp.exp(scores - total_ref[0][:, :1])
                prob_grad = lax.dot_general(
                    do_ref[...], v_ref[:keys], (((1,), (1,)), ((), ())), preferred_element_type=F32
                )
                centre = jnp.sum(probs * prob_grad, axis=-1, keepdims=True)
                score_grad = (probs * (prob_grad - centre)).astype(BF16)
                probs_low = probs.astype(BF16)
                dq_ref[...] = (dot(score_grad, k_ref[:keys]) * scale).astype(BF16)
                half = turned_cols // 2
                lanes = lax.broadcasted_iota(jnp.int32, (block, turned_cols), 1)
                lanes = lanes % half // (ROPE // 2)
                turned_grad = dot(score_grad, kr_ref[:keys]) * scale
                dr_ref[n * block : keys] += jnp.where(lanes == head, turned_grad, 0.0)
                dk_acc[:keys] += dot_tn(score_grad, q_ref[...]) * scale
                dkr_ref[:keys] += dot_tn(score_grad, turned) * scale
                dv_acc[:keys] += dot_tn(probs_low, do_ref[...])

        @pl.when(step == steps - 1)
        def _():
            dkv_ref[:, :NOPE] = dk_acc[...].astype(BF16)
            dkv_ref[:, NOPE:] = dv_acc[...].astype(BF16)

    return pl.pallas_call(
        kernel,
        out_shape=(
            jax.ShapeDtypeStruct((rows, heads * NOPE), BF16),
            jax.ShapeDtypeStruct((rows, turned_cols), F32),
            jax.ShapeDtypeStruct((rows, heads * (NOPE + VDIM)), BF16),
            jax.ShapeDtypeStruct((rows, turned_cols), F32),
        ),
        grid_spec=pltpu.PrefetchScalarGridSpec(
            num_scalar_prefetch=1,
            grid=(heads, steps),
            in_specs=[
                pl.BlockSpec((block, NOPE), lambda h, i, n: (i, h)),
                pl.BlockSpec((block, turned_cols), lambda h, i, n: (i, 0)),
                pl.BlockSpec((rows, NOPE), lambda h, i, n: (0, 2 * h)),
                pl.BlockSpec((rows, VDIM), lambda h, i, n: (0, 2 * h + 1)),
                pl.BlockSpec((rows, turned_cols), lambda h, i, n: (0, 0)),
                pl.BlockSpec((block, VDIM), lambda h, i, n: (i, h)),
                pl.BlockSpec((1, block, 128), lambda h, i, n: (h, i, 0)),
            ],
            out_specs=(
                pl.BlockSpec((block, NOPE), lambda h, i, n: (i, h)),
                pl.BlockSpec((rows, turned_cols), lambda h, i, n: (0, 0)),
                pl.BlockSpec((rows, NOPE + VDIM), lambda h, i, n: (0, h)),
                pl.BlockSpec((rows, turned_cols), lambda h, i, n: (0, 0)),
            ),
            scratch_shapes=[pltpu.VMEM((rows, NOPE), F32), pltpu.VMEM((rows, VDIM), F32)],
        ),
        cost_estimate=pl.CostEstimate(
            flops=heads * rows * rows * 1600,
            bytes_accessed=16 * rows * heads * 512,
            transcendentals=heads * rows * rows,
        ),
        compiler_params=pltpu.CompilerParams(vmem_limit_bytes=40 << 20),
        name="attend_back",
    )(length, query, query_rope, kv, kv, key_rope, out_grad, log_totals)


def in_order(values, me, count):
    zero = jnp.zeros_like(values[0])
    ordered = []
    for j in range(count):
        total = zero
        for k in range(count):
            total = jnp.where((me ^ k) == j, values[k], total)
        ordered.append(total)
    return jnp.stack(ordered)


def body(
    lay,
    hidden,
    lengths,
    routes,
    attn_gain,
    w_query,
    w_kv_down,
    kv_gain,
    w_kv_up,
    w_out,
    ffn_gain,
    w_router,
    w_expert_in,
    w_expert_out,
    w_shared_in,
    w_shared_out,
    cotangent,
):
    rows, width = hidden.shape
    nz, nt, nq, ndp = lay.z, lay.t, lay.q, lay.dp
    me_dp = lax.axis_index("dp")
    me_t = lax.axis_index("tensor")
    me_z = me_dp // nq
    me_c = me_dp % nq
    part = width // nt
    d_loc = w_query.shape[0]
    f_loc = w_expert_out.shape[1]
    ffe = f_loc * nt
    heads = w_query.shape[1] // (NOPE + ROPE)
    score_scale = (NOPE + ROPE) ** (-0.5)

    def own_part(values):
        return lax.dynamic_slice_in_dim(values, me_t * part, part, 1)

    def gather_z(values):
        return lax.all_gather(values, "dp", axis=0, tiled=False, axis_index_groups=lay.z_groups)

    def scatter_z(values):
        return lax.psum_scatter(
            values, "dp", scatter_dimension=0, tiled=False, axis_index_groups=lay.z_groups
        )

    def gather_t(values):
        return lax.all_gather(values, "tensor", axis=1, tiled=True)

    def scatter_t(values):
        return lax.psum_scatter(
            values.astype(BF16), "tensor", scatter_dimension=1, tiled=True
        ).astype(F32)

    def swap_t(values):
        return lax.all_to_all(values, "tensor", split_axis=0, concat_axis=0, tiled=True)

    def swap_z(values):
        return lax.all_to_all(
            values,
            "dp",
            split_axis=0,
            concat_axis=0,
            axis_index_groups=lay.z_groups,
            tiled=True,
        )

    def gather_t_direct(values):
        return join_columns([lay.over_t(values, k) for k in range(nt)], me_t, nt)

    def part_for(values, k):
        return lax.dynamic_slice_in_dim(values, (me_t ^ k) * part, part, 1)

    def scatter_t_direct(values):
        total = part_for(values, 0)
        for k in range(1, nt):
            total = total + lay.over_t(part_for(values, k).astype(BF16), k).astype(F32)
        return total

    ids = jnp.stack([me_z, me_c, me_t]).astype(jnp.int32)

    packed = jnp.concatenate(
        [jnp.swapaxes(w_expert_in, 2, 3), w_expert_out[:, None]], 1
    ).reshape(nz, nt, 3, f_loc, d_loc)
    by_column = swap_t(jnp.swapaxes(packed, 0, 1))

    lat_loc = kv_gain.shape[0]
    q_rows, down_rows, out_rows = w_query.shape[1], w_kv_down.shape[1], w_out.shape[0]
    half = ROPE // 2

    def by_kind(turned):
        split = turned.reshape(heads, NOPE + ROPE, -1)
        return jnp.concatenate(
            [
                split[:, :NOPE].reshape(heads * NOPE, -1),
                split[:, NOPE : NOPE + half].reshape(heads * half, -1),
                split[:, NOPE + half :].reshape(heads * half, -1),
            ],
            0,
        )

    def by_head(rows_in):
        nope = rows_in[: heads * NOPE].reshape(heads, NOPE, -1)
        first = rows_in[heads * NOPE : heads * (NOPE + half)].reshape(heads, half, -1)
        second = rows_in[heads * (NOPE + half) :].reshape(heads, half, -1)
        return jnp.concatenate([nope, first, second], 1).reshape(heads * (NOPE + ROPE), -1)

    gains = jnp.stack([attn_gain, ffn_gain, jnp.pad(kv_gain, (0, d_loc - lat_loc))])
    front_pack = jnp.concatenate(
        [
            by_kind(jnp.transpose(w_query)),
            jnp.transpose(w_kv_down),
            jnp.transpose(w_router),
            jnp.pad(gains, ((0, 13), (0, 0))),
            w_out,
            w_kv_up.reshape(-1, d_loc),
        ],
        0,
    )
    front = lax.all_gather(front_pack, "dp", axis=0, tiled=False)

    valid_length = lengths[0]
    valid_rows = lax.broadcasted_iota(jnp.int32, (rows, 1), 0) < valid_length
    cot_low = jnp.where(valid_rows, cotangent, jnp.zeros_like(cotangent))
    cot_part = own_part(cot_low)
    route_own = jnp.pad(jnp.transpose(routes), ((0, -TOP % 8), (0, 0)), constant_values=-1)
    route_all = in_order([lay.over_z(route_own, k) for k in range(nz)], me_z, nz)
    inputs = hidden.astype(F32)
    attn_inverse = inverse_rms(inputs)
    cosine, sine = angle_tables(rows)
    wide_cos, wide_sin = jnp.tile(cosine, (1, heads)), jnp.tile(sine, (1, heads))
    front, attn_inverse, wide_cos, wide_sin, route_all = lax.optimization_barrier(
        (front, attn_inverse, wide_cos, wide_sin, route_all)
    )

    plane_ids = me_z * nt + jnp.arange(nt, dtype=jnp.int32)
    member = jnp.any(route_all[:, :, :, None] == plane_ids[None, None, None, :], axis=1)
    row_ids = lax.broadcasted_iota(jnp.int32, (rows, rows), 0)
    col_ids = lax.broadcasted_iota(jnp.int32, (rows, rows), 1)
    before = (col_ids < row_ids).astype(BF16)
    position = jnp.einsum("ij,sje->sei", before, member.astype(BF16), preferred_element_type=F32)
    key = jnp.where(jnp.swapaxes(member, 1, 2), position.astype(jnp.int32), -1)
    slots_iota = lax.broadcasted_iota(jnp.int32, (1, 1, CAP, 1), 2)

    def place_of(keys):
        return (keys[:, :, None, :] == slots_iota).astype(BF16)

    place = place_of(key)
    own_key = lax.dynamic_index_in_dim(key, me_t, 1, keepdims=False)
    own_place = own_key[:, None, :] == slots_iota[0]

    def pick_rows(values):
        picked = jnp.einsum("sepk,skd->espd", place, values, preferred_element_type=F32)
        return picked.astype(BF16).reshape(nt, nz * CAP, part)

    def send_out(picked):
        return jnp.swapaxes(swap_t(picked), 0, 1).reshape(nz * CAP, width)

    def send_back(values):
        return swap_t(jnp.swapaxes(values.reshape(nz * CAP, nt, part), 0, 1))

    def combine(parts):
        parts = parts.reshape(nt, nz, CAP, part)
        summed = jnp.einsum("sepk,espd->skd", place, parts, preferred_element_type=F32)
        return summed.astype(BF16)


    def rows_of(first, count):
        return jnp.swapaxes(front[:, first : first + count], 0, 1).reshape(count, width)

    query_t = rows_of(0, q_rows)
    down_t = rows_of(q_rows, down_rows)
    at = q_rows + down_rows
    router_t = rows_of(at, EXPERTS)
    gain_attn = front[:, at + EXPERTS].reshape(-1)
    gain_ffn = front[:, at + EXPERTS + 1].reshape(-1)
    gain_kv = front[:, at + EXPERTS + 2, :lat_loc].reshape(-1)
    at = at + 2 * EXPERTS
    out_w = rows_of(at, out_rows)
    up_w = front[:, at + out_rows :].reshape(LATENT, heads * (NOPE + VDIM))

    attn_scale = gain_attn.astype(F32)
    normed_low = (inputs * attn_inverse * attn_scale).astype(BF16)
    query = dot_nt(normed_low, query_t)
    nope_cols = heads * NOPE
    query_nope = query[:, :nope_cols].astype(BF16)
    query_rope = jnp.concatenate(
        rotate(
            query[:, nope_cols : nope_cols + heads * half],
            query[:, nope_cols + heads * half :],
            wide_cos,
            wide_sin,
        ),
        1,
    ).astype(BF16)
    latent_all = dot_nt(normed_low, down_t)
    latent_all, by_column = lax.optimization_barrier((latent_all, by_column))
    by_column = jnp.transpose(by_column, (2, 1, 0, 3, 4))
    by_plane = [swap_z(by_column[g]) for g in range(2)]
    latent = latent_all[:, :LATENT]
    kv_inverse = inverse_rms(latent)
    latent_hat = latent * kv_inverse
    kv_scale = gain_kv.astype(F32)
    latent_low = (latent_hat * kv_scale).astype(BF16)
    key_turned = jnp.concatenate(
        rotate(
            latent_all[:, LATENT : LATENT + half],
            latent_all[:, LATENT + half :],
            wide_cos[:, :half],
            wide_sin[:, :half],
        ),
        1,
    ).astype(BF16)
    copies = (2 * half, 2 * heads * half)
    to_col = lax.broadcasted_iota(jnp.int32, copies, 1)
    from_col = to_col // (heads * half) * half + to_col % half
    repeat = (lax.broadcasted_iota(jnp.int32, copies, 0) == from_col).astype(BF16)
    key_rope = dot(key_turned, repeat).astype(BF16)
    keys_values = dot(latent_low, up_w).astype(BF16)
    attended_low, log_totals = attend(
        lengths, query_nope, query_rope, keys_values, key_rope, heads, score_scale
    )
    attn_part, by_plane[0] = lax.optimization_barrier((dot(attended_low, out_w), by_plane[0]))
    attn_sum = scatter_t(attn_part)
    residual = own_part(hidden).astype(F32) + attn_sum

    def row_mean(values):
        partial = jnp.sum(values, axis=-1).reshape(-1, 128)
        return lax.psum(partial, "tensor").reshape(-1, 1) * (1.0 / width)

    ffn_inverse = lax.rsqrt(row_mean(residual * residual) + EPSILON)
    ffn_hat = residual * ffn_inverse
    ffn_scale = lax.dynamic_slice_in_dim(gain_ffn, me_t * part, part, 0).astype(F32)
    ffn_part = (ffn_hat * ffn_scale).astype(BF16)

    ffn_part, by_plane[1] = lax.optimization_barrier((ffn_part, by_plane[1]))
    ffn_all = gather_z(ffn_part)
    ffn_low = gather_t_direct(ffn_part)
    ffn_all, ffn_low, cot_ready = lax.optimization_barrier((ffn_all, ffn_low, cot_part))
    picked, by_plane[0], by_plane[1] = lax.optimization_barrier(
        (pick_rows(ffn_all), by_plane[0], by_plane[1])
    )
    expert_rows = send_out(picked)
    shared_pack = jnp.concatenate(
        [jnp.swapaxes(w_shared_in, 1, 2).reshape(-1, d_loc), w_shared_out], 0
    )
    def own_weights(matrices, order):
        pieces = [by_plane[g].reshape(nz * nt, f_loc, d_loc) for g in matrices]
        stacks = [lay.over_c(piece, k) for k in range(nq) for piece in pieces]
        return lay_out_weights(lay, order, stacks, f_loc, d_loc, width)

    own_in = own_weights((0, 1), ids * jnp.array([0, 1, 1], jnp.int32))
    cot_all, last_column, own_in = lax.optimization_barrier(
        (gather_z(cot_ready), by_column[2], own_in)
    )
    by_plane.append(
        jnp.stack(
            [
                lay.over_z(lax.dynamic_index_in_dim(last_column, me_z ^ k, 0, keepdims=False), k)
                for k in range(nz)
            ]
        )
    )

    by_plane[2], shared_pack, cot_picked = lax.optimization_barrier(
        (by_plane[2], shared_pack, pick_rows(cot_all))
    )
    cot_rows = send_out(cot_picked)
    shared_all = lax.all_gather(shared_pack, "dp", axis=0, tiled=False)
    own_out = own_weights((2,), ids)
    router_probs = jax.nn.softmax(dot_nt(ffn_low, router_t), axis=-1)
    probs_turned = jnp.transpose(router_probs).reshape(EXPERTS, -1, 128)
    own_probs = in_order(
        [
            lay.over_z(
                lax.dynamic_index_in_dim(
                    probs_turned, (me_z ^ k) * nt + me_t, 0, keepdims=False
                ),
                k,
            )
            for k in range(nz)
        ],
        me_z,
        nz,
    ).reshape(nz, rows)
    gate_rows = jnp.sum(jnp.where(own_place, own_probs[:, None, :], 0.0), axis=-1).reshape(
        nz * CAP, 1
    )
    gate_up = dot_nt(expert_rows, own_in)
    gate_pre, up_pre = gate_up[:, :ffe], gate_up[:, ffe:]
    gate_sig = jax.nn.sigmoid(gate_pre)
    gate_silu = gate_pre * gate_sig
    active = (gate_silu * up_pre).astype(BF16)
    rows_out = (dot(active, own_out) * gate_rows).astype(BF16)
    rows_out, cot_rows, shared_all = lax.optimization_barrier((rows_out, cot_rows, shared_all))
    out_parts = send_back(rows_out)
    active_grad_raw = dot_nt(cot_rows, own_out)
    gate_grad = jnp.sum(active.astype(F32) * active_grad_raw, axis=-1).reshape(nz, CAP)
    active_grad = active_grad_raw * gate_rows
    pre_low = jnp.concatenate(
        [
            active_grad * up_pre * gate_sig * (1.0 + gate_pre * (1.0 - gate_sig)),
            active_grad * gate_silu,
        ],
        1,
    ).astype(BF16)
    gated_active = (active.astype(F32) * gate_rows).astype(BF16)
    ffs = w_shared_out.shape[0]
    shared_in = jnp.swapaxes(shared_all[:, : 2 * ffs], 0, 1).reshape(2 * ffs, width)
    shared_out = jnp.swapaxes(shared_all[:, 2 * ffs :], 0, 1).reshape(ffs, width)
    shared_pre = dot_nt(ffn_low, shared_in)
    shared_gate, shared_up = shared_pre[:, :ffs], shared_pre[:, ffs:]
    shared_sig = jax.nn.sigmoid(shared_gate)
    shared_silu = shared_gate * shared_sig
    shared_act = (shared_silu * shared_up).astype(BF16)
    shared_full = dot(shared_act, shared_out)
    shared_act_grad = dot_nt(cot_low, shared_out)
    shared_pre_grad = jnp.concatenate(
        [
            shared_act_grad * shared_up * shared_sig * (1.0 + shared_gate * (1.0 - shared_sig)),
            shared_act_grad * shared_silu,
        ],
        1,
    ).astype(BF16)
    grad_shared_in = dot_tn(shared_pre_grad, ffn_low)
    grad_shared_out = dot_tn(shared_act, cot_low)

    out_parts, pre_low, shared_full = lax.optimization_barrier((out_parts, pre_low, shared_full))
    rows_grad = dot(pre_low, own_in).astype(BF16)
    rows_grad, out_parts = lax.optimization_barrier((rows_grad, out_parts))
    grad_parts = send_back(rows_grad)
    rows_grad, shared_late = lax.optimization_barrier((rows_grad, shared_pre_grad))
    shared_grad_full = dot(shared_late, shared_in)
    routed, pre_low, gated_active, shared_part = lax.optimization_barrier(
        (combine(out_parts), pre_low, gated_active, scatter_t(shared_full))
    )
    routed = scatter_z(routed).astype(F32)
    token_grad = jnp.sum(jnp.where(own_place, gate_grad[:, :, None], 0.0), axis=1)
    token_grad = token_grad.reshape(nz, -1, 128)
    token_plane = jnp.stack(
        [
            lay.over_z(lax.dynamic_index_in_dim(token_grad, me_z ^ k, 0, keepdims=False), k)
            for k in range(nz)
        ]
    )
    token_home = jnp.stack([lay.over_t(token_plane, k) for k in range(nt)])
    experts = jnp.arange(EXPERTS, dtype=jnp.int32)
    came_from = (me_t ^ (experts % nt)) * nz + (me_z ^ (experts // nt))
    probs_grad = lax.dot_general(
        token_home.reshape(EXPERTS, rows),
        (experts[:, None] == came_from[None, :]).astype(F32),
        (((0,), (0,)), ((), ())),
        precision=lax.Precision.HIGHEST,
        preferred_element_type=F32,
    )

    grad_in_own = dot_tn(pre_low, expert_rows).astype(BF16)
    grad_out_own = dot_tn(gated_active, cot_rows).astype(BF16)
    grad_parts, grad_in_own, grad_out_own, probs_grad, shared_grad_full = lax.optimization_barrier(
        (grad_parts, grad_in_own, grad_out_own, probs_grad, shared_grad_full)
    )
    routed, shared_ready = lax.optimization_barrier(
        (
            routed,
            jnp.swapaxes(shared_grad_full.astype(BF16).reshape(rows, nt, part), 0, 1),
        )
    )
    shared_grad = jnp.sum(swap_t(shared_ready).astype(F32), axis=0)
    grad_pieces = take_apart(lay, ids, grad_in_own, grad_out_own, f_loc, d_loc, width)
    routed_grad = scatter_z(combine(grad_parts)).astype(F32)
    grad_class = [
        sum(lay.over_c(grad_pieces[3 * k + g], k).astype(F32) for k in range(nq)).astype(BF16)
        for g in range(3)
    ]
    routed_grad, grad_class = lax.optimization_barrier((routed_grad, grad_class))
    grad_plane = [swap_z(grad_class[g].reshape(nz, nt, f_loc, d_loc)) for g in range(3)]

    logits_grad = router_probs * (
        probs_grad - jnp.sum(router_probs * probs_grad, axis=-1, keepdims=True)
    )
    router_part = lax.dot_general(
        logits_grad,
        ffn_low.astype(F32),
        (((0,), (0,)), ((), ())),
        precision=lax.Precision.HIGHEST,
        preferred_element_type=F32,
    )
    router_slice = lax.dynamic_slice_in_dim(router_t, me_t * part, part, 1)
    ffn_grad = (
        shared_grad
        + routed_grad
        + lax.dot_general(
            logits_grad,
            router_slice.astype(F32),
            (((1,), (0,)), ((), ())),
            precision=lax.Precision.HIGHEST,
            preferred_element_type=F32,
        )
    )
    scaled = ffn_scale * ffn_grad
    ffn_gain_part = jnp.sum(ffn_grad * ffn_hat, axis=0)
    residual_grad = cot_part.astype(F32) + ffn_inverse * (
        scaled - ffn_hat * row_mean(ffn_hat * scaled)
    )
    residual_low = gather_t(residual_grad.astype(BF16))

    def sum_dp(values):
        return lax.psum_scatter(values, "dp", scatter_dimension=0, tiled=False).astype(F32)

    def by_owner(values):
        return jnp.swapaxes(values.astype(BF16).reshape(-1, ndp, d_loc), 0, 1)

    shared_grads = jnp.concatenate([by_owner(grad_shared_in), by_owner(grad_shared_out)], 1)
    output_part = lax.optimization_barrier((residual + routed + shared_part).astype(BF16))
    residual_low, shared_grads, grad_plane[0], output_part = lax.optimization_barrier(
        (residual_low, shared_grads, grad_plane[0], output_part)
    )
    grad_out_w = dot_tn(attended_low, residual_low)
    attended_grad = dot_nt(residual_low, out_w).astype(BF16)
    query_nope_grad, query_turned_grad, kv_grad, rope_grad = attend_back(
        lengths,
        query_nope,
        query_rope,
        keys_values,
        key_rope,
        attended_grad,
        log_totals,
        heads,
        score_scale,
    )
    def to_columns(values):
        return [
            lay.over_t(lax.dynamic_index_in_dim(values, me_t ^ k, 1, keepdims=False), k)
            for k in range(nt)
        ]

    grad_home = [to_columns(grad_plane[0]), None, None]
    query_turned_grad, grad_plane[1], grad_home[0], shared_grads = lax.optimization_barrier(
        (query_turned_grad, grad_plane[1], grad_home[0], shared_grads)
    )
    shared_sum = sum_dp(shared_grads)
    turned_first, turned_second = rotate_back(
        query_turned_grad[:, : heads * half], query_turned_grad[:, heads * half :], wide_cos, wide_sin
    )
    query_grad = jnp.concatenate(
        [query_nope_grad, turned_first.astype(BF16), turned_second.astype(BF16)], 1
    )
    rope_sum = rope_grad.reshape(rows, 2, heads, half).sum(2)
    key_rope_part = jnp.concatenate(
        rotate_back(
            rope_sum[:, 0], rope_sum[:, 1], wide_cos[:, :half], wide_sin[:, :half]
        ),
        1,
    )
    latent_part = dot_nt(kv_grad, up_w)
    grad_kv_gain = jnp.sum(latent_part * latent_hat, axis=0)
    scaled_kv = kv_scale * latent_part
    latent_back = kv_inverse * (
        scaled_kv - latent_hat * jnp.mean(latent_hat * scaled_kv, axis=-1, keepdims=True)
    )
    down_grad = jnp.concatenate([latent_back, key_rope_part], -1).astype(BF16)
    normed_full, output = lax.optimization_barrier(
        (dot(query_grad, query_t) + dot(down_grad, down_t), gather_t(output_part))
    )
    pieces = [lay.over_t(part_for(normed_full, k).astype(BF16), k) for k in range(1, nt)]
    pieces[0], query_grad, kv_grad, down_grad = lax.optimization_barrier(
        (pieces[0], query_grad, kv_grad, down_grad)
    )
    normed_grad = part_for(normed_full, 0) + sum(piece.astype(F32) for piece in pieces)
    normed_grad, grad_plane[2], grad_home[1] = lax.optimization_barrier(
        (normed_grad, grad_plane[2], to_columns(grad_plane[1]))
    )
    attn_hat = own_part(hidden).astype(F32) * attn_inverse
    scaled_in = lax.dynamic_slice_in_dim(attn_scale, me_t * part, part, 0) * normed_grad
    attn_gain_part = jnp.sum(normed_grad * attn_hat, axis=0)
    input_grad = residual_grad + attn_inverse * (
        scaled_in - attn_hat * row_mean(attn_hat * scaled_in)
    )
    input_low, grad_plane[2] = lax.optimization_barrier((input_grad.astype(BF16), grad_plane[2]))
    grad_home[2] = to_columns(grad_plane[2])
    grad_expert_in, grad_expert_out = home_gradients(lay, ids, grad_home, f_loc, d_loc)
    grad_hidden = gather_t_direct(input_low)

    def spread(values):
        return lax.dynamic_update_slice(
            jnp.zeros((1, width), F32), values[None], (jnp.int32(0), me_t * part)
        )

    kv_gain_row = jnp.pad(
        grad_kv_gain.reshape(ndp, lat_loc), ((0, 0), (0, d_loc - lat_loc))
    ).reshape(1, width)
    gain_grads = jnp.concatenate([spread(attn_gain_part), spread(ffn_gain_part), kv_gain_row], 0)
    front_sum = sum_dp(
        jnp.concatenate(
            [
                by_owner(dot_tn(down_grad, normed_low)),
                by_owner(jnp.pad(gain_grads, ((0, 13), (0, 0)))),
                by_owner(router_part),
                by_owner(dot_tn(query_grad, normed_low)),
                by_owner(grad_out_w),
                dot_tn(latent_low, kv_grad).astype(BF16).reshape(ndp, -1, d_loc),
            ],
            1,
        )
    )
    own_sum = front_sum[: down_rows + EXPERTS]
    own_low = own_sum.astype(BF16)
    for k in range(1, nt):
        own_sum = own_sum + lay.over_t(own_low, k).astype(F32)
    at = down_rows + 2 * EXPERTS
    return (
        output,
        grad_hidden,
        own_sum[down_rows],
        jnp.transpose(by_head(front_sum[at : at + q_rows])),
        jnp.transpose(own_sum[:down_rows]),
        own_sum[down_rows + 2, :lat_loc],
        front_sum[at + q_rows + out_rows :].reshape(w_kv_up.shape),
        front_sum[at + q_rows : at + q_rows + out_rows],
        own_sum[down_rows + 1],
        jnp.transpose(front_sum[down_rows + EXPERTS : at]),
        grad_expert_in,
        grad_expert_out,
        jnp.swapaxes(shared_sum[: 2 * ffs].reshape(2, ffs, d_loc), 1, 2),
        shared_sum[2 * ffs :],
    )


def solution(mesh):
    return jax.shard_map(
        functools.partial(body, Layout(mesh.shape["dp"], mesh.shape["tensor"])),
        mesh=mesh,
        in_specs=(
            P("dp", None),
            P("dp"),
            P("dp", None),
            P("dp"),
            P("dp", "tensor"),
            P("dp", None),
            P("dp"),
            P("dp", "tensor"),
            P("tensor", "dp"),
            P("dp"),
            P("dp", None),
            P(None, None, "dp", "tensor"),
            P(None, "tensor", "dp"),
            P(None, "dp", "tensor"),
            P("tensor", "dp"),
            P("dp", None),
        ),
        out_specs=(
            P("dp", None),
            P("dp", None),
            P("dp"),
            P("dp", "tensor"),
            P("dp", None),
            P("dp"),
            P("dp", "tensor"),
            P("tensor", "dp"),
            P("dp"),
            P("dp", None),
            P(None, None, "dp", "tensor"),
            P(None, "tensor", "dp"),
            P(None, "dp", "tensor"),
            P("tensor", "dp"),
        ),
        check_vma=False,
    )
```

```python
import functools
import math

import jax
import jax.numpy as jnp
from jax import lax
from jax.experimental import pallas as pl
from jax.experimental.pallas import tpu as pltpu
from jax.sharding import PartitionSpec as P

NOPE = 128
ROPE = 64
VDIM = 128
LATENT = 512
TOP = 6
EXPERTS = 16
CAP = 512

EPSILON = 1e-06
NEGATIVE = -1e30
F32 = jnp.float32
BF16 = jnp.bfloat16


def dot(a, b):
    return jnp.dot(a, b, preferred_element_type=F32)


def dot_nt(a, b):
    return lax.dot_general(a, b, (((1,), (1,)), ((), ())), preferred_element_type=F32)


def dot_tn(a, b):
    return lax.dot_general(a, b, (((0,), (0,)), ((), ())), preferred_element_type=F32)


def rotate(first, second, cosine, sine):
    return first * cosine - second * sine, second * cosine + first * sine


def rotate_back(first, second, cosine, sine):
    return first * cosine + second * sine, second * cosine - first * sine


def angle_tables(rows_count):
    positions = jnp.arange(rows_count, dtype=F32)
    freqs = jnp.exp(jnp.arange(ROPE // 2, dtype=F32) * (-2.0 * math.log(10000.0) / ROPE))
    angles = positions[:, None] * freqs[None, :]
    return (jnp.cos(angles), jnp.sin(angles))


def inverse_rms(values):
    return lax.rsqrt(jnp.mean(values * values, axis=-1, keepdims=True) + EPSILON)


class Layout:
    def __init__(self, n_dp, n_tensor):
        self.dp, self.t = n_dp, n_tensor
        self.q = n_dp * n_tensor // EXPERTS
        self.z = n_dp // self.q
        if self.z * self.t != EXPERTS or self.z * self.q != n_dp:
            raise ValueError("mesh")
        self.z_groups = [[c + self.q * z for z in range(self.z)] for c in range(self.q)]

    def over_t(self, values, k):
        if k == 0:
            return values
        return lax.ppermute(values, "tensor", [(i, i ^ k) for i in range(self.t)])

    def over_z(self, values, k):
        if k == 0:
            return values
        return lax.ppermute(values, "dp", [(d, d ^ (k * self.q)) for d in range(self.dp)])

    def over_c(self, values, k):
        if k == 0:
            return values
        return lax.ppermute(values, "dp", [(d, d ^ k) for d in range(self.dp)])


def lay_out_weights(lay, ids, stacks, f_loc, d_loc, width):
    ffe = f_loc * lay.t
    count = len(stacks) // lay.q

    def kernel(ids_ref, *refs):
        for kc in range(lay.q):
            columns = pl.ds(pl.multiple_of((ids_ref[1] ^ kc) * d_loc, 128), d_loc)
            for g in range(count):
                refs[-1][g, :, columns] = refs[count * kc + g][0]

    own = pl.pallas_call(
        kernel,
        out_shape=jax.ShapeDtypeStruct((count, ffe, width), BF16),
        grid_spec=pltpu.PrefetchScalarGridSpec(
            num_scalar_prefetch=1,
            grid=(lay.t, lay.z),
            in_specs=[
                pl.BlockSpec(
                    (1, f_loc, d_loc), lambda kt, kz, ids: ((kz ^ ids[0]) * lay.t + kt, 0, 0)
                )
            ]
            * len(stacks),
            out_specs=pl.BlockSpec(
                (count, f_loc, lay.q * d_loc), lambda kt, kz, ids: (0, kt, kz)
            ),
        ),
        cost_estimate=pl.CostEstimate(
            flops=0, bytes_accessed=4 * count * ffe * width, transcendentals=0
        ),
        compiler_params=pltpu.CompilerParams(vmem_limit_bytes=32 << 20),
        name="lay_out_weights",
    )(ids, *stacks)
    return own.reshape(count * ffe, width)


def take_apart(lay, ids, grad_in, grad_out, f_loc, d_loc, width):
    ffe = f_loc * lay.t

    def kernel(ids_ref, in_ref, out_ref, *targets):
        for kc in range(lay.q):
            columns = pl.ds(pl.multiple_of((ids_ref[1] ^ kc) * d_loc, 128), d_loc)
            for g in range(2):
                targets[3 * kc + g][0] = in_ref[g, :, columns]
            targets[3 * kc + 2][0] = out_ref[:, columns]

    shape = jax.ShapeDtypeStruct((lay.t * lay.z, f_loc, d_loc), BF16)
    spec = pl.BlockSpec((1, f_loc, d_loc), lambda kt, kz, ids: (kz * lay.t + kt, 0, 0))
    return pl.pallas_call(
        kernel,
        out_shape=(shape,) * (3 * lay.q),
        grid_spec=pltpu.PrefetchScalarGridSpec(
            num_scalar_prefetch=1,
            grid=(lay.t, lay.z),
            in_specs=[
                pl.BlockSpec((2, f_loc, lay.q * d_loc), lambda kt, kz, ids: (0, kt, kz)),
                pl.BlockSpec((f_loc, lay.q * d_loc), lambda kt, kz, ids: (kt, kz)),
            ],
            out_specs=(spec,) * (3 * lay.q),
        ),
        cost_estimate=pl.CostEstimate(
            flops=0, bytes_accessed=12 * ffe * width, transcendentals=0
        ),
        compiler_params=pltpu.CompilerParams(vmem_limit_bytes=32 << 20),
        name="take_apart",
    )(ids, grad_in.reshape(2, ffe, width), grad_out)


def home_gradients(lay, ids, parts, f_loc, d_loc):
    def kernel(ids_ref, *refs):
        sources, (in_ref, out_ref) = refs[: 3 * lay.t], refs[3 * lay.t :]
        for k in range(lay.t):

            @pl.when((pl.program_id(1) ^ ids_ref[2]) == k)
            def _(k=k):
                for g in range(2):
                    in_ref[0, g] = sources[g * lay.t + k][0].astype(F32)
                out_ref[0] = sources[2 * lay.t + k][0].astype(F32)

    grad_in, grad_out = pl.pallas_call(
        kernel,
        out_shape=(
            jax.ShapeDtypeStruct((EXPERTS, 2, f_loc, d_loc), F32),
            jax.ShapeDtypeStruct((EXPERTS, f_loc, d_loc), F32),
        ),
        grid_spec=pltpu.PrefetchScalarGridSpec(
            num_scalar_prefetch=1,
            grid=(lay.z, lay.t),
            in_specs=[pl.BlockSpec((1, f_loc, d_loc), lambda z, t, ids: (z, 0, 0))] * (3 * lay.t),
            out_specs=(
                pl.BlockSpec((1, 2, f_loc, d_loc), lambda z, t, ids: (z * lay.t + t, 0, 0, 0)),
                pl.BlockSpec((1, f_loc, d_loc), lambda z, t, ids: (z * lay.t + t, 0, 0)),
            ),
        ),
        cost_estimate=pl.CostEstimate(
            flops=0, bytes_accessed=18 * EXPERTS * f_loc * d_loc, transcendentals=0
        ),
        compiler_params=pltpu.CompilerParams(vmem_limit_bytes=32 << 20),
        name="home_gradients",
    )(ids, *[piece for part in parts for piece in part])
    return jnp.swapaxes(grad_in, 2, 3), grad_out


def join_columns(parts, me, count):
    rows, part = parts[0].shape
    block = min(512, rows)

    def kernel(me_ref, *refs):
        for k in range(count):

            @pl.when(pl.program_id(1) == k)
            def _(k=k):
                refs[count][...] = refs[k][...]

    return pl.pallas_call(
        kernel,
        out_shape=jax.ShapeDtypeStruct((rows, count * part), parts[0].dtype),
        grid_spec=pltpu.PrefetchScalarGridSpec(
            num_scalar_prefetch=1,
            grid=(rows // block, count),
            in_specs=[pl.BlockSpec((block, part), lambda i, k, me: (i, 0))] * count,
            out_specs=pl.BlockSpec((block, part), lambda i, k, me: (i, me[0] ^ k)),
        ),
        cost_estimate=pl.CostEstimate(
            flops=0, bytes_accessed=4 * rows * part * count, transcendentals=0
        ),
        name="join_columns",
    )(me.reshape(1).astype(jnp.int32), *parts)


def score_block(q_ref, r_ref, k_ref, kr_ref, head, step, keys, block, length, scale):
    half = r_ref.shape[1] // 2
    lanes = lax.broadcasted_iota(jnp.int32, r_ref.shape, 1) % half // (ROPE // 2)
    turned = jnp.where(lanes == head, r_ref[...], jnp.zeros_like(r_ref))
    raw = lax.dot_general(
        q_ref[...], k_ref[:keys], (((1,), (1,)), ((), ())), preferred_element_type=F32
    ) + lax.dot_general(
        turned, kr_ref[:keys], (((1,), (1,)), ((), ())), preferred_element_type=F32
    )
    rows = lax.broadcasted_iota(jnp.int32, raw.shape, 0) + step * block
    cols = lax.broadcasted_iota(jnp.int32, raw.shape, 1)
    allowed = (cols <= rows) & (cols < length)
    return jnp.where(allowed, raw * scale, NEGATIVE), turned


def attend(length, query, query_rope, kv, key_rope, heads, scale):
    rows = query.shape[0]
    block = min(256, rows)
    steps = rows // block

    def kernel(len_ref, q_ref, r_ref, k_ref, v_ref, kr_ref, o_ref, total_ref):
        head, step = pl.program_id(0), pl.program_id(1)
        for n in range(steps):

            @pl.when(step == n)
            def _(n=n):
                keys = (n + 1) * block
                scores, _ = score_block(
                    q_ref, r_ref, k_ref, kr_ref, head, n, keys, block, len_ref[0], scale
                )
                highest = jnp.max(scores, axis=-1, keepdims=True)
                expo = jnp.exp(scores - highest)
                totals = jnp.sum(expo, axis=-1, keepdims=True)
                weights = (expo * (1.0 / totals)).astype(BF16)
                o_ref[...] = dot(weights, v_ref[:keys]).astype(BF16)
                total_ref[0] = jnp.broadcast_to(highest + jnp.log(totals), (block, 128))

    return pl.pallas_call(
        kernel,
        out_shape=(
            jax.ShapeDtypeStruct((rows, heads * VDIM), BF16),
            jax.ShapeDtypeStruct((heads, rows, 128), F32),
        ),
        grid_spec=pltpu.PrefetchScalarGridSpec(
            num_scalar_prefetch=1,
            grid=(heads, steps),
            in_specs=[
                pl.BlockSpec((block, NOPE), lambda h, i, n: (i, h)),
                pl.BlockSpec((block, query_rope.shape[1]), lambda h, i, n: (i, 0)),
                pl.BlockSpec((rows, NOPE), lambda h, i, n: (0, 2 * h)),
                pl.BlockSpec((rows, VDIM), lambda h, i, n: (0, 2 * h + 1)),
                pl.BlockSpec((rows, key_rope.shape[1]), lambda h, i, n: (0, 0)),
            ],
            out_specs=(
                pl.BlockSpec((block, VDIM), lambda h, i, n: (i, h)),
                pl.BlockSpec((1, block, 128), lambda h, i, n: (h, i, 0)),
            ),
        ),
        cost_estimate=pl.CostEstimate(
            flops=heads * rows * rows * 512,
            bytes_accessed=8 * rows * heads * 512,
            transcendentals=heads * rows * rows,
        ),
        compiler_params=pltpu.CompilerParams(vmem_limit_bytes=32 << 20),
        name="attend",
    )(length, query, query_rope, kv, kv, key_rope)


def attend_back(length, query, query_rope, kv, key_rope, out_grad, log_totals, heads, scale):
    rows = query.shape[0]
    block = min(256, rows)
    steps = rows // block
    turned_cols = query_rope.shape[1]

    def kernel(
        len_ref, q_ref, r_ref, k_ref, v_ref, kr_ref, do_ref, total_ref,
        dq_ref, dr_ref, dkv_ref, dkr_ref, dk_acc, dv_acc,
    ):
        head, step = pl.program_id(0), pl.program_id(1)

        @pl.when(step == 0)
        def _():
            dk_acc[...] = jnp.zeros_like(dk_acc)
            dv_acc[...] = jnp.zeros_like(dv_acc)

        @pl.when((step == 0) & (head == 0))
        def _():
            dr_ref[...] = jnp.zeros_like(dr_ref)
            dkr_ref[...] = jnp.zeros_like(dkr_ref)

        for n in range(steps):

            @pl.when(step == n)
            def _(n=n):
                keys = (n + 1) * block
                scores, turned = score_block(
                    q_ref, r_ref, k_ref, kr_ref, head, n, keys, block, len_ref[0], scale
                )
                probs = jnp.exp(scores - total_ref[0][:, :1])
                prob_grad = lax.dot_general(
                    do_ref[...], v_ref[:keys], (((1,), (1,)), ((), ())), preferred_element_type=F32
                )
                centre = jnp.sum(probs * prob_grad, axis=-1, keepdims=True)
                score_grad = (probs * (prob_grad - centre)).astype(BF16)
                probs_low = probs.astype(BF16)
                dq_ref[...] = (dot(score_grad, k_ref[:keys]) * scale).astype(BF16)
                half = turned_cols // 2
                lanes = lax.broadcasted_iota(jnp.int32, (block, turned_cols), 1)
                lanes = lanes % half // (ROPE // 2)
                turned_grad = dot(score_grad, kr_ref[:keys]) * scale
                dr_ref[n * block : keys] += jnp.where(lanes == head, turned_grad, 0.0)
                dk_acc[:keys] += dot_tn(score_grad, q_ref[...]) * scale
                dkr_ref[:keys] += dot_tn(score_grad, turned) * scale
                dv_acc[:keys] += dot_tn(probs_low, do_ref[...])

        @pl.when(step == steps - 1)
        def _():
            dkv_ref[:, :NOPE] = dk_acc[...].astype(BF16)
            dkv_ref[:, NOPE:] = dv_acc[...].astype(BF16)

    return pl.pallas_call(
        kernel,
        out_shape=(
            jax.ShapeDtypeStruct((rows, heads * NOPE), BF16),
            jax.ShapeDtypeStruct((rows, turned_cols), F32),
            jax.ShapeDtypeStruct((rows, heads * (NOPE + VDIM)), BF16),
            jax.ShapeDtypeStruct((rows, turned_cols), F32),
        ),
        grid_spec=pltpu.PrefetchScalarGridSpec(
            num_scalar_prefetch=1,
            grid=(heads, steps),
            in_specs=[
                pl.BlockSpec((block, NOPE), lambda h, i, n: (i, h)),
                pl.BlockSpec((block, turned_cols), lambda h, i, n: (i, 0)),
                pl.BlockSpec((rows, NOPE), lambda h, i, n: (0, 2 * h)),
                pl.BlockSpec((rows, VDIM), lambda h, i, n: (0, 2 * h + 1)),
                pl.BlockSpec((rows, turned_cols), lambda h, i, n: (0, 0)),
                pl.BlockSpec((block, VDIM), lambda h, i, n: (i, h)),
                pl.BlockSpec((1, block, 128), lambda h, i, n: (h, i, 0)),
            ],
            out_specs=(
                pl.BlockSpec((block, NOPE), lambda h, i, n: (i, h)),
                pl.BlockSpec((rows, turned_cols), lambda h, i, n: (0, 0)),
                pl.BlockSpec((rows, NOPE + VDIM), lambda h, i, n: (0, h)),
                pl.BlockSpec((rows, turned_cols), lambda h, i, n: (0, 0)),
            ),
            scratch_shapes=[pltpu.VMEM((rows, NOPE), F32), pltpu.VMEM((rows, VDIM), F32)],
        ),
        cost_estimate=pl.CostEstimate(
            flops=heads * rows * rows * 1600,
            bytes_accessed=16 * rows * heads * 512,
            transcendentals=heads * rows * rows,
        ),
        compiler_params=pltpu.CompilerParams(vmem_limit_bytes=40 << 20),
        name="attend_back",
    )(length, query, query_rope, kv, kv, key_rope, out_grad, log_totals)


def in_order(values, me, count):
    zero = jnp.zeros_like(values[0])
    ordered = []
    for j in range(count):
        total = zero
        for k in range(count):
            total = jnp.where((me ^ k) == j, values[k], total)
        ordered.append(total)
    return jnp.stack(ordered)


def body(
    lay,
    hidden,
    lengths,
    routes,
    attn_gain,
    w_query,
    w_kv_down,
    kv_gain,
    w_kv_up,
    w_out,
    ffn_gain,
    w_router,
    w_expert_in,
    w_expert_out,
    w_shared_in,
    w_shared_out,
    cotangent,
):
    rows, width = hidden.shape
    nz, nt, nq, ndp = lay.z, lay.t, lay.q, lay.dp
    me_dp = lax.axis_index("dp")
    me_t = lax.axis_index("tensor")
    me_z = me_dp // nq
    me_c = me_dp % nq
    part = width // nt
    d_loc = w_query.shape[0]
    f_loc = w_expert_out.shape[1]
    ffe = f_loc * nt
    heads = w_query.shape[1] // (NOPE + ROPE)
    score_scale = (NOPE + ROPE) ** (-0.5)

    def own_part(values):
        return lax.dynamic_slice_in_dim(values, me_t * part, part, 1)

    def gather_z(values):
        return lax.all_gather(values, "dp", axis=0, tiled=False, axis_index_groups=lay.z_groups)

    def scatter_z(values):
        return lax.psum_scatter(
            values, "dp", scatter_dimension=0, tiled=False, axis_index_groups=lay.z_groups
        )

    def gather_t(values):
        return lax.all_gather(values, "tensor", axis=1, tiled=True)

    def scatter_t(values):
        return lax.psum_scatter(
            values.astype(BF16), "tensor", scatter_dimension=1, tiled=True
        ).astype(F32)

    def swap_t(values):
        return lax.all_to_all(values, "tensor", split_axis=0, concat_axis=0, tiled=True)

    def swap_z(values):
        return lax.all_to_all(
            values,
            "dp",
            split_axis=0,
            concat_axis=0,
            axis_index_groups=lay.z_groups,
            tiled=True,
        )

    def gather_t_direct(values):
        return join_columns([lay.over_t(values, k) for k in range(nt)], me_t, nt)

    def part_for(values, k):
        return lax.dynamic_slice_in_dim(values, (me_t ^ k) * part, part, 1)

    def scatter_t_direct(values):
        total = part_for(values, 0)
        for k in range(1, nt):
            total = total + lay.over_t(part_for(values, k).astype(BF16), k).astype(F32)
        return total

    ids = jnp.stack([me_z, me_c, me_t]).astype(jnp.int32)

    packed = jnp.concatenate(
        [jnp.swapaxes(w_expert_in, 2, 3), w_expert_out[:, None]], 1
    ).reshape(nz, nt, 3, f_loc, d_loc)
    by_column = swap_t(jnp.swapaxes(packed, 0, 1))

    lat_loc = kv_gain.shape[0]
    q_rows, down_rows, out_rows = w_query.shape[1], w_kv_down.shape[1], w_out.shape[0]
    half = ROPE // 2

    def by_kind(turned):
        split = turned.reshape(heads, NOPE + ROPE, -1)
        return jnp.concatenate(
            [
                split[:, :NOPE].reshape(heads * NOPE, -1),
                split[:, NOPE : NOPE + half].reshape(heads * half, -1),
                split[:, NOPE + half :].reshape(heads * half, -1),
            ],
            0,
        )

    def by_head(rows_in):
        nope = rows_in[: heads * NOPE].reshape(heads, NOPE, -1)
        first = rows_in[heads * NOPE : heads * (NOPE + half)].reshape(heads, half, -1)
        second = rows_in[heads * (NOPE + half) :].reshape(heads, half, -1)
        return jnp.concatenate([nope, first, second], 1).reshape(heads * (NOPE + ROPE), -1)

    gains = jnp.stack([attn_gain, ffn_gain, jnp.pad(kv_gain, (0, d_loc - lat_loc))])
    front_pack = jnp.concatenate(
        [
            by_kind(jnp.transpose(w_query)),
            jnp.transpose(w_kv_down),
            jnp.transpose(w_router),
            jnp.pad(gains, ((0, 13), (0, 0))),
            w_out,
            w_kv_up.reshape(-1, d_loc),
        ],
        0,
    )
    front = lax.all_gather(front_pack, "dp", axis=0, tiled=False)

    valid_length = lengths[0]
    valid_rows = lax.broadcasted_iota(jnp.int32, (rows, 1), 0) < valid_length
    cot_low = jnp.where(valid_rows, cotangent, jnp.zeros_like(cotangent))
    cot_part = own_part(cot_low)
    route_own = jnp.pad(jnp.transpose(routes), ((0, -TOP % 8), (0, 0)), constant_values=-1)
    route_all = in_order([lay.over_z(route_own, k) for k in range(nz)], me_z, nz)
    inputs = hidden.astype(F32)
    attn_inverse = inverse_rms(inputs)
    cosine, sine = angle_tables(rows)
    wide_cos, wide_sin = jnp.tile(cosine, (1, heads)), jnp.tile(sine, (1, heads))
    front, attn_inverse, wide_cos, wide_sin, route_all = lax.optimization_barrier(
        (front, attn_inverse, wide_cos, wide_sin, route_all)
    )

    plane_ids = me_z * nt + jnp.arange(nt, dtype=jnp.int32)
    member = jnp.any(route_all[:, :, :, None] == plane_ids[None, None, None, :], axis=1)
    row_ids = lax.broadcasted_iota(jnp.int32, (rows, rows), 0)
    col_ids = lax.broadcasted_iota(jnp.int32, (rows, rows), 1)
    before = (col_ids < row_ids).astype(BF16)
    position = jnp.einsum("ij,sje->sei", before, member.astype(BF16), preferred_element_type=F32)
    key = jnp.where(jnp.swapaxes(member, 1, 2), position.astype(jnp.int32), -1)
    slots_iota = lax.broadcasted_iota(jnp.int32, (1, 1, CAP, 1), 2)

    def place_of(keys):
        return (keys[:, :, None, :] == slots_iota).astype(BF16)

    place = place_of(key)
    own_key = lax.dynamic_index_in_dim(key, me_t, 1, keepdims=False)
    own_place = own_key[:, None, :] == slots_iota[0]

    def pick_rows(values):
        picked = jnp.einsum("sepk,skd->espd", place, values, preferred_element_type=F32)
        return picked.astype(BF16).reshape(nt, nz * CAP, part)

    def send_out(picked):
        return jnp.swapaxes(swap_t(picked), 0, 1).reshape(nz * CAP, width)

    def send_back(values):
        return swap_t(jnp.swapaxes(values.reshape(nz * CAP, nt, part), 0, 1))

    def combine(parts):
        parts = parts.reshape(nt, nz, CAP, part)
        summed = jnp.einsum("sepk,espd->skd", place, parts, preferred_element_type=F32)
        return summed.astype(BF16)


    def rows_of(first, count):
        return jnp.swapaxes(front[:, first : first + count], 0, 1).reshape(count, width)

    query_t = rows_of(0, q_rows)
    down_t = rows_of(q_rows, down_rows)
    at = q_rows + down_rows
    router_t = rows_of(at, EXPERTS)
    gain_attn = front[:, at + EXPERTS].reshape(-1)
    gain_ffn = front[:, at + EXPERTS + 1].reshape(-1)
    gain_kv = front[:, at + EXPERTS + 2, :lat_loc].reshape(-1)
    at = at + 2 * EXPERTS
    out_w = rows_of(at, out_rows)
    up_w = front[:, at + out_rows :].reshape(LATENT, heads * (NOPE + VDIM))

    attn_scale = gain_attn.astype(F32)
    normed_low = (inputs * attn_inverse * attn_scale).astype(BF16)
    query = dot_nt(normed_low, query_t)
    nope_cols = heads * NOPE
    query_nope = query[:, :nope_cols].astype(BF16)
    query_rope = jnp.concatenate(
        rotate(
            query[:, nope_cols : nope_cols + heads * half],
            query[:, nope_cols + heads * half :],
            wide_cos,
            wide_sin,
        ),
        1,
    ).astype(BF16)
    latent_all = dot_nt(normed_low, down_t)
    latent_all, by_column = lax.optimization_barrier((latent_all, by_column))
    by_column = jnp.transpose(by_column, (2, 1, 0, 3, 4))
    by_plane = [swap_z(by_column[g]) for g in range(2)]
    latent = latent_all[:, :LATENT]
    kv_inverse = inverse_rms(latent)
    latent_hat = latent * kv_inverse
    kv_scale = gain_kv.astype(F32)
    latent_low = (latent_hat * kv_scale).astype(BF16)
    key_turned = jnp.concatenate(
        rotate(
            latent_all[:, LATENT : LATENT + half],
            latent_all[:, LATENT + half :],
            wide_cos[:, :half],
            wide_sin[:, :half],
        ),
        1,
    ).astype(BF16)
    copies = (2 * half, 2 * heads * half)
    to_col = lax.broadcasted_iota(jnp.int32, copies, 1)
    from_col = to_col // (heads * half) * half + to_col % half
    repeat = (lax.broadcasted_iota(jnp.int32, copies, 0) == from_col).astype(BF16)
    key_rope = dot(key_turned, repeat).astype(BF16)
    keys_values = dot(latent_low, up_w).astype(BF16)
    attended_low, log_totals = attend(
        lengths, query_nope, query_rope, keys_values, key_rope, heads, score_scale
    )
    attn_part, by_plane[0] = lax.optimization_barrier((dot(attended_low, out_w), by_plane[0]))
    attn_sum = scatter_t(attn_part)
    residual = own_part(hidden).astype(F32) + attn_sum

    def row_mean(values):
        partial = jnp.sum(values, axis=-1).reshape(-1, 128)
        return lax.psum(partial, "tensor").reshape(-1, 1) * (1.0 / width)

    ffn_inverse = lax.rsqrt(row_mean(residual * residual) + EPSILON)
    ffn_hat = residual * ffn_inverse
    ffn_scale = lax.dynamic_slice_in_dim(gain_ffn, me_t * part, part, 0).astype(F32)
    ffn_part = (ffn_hat * ffn_scale).astype(BF16)

    ffn_part, by_plane[1] = lax.optimization_barrier((ffn_part, by_plane[1]))
    ffn_all = gather_z(ffn_part)
    ffn_low = gather_t_direct(ffn_part)
    ffn_all, ffn_low, cot_ready = lax.optimization_barrier((ffn_all, ffn_low, cot_part))
    picked, by_plane[0], by_plane[1] = lax.optimization_barrier(
        (pick_rows(ffn_all), by_plane[0], by_plane[1])
    )
    expert_rows = send_out(picked)
    shared_pack = jnp.concatenate(
        [jnp.swapaxes(w_shared_in, 1, 2).reshape(-1, d_loc), w_shared_out], 0
    )
    def own_weights(matrices, order):
        pieces = [by_plane[g].reshape(nz * nt, f_loc, d_loc) for g in matrices]
        stacks = [lay.over_c(piece, k) for k in range(nq) for piece in pieces]
        return lay_out_weights(lay, order, stacks, f_loc, d_loc, width)

    own_in = own_weights((0, 1), ids * jnp.array([0, 1, 1], jnp.int32))
    cot_all, last_column, own_in = lax.optimization_barrier(
        (gather_z(cot_ready), by_column[2], own_in)
    )
    by_plane.append(
        jnp.stack(
            [
                lay.over_z(lax.dynamic_index_in_dim(last_column, me_z ^ k, 0, keepdims=False), k)
                for k in range(nz)
            ]
        )
    )

    by_plane[2], shared_pack, cot_picked = lax.optimization_barrier(
        (by_plane[2], shared_pack, pick_rows(cot_all))
    )
    cot_rows = send_out(cot_picked)
    shared_all = lax.all_gather(shared_pack, "dp", axis=0, tiled=False)
    own_out = own_weights((2,), ids)
    router_probs = jax.nn.softmax(dot_nt(ffn_low, router_t), axis=-1)
    probs_turned = jnp.transpose(router_probs).reshape(EXPERTS, -1, 128)
    own_probs = in_order(
        [
            lay.over_z(
                lax.dynamic_index_in_dim(
                    probs_turned, (me_z ^ k) * nt + me_t, 0, keepdims=False
                ),
                k,
            )
            for k in range(nz)
        ],
        me_z,
        nz,
    ).reshape(nz, rows)
    gate_rows = jnp.sum(jnp.where(own_place, own_probs[:, None, :], 0.0), axis=-1).reshape(
        nz * CAP, 1
    )
    gate_up = dot_nt(expert_rows, own_in)
    gate_pre, up_pre = gate_up[:, :ffe], gate_up[:, ffe:]
    gate_sig = jax.nn.sigmoid(gate_pre)
    gate_silu = gate_pre * gate_sig
    active = (gate_silu * up_pre).astype(BF16)
    rows_out = (dot(active, own_out) * gate_rows).astype(BF16)
    rows_out, cot_rows, shared_all = lax.optimization_barrier((rows_out, cot_rows, shared_all))
    out_parts = send_back(rows_out)
    active_grad_raw = dot_nt(cot_rows, own_out)
    gate_grad = jnp.sum(active.astype(F32) * active_grad_raw, axis=-1).reshape(nz, CAP)
    active_grad = active_grad_raw * gate_rows
    pre_low = jnp.concatenate(
        [
            active_grad * up_pre * gate_sig * (1.0 + gate_pre * (1.0 - gate_sig)),
            active_grad * gate_silu,
        ],
        1,
    ).astype(BF16)
    gated_active = (active.astype(F32) * gate_rows).astype(BF16)
    ffs = w_shared_out.shape[0]
    shared_in = jnp.swapaxes(shared_all[:, : 2 * ffs], 0, 1).reshape(2 * ffs, width)
    shared_out = jnp.swapaxes(shared_all[:, 2 * ffs :], 0, 1).reshape(ffs, width)
    shared_pre = dot_nt(ffn_low, shared_in)
    shared_gate, shared_up = shared_pre[:, :ffs], shared_pre[:, ffs:]
    shared_sig = jax.nn.sigmoid(shared_gate)
    shared_silu = shared_gate * shared_sig
    shared_act = (shared_silu * shared_up).astype(BF16)
    shared_full = dot(shared_act, shared_out)
    shared_act_grad = dot_nt(cot_low, shared_out)
    shared_pre_grad = jnp.concatenate(
        [
            shared_act_grad * shared_up * shared_sig * (1.0 + shared_gate * (1.0 - shared_sig)),
            shared_act_grad * shared_silu,
        ],
        1,
    ).astype(BF16)
    grad_shared_in = dot_tn(shared_pre_grad, ffn_low)
    grad_shared_out = dot_tn(shared_act, cot_low)

    out_parts, pre_low, shared_full = lax.optimization_barrier((out_parts, pre_low, shared_full))
    rows_grad = dot(pre_low, own_in).astype(BF16)
    rows_grad, out_parts = lax.optimization_barrier((rows_grad, out_parts))
    grad_parts = send_back(rows_grad)
    rows_grad, shared_late = lax.optimization_barrier((rows_grad, shared_pre_grad))
    shared_grad_full = dot(shared_late, shared_in)
    routed, pre_low, gated_active = lax.optimization_barrier(
        (combine(out_parts), pre_low, gated_active)
    )
    routed = scatter_z(routed).astype(F32)
    token_grad = jnp.sum(jnp.where(own_place, gate_grad[:, :, None], 0.0), axis=1)
    token_grad = token_grad.reshape(nz, -1, 128)
    token_plane = jnp.stack(
        [
            lay.over_z(lax.dynamic_index_in_dim(token_grad, me_z ^ k, 0, keepdims=False), k)
            for k in range(nz)
        ]
    )
    token_home = jnp.stack([lay.over_t(token_plane, k) for k in range(nt)])
    experts = jnp.arange(EXPERTS, dtype=jnp.int32)
    came_from = (me_t ^ (experts % nt)) * nz + (me_z ^ (experts // nt))
    probs_grad = lax.dot_general(
        token_home.reshape(EXPERTS, rows),
        (experts[:, None] == came_from[None, :]).astype(F32),
        (((0,), (0,)), ((), ())),
        precision=lax.Precision.HIGHEST,
        preferred_element_type=F32,
    )

    grad_in_own = dot_tn(pre_low, expert_rows).astype(BF16)
    grad_out_own = dot_tn(gated_active, cot_rows).astype(BF16)
    grad_parts, grad_in_own, grad_out_own, probs_grad, shared_grad_full = lax.optimization_barrier(
        (grad_parts, grad_in_own, grad_out_own, probs_grad, shared_grad_full)
    )
    routed, shared_ready = lax.optimization_barrier(
        (
            routed,
            jnp.swapaxes(shared_grad_full.astype(BF16).reshape(rows, nt, part), 0, 1),
        )
    )
    shared_grad = jnp.sum(swap_t(shared_ready).astype(F32), axis=0)
    grad_pieces = take_apart(lay, ids, grad_in_own, grad_out_own, f_loc, d_loc, width)
    grad_pieces, shared_full = lax.optimization_barrier((grad_pieces, shared_full))
    shared_part = scatter_t(shared_full)
    routed_grad = scatter_z(combine(grad_parts)).astype(F32)
    grad_class = [
        sum(lay.over_c(grad_pieces[3 * k + g], k).astype(F32) for k in range(nq)).astype(BF16)
        for g in range(3)
    ]
    routed_grad, grad_class = lax.optimization_barrier((routed_grad, grad_class))
    grad_plane = [swap_z(grad_class[g].reshape(nz, nt, f_loc, d_loc)) for g in range(3)]

    logits_grad = router_probs * (
        probs_grad - jnp.sum(router_probs * probs_grad, axis=-1, keepdims=True)
    )
    router_part = lax.dot_general(
        logits_grad,
        ffn_low.astype(F32),
        (((0,), (0,)), ((), ())),
        precision=lax.Precision.HIGHEST,
        preferred_element_type=F32,
    )
    router_slice = lax.dynamic_slice_in_dim(router_t, me_t * part, part, 1)
    ffn_grad = (
        shared_grad
        + routed_grad
        + lax.dot_general(
            logits_grad,
            router_slice.astype(F32),
            (((1,), (0,)), ((), ())),
            precision=lax.Precision.HIGHEST,
            preferred_element_type=F32,
        )
    )
    scaled = ffn_scale * ffn_grad
    ffn_gain_part = jnp.sum(ffn_grad * ffn_hat, axis=0)
    residual_grad = cot_part.astype(F32) + ffn_inverse * (
        scaled - ffn_hat * row_mean(ffn_hat * scaled)
    )
    residual_ready, shared_part = lax.optimization_barrier(
        (residual_grad.astype(BF16), shared_part)
    )
    residual_low = gather_t(residual_ready)

    def sum_dp(values):
        return lax.psum_scatter(values, "dp", scatter_dimension=0, tiled=False).astype(F32)

    def by_owner(values):
        return jnp.swapaxes(values.astype(BF16).reshape(-1, ndp, d_loc), 0, 1)

    shared_grads = jnp.concatenate([by_owner(grad_shared_in), by_owner(grad_shared_out)], 1)
    output_part = lax.optimization_barrier((residual + routed + shared_part).astype(BF16))
    residual_low, shared_grads, grad_plane[0], output_part = lax.optimization_barrier(
        (residual_low, shared_grads, grad_plane[0], output_part)
    )
    grad_out_w = dot_tn(attended_low, residual_low)
    attended_grad = dot_nt(residual_low, out_w).astype(BF16)
    query_nope_grad, query_turned_grad, kv_grad, rope_grad = attend_back(
        lengths,
        query_nope,
        query_rope,
        keys_values,
        key_rope,
        attended_grad,
        log_totals,
        heads,
        score_scale,
    )
    def to_columns(values):
        return [
            lay.over_t(lax.dynamic_index_in_dim(values, me_t ^ k, 1, keepdims=False), k)
            for k in range(nt)
        ]

    grad_home = [to_columns(grad_plane[0]), None, None]
    query_turned_grad, grad_plane[1], grad_home[0], shared_grads = lax.optimization_barrier(
        (query_turned_grad, grad_plane[1], grad_home[0], shared_grads)
    )
    shared_sum = sum_dp(shared_grads)
    turned_first, turned_second = rotate_back(
        query_turned_grad[:, : heads * half], query_turned_grad[:, heads * half :], wide_cos, wide_sin
    )
    query_grad = jnp.concatenate(
        [query_nope_grad, turned_first.astype(BF16), turned_second.astype(BF16)], 1
    )
    rope_sum = rope_grad.reshape(rows, 2, heads, half).sum(2)
    key_rope_part = jnp.concatenate(
        rotate_back(
            rope_sum[:, 0], rope_sum[:, 1], wide_cos[:, :half], wide_sin[:, :half]
        ),
        1,
    )
    latent_part = dot_nt(kv_grad, up_w)
    grad_kv_gain = jnp.sum(latent_part * latent_hat, axis=0)
    scaled_kv = kv_scale * latent_part
    latent_back = kv_inverse * (
        scaled_kv - latent_hat * jnp.mean(latent_hat * scaled_kv, axis=-1, keepdims=True)
    )
    down_grad = jnp.concatenate([latent_back, key_rope_part], -1).astype(BF16)
    normed_full, output = lax.optimization_barrier(
        (dot(query_grad, query_t) + dot(down_grad, down_t), gather_t(output_part))
    )
    pieces = [lay.over_t(part_for(normed_full, k).astype(BF16), k) for k in range(1, nt)]
    pieces[0], query_grad, kv_grad, down_grad = lax.optimization_barrier(
        (pieces[0], query_grad, kv_grad, down_grad)
    )
    normed_grad = part_for(normed_full, 0) + sum(piece.astype(F32) for piece in pieces)
    normed_grad, grad_plane[2], grad_home[1] = lax.optimization_barrier(
        (normed_grad, grad_plane[2], to_columns(grad_plane[1]))
    )
    attn_hat = own_part(hidden).astype(F32) * attn_inverse
    scaled_in = lax.dynamic_slice_in_dim(attn_scale, me_t * part, part, 0) * normed_grad
    attn_gain_part = jnp.sum(normed_grad * attn_hat, axis=0)
    input_grad = residual_grad + attn_inverse * (
        scaled_in - attn_hat * row_mean(attn_hat * scaled_in)
    )
    input_low, grad_plane[2] = lax.optimization_barrier((input_grad.astype(BF16), grad_plane[2]))
    grad_home[2] = to_columns(grad_plane[2])
    grad_expert_in, grad_expert_out = home_gradients(lay, ids, grad_home, f_loc, d_loc)
    grad_hidden = gather_t_direct(input_low)

    def spread(values):
        return lax.dynamic_update_slice(
            jnp.zeros((1, width), F32), values[None], (jnp.int32(0), me_t * part)
        )

    kv_gain_row = jnp.pad(
        grad_kv_gain.reshape(ndp, lat_loc), ((0, 0), (0, d_loc - lat_loc))
    ).reshape(1, width)
    gain_grads = jnp.concatenate([spread(attn_gain_part), spread(ffn_gain_part), kv_gain_row], 0)
    front_sum = sum_dp(
        jnp.concatenate(
            [
                by_owner(dot_tn(down_grad, normed_low)),
                by_owner(jnp.pad(gain_grads, ((0, 13), (0, 0)))),
                by_owner(router_part),
                by_owner(dot_tn(query_grad, normed_low)),
                by_owner(grad_out_w),
                dot_tn(latent_low, kv_grad).astype(BF16).reshape(ndp, -1, d_loc),
            ],
            1,
        )
    )
    own_sum = front_sum[: down_rows + EXPERTS]
    own_low = own_sum.astype(BF16)
    for k in range(1, nt):
        own_sum = own_sum + lay.over_t(own_low, k).astype(F32)
    at = down_rows + 2 * EXPERTS
    return (
        output,
        grad_hidden,
        own_sum[down_rows],
        jnp.transpose(by_head(front_sum[at : at + q_rows])),
        jnp.transpose(own_sum[:down_rows]),
        own_sum[down_rows + 2, :lat_loc],
        front_sum[at + q_rows + out_rows :].reshape(w_kv_up.shape),
        front_sum[at + q_rows : at + q_rows + out_rows],
        own_sum[down_rows + 1],
        jnp.transpose(front_sum[down_rows + EXPERTS : at]),
        grad_expert_in,
        grad_expert_out,
        jnp.swapaxes(shared_sum[: 2 * ffs].reshape(2, ffs, d_loc), 1, 2),
        shared_sum[2 * ffs :],
    )


def solution(mesh):
    return jax.shard_map(
        functools.partial(body, Layout(mesh.shape["dp"], mesh.shape["tensor"])),
        mesh=mesh,
        in_specs=(
            P("dp", None),
            P("dp"),
            P("dp", None),
            P("dp"),
            P("dp", "tensor"),
            P("dp", None),
            P("dp"),
            P("dp", "tensor"),
            P("tensor", "dp"),
            P("dp"),
            P("dp", None),
            P(None, None, "dp", "tensor"),
            P(None, "tensor", "dp"),
            P(None, "dp", "tensor"),
            P("tensor", "dp"),
            P("dp", None),
        ),
        out_specs=(
            P("dp", None),
            P("dp", None),
            P("dp"),
            P("dp", "tensor"),
            P("dp", None),
            P("dp"),
            P("dp", "tensor"),
            P("tensor", "dp"),
            P("dp"),
            P("dp", None),
            P(None, None, "dp", "tensor"),
            P(None, "tensor", "dp"),
            P(None, "dp", "tensor"),
            P("tensor", "dp"),
        ),
        check_vma=False,
    )
```
